32 devices in a mesh: ctx: 16 (over z, x, core), wsh: 2 (over y).
Axes of the slice: x: 2, y: 2, z: 4, core: 2. Of those that a mesh axis runs over, the one named last changes fastest.
Arguments:
- tokens: bfloat16 [2, 4096, 1024], P('wsh', 'ctx'), may hold values from -6 to 6
- ln1_gain: bfloat16 [1024], P('wsh'), may hold values from 0.5 to 1.5
- ln1_bias: bfloat16 [1024], P('wsh'), may hold values from -1.25 to 1.25
- ln2_gain: bfloat16 [1024], P('wsh'), may hold values from 0.5 to 1.5
- ln2_bias: bfloat16 [1024], P('wsh'), may hold values from -1.25 to 1.25
- w_qkv: bfloat16 [1024, 3072], P('wsh'), may hold values from -0.1875 to 0.1875
- b_qkv: bfloat16 [3072], P('wsh'), may hold values from -0.625 to 0.625
- w_out: bfloat16 [1024, 1024], P('wsh'), may hold values from -2 to 2
- b_out: bfloat16 [1024], P('wsh'), may hold values from -3 to 3
- w_up: bfloat16 [1024, 4096], P('wsh'), may hold values from -0.1875 to 0.1875
- b_up: bfloat16 [4096], P('wsh'), may hold values from -3 to 3
- w_down: bfloat16 [4096, 1024], P('wsh'), may hold values from -0.09375 to 0.09375
- b_down: bfloat16 [1024], P('wsh'), may hold values from -3 to 3
- lengths: int32 [2], P('wsh'), may hold values from 1024 to 4096, as said below
- block_map: int32 [32], replicated, may hold values from 0 to 31, as said below
- cotangent: bfloat16 [2, 4096, 1024], P('wsh', 'ctx'), may hold values from -6 to 6
Outputs:
- output: bfloat16 [2, 4096, 1024], P('wsh', 'ctx')
- grad_tokens: float32 [2, 4096, 1024], P('wsh', 'ctx')
- grad_ln1_gain: float32 [1024], P('wsh')
- grad_ln1_bias: float32 [1024], P('wsh')
- grad_ln2_gain: float32 [1024], P('wsh')
- grad_ln2_bias: float32 [1024], P('wsh')
- grad_w_qkv: float32 [1024, 3072], P('wsh')
- grad_b_qkv: float32 [3072], P('wsh')
- grad_w_out: float32 [1024, 1024], P('wsh')
- grad_b_out: float32 [1024], P('wsh')
- grad_w_up: float32 [1024, 4096], P('wsh')
- grad_b_up: float32 [4096], P('wsh')
- grad_w_down: float32 [4096, 1024], P('wsh')
- grad_b_down: float32 [1024], P('wsh')
The draws below stay inside these ranges and needn't reach their ends.
Inputs may be any that keep to these rules, and one draw needn't show every extreme that they name: `lengths`: some slot is full (4096 valid tokens) in every draw; tokens at positions from a slot's length on are padding. `block_map`: A permutation of the 32 position blocks; stored blocks 2c and 2c + 1 hold two blocks whose indices sum to 31.
All inputs are finite; a program needn't handle non-finite values.
Results may differ from the reference program's by a relative error of at most 0.019.
Values may be sent and summed in bfloat16 or wider, within the bound.
No kernel may reach another device: no remote copies, remote signals or barrier semaphores. Data moves between devices by JAX's collectives and lax.ppermute only.
A program may use at most 320 MiB of HBM per device.

```python
import math
import jax
import jax.numpy as jnp
from jax import lax

D = 1024
H = 16
HD = 64
FF = 4096
ROT = 16
HB = 128
SEQ = 4096
SLOTS = 2
BLOCKS = 32


def draw_lengths(key, part):
    drawn = jax.random.randint(jax.random.fold_in(key, 11), (SLOTS,), SEQ // 4, SEQ + 1)
    full_slot = jax.random.randint(jax.random.fold_in(key, 12), (), 0, SLOTS)
    return jnp.where(jnp.arange(SLOTS) == full_slot, SEQ, drawn).astype(jnp.int32)


def draw_block_map(key, part):
    pair_count = BLOCKS // 2
    pairs = jax.random.permutation(jax.random.fold_in(key, 21), pair_count).astype(jnp.int32)
    flips = jax.random.randint(jax.random.fold_in(key, 22), (pair_count,), 0, 2).astype(jnp.int32)
    leading = jnp.where(flips == 1, BLOCKS - 1 - pairs, pairs)
    trailing = BLOCKS - 1 - leading
    return jnp.stack([leading, trailing], axis=1).reshape(BLOCKS).astype(jnp.int32)


def block_scale(stream_key, shape, shards, least, top_value):
    def one(position, blocks):
        heights = jax.random.uniform(jax.random.fold_in(jax.random.fold_in(stream_key, 6), position), (blocks,), jnp.float32, least / len(shards), top_value / len(shards))
        return jnp.repeat(jnp.exp(heights), shape[position] // blocks).reshape((-1,) + (1,) * (len(shape) - position - 1))

    factor_of = one(*shards[0])
    for cut in shards[1:]:
        factor_of = factor_of * one(*cut)
    return factor_of


def gaussian(own_key, extent, deviation, limit, cuts=(), kind=jnp.bfloat16):
    level = block_scale(own_key, extent, cuts, -0.22, 0.18) if cuts else 1.0
    values = jax.random.normal(own_key, extent, jnp.float32) * deviation * level
    return jnp.minimum(jnp.maximum(values, -limit), limit).astype(kind)


def setup_inputs(seed: int = 0) -> dict:
    key_of = jax.random.split(jax.random.key(seed), 17)
    return {
        "tokens": gaussian(key_of[0], (SLOTS, SEQ, D), 1.0, 6.0, ((0, 2), (1, 16))),
        "ln1_gain": jnp.clip(1.0 + 0.1 * jax.random.normal(key_of[1], (D,), jnp.float32), 0.5, 1.5).astype(jnp.bfloat16),
        "ln1_bias": gaussian(key_of[2], (D,), 0.2, 1.25, ((0, 2),)),
        "ln2_gain": jnp.clip(1.0 + 0.1 * jax.random.normal(key_of[3], (D,), jnp.float32), 0.5, 1.5).astype(jnp.bfloat16),
        "ln2_bias": gaussian(key_of[4], (D,), 0.2, 1.25, ((0, 2),)),
        "w_qkv": gaussian(key_of[5], (D, 3 * D), D ** -0.5, 0.1875, ((0, 2),)),
        "b_qkv": gaussian(key_of[6], (3 * D,), 0.1, 0.625, ((0, 2),)),
        "w_out": gaussian(key_of[7], (D, D), 8 ** -0.5, 2.0, ((0, 2),)),
        "b_out": gaussian(key_of[8], (D,), 0.5, 3.0, ((0, 2),)),
        "w_up": gaussian(key_of[9], (D, FF), D ** -0.5, 0.1875, ((0, 2),)),
        "b_up": gaussian(key_of[10], (FF,), 0.5, 3.0, ((0, 2),)),
        "w_down": gaussian(key_of[11], (FF, D), FF ** -0.5, 0.09375, ((0, 2),)),
        "b_down": gaussian(key_of[12], (D,), 0.5, 3.0, ((0, 2),)),
        "lengths": draw_lengths(jax.random.fold_in(key_of[16], 71), 0),
        "block_map": draw_block_map(jax.random.fold_in(key_of[16], 71), 0),
        "cotangent": gaussian(key_of[15], (SLOTS, SEQ, D), 1.0, 6.0, ((0, 2), (1, 16))),
    }


@jax.custom_vjp
def low(v):
    return lax.optimization_barrier(v.astype(jnp.bfloat16)).astype(jnp.float32)

@jax.custom_vjp
def low_back(v):
    return v

def low_keep(v):
    return (low(v), None)

def low_pass(kept, grad):
    return (grad,)

def back_keep(v):
    return (v, None)

def back_low(kept, grad):
    return (low(grad),)
low.defvjp(low_keep, low_pass)
low_back.defvjp(back_keep, back_low)
epsilon = 1e-05

def product(left, right):
    return jnp.dot(left, right, precision=lax.Precision.HIGHEST, preferred_element_type=jnp.float32)

def layer_norm(values, norm_gain, norm_shift):
    average = lax.optimization_barrier(jnp.mean(values, axis=-1, keepdims=True))
    centred = values - average
    variance = lax.optimization_barrier(jnp.mean(centred * centred, axis=-1, keepdims=True))
    return centred * lax.rsqrt(variance + epsilon) * norm_gain + norm_shift

def rotary(values, positions):
    half_rot = ROT // 2
    frequency = 10000.0 ** (-jnp.arange(half_rot, dtype=jnp.float32) * 2.0 / ROT)
    angles = positions.astype(jnp.float32)[:, None] * frequency[None, :]
    cosine_table = jnp.cos(angles)[:, None, :]
    sine_table = jnp.sin(angles)[:, None, :]
    leading = values[..., :half_rot]
    trailing = values[..., half_rot:ROT]
    return jnp.concatenate([leading * cosine_table - trailing * sine_table, trailing * cosine_table + leading * sine_table, values[..., ROT:]], axis=-1)

def attend_block(query_block, query_pos, key_rows, value_rows, key_pos, key_live):
    raw_scores = low_back(jnp.einsum('qhd,khd->hqk', query_block, key_rows, precision=lax.Precision.HIGHEST))
    allowed = (key_pos[None, :] <= query_pos[:, None]) & key_live[None, :]
    scores = jnp.where(allowed[None], raw_scores * (1.0 / math.sqrt(HD)), -1e+30)
    weights = jax.nn.softmax(scores, axis=-1)
    return jnp.einsum('hqk,khd->qhd', low(weights), value_rows, precision=lax.Precision.HIGHEST)

def slot_forward(tokens_slot, length, params, positions):
    norm1_gain, norm1_shift, norm2_gain, norm2_shift, qkv_weight, qkv_bias, out_weight, out_bias, up_weight, up_bias, down_weight, down_bias = params
    live_rows = (positions < length).astype(jnp.float32)
    key_live = positions < length
    attn_in = low(layer_norm(tokens_slot, norm1_gain, norm1_shift))
    mlp_in = low(layer_norm(tokens_slot, norm2_gain, norm2_shift))
    projected = low_back(product(attn_in, qkv_weight) + qkv_bias).reshape(SEQ, 3, H, HD)
    queries = low(rotary(projected[:, 0], positions))
    key_rows = low(rotary(projected[:, 1], positions))
    value_rows = low(projected[:, 2])
    block_rows = math.gcd(SEQ, 512)
    query_blocks = queries.reshape(SEQ // block_rows, block_rows, H, HD)
    pos_blocks = positions.reshape(SEQ // block_rows, block_rows)

    def one_block(block_pair):
        return attend_block(block_pair[0], block_pair[1], key_rows, value_rows, positions, key_live)
    attended = lax.map(jax.checkpoint(one_block), (query_blocks, pos_blocks))
    context = low_back(low(attended.reshape(SEQ, D)))
    hidden = low_back(product(mlp_in, up_weight) + up_bias)
    activated = low(jax.nn.gelu(hidden, approximate=False))
    branch = low_back(product(context, out_weight) + out_bias + product(activated, down_weight) + down_bias)
    return live_rows[:, None] * (tokens_slot + branch)

def forward(token_rows, params, lengths, positions):

    def per_slot(slot_pair):
        return slot_forward(slot_pair[0], slot_pair[1], params, positions)
    return lax.map(per_slot, (token_rows, lengths))

def reference(tokens, ln1_gain, ln1_bias, ln2_gain, ln2_bias, w_qkv, b_qkv, w_out, b_out, w_up, b_up, w_down, b_down, lengths, block_map, cotangent):
    positions = (block_map[:, None] * HB + jnp.arange(HB, dtype=jnp.int32)[None, :]).reshape(SEQ).astype(jnp.int32)
    params = tuple((parameter.astype(jnp.float32) for parameter in (ln1_gain, ln1_bias, ln2_gain, ln2_bias, w_qkv, b_qkv, w_out, b_out, w_up, b_up, w_down, b_down)))
    token_rows = tokens.astype(jnp.float32)

    def layer_apply(rows_in, params_in):
        return forward(rows_in, params_in, lengths, positions)
    output, pullback = jax.vjp(layer_apply, token_rows, params)
    grad_rows, grads = pullback(cotangent.astype(jnp.float32))
    return (output.astype(jnp.bfloat16), grad_rows, grads[0], grads[1], grads[2], grads[3], grads[4], grads[5], grads[6], grads[7], grads[8], grads[9], grads[10], grads[11])
```

```python
from functools import partial
import math

import jax
import jax.numpy as jnp
from jax import lax
from jax.experimental import pallas as pl
from jax.experimental.pallas import tpu as pltpu
from jax.sharding import PartitionSpec as P

H = 16
HD = 64
ROT = 16


epsilon = 1e-05


def norm_forward(values, norm_gain, norm_shift):
    average = jnp.mean(values, axis=-1, keepdims=True)
    centred = values - average
    variance = jnp.mean(centred * centred, axis=-1, keepdims=True)
    inverse = lax.rsqrt(variance + epsilon)
    normed = centred * inverse
    return (normed * norm_gain + norm_shift, normed, inverse)


def norm_backward(grad_out, normed, inverse, norm_gain):
    scaled = grad_out * norm_gain
    adjusted = (
        scaled
        - jnp.mean(scaled, axis=-1, keepdims=True)
        - normed * jnp.mean(scaled * normed, axis=-1, keepdims=True)
    )
    return (adjusted * inverse, jnp.sum(grad_out * normed, axis=0), jnp.sum(grad_out, axis=0))


def rotary_tables(positions):
    half_rot = ROT // 2
    frequency = 10000.0 ** (-jnp.arange(half_rot, dtype=jnp.float32) * 2.0 / ROT)
    angles = positions.astype(jnp.float32)[:, None] * frequency[None, :]
    return (jnp.cos(angles)[:, None, :], jnp.sin(angles)[:, None, :])


def rotate_forward(values, cosine_table, sine_table):
    half_rot = ROT // 2
    leading = values[..., :half_rot]
    trailing = values[..., half_rot:ROT]
    return jnp.concatenate(
        [
            leading * cosine_table - trailing * sine_table,
            trailing * cosine_table + leading * sine_table,
            values[..., ROT:],
        ],
        axis=-1,
    )


def rotate_backward(grads, cosine_table, sine_table):
    half_rot = ROT // 2
    leading = grads[..., :half_rot]
    trailing = grads[..., half_rot:ROT]
    return jnp.concatenate(
        [
            leading * cosine_table + trailing * sine_table,
            trailing * cosine_table - leading * sine_table,
            grads[..., ROT:],
        ],
        axis=-1,
    )


def masked_scores(query_rows, key_rows, query_pos, key_pos, key_live):
    raw_scores = jnp.einsum(
        "qhd,khd->hqk", query_rows, key_rows, preferred_element_type=jnp.float32
    )
    allowed = (key_pos[None, :] <= query_pos[:, None]) & key_live[None, :]
    return (jnp.where(allowed[None], raw_scores * (1.0 / math.sqrt(HD)), -1e30), allowed)


def score_grads(
    query_rows, key_rows, value_rows, grad_rows, query_pos, key_pos, key_live, log_total, row_dots
):
    scores = masked_scores(query_rows, key_rows, query_pos, key_pos, key_live)[0]
    probability = jnp.exp(scores - log_total[..., None])
    grad_prob = jnp.einsum(
        "qhd,khd->hqk", grad_rows, value_rows, preferred_element_type=jnp.float32
    )
    grad_score = (probability * (grad_prob - row_dots[..., None]) * (1.0 / math.sqrt(HD))).astype(
        jnp.bfloat16
    )
    return (probability.astype(jnp.bfloat16), grad_score)


def shards(
    tokens,
    ln1_gain,
    ln1_bias,
    ln2_gain,
    ln2_bias,
    w_qkv,
    b_qkv,
    w_out,
    b_out,
    w_up,
    b_up,
    w_down,
    b_down,
    lengths,
    block_map,
    cotangent,
):
    gathered = (
        lax.all_gather(ln1_gain, "wsh", axis=0, tiled=True),
        lax.all_gather(ln1_bias, "wsh", axis=0, tiled=True),
        lax.all_gather(ln2_gain, "wsh", axis=0, tiled=True),
        lax.all_gather(ln2_bias, "wsh", axis=0, tiled=True),
        lax.all_gather(w_qkv, "wsh", axis=0, tiled=True),
        lax.all_gather(b_qkv, "wsh", axis=0, tiled=True),
        lax.all_gather(w_out, "wsh", axis=0, tiled=True),
        lax.all_gather(b_out, "wsh", axis=0, tiled=True),
        lax.all_gather(w_up, "wsh", axis=0, tiled=True),
        lax.all_gather(b_up, "wsh", axis=0, tiled=True),
        lax.all_gather(w_down, "wsh", axis=0, tiled=True),
        lax.all_gather(b_down, "wsh", axis=0, tiled=True),
    )
    (
        norm1_gain,
        norm1_shift,
        norm2_gain,
        norm2_shift,
        qkv_weight,
        qkv_bias,
        out_weight,
        out_bias,
        up_weight,
        up_bias,
        down_weight,
        down_bias,
    ) = gathered
    tok_rows = tokens.shape[1]
    model_width = tokens.shape[2]
    half_rows = tok_rows // 2
    seq_rows = tok_rows * lax.axis_size("ctx")
    head_count = H
    head_size = HD
    ctx_index = lax.axis_index("ctx")
    own_blocks = lax.dynamic_slice_in_dim(block_map, 2 * ctx_index, 2)
    local_offsets = jnp.arange(half_rows, dtype=jnp.int32)
    positions = (own_blocks[:, None] * half_rows + local_offsets[None, :]).reshape(tok_rows)
    key_pos = (block_map[:, None] * half_rows + local_offsets[None, :]).reshape(seq_rows)
    length = lengths[0]
    own_live = positions < length
    live_rows = own_live.astype(jnp.float32)
    key_live = key_pos < length
    gain_first = norm1_gain.astype(jnp.float32)
    gain_second = norm2_gain.astype(jnp.float32)
    token_rows = tokens[0].astype(jnp.float32)
    normal_first, normed_first, inverse_first = norm_forward(
        token_rows, gain_first, norm1_shift.astype(jnp.float32)
    )
    normal_second, normed_second, inverse_second = norm_forward(
        token_rows, gain_second, norm2_shift.astype(jnp.float32)
    )
    attn_in = normal_first.astype(jnp.bfloat16)
    mlp_in = normal_second.astype(jnp.bfloat16)
    projected = (
        jnp.dot(attn_in, qkv_weight, preferred_element_type=jnp.float32)
        + qkv_bias.astype(jnp.float32)
    ).reshape(tok_rows, 3, head_count, head_size)
    cosine_table, sine_table = rotary_tables(positions)
    queries = rotate_forward(projected[:, 0], cosine_table, sine_table).astype(jnp.bfloat16)
    key_own = (
        rotate_forward(projected[:, 1], cosine_table, sine_table)
        .astype(jnp.bfloat16)
        .reshape(tok_rows, model_width)
    )
    value_own = projected[:, 2].astype(jnp.bfloat16).reshape(tok_rows, model_width)
    keys_all, values_all = (
        lax.all_gather(key_own, "ctx", axis=0, tiled=True),
        lax.all_gather(value_own, "ctx", axis=0, tiled=True),
    )
    block_len = math.gcd(seq_rows, 1024)
    block_count = seq_rows // block_len
    key_stack = keys_all.reshape(block_count, block_len, head_count, head_size)
    value_stack = values_all.reshape(block_count, block_len, head_count, head_size)
    pos_stack = key_pos.reshape(block_count, block_len)
    live_stack = key_live.reshape(block_count, block_len)

    def stats_step(running, key_part):
        key_block, pos_block, live_block = key_part
        scores, allowed = masked_scores(queries, key_block, positions, pos_block, live_block)
        peak_score = jnp.maximum(running[0], jnp.max(scores, axis=-1))
        exp_total = running[1] * jnp.exp(running[0] - peak_score) + jnp.sum(
            jnp.where(allowed[None], jnp.exp(scores - peak_score[..., None]), 0.0), axis=-1
        )
        return ((peak_score, exp_total), None)

    start_peak = jnp.full((head_count, tok_rows), -1e30, jnp.float32)
    final_state = lax.scan(
        stats_step, (start_peak, jnp.zeros_like(start_peak)), (key_stack, pos_stack, live_stack)
    )[0]
    log_total = final_state[0] + jnp.log(final_state[1])

    def value_step(running, key_part):
        key_block, value_block, pos_block, live_block = key_part
        scores = masked_scores(queries, key_block, positions, pos_block, live_block)[0]
        probability = jnp.exp(scores - log_total[..., None]).astype(jnp.bfloat16)
        return (
            running
            + jnp.einsum(
                "hqk,khd->qhd", probability, value_block, preferred_element_type=jnp.float32
            ),
            None,
        )

    zero_heads = jnp.zeros((tok_rows, head_count, head_size), jnp.float32)
    attended = lax.scan(value_step, zero_heads, (key_stack, value_stack, pos_stack, live_stack))[0]
    context_low = attended.reshape(tok_rows, model_width).astype(jnp.bfloat16)
    hidden = jnp.dot(mlp_in, up_weight, preferred_element_type=jnp.float32) + up_bias.astype(
        jnp.float32
    )
    activated, gelu_pull = jax.vjp(partial(jax.nn.gelu, approximate=False), hidden)
    act_low = activated.astype(jnp.bfloat16)
    branch = (
        jnp.dot(context_low, out_weight, preferred_element_type=jnp.float32)
        + out_bias.astype(jnp.float32)
        + jnp.dot(act_low, down_weight, preferred_element_type=jnp.float32)
        + down_bias.astype(jnp.float32)
    )
    output_rows = (live_rows[:, None] * (token_rows + branch)).astype(jnp.bfloat16)
    cot_rows = cotangent[0].astype(jnp.float32)
    grad_branch = (live_rows[:, None] * cot_rows).astype(jnp.bfloat16)
    grad_w_out = jnp.einsum(
        "tc,td->cd", context_low, grad_branch, preferred_element_type=jnp.float32
    )
    grad_w_down = jnp.einsum("tc,td->cd", act_low, grad_branch, preferred_element_type=jnp.float32)
    grad_branch_sum = jnp.sum(grad_branch.astype(jnp.float32), axis=0)
    grad_act = jnp.einsum("td,cd->tc", grad_branch, down_weight, preferred_element_type=jnp.float32)
    grad_hidden = gelu_pull(grad_act)[0].astype(jnp.bfloat16)
    grad_w_up = jnp.einsum("tc,td->cd", mlp_in, grad_hidden, preferred_element_type=jnp.float32)
    grad_b_up = jnp.sum(grad_hidden.astype(jnp.float32), axis=0)
    grad_mlp_in = jnp.einsum(
        "td,cd->tc", grad_hidden, up_weight, preferred_element_type=jnp.float32
    )
    grad_context = jnp.einsum(
        "td,cd->tc", grad_branch, out_weight, preferred_element_type=jnp.float32
    ).astype(jnp.bfloat16)
    grad_heads = grad_context.reshape(tok_rows, head_count, head_size)
    row_dots = jnp.sum(grad_heads.astype(jnp.float32) * attended, axis=-1).T

    def grad_step(running, key_part):
        key_block, value_block, pos_block, live_block = key_part
        prob_low, grad_score = score_grads(
            queries,
            key_block,
            value_block,
            grad_heads,
            positions,
            pos_block,
            live_block,
            log_total,
            row_dots,
        )
        query_sum = running + jnp.einsum(
            "hqk,khd->qhd", grad_score, key_block, preferred_element_type=jnp.float32
        )
        key_term = jnp.einsum(
            "hqk,qhd->khd", grad_score, queries, preferred_element_type=jnp.float32
        )
        value_term = jnp.einsum(
            "hqk,qhd->khd", prob_low, grad_heads, preferred_element_type=jnp.float32
        )
        return (query_sum, (key_term, value_term))

    query_grad, term_stacks = lax.scan(
        grad_step, zero_heads, (key_stack, value_stack, pos_stack, live_stack)
    )
    key_grad, value_grad = (
        lax.psum_scatter(
            term_stacks[0].reshape(seq_rows, model_width).astype(jnp.bfloat16),
            "ctx",
            scatter_dimension=0,
            tiled=True,
        ).astype(jnp.float32),
        lax.psum_scatter(
            term_stacks[1].reshape(seq_rows, model_width).astype(jnp.bfloat16),
            "ctx",
            scatter_dimension=0,
            tiled=True,
        ).astype(jnp.float32),
    )
    key_grad = key_grad.reshape(tok_rows, head_count, head_size)
    value_grad = value_grad.reshape(tok_rows, head_count, head_size)
    grad_projected = (
        jnp.stack(
            [
                rotate_backward(query_grad, cosine_table, sine_table),
                rotate_backward(key_grad, cosine_table, sine_table),
                value_grad,
            ],
            axis=1,
        )
        .reshape(tok_rows, 3 * model_width)
        .astype(jnp.bfloat16)
    )
    grad_w_qkv = jnp.einsum(
        "tc,td->cd", attn_in, grad_projected, preferred_element_type=jnp.float32
    )
    grad_b_qkv = jnp.sum(grad_projected.astype(jnp.float32), axis=0)
    grad_attn_in = jnp.einsum(
        "td,cd->tc", grad_projected, qkv_weight, preferred_element_type=jnp.float32
    )
    grad_input_first, grad_gain_first, grad_shift_first = norm_backward(
        grad_attn_in, normed_first, inverse_first, gain_first
    )
    grad_input_second, grad_gain_second, grad_shift_second = norm_backward(
        grad_mlp_in, normed_second, inverse_second, gain_second
    )
    grad_input = live_rows[:, None] * cot_rows + grad_input_first + grad_input_second
    shares = (
        lax.psum_scatter(
            grad_gain_first.astype(jnp.bfloat16), "wsh", scatter_dimension=0, tiled=True
        ).astype(jnp.float32),
        lax.psum_scatter(
            grad_shift_first.astype(jnp.bfloat16), "wsh", scatter_dimension=0, tiled=True
        ).astype(jnp.float32),
        lax.psum_scatter(
            grad_gain_second.astype(jnp.bfloat16), "wsh", scatter_dimension=0, tiled=True
        ).astype(jnp.float32),
        lax.psum_scatter(
            grad_shift_second.astype(jnp.bfloat16), "wsh", scatter_dimension=0, tiled=True
        ).astype(jnp.float32),
        lax.psum_scatter(
            grad_w_qkv.astype(jnp.bfloat16), "wsh", scatter_dimension=0, tiled=True
        ).astype(jnp.float32),
        lax.psum_scatter(
            grad_b_qkv.astype(jnp.bfloat16), "wsh", scatter_dimension=0, tiled=True
        ).astype(jnp.float32),
        lax.psum_scatter(
            grad_w_out.astype(jnp.bfloat16), "wsh", scatter_dimension=0, tiled=True
        ).astype(jnp.float32),
        lax.psum_scatter(
            grad_branch_sum.astype(jnp.bfloat16), "wsh", scatter_dimension=0, tiled=True
        ).astype(jnp.float32),
        lax.psum_scatter(
            grad_w_up.astype(jnp.bfloat16), "wsh", scatter_dimension=0, tiled=True
        ).astype(jnp.float32),
        lax.psum_scatter(
            grad_b_up.astype(jnp.bfloat16), "wsh", scatter_dimension=0, tiled=True
        ).astype(jnp.float32),
        lax.psum_scatter(
            grad_w_down.astype(jnp.bfloat16), "wsh", scatter_dimension=0, tiled=True
        ).astype(jnp.float32),
        lax.psum_scatter(
            grad_branch_sum.astype(jnp.bfloat16), "wsh", scatter_dimension=0, tiled=True
        ).astype(jnp.float32),
    )
    totals = (
        lax.psum(shares[0].astype(jnp.bfloat16), "ctx").astype(jnp.float32),
        lax.psum(shares[1].astype(jnp.bfloat16), "ctx").astype(jnp.float32),
        lax.psum(shares[2].astype(jnp.bfloat16), "ctx").astype(jnp.float32),
        lax.psum(shares[3].astype(jnp.bfloat16), "ctx").astype(jnp.float32),
        lax.psum(shares[4].astype(jnp.bfloat16), "ctx").astype(jnp.float32),
        lax.psum(shares[5].astype(jnp.bfloat16), "ctx").astype(jnp.float32),
        lax.psum(shares[6].astype(jnp.bfloat16), "ctx").astype(jnp.float32),
        lax.psum(shares[7].astype(jnp.bfloat16), "ctx").astype(jnp.float32),
        lax.psum(shares[8].astype(jnp.bfloat16), "ctx").astype(jnp.float32),
        lax.psum(shares[9].astype(jnp.bfloat16), "ctx").astype(jnp.float32),
        lax.psum(shares[10].astype(jnp.bfloat16), "ctx").astype(jnp.float32),
        lax.psum(shares[11].astype(jnp.bfloat16), "ctx").astype(jnp.float32),
    )
    return (
        output_rows[None],
        grad_input[None],
        totals[0],
        totals[1],
        totals[2],
        totals[3],
        totals[4],
        totals[5],
        totals[6],
        totals[7],
        totals[8],
        totals[9],
        totals[10],
        totals[11],
    )


HB = 128
NEG=-1e30
f32=jnp.float32; bf16=jnp.bfloat16

def _nn(a,b): return lax.dot_general(a,b,(((1,),(0,)),((),())),preferred_element_type=f32)
def _nt(a,b): return lax.dot_general(a,b,(((1,),(1,)),((),())),preferred_element_type=f32)

def attn_fwd_kernel(bm, x_ref, o_ref, lse_ref, q_s, kt_s, v_s, *, nblk, bq, bk):
    def perm(i,_):
        p=bm[i]; c=i//2; l=pl.multiple_of((i%2)*HB,HB); d=pl.multiple_of(p*HB,HB)
        q_s[:,pl.ds(d,HB)]=x_ref[c,0:64,pl.ds(l,HB)]*bf16(0.125)
        kt_s[pl.ds(d,HB),:]=x_ref[c,64:128,pl.ds(l,HB)].astype(f32).T.astype(bf16)
        v_s[:,pl.ds(d,HB)]=x_ref[c,128:192,pl.ds(l,HB)]
        return 0
    lax.fori_loop(0,nblk,perm,0)
    S=nblk*HB; nq=S//bq; r=bq//bk
    def step(q,qo,ko,carry,mask):
        m,l,acc=carry
        s=_nn(kt_s[pl.ds(ko,bk),:],q)
        if mask is not None: s=jnp.where(mask,s,NEG)
        mn=jnp.maximum(m,jnp.max(s,axis=0,keepdims=True))
        a=jnp.exp(m-mn); p=jnp.exp(s-mn)
        l=l*a+jnp.sum(p,axis=0,keepdims=True)
        acc=acc*a+_nn(v_s[:,pl.ds(ko,bk)],p.astype(bf16))
        return mn,l,acc
    ki=lax.broadcasted_iota(jnp.int32,(bk,bq),0); qi_=lax.broadcasted_iota(jnp.int32,(bk,bq),1)
    def qloop(i,_):
        qo=pl.multiple_of(i*bq,bq)
        q=q_s[:,pl.ds(qo,bq)]
        c=(jnp.full((1,bq),NEG,f32),jnp.zeros((1,bq),f32),jnp.zeros((64,bq),f32))
        c=lax.fori_loop(0,i*r,lambda j,c: step(q,qo,pl.multiple_of(j*bk,bk),c,None),c)
        for t in range(r):
            c=step(q,qo,pl.multiple_of(qo+t*bk,bk),c,ki+t*bk<=qi_)
        m,l,acc=c
        q_s[:,pl.ds(qo,bq)]=(acc*(1.0/l)).astype(bf16)
        lse_ref[:,pl.ds(qo,bq)]=m+jnp.log(l)
        return 0
    lax.fori_loop(0,nq,qloop,0)
    def unperm(i,_):
        p=bm[i]; c=i//2; l=pl.multiple_of((i%2)*HB,HB); d=pl.multiple_of(p*HB,HB)
        o_ref[c,:,pl.ds(l,HB)]=q_s[:,pl.ds(d,HB)]
        return 0
    lax.fori_loop(0,nblk,unperm,0)

def attn_fwd(bm,x,*,bq=512,bk=512):
    n=x.shape[0]; S=n*256; nblk=2*n
    bq=math.gcd(S,bq); bk=math.gcd(bq,bk)
    return pl.pallas_call(
        lambda *a: attn_fwd_kernel(*a,nblk=nblk,bq=bq,bk=bk),
        out_shape=(jax.ShapeDtypeStruct((n,64,256),bf16),jax.ShapeDtypeStruct((1,S),f32)),
        in_specs=[pl.BlockSpec(memory_space=pltpu.SMEM),pl.BlockSpec(memory_space=pltpu.VMEM)],
        out_specs=(pl.BlockSpec(memory_space=pltpu.VMEM),pl.BlockSpec(memory_space=pltpu.VMEM)),
        scratch_shapes=[pltpu.VMEM((64,S),bf16),pltpu.VMEM((S,64),bf16),pltpu.VMEM((64,S),bf16)],
        compiler_params=pltpu.CompilerParams(vmem_limit_bytes=56<<20),name="attn_fwd")(bm,x)

def attn_bwd_kernel(bm, x_ref, o_ref, do_ref, lse_ref, cs_ref, g_ref, q_s, kt_s, k_s, vt_s, do_s, dl_s, dq_s, dk_s, dv_s, *, nblk, bq, bk):
    def perm(i,_):
        p=bm[i]; c=i//2; l=pl.multiple_of((i%2)*HB,HB); d=pl.multiple_of(p*HB,HB)
        q_s[:,pl.ds(d,HB)]=x_ref[c,0:64,pl.ds(l,HB)]*bf16(0.125)
        k=x_ref[c,64:128,pl.ds(l,HB)]
        k_s[:,pl.ds(d,HB)]=k*bf16(0.125)
        kt_s[pl.ds(d,HB),:]=k.astype(f32).T.astype(bf16)
        vt_s[pl.ds(d,HB),:]=x_ref[c,128:192,pl.ds(l,HB)].astype(f32).T.astype(bf16)
        do=do_ref[c,:,pl.ds(l,HB)]
        do_s[:,pl.ds(d,HB)]=do
        dl_s[:,pl.ds(d,HB)]=jnp.sum(do.astype(f32)*o_ref[c,:,pl.ds(l,HB)].astype(f32),axis=0,keepdims=True)
        return 0
    lax.fori_loop(0,nblk,perm,0)
    S=nblk*HB; nq=S//bq; r=bq//bk
    dk_s[...]=jnp.zeros_like(dk_s); dv_s[...]=jnp.zeros_like(dv_s)
    def step(q,do,lse,dl,ko,dq,mask):
        s=_nn(kt_s[pl.ds(ko,bk),:],q)
        p=jnp.exp(s-lse)
        if mask is not None: p=jnp.where(mask,p,0.0)
        dp=_nn(vt_s[pl.ds(ko,bk),:],do)
        ds=(p*(dp-dl)).astype(bf16)
        pb=p.astype(bf16)
        dv_s[:,pl.ds(ko,bk)]+=_nt(do,pb)
        dk_s[:,pl.ds(ko,bk)]+=_nt(q,ds)
        return dq+_nn(k_s[:,pl.ds(ko,bk)],ds)
    ki=lax.broadcasted_iota(jnp.int32,(bk,bq),0); qi_=lax.broadcasted_iota(jnp.int32,(bk,bq),1)
    def qloop(i,_):
        qo=pl.multiple_of(i*bq,bq)
        q=q_s[:,pl.ds(qo,bq)]; do=do_s[:,pl.ds(qo,bq)]; lse=lse_ref[:,pl.ds(qo,bq)]; dl=dl_s[:,pl.ds(qo,bq)]
        dq=jnp.zeros((64,bq),f32)
        dq=lax.fori_loop(0,i*r,lambda j,c: step(q,do,lse,dl,pl.multiple_of(j*bk,bk),c,None),dq)
        for t in range(r):
            dq=step(q,do,lse,dl,pl.multiple_of(qo+t*bk,bk),dq,ki+t*bk<=qi_)
        dq_s[:,pl.ds(qo,bq)]=dq
        return 0
    lax.fori_loop(0,nq,qloop,0)
    def unperm(i,_):
        p=bm[i]; c=i//2; l=pl.multiple_of((i%2)*HB,HB); d=pl.multiple_of(p*HB,HB)
        cos=cs_ref[0:8,pl.ds(d,HB)]; sin=cs_ref[8:16,pl.ds(d,HB)]
        for n_,src in ((0,dq_s),(1,dk_s)):
            g=src[:,pl.ds(d,HB)]
            a=g[0:8]; b=g[8:16]
            full=jnp.concatenate([a*cos+b*sin,b*cos-a*sin,g[16:64]],axis=0)
            g_ref[c,64*n_:64*n_+64,pl.ds(l,HB)]=full.astype(bf16)
        g_ref[c,128:192,pl.ds(l,HB)]=dv_s[:,pl.ds(d,HB)].astype(bf16)
        return 0
    lax.fori_loop(0,nblk,unperm,0)

def attn_bwd(bm,x,o,do,lse,cs,*,bq=512,bk=512):
    n=x.shape[0]; S=n*256; nblk=2*n
    bq=math.gcd(S,bq); bk=math.gcd(bq,bk)
    vm=pl.BlockSpec(memory_space=pltpu.VMEM)
    return pl.pallas_call(
        lambda *a: attn_bwd_kernel(*a,nblk=nblk,bq=bq,bk=bk),
        out_shape=jax.ShapeDtypeStruct((n,192,256),bf16),
        in_specs=[pl.BlockSpec(memory_space=pltpu.SMEM)]+[vm]*5,
        out_specs=vm,
        scratch_shapes=[pltpu.VMEM((64,S),bf16),pltpu.VMEM((S,64),bf16),pltpu.VMEM((64,S),bf16),pltpu.VMEM((S,64),bf16),pltpu.VMEM((64,S),bf16),
                        pltpu.VMEM((1,S),f32),pltpu.VMEM((64,S),f32),pltpu.VMEM((64,S),f32),pltpu.VMEM((64,S),f32)],
        compiler_params=pltpu.CompilerParams(vmem_limit_bytes=56<<20),name="attn_bwd")(bm,x,o,do,lse,cs)


SWAP = [(0, 1), (1, 0)]


def fast_fits(mesh):
    return mesh.shape["wsh"] == 2 and mesh.shape["ctx"] == H


def mlp_kernel(x_ref, dy_ref, wu_ref, wd_ref, bu_ref, y_ref, dx_ref, gu_ref, gd_ref, gb_ref, xt_s):
    first = pl.program_id(0) == 0

    @pl.when(first)
    def _():
        xt_s[...] = x_ref[...].astype(f32).T.astype(bf16)

    x = x_ref[...]
    dy = dy_ref[...]
    wu = wu_ref[...]
    wd = wd_ref[...]
    u = _nn(x, wu) + bu_ref[...]
    cdf = 0.5 * (1.0 + lax.erf(u * (1.0 / math.sqrt(2.0))))
    pdf = jnp.exp(-0.5 * u * u) * (1.0 / math.sqrt(2.0 * math.pi))
    act = (u * cdf).astype(bf16)
    du = (_nt(dy, wd) * (cdf + u * pdf)).astype(bf16)
    y = _nn(act, wd)
    dx = _nt(du, wu)

    @pl.when(first)
    def _():
        y_ref[...] = y
        dx_ref[...] = dx

    @pl.when(jnp.logical_not(first))
    def _():
        y_ref[...] += y
        dx_ref[...] += dx

    gd_ref[...] = lax.dot_general(
        act, dy, (((0,), (0,)), ((), ())), preferred_element_type=f32
    ).astype(bf16)
    gu_ref[...] = _nn(xt_s[...], du).astype(bf16)
    gb_ref[...] = jnp.sum(du.astype(f32), axis=0, keepdims=True)


def mlp(x, dy, wu, wd, bu, tile=256):
    rows, width = x.shape
    hidden = wu.shape[1]
    whole = pl.BlockSpec((rows, width), lambda i: (0, 0))
    cols = pl.BlockSpec((width, tile), lambda i: (0, i))
    down = pl.BlockSpec((tile, width), lambda i: (i, 0))
    vec = pl.BlockSpec((1, tile), lambda i: (0, i))
    return pl.pallas_call(
        mlp_kernel,
        grid=(hidden // tile,),
        in_specs=[whole, whole, cols, down, vec],
        out_specs=(whole, whole, cols, down, vec),
        out_shape=(
            jax.ShapeDtypeStruct((rows, width), f32),
            jax.ShapeDtypeStruct((rows, width), f32),
            jax.ShapeDtypeStruct((width, hidden), bf16),
            jax.ShapeDtypeStruct((hidden, width), bf16),
            jax.ShapeDtypeStruct((1, hidden), f32),
        ),
        scratch_shapes=[pltpu.VMEM((width, rows), bf16)],
        compiler_params=pltpu.CompilerParams(vmem_limit_bytes=56 << 20),
        name="mlp",
    )(x, dy, wu, wd, bu)


def fast_shards(
    tokens,
    ln1_gain,
    ln1_bias,
    ln2_gain,
    ln2_bias,
    w_qkv,
    b_qkv,
    w_out,
    b_out,
    w_up,
    b_up,
    w_down,
    b_down,
    lengths,
    block_map,
    cotangent,
):
    ctx = lax.axis_index("ctx")
    me = lax.axis_index("wsh")
    core = ctx % 2
    n_ctx = lax.axis_size("ctx")
    rows, width = tokens.shape[1:]
    half = width // 2
    seq = rows * n_ctx
    heads = H // 2
    hid = w_up.shape[1] // 2
    pair_perm = [(i, i ^ 1) for i in range(n_ctx)]

    def swap(v):
        return lax.ppermute(v, "wsh", SWAP)

    def fetch_rows(mine, other):
        q = half // 2
        got = swap(lax.dynamic_slice_in_dim(other, core * q, q))
        sib = lax.ppermute(got, "ctx", pair_perm)
        out = jnp.zeros((width, mine.shape[1]), mine.dtype)
        out = lax.dynamic_update_slice_in_dim(out, mine, me * half, 0)
        base = (1 - me) * half
        out = lax.dynamic_update_slice_in_dim(out, got, base + core * q, 0)
        return lax.dynamic_update_slice_in_dim(out, sib, base + (1 - core) * q, 0)

    len_parts = jnp.stack([lengths[0] // 64, lengths[0] % 64]).astype(bf16)
    small = jnp.concatenate(
        [ln1_gain, ln1_bias, ln2_gain, ln2_bias, b_out, b_down, b_qkv, len_parts, jnp.zeros((126,), bf16)]
    )
    small = lax.all_gather(small, "wsh", axis=0, tiled=False)
    vec = lambda i: small[:, i * half : (i + 1) * half].reshape(width).astype(f32)
    g1, s1, g2, s2, bo, bd = [vec(i) for i in range(6)]
    qkv_bias = small[:, 6 * half : 9 * half].reshape(3, 2, half).astype(f32)
    qkv_bias = lax.dynamic_index_in_dim(qkv_bias, me, 1, keepdims=False).reshape(3 * half)
    lens = small[:, 9 * half : 9 * half + 2].astype(jnp.int32)
    lens = lens[:, 0] * 64 + lens[:, 1]
    other_len = lens[1 - me]

    x2 = jnp.stack([tokens[0], swap(tokens[0])])
    cot2 = jnp.stack([cotangent[0], swap(cotangent[0])])
    wq4 = w_qkv.reshape(half, 3, 2, half)
    wq_mine = lax.dynamic_index_in_dim(wq4, me, 2, keepdims=False).reshape(half, 3 * half)
    wq_send = lax.dynamic_index_in_dim(wq4, 1 - me, 2, keepdims=False).reshape(half, 3 * half)
    wq = fetch_rows(wq_mine, wq_send)
    wu_mine = lax.dynamic_slice_in_dim(w_up, me * hid, hid, 1)
    wu_send = lax.dynamic_slice_in_dim(w_up, (1 - me) * hid, hid, 1)
    wu = fetch_rows(wu_mine, wu_send)

    own_blocks = lax.dynamic_slice_in_dim(block_map, 2 * ctx, 2)
    offs = jnp.arange(HB, dtype=jnp.int32)
    positions = (own_blocks[:, None] * HB + offs[None, :]).reshape(rows)
    live2 = jnp.stack([positions < lengths[0], positions < other_len]).astype(f32)[..., None]
    freq = 10000.0 ** (-jnp.arange(ROT // 2, dtype=f32) * 2.0 / ROT)
    ang = freq[:, None] * jnp.arange(seq, dtype=jnp.int32).astype(f32)[None, :]
    table = jnp.concatenate([jnp.cos(ang), jnp.sin(ang)])
    own_ang = freq[:, None] * positions.astype(f32)[None, :]
    cos = jnp.cos(own_ang)[None, :, None, :]
    sin = jnp.sin(own_ang)[None, :, None, :]

    xf = x2.astype(f32)
    mean = jnp.mean(xf, axis=-1, keepdims=True)
    cen = xf - mean
    inv = lax.rsqrt(jnp.mean(cen * cen, axis=-1, keepdims=True) + epsilon)
    xhat = cen * inv
    attn_in = (xhat * g1 + s1).astype(bf16)
    mlp_in = (xhat * g2 + s2).astype(bf16)
    dy2 = (live2 * cot2.astype(f32)).astype(bf16)

    qkv = lax.dot_general(
        wq, attn_in.reshape(2 * rows, width), (((0,), (1,)), ((), ())), preferred_element_type=f32
    )
    qkv = (qkv + qkv_bias[:, None]).reshape(3, heads, HD, 2, rows)

    def rope(v):
        a = v[:, :8]
        b = v[:, 8:16]
        return jnp.concatenate([a * cos - b * sin, b * cos + a * sin, v[:, 16:]], axis=1)

    parts = jnp.stack([rope(qkv[0]), rope(qkv[1]), qkv[2]]).astype(bf16)
    send = parts.transpose(3, 1, 0, 2, 4).reshape(2 * heads, 3 * HD, rows)
    dctx = jnp.einsum("ed,std->set", w_out, dy2, preferred_element_type=f32).astype(bf16)
    dctx = dctx.reshape(2 * heads, HD, rows)

    def exchange(v):
        return lax.all_to_all(v, "ctx", 0, 0, tiled=False)

    qkv_head = exchange(send)
    do_head = exchange(dctx)

    y_mlp, d_mlp, g_up, g_down, gb_up = mlp(
        mlp_in.reshape(2 * rows, width),
        dy2.reshape(2 * rows, width),
        wu,
        w_down,
        b_up.astype(f32)[None, :],
    )
    up_keep = lax.dynamic_slice_in_dim(g_up, me * half, half, 0)
    up_send = lax.dynamic_slice_in_dim(g_up, (1 - me) * half, half, 0)
    up_got = swap(up_send)

    def join_cols(keep, got, n):
        a = keep.reshape(half, -1, n)
        b = got.reshape(half, -1, n)
        pair = jnp.where(me == 0, jnp.stack([a, b], axis=2), jnp.stack([b, a], axis=2))
        return pair.reshape(half, -1)

    tot_down, tot_up = lax.psum((g_down, join_cols(up_keep, up_got, hid)), "ctx")

    o_head, lse = attn_fwd(block_map, qkv_head, bq=1024, bk=1024)
    ob = exchange(o_head).reshape(2, half, rows)
    g_head = attn_bwd(block_map, qkv_head, o_head, do_head, lse, table)
    d_qkv = exchange(g_head).reshape(2, heads, 3, HD, rows)
    d_qkv = d_qkv.transpose(0, 2, 1, 3, 4).reshape(2, 3 * half, rows)

    part = jnp.einsum("sct,cd->std", ob, w_out, preferred_element_type=f32) + y_mlp.reshape(
        2, rows, width
    )
    y_got = swap(part[1].astype(bf16)).astype(f32)
    output = (live2[0] * (xf[0] + part[0] + y_got + bo + bd)).astype(bf16)
    g_out = jnp.einsum("sct,std->cd", ob, dy2, preferred_element_type=f32).astype(bf16)

    g_qkv = jnp.einsum("stf,sct->fc", attn_in, d_qkv, preferred_element_type=f32).astype(bf16)
    d_attn = jnp.einsum("sct,fc->stf", d_qkv, wq, preferred_element_type=f32)
    q_keep = lax.dynamic_slice_in_dim(g_qkv, me * half, half, 0)
    q_send = lax.dynamic_slice_in_dim(g_qkv, (1 - me) * half, half, 0)
    q_tot = join_cols(q_keep, swap(q_send), half)
    q_tot, g_out, tot_down, tot_up = lax.optimization_barrier((q_tot, g_out, tot_down, tot_up))
    tot_out, tot_qkv = lax.psum((g_out, q_tot), "ctx")

    d_mlp = d_mlp.reshape(2, rows, width)
    e = d_attn * g1 + d_mlp * g2
    e_own = e[0] + swap(e[1].astype(bf16)).astype(f32)
    dx = inv[0] * (
        e_own
        - jnp.mean(e_own, axis=-1, keepdims=True)
        - xhat[0] * jnp.mean(e_own * xhat[0], axis=-1, keepdims=True)
    )
    grad_tokens = live2[0] * cot2[0].astype(f32) + dx

    both = (0, 1)
    gb_qkv = jnp.sum(d_qkv.astype(f32), axis=(0, 2)).reshape(3, 1, half)
    mine = (jnp.arange(2) == me).astype(f32)
    gb_qkv = (gb_qkv * mine[None, :, None]).reshape(3 * width)
    gb_hid = (gb_up * mine[:, None]).reshape(2 * hid)
    flat = jnp.concatenate(
        [
            jnp.sum(d_attn * xhat, axis=both),
            jnp.sum(d_attn, axis=both),
            jnp.sum(d_mlp * xhat, axis=both),
            jnp.sum(d_mlp, axis=both),
            jnp.sum(dy2[0].astype(f32), axis=0),
            gb_qkv,
            gb_hid,
        ]
    )
    flat = lax.psum(flat, ("ctx", "wsh"))

    def own(start, size):
        return lax.dynamic_slice_in_dim(flat, start + me * size, size)

    gb_out = own(4 * width, half)
    return (
        output[None],
        grad_tokens[None],
        own(0, half),
        own(width, half),
        own(2 * width, half),
        own(3 * width, half),
        tot_qkv.astype(f32),
        own(5 * width, 3 * half),
        tot_out.astype(f32),
        gb_out,
        tot_up.astype(f32),
        own(8 * width, hid),
        tot_down.astype(f32),
        gb_out,
    )


def solution(mesh):
    placed = (
        P("wsh", "ctx", None),
        P("wsh"),
        P("wsh"),
        P("wsh"),
        P("wsh"),
        P("wsh", None),
        P("wsh"),
        P("wsh", None),
        P("wsh"),
        P("wsh", None),
        P("wsh"),
        P("wsh", None),
        P("wsh"),
        P("wsh"),
        P(),
        P("wsh", "ctx", None),
    )
    body = fast_shards if fast_fits(mesh) else shards
    return jax.shard_map(
        body,
        mesh=mesh,
        in_specs=placed,
        out_specs=(
            P("wsh", "ctx", None),
            P("wsh", "ctx", None),
            P("wsh"),
            P("wsh"),
            P("wsh"),
            P("wsh"),
            P("wsh", None),
            P("wsh"),
            P("wsh", None),
            P("wsh"),
            P("wsh", None),
            P("wsh"),
            P("wsh", None),
            P("wsh"),
        ),
        check_vma=False,
    )
```

```python
from functools import partial
import math

import jax
import jax.numpy as jnp
from jax import lax
from jax.experimental import pallas as pl
from jax.experimental.pallas import tpu as pltpu
from jax.sharding import PartitionSpec as P

H = 16
HD = 64
ROT = 16


epsilon = 1e-05


def norm_forward(values, norm_gain, norm_shift):
    average = jnp.mean(values, axis=-1, keepdims=True)
    centred = values - average
    variance = jnp.mean(centred * centred, axis=-1, keepdims=True)
    inverse = lax.rsqrt(variance + epsilon)
    normed = centred * inverse
    return (normed * norm_gain + norm_shift, normed, inverse)


def norm_backward(grad_out, normed, inverse, norm_gain):
    scaled = grad_out * norm_gain
    adjusted = (
        scaled
        - jnp.mean(scaled, axis=-1, keepdims=True)
        - normed * jnp.mean(scaled * normed, axis=-1, keepdims=True)
    )
    return (adjusted * inverse, jnp.sum(grad_out * normed, axis=0), jnp.sum(grad_out, axis=0))


def rotary_tables(positions):
    half_rot = ROT // 2
    frequency = 10000.0 ** (-jnp.arange(half_rot, dtype=jnp.float32) * 2.0 / ROT)
    angles = positions.astype(jnp.float32)[:, None] * frequency[None, :]
    return (jnp.cos(angles)[:, None, :], jnp.sin(angles)[:, None, :])


def rotate_forward(values, cosine_table, sine_table):
    half_rot = ROT // 2
    leading = values[..., :half_rot]
    trailing = values[..., half_rot:ROT]
    return jnp.concatenate(
        [
            leading * cosine_table - trailing * sine_table,
            trailing * cosine_table + leading * sine_table,
            values[..., ROT:],
        ],
        axis=-1,
    )


def rotate_backward(grads, cosine_table, sine_table):
    half_rot = ROT // 2
    leading = grads[..., :half_rot]
    trailing = grads[..., half_rot:ROT]
    return jnp.concatenate(
        [
            leading * cosine_table + trailing * sine_table,
            trailing * cosine_table - leading * sine_table,
            grads[..., ROT:],
        ],
        axis=-1,
    )


def masked_scores(query_rows, key_rows, query_pos, key_pos, key_live):
    raw_scores = jnp.einsum(
        "qhd,khd->hqk", query_rows, key_rows, preferred_element_type=jnp.float32
    )
    allowed = (key_pos[None, :] <= query_pos[:, None]) & key_live[None, :]
    return (jnp.where(allowed[None], raw_scores * (1.0 / math.sqrt(HD)), -1e30), allowed)


def score_grads(
    query_rows, key_rows, value_rows, grad_rows, query_pos, key_pos, key_live, log_total, row_dots
):
    scores = masked_scores(query_rows, key_rows, query_pos, key_pos, key_live)[0]
    probability = jnp.exp(scores - log_total[..., None])
    grad_prob = jnp.einsum(
        "qhd,khd->hqk", grad_rows, value_rows, preferred_element_type=jnp.float32
    )
    grad_score = (probability * (grad_prob - row_dots[..., None]) * (1.0 / math.sqrt(HD))).astype(
        jnp.bfloat16
    )
    return (probability.astype(jnp.bfloat16), grad_score)


def shards(
    tokens,
    ln1_gain,
    ln1_bias,
    ln2_gain,
    ln2_bias,
    w_qkv,
    b_qkv,
    w_out,
    b_out,
    w_up,
    b_up,
    w_down,
    b_down,
    lengths,
    block_map,
    cotangent,
):
    gathered = (
        lax.all_gather(ln1_gain, "wsh", axis=0, tiled=True),
        lax.all_gather(ln1_bias, "wsh", axis=0, tiled=True),
        lax.all_gather(ln2_gain, "wsh", axis=0, tiled=True),
        lax.all_gather(ln2_bias, "wsh", axis=0, tiled=True),
        lax.all_gather(w_qkv, "wsh", axis=0, tiled=True),
        lax.all_gather(b_qkv, "wsh", axis=0, tiled=True),
        lax.all_gather(w_out, "wsh", axis=0, tiled=True),
        lax.all_gather(b_out, "wsh", axis=0, tiled=True),
        lax.all_gather(w_up, "wsh", axis=0, tiled=True),
        lax.all_gather(b_up, "wsh", axis=0, tiled=True),
        lax.all_gather(w_down, "wsh", axis=0, tiled=True),
        lax.all_gather(b_down, "wsh", axis=0, tiled=True),
    )
    (
        norm1_gain,
        norm1_shift,
        norm2_gain,
        norm2_shift,
        qkv_weight,
        qkv_bias,
        out_weight,
        out_bias,
        up_weight,
        up_bias,
        down_weight,
        down_bias,
    ) = gathered
    tok_rows = tokens.shape[1]
    model_width = tokens.shape[2]
    half_rows = tok_rows // 2
    seq_rows = tok_rows * lax.axis_size("ctx")
    head_count = H
    head_size = HD
    ctx_index = lax.axis_index("ctx")
    own_blocks = lax.dynamic_slice_in_dim(block_map, 2 * ctx_index, 2)
    local_offsets = jnp.arange(half_rows, dtype=jnp.int32)
    positions = (own_blocks[:, None] * half_rows + local_offsets[None, :]).reshape(tok_rows)
    key_pos = (block_map[:, None] * half_rows + local_offsets[None, :]).reshape(seq_rows)
    length = lengths[0]
    own_live = positions < length
    live_rows = own_live.astype(jnp.float32)
    key_live = key_pos < length
    gain_first = norm1_gain.astype(jnp.float32)
    gain_second = norm2_gain.astype(jnp.float32)
    token_rows = tokens[0].astype(jnp.float32)
    normal_first, normed_first, inverse_first = norm_forward(
        token_rows, gain_first, norm1_shift.astype(jnp.float32)
    )
    normal_second, normed_second, inverse_second = norm_forward(
        token_rows, gain_second, norm2_shift.astype(jnp.float32)
    )
    attn_in = normal_first.astype(jnp.bfloat16)
    mlp_in = normal_second.astype(jnp.bfloat16)
    projected = (
        jnp.dot(attn_in, qkv_weight, preferred_element_type=jnp.float32)
        + qkv_bias.astype(jnp.float32)
    ).reshape(tok_rows, 3, head_count, head_size)
    cosine_table, sine_table = rotary_tables(positions)
    queries = rotate_forward(projected[:, 0], cosine_table, sine_table).astype(jnp.bfloat16)
    key_own = (
        rotate_forward(projected[:, 1], cosine_table, sine_table)
        .astype(jnp.bfloat16)
        .reshape(tok_rows, model_width)
    )
    value_own = projected[:, 2].astype(jnp.bfloat16).reshape(tok_rows, model_width)
    keys_all, values_all = (
        lax.all_gather(key_own, "ctx", axis=0, tiled=True),
        lax.all_gather(value_own, "ctx", axis=0, tiled=True),
    )
    block_len = math.gcd(seq_rows, 1024)
    block_count = seq_rows // block_len
    key_stack = keys_all.reshape(block_count, block_len, head_count, head_size)
    value_stack = values_all.reshape(block_count, block_len, head_count, head_size)
    pos_stack = key_pos.reshape(block_count, block_len)
    live_stack = key_live.reshape(block_count, block_len)

    def stats_step(running, key_part):
        key_block, pos_block, live_block = key_part
        scores, allowed = masked_scores(queries, key_block, positions, pos_block, live_block)
        peak_score = jnp.maximum(running[0], jnp.max(scores, axis=-1))
        exp_total = running[1] * jnp.exp(running[0] - peak_score) + jnp.sum(
            jnp.where(allowed[None], jnp.exp(scores - peak_score[..., None]), 0.0), axis=-1
        )
        return ((peak_score, exp_total), None)

    start_peak = jnp.full((head_count, tok_rows), -1e30, jnp.float32)
    final_state = lax.scan(
        stats_step, (start_peak, jnp.zeros_like(start_peak)), (key_stack, pos_stack, live_stack)
    )[0]
    log_total = final_state[0] + jnp.log(final_state[1])

    def value_step(running, key_part):
        key_block, value_block, pos_block, live_block = key_part
        scores = masked_scores(queries, key_block, positions, pos_block, live_block)[0]
        probability = jnp.exp(scores - log_total[..., None]).astype(jnp.bfloat16)
        return (
            running
            + jnp.einsum(
                "hqk,khd->qhd", probability, value_block, preferred_element_type=jnp.float32
            ),
            None,
        )

    zero_heads = jnp.zeros((tok_rows, head_count, head_size), jnp.float32)
    attended = lax.scan(value_step, zero_heads, (key_stack, value_stack, pos_stack, live_stack))[0]
    context_low = attended.reshape(tok_rows, model_width).astype(jnp.bfloat16)
    hidden = jnp.dot(mlp_in, up_weight, preferred_element_type=jnp.float32) + up_bias.astype(
        jnp.float32
    )
    activated, gelu_pull = jax.vjp(partial(jax.nn.gelu, approximate=False), hidden)
    act_low = activated.astype(jnp.bfloat16)
    branch = (
        jnp.dot(context_low, out_weight, preferred_element_type=jnp.float32)
        + out_bias.astype(jnp.float32)
        + jnp.dot(act_low, down_weight, preferred_element_type=jnp.float32)
        + down_bias.astype(jnp.float32)
    )
    output_rows = (live_rows[:, None] * (token_rows + branch)).astype(jnp.bfloat16)
    cot_rows = cotangent[0].astype(jnp.float32)
    grad_branch = (live_rows[:, None] * cot_rows).astype(jnp.bfloat16)
    grad_w_out = jnp.einsum(
        "tc,td->cd", context_low, grad_branch, preferred_element_type=jnp.float32
    )
    grad_w_down = jnp.einsum("tc,td->cd", act_low, grad_branch, preferred_element_type=jnp.float32)
    grad_branch_sum = jnp.sum(grad_branch.astype(jnp.float32), axis=0)
    grad_act = jnp.einsum("td,cd->tc", grad_branch, down_weight, preferred_element_type=jnp.float32)
    grad_hidden = gelu_pull(grad_act)[0].astype(jnp.bfloat16)
    grad_w_up = jnp.einsum("tc,td->cd", mlp_in, grad_hidden, preferred_element_type=jnp.float32)
    grad_b_up = jnp.sum(grad_hidden.astype(jnp.float32), axis=0)
    grad_mlp_in = jnp.einsum(
        "td,cd->tc", grad_hidden, up_weight, preferred_element_type=jnp.float32
    )
    grad_context = jnp.einsum(
        "td,cd->tc", grad_branch, out_weight, preferred_element_type=jnp.float32
    ).astype(jnp.bfloat16)
    grad_heads = grad_context.reshape(tok_rows, head_count, head_size)
    row_dots = jnp.sum(grad_heads.astype(jnp.float32) * attended, axis=-1).T

    def grad_step(running, key_part):
        key_block, value_block, pos_block, live_block = key_part
        prob_low, grad_score = score_grads(
            queries,
            key_block,
            value_block,
            grad_heads,
            positions,
            pos_block,
            live_block,
            log_total,
            row_dots,
        )
        query_sum = running + jnp.einsum(
            "hqk,khd->qhd", grad_score, key_block, preferred_element_type=jnp.float32
        )
        key_term = jnp.einsum(
            "hqk,qhd->khd", grad_score, queries, preferred_element_type=jnp.float32
        )
        value_term = jnp.einsum(
            "hqk,qhd->khd", prob_low, grad_heads, preferred_element_type=jnp.float32
        )
        return (query_sum, (key_term, value_term))

    query_grad, term_stacks = lax.scan(
        grad_step, zero_heads, (key_stack, value_stack, pos_stack, live_stack)
    )
    key_grad, value_grad = (
        lax.psum_scatter(
            term_stacks[0].reshape(seq_rows, model_width).astype(jnp.bfloat16),
            "ctx",
            scatter_dimension=0,
            tiled=True,
        ).astype(jnp.float32),
        lax.psum_scatter(
            term_stacks[1].reshape(seq_rows, model_width).astype(jnp.bfloat16),
            "ctx",
            scatter_dimension=0,
            tiled=True,
        ).astype(jnp.float32),
    )
    key_grad = key_grad.reshape(tok_rows, head_count, head_size)
    value_grad = value_grad.reshape(tok_rows, head_count, head_size)
    grad_projected = (
        jnp.stack(
            [
                rotate_backward(query_grad, cosine_table, sine_table),
                rotate_backward(key_grad, cosine_table, sine_table),
                value_grad,
            ],
            axis=1,
        )
        .reshape(tok_rows, 3 * model_width)
        .astype(jnp.bfloat16)
    )
    grad_w_qkv = jnp.einsum(
        "tc,td->cd", attn_in, grad_projected, preferred_element_type=jnp.float32
    )
    grad_b_qkv = jnp.sum(grad_projected.astype(jnp.float32), axis=0)
    grad_attn_in = jnp.einsum(
        "td,cd->tc", grad_projected, qkv_weight, preferred_element_type=jnp.float32
    )
    grad_input_first, grad_gain_first, grad_shift_first = norm_backward(
        grad_attn_in, normed_first, inverse_first, gain_first
    )
    grad_input_second, grad_gain_second, grad_shift_second = norm_backward(
        grad_mlp_in, normed_second, inverse_second, gain_second
    )
    grad_input = live_rows[:, None] * cot_rows + grad_input_first + grad_input_second
    shares = (
        lax.psum_scatter(
            grad_gain_first.astype(jnp.bfloat16), "wsh", scatter_dimension=0, tiled=True
        ).astype(jnp.float32),
        lax.psum_scatter(
            grad_shift_first.astype(jnp.bfloat16), "wsh", scatter_dimension=0, tiled=True
        ).astype(jnp.float32),
        lax.psum_scatter(
            grad_gain_second.astype(jnp.bfloat16), "wsh", scatter_dimension=0, tiled=True
        ).astype(jnp.float32),
        lax.psum_scatter(
            grad_shift_second.astype(jnp.bfloat16), "wsh", scatter_dimension=0, tiled=True
        ).astype(jnp.float32),
        lax.psum_scatter(
            grad_w_qkv.astype(jnp.bfloat16), "wsh", scatter_dimension=0, tiled=True
        ).astype(jnp.float32),
        lax.psum_scatter(
            grad_b_qkv.astype(jnp.bfloat16), "wsh", scatter_dimension=0, tiled=True
        ).astype(jnp.float32),
        lax.psum_scatter(
            grad_w_out.astype(jnp.bfloat16), "wsh", scatter_dimension=0, tiled=True
        ).astype(jnp.float32),
        lax.psum_scatter(
            grad_branch_sum.astype(jnp.bfloat16), "wsh", scatter_dimension=0, tiled=True
        ).astype(jnp.float32),
        lax.psum_scatter(
            grad_w_up.astype(jnp.bfloat16), "wsh", scatter_dimension=0, tiled=True
        ).astype(jnp.float32),
        lax.psum_scatter(
            grad_b_up.astype(jnp.bfloat16), "wsh", scatter_dimension=0, tiled=True
        ).astype(jnp.float32),
        lax.psum_scatter(
            grad_w_down.astype(jnp.bfloat16), "wsh", scatter_dimension=0, tiled=True
        ).astype(jnp.float32),
        lax.psum_scatter(
            grad_branch_sum.astype(jnp.bfloat16), "wsh", scatter_dimension=0, tiled=True
        ).astype(jnp.float32),
    )
    totals = (
        lax.psum(shares[0].astype(jnp.bfloat16), "ctx").astype(jnp.float32),
        lax.psum(shares[1].astype(jnp.bfloat16), "ctx").astype(jnp.float32),
        lax.psum(shares[2].astype(jnp.bfloat16), "ctx").astype(jnp.float32),
        lax.psum(shares[3].astype(jnp.bfloat16), "ctx").astype(jnp.float32),
        lax.psum(shares[4].astype(jnp.bfloat16), "ctx").astype(jnp.float32),
        lax.psum(shares[5].astype(jnp.bfloat16), "ctx").astype(jnp.float32),
        lax.psum(shares[6].astype(jnp.bfloat16), "ctx").astype(jnp.float32),
        lax.psum(shares[7].astype(jnp.bfloat16), "ctx").astype(jnp.float32),
        lax.psum(shares[8].astype(jnp.bfloat16), "ctx").astype(jnp.float32),
        lax.psum(shares[9].astype(jnp.bfloat16), "ctx").astype(jnp.float32),
        lax.psum(shares[10].astype(jnp.bfloat16), "ctx").astype(jnp.float32),
        lax.psum(shares[11].astype(jnp.bfloat16), "ctx").astype(jnp.float32),
    )
    return (
        output_rows[None],
        grad_input[None],
        totals[0],
        totals[1],
        totals[2],
        totals[3],
        totals[4],
        totals[5],
        totals[6],
        totals[7],
        totals[8],
        totals[9],
        totals[10],
        totals[11],
    )


HB = 128
NEG=-1e30
f32=jnp.float32; bf16=jnp.bfloat16

def _nn(a,b): return lax.dot_general(a,b,(((1,),(0,)),((),())),preferred_element_type=f32)
def _nt(a,b): return lax.dot_general(a,b,(((1,),(1,)),((),())),preferred_element_type=f32)

def attn_fwd_kernel(bm, x_ref, o_ref, lse_ref, q_s, kt_s, v_s, *, nblk, bq, bk):
    def perm(i,_):
        p=bm[i]; c=i//2; l=pl.multiple_of((i%2)*HB,HB); d=pl.multiple_of(p*HB,HB)
        q_s[:,pl.ds(d,HB)]=x_ref[c,0:64,pl.ds(l,HB)]*bf16(0.125)
        kt_s[pl.ds(d,HB),:]=x_ref[c,64:128,pl.ds(l,HB)].astype(f32).T.astype(bf16)
        v_s[:,pl.ds(d,HB)]=x_ref[c,128:192,pl.ds(l,HB)]
        return 0
    lax.fori_loop(0,nblk,perm,0)
    S=nblk*HB; nq=S//bq; r=bq//bk
    def step(q,qo,ko,carry,mask):
        m,l,acc=carry
        s=_nn(kt_s[pl.ds(ko,bk),:],q)
        if mask is not None: s=jnp.where(mask,s,NEG)
        mn=jnp.maximum(m,jnp.max(s,axis=0,keepdims=True))
        a=jnp.exp(m-mn); p=jnp.exp(s-mn)
        l=l*a+jnp.sum(p,axis=0,keepdims=True)
        acc=acc*a+_nn(v_s[:,pl.ds(ko,bk)],p.astype(bf16))
        return mn,l,acc
    ki=lax.broadcasted_iota(jnp.int32,(bk,bq),0); qi_=lax.broadcasted_iota(jnp.int32,(bk,bq),1)
    def qloop(i,_):
        qo=pl.multiple_of(i*bq,bq)
        q=q_s[:,pl.ds(qo,bq)]
        c=(jnp.full((1,bq),NEG,f32),jnp.zeros((1,bq),f32),jnp.zeros((64,bq),f32))
        c=lax.fori_loop(0,i*r,lambda j,c: step(q,qo,pl.multiple_of(j*bk,bk),c,None),c)
        for t in range(r):
            c=step(q,qo,pl.multiple_of(qo+t*bk,bk),c,ki+t*bk<=qi_)
        m,l,acc=c
        q_s[:,pl.ds(qo,bq)]=(acc*(1.0/l)).astype(bf16)
        lse_ref[:,pl.ds(qo,bq)]=m+jnp.log(l)
        return 0
    lax.fori_loop(0,nq,qloop,0)
    def unperm(i,_):
        p=bm[i]; c=i//2; l=pl.multiple_of((i%2)*HB,HB); d=pl.multiple_of(p*HB,HB)
        o_ref[c,:,pl.ds(l,HB)]=q_s[:,pl.ds(d,HB)]
        return 0
    lax.fori_loop(0,nblk,unperm,0)

def attn_fwd(bm,x,*,bq=512,bk=512):
    n=x.shape[0]; S=n*256; nblk=2*n
    bq=math.gcd(S,bq); bk=math.gcd(bq,bk)
    return pl.pallas_call(
        lambda *a: attn_fwd_kernel(*a,nblk=nblk,bq=bq,bk=bk),
        out_shape=(jax.ShapeDtypeStruct((n,64,256),bf16),jax.ShapeDtypeStruct((1,S),f32)),
        in_specs=[pl.BlockSpec(memory_space=pltpu.SMEM),pl.BlockSpec(memory_space=pltpu.VMEM)],
        out_specs=(pl.BlockSpec(memory_space=pltpu.VMEM),pl.BlockSpec(memory_space=pltpu.VMEM)),
        scratch_shapes=[pltpu.VMEM((64,S),bf16),pltpu.VMEM((S,64),bf16),pltpu.VMEM((64,S),bf16)],
        compiler_params=pltpu.CompilerParams(vmem_limit_bytes=56<<20),name="attn_fwd")(bm,x)

def attn_bwd_kernel(bm, x_ref, o_ref, do_ref, lse_ref, cs_ref, g_ref, q_s, kt_s, k_s, vt_s, do_s, dl_s, dq_s, dk_s, dv_s, *, nblk, bq, bk):
    def perm(i,_):
        p=bm[i]; c=i//2; l=pl.multiple_of((i%2)*HB,HB); d=pl.multiple_of(p*HB,HB)
        q_s[:,pl.ds(d,HB)]=x_ref[c,0:64,pl.ds(l,HB)]*bf16(0.125)
        k=x_ref[c,64:128,pl.ds(l,HB)]
        k_s[:,pl.ds(d,HB)]=k*bf16(0.125)
        kt_s[pl.ds(d,HB),:]=k.astype(f32).T.astype(bf16)
        vt_s[pl.ds(d,HB),:]=x_ref[c,128:192,pl.ds(l,HB)].astype(f32).T.astype(bf16)
        do=do_ref[c,:,pl.ds(l,HB)]
        do_s[:,pl.ds(d,HB)]=do
        dl_s[:,pl.ds(d,HB)]=jnp.sum(do.astype(f32)*o_ref[c,:,pl.ds(l,HB)].astype(f32),axis=0,keepdims=True)
        return 0
    lax.fori_loop(0,nblk,perm,0)
    S=nblk*HB; nq=S//bq; r=bq//bk
    dk_s[...]=jnp.zeros_like(dk_s); dv_s[...]=jnp.zeros_like(dv_s)
    def step(q,do,lse,dl,ko,dq,mask):
        s=_nn(kt_s[pl.ds(ko,bk),:],q)
        p=jnp.exp(s-lse)
        if mask is not None: p=jnp.where(mask,p,0.0)
        dp=_nn(vt_s[pl.ds(ko,bk),:],do)
        ds=(p*(dp-dl)).astype(bf16)
        pb=p.astype(bf16)
        dv_s[:,pl.ds(ko,bk)]+=_nt(do,pb)
        dk_s[:,pl.ds(ko,bk)]+=_nt(q,ds)
        return dq+_nn(k_s[:,pl.ds(ko,bk)],ds)
    ki=lax.broadcasted_iota(jnp.int32,(bk,bq),0); qi_=lax.broadcasted_iota(jnp.int32,(bk,bq),1)
    def qloop(i,_):
        qo=pl.multiple_of(i*bq,bq)
        q=q_s[:,pl.ds(qo,bq)]; do=do_s[:,pl.ds(qo,bq)]; lse=lse_ref[:,pl.ds(qo,bq)]; dl=dl_s[:,pl.ds(qo,bq)]
        dq=jnp.zeros((64,bq),f32)
        dq=lax.fori_loop(0,i*r,lambda j,c: step(q,do,lse,dl,pl.multiple_of(j*bk,bk),c,None),dq)
        for t in range(r):
            dq=step(q,do,lse,dl,pl.multiple_of(qo+t*bk,bk),dq,ki+t*bk<=qi_)
        dq_s[:,pl.ds(qo,bq)]=dq
        return 0
    lax.fori_loop(0,nq,qloop,0)
    def unperm(i,_):
        p=bm[i]; c=i//2; l=pl.multiple_of((i%2)*HB,HB); d=pl.multiple_of(p*HB,HB)
        cos=cs_ref[0:8,pl.ds(d,HB)]; sin=cs_ref[8:16,pl.ds(d,HB)]
        for n_,src in ((0,dq_s),(1,dk_s)):
            g=src[:,pl.ds(d,HB)]
            a=g[0:8]; b=g[8:16]
            full=jnp.concatenate([a*cos+b*sin,b*cos-a*sin,g[16:64]],axis=0)
            g_ref[c,64*n_:64*n_+64,pl.ds(l,HB)]=full.astype(bf16)
        g_ref[c,128:192,pl.ds(l,HB)]=dv_s[:,pl.ds(d,HB)].astype(bf16)
        return 0
    lax.fori_loop(0,nblk,unperm,0)

def attn_bwd(bm,x,o,do,lse,cs,*,bq=512,bk=512):
    n=x.shape[0]; S=n*256; nblk=2*n
    bq=math.gcd(S,bq); bk=math.gcd(bq,bk)
    vm=pl.BlockSpec(memory_space=pltpu.VMEM)
    return pl.pallas_call(
        lambda *a: attn_bwd_kernel(*a,nblk=nblk,bq=bq,bk=bk),
        out_shape=jax.ShapeDtypeStruct((n,192,256),bf16),
        in_specs=[pl.BlockSpec(memory_space=pltpu.SMEM)]+[vm]*5,
        out_specs=vm,
        scratch_shapes=[pltpu.VMEM((64,S),bf16),pltpu.VMEM((S,64),bf16),pltpu.VMEM((64,S),bf16),pltpu.VMEM((S,64),bf16),pltpu.VMEM((64,S),bf16),
                        pltpu.VMEM((1,S),f32),pltpu.VMEM((64,S),f32),pltpu.VMEM((64,S),f32),pltpu.VMEM((64,S),f32)],
        compiler_params=pltpu.CompilerParams(vmem_limit_bytes=56<<20),name="attn_bwd")(bm,x,o,do,lse,cs)


SWAP = [(0, 1), (1, 0)]


def fast_fits(mesh):
    return mesh.shape["wsh"] == 2 and mesh.shape["ctx"] == H


def _params(mb=56):
    return pltpu.CompilerParams(vmem_limit_bytes=mb << 20)


def _norm(x):
    xf = x.astype(f32)
    cen = xf - jnp.mean(xf, axis=-1, keepdims=True)
    inv = lax.rsqrt(jnp.mean(cen * cen, axis=-1, keepdims=True) + epsilon)
    return cen * inv, inv


def _pieces(ids):
    me, core = ids[0], ids[1]
    return me, core


def qkv_kernel(
    ids, xo_ref, xg_ref, n_ref, wq_ref, wk_ref, wv_ref, gq_ref, gk_ref, gv_ref, sq_ref, sk_ref, sv_ref,
    bq_ref, bk_ref, bv_ref, cs_ref, send_ref, ain_ref, min_ref
):
    rows, width = xo_ref.shape
    half = width // 2
    q4 = half // 2

    @pl.when(pl.program_id(0) == 0)
    def _():
        for s in range(2):
            x = xo_ref[...] if s == 0 else jnp.concatenate([xg_ref[0:rows, :], xg_ref[rows:, :]], axis=1)
            xhat, _ = _norm(x)
            ain_ref[s * rows : (s + 1) * rows, :] = (xhat * n_ref[0:1, :] + n_ref[1:2, :]).astype(bf16)
            min_ref[s * rows : (s + 1) * rows, :] = (xhat * n_ref[2:3, :] + n_ref[3:4, :]).astype(bf16)

    me = ids[0]
    core = ids[1]
    base = (1 - me) * half
    a_own = ain_ref[:, pl.ds(pl.multiple_of(me * half, half), half)]
    a_got = ain_ref[:, pl.ds(pl.multiple_of(base + core * q4, q4), q4)]
    a_sib = ain_ref[:, pl.ds(pl.multiple_of(base + (1 - core) * q4, q4), q4)]
    cos = cs_ref[0:8, :]
    sin = cs_ref[8:16, :]
    for n, (w, g, sb, b) in enumerate(
        (
            (wq_ref, gq_ref, sq_ref, bq_ref),
            (wk_ref, gk_ref, sk_ref, bk_ref),
            (wv_ref, gv_ref, sv_ref, bv_ref),
        )
    ):
        t = _nn(a_own, w[...]) + _nn(a_got, g[...]) + _nn(a_sib, sb[...]) + b[...]
        t = t.T
        for s in range(2):
            for k in range(2):
                v = t[k * HD : (k + 1) * HD, s * rows : (s + 1) * rows]
                if n < 2:
                    lead = v[0:8]
                    trail = v[8:16]
                    v = jnp.concatenate([lead * cos - trail * sin, trail * cos + lead * sin, v[16:]], axis=0)
                send_ref[s, k, n * HD : (n + 1) * HD, :] = v.astype(bf16)


def _wq_specs(half, width, rows):
    own = lambda p: pl.BlockSpec((half, 128), lambda i, ids: (0, p * (width // 128) + ids[0] * (half // 128) + i))
    got = lambda p: pl.BlockSpec((half // 2, 128), lambda i, ids: (2 * rows // (half // 2) + p, i))
    sib = lambda p: pl.BlockSpec((half // 2, 128), lambda i, ids: (p, i))
    return [own(p) for p in range(3)] + [got(p) for p in range(3)] + [sib(p) for p in range(3)]


def _x_got_spec(rows, half):
    return pl.BlockSpec((2 * rows, half), lambda i, ids: (0, 0))


def qkv_forward(ids, xo, got, norms, w_own, w_sib, bias, cs):
    rows, width = xo.shape
    half = width // 2
    full = lambda a: pl.BlockSpec(a.shape, lambda i, ids: (0,) * a.ndim)
    bsp = lambda p: pl.BlockSpec((1, 128), lambda i, ids: (0, p * (half // 128) + i))
    heads = half // HD
    res = lambda: pl.BlockSpec((2 * rows, width), lambda i, ids: (0, 0))
    return pl.pallas_call(
        qkv_kernel,
        grid_spec=pltpu.PrefetchScalarGridSpec(
            num_scalar_prefetch=1,
            grid=(half // 128,),
            in_specs=[full(xo), _x_got_spec(rows, half), full(norms)]
            + _wq_specs(half, width, rows)
            + [bsp(p) for p in range(3)]
            + [full(cs)],
            out_specs=(pl.BlockSpec((2, 2, 3 * HD, rows), lambda i, ids: (0, i, 0, 0)), res(), res()),
        ),
        out_shape=(
            jax.ShapeDtypeStruct((2, heads, 3 * HD, rows), bf16),
            jax.ShapeDtypeStruct((2 * rows, width), bf16),
            jax.ShapeDtypeStruct((2 * rows, width), bf16),
        ),
        compiler_params=_params(),
        name="qkv_forward",
    )(ids, xo, got, norms, w_own, w_own, w_own, got, got, got, w_sib, w_sib, w_sib, bias, bias, bias, cs)


def mlp_kernel(
    ids, x_ref, dy_ref, wo_ref, wg_ref, ws_ref, wd_ref, bu_ref, y_ref, dx_ref, gu_ref, gd_ref, gb_ref, xt_s
):
    first = pl.program_id(0) == 0
    rows, width = x_ref.shape
    half = width // 2
    q4 = half // 2
    me = ids[0]
    core = ids[1]
    base = (1 - me) * half
    spans = (
        (pl.multiple_of(me * half, half), half, wo_ref),
        (pl.multiple_of(base + core * q4, q4), q4, wg_ref),
        (pl.multiple_of(base + (1 - core) * q4, q4), q4, ws_ref),
    )

    @pl.when(first)
    def _():
        xt_s[...] = x_ref[...].astype(f32).T.astype(bf16)
        y_ref[...] = jnp.zeros_like(y_ref)
        dx_ref[...] = jnp.zeros_like(dx_ref)

    dy = dy_ref[...]
    wd = wd_ref[...]
    u = bu_ref[...] + sum(_nn(x_ref[:, pl.ds(o, n)], w[...]) for o, n, w in spans)
    cdf = 0.5 * (1.0 + lax.erf(u * (1.0 / math.sqrt(2.0))))
    pdf = jnp.exp(-0.5 * u * u) * (1.0 / math.sqrt(2.0 * math.pi))
    act = (u * cdf).astype(bf16)
    du = (_nt(dy, wd) * (cdf + u * pdf)).astype(bf16)
    y_ref[...] += _nn(act, wd)
    for o, n, w in spans:
        dx_ref[:, pl.ds(o, n)] += _nt(du, w[...])
    gd_ref[...] = lax.dot_general(
        act, dy, (((0,), (0,)), ((), ())), preferred_element_type=f32
    ).astype(bf16)
    gu = _nn(xt_s[...], du).astype(bf16)
    n = gu_ref.shape[0]
    r = half // n
    for h in range(2):
        for c in range(n):
            gu_ref[c, h * r : (h + 1) * r, :] = gu[h * half + c * r : h * half + (c + 1) * r, :]
    gb_ref[...] = jnp.sum(du.astype(f32), axis=0, keepdims=True)


def mlp(ids, x, dy, w_own, w_got, w_sib, wd, bu, n, tile=256):
    rows, width = x.shape
    half = width // 2
    hidden = w_got.shape[1]
    steps = hidden // tile
    whole = pl.BlockSpec((rows, width), lambda i, ids: (0, 0))
    down = pl.BlockSpec((tile, width), lambda i, ids: (i, 0))
    vec = pl.BlockSpec((1, tile), lambda i, ids: (0, i))
    return pl.pallas_call(
        mlp_kernel,
        grid_spec=pltpu.PrefetchScalarGridSpec(
            num_scalar_prefetch=1,
            grid=(steps,),
            in_specs=[
                whole,
                whole,
                pl.BlockSpec((half, tile), lambda i, ids: (0, ids[0] * steps + i)),
                pl.BlockSpec((half // 2, tile), lambda i, ids: (0, i)),
                pl.BlockSpec((half // 2, tile), lambda i, ids: (0, i)),
                down,
                vec,
            ],
            out_specs=(whole, whole, pl.BlockSpec((n, width // n, tile), lambda i, ids: (0, 0, i)), down, vec),
            scratch_shapes=[pltpu.VMEM((width, rows), bf16)],
        ),
        out_shape=(
            jax.ShapeDtypeStruct((rows, width), f32),
            jax.ShapeDtypeStruct((rows, width), f32),
            jax.ShapeDtypeStruct((n, width // n, hidden), bf16),
            jax.ShapeDtypeStruct((hidden, width), bf16),
            jax.ShapeDtypeStruct((1, hidden), f32),
        ),
        compiler_params=_params(),
        cost_estimate=pl.CostEstimate(
            flops=12 * rows * width * hidden, transcendentals=2 * rows * hidden, bytes_accessed=24 << 20
        ),
        name="mlp",
    )(ids, x, dy, w_own, w_got, w_sib, wd, bu)


def qkv_back_kernel(
    ids, d_ref, a_ref, xo_ref, xg_ref, n_ref, wq_ref, wk_ref, wv_ref, gq_ref, gk_ref, gv_ref, sq_ref, sk_ref,
    sv_ref, dm_ref, ob_ref, dy_ref, gb_ref, ga_ref, gb2_ref, eo_ref, ex_ref, at_s, da_s, bs_s
):
    rows, width = xo_ref.shape
    half = width // 2
    q4 = half // 2
    me = ids[0]
    core = ids[1]
    base = (1 - me) * half
    i = pl.program_id(0)
    outs = (ga_ref, gb2_ref)
    n = ga_ref.shape[0]
    r = half // (2 * n)
    lanes = pl.ds(pl.multiple_of(i * 128, 128), 128)

    @pl.when(i == 0)
    def _():
        at_s[...] = a_ref[...].astype(f32).T.astype(bf16)
        da_s[...] = jnp.zeros_like(da_s)

    ones = jnp.ones((8, rows), bf16)
    for p, (w, gw, sw) in enumerate(
        ((wq_ref, gq_ref, sq_ref), (wk_ref, gk_ref, sk_ref), (wv_ref, gv_ref, sv_ref))
    ):
        g = jnp.zeros((width, 128), f32)
        b = jnp.zeros((8, 128), f32)
        for s in range(2):
            dp = jnp.concatenate([d_ref[s, k, p * HD : (p + 1) * HD, :] for k in range(2)], axis=0)
            g = g + _nt(at_s[:, s * rows : (s + 1) * rows], dp)
            b = b + _nt(ones, dp)
            dt = dp.astype(f32).T.astype(bf16)
            for o, m, ref in (
                (pl.multiple_of(me * half, half), half, w),
                (pl.multiple_of(base + core * q4, q4), q4, gw),
                (pl.multiple_of(base + (1 - core) * q4, q4), q4, sw),
            ):
                da_s[s * rows : (s + 1) * rows, pl.ds(o, m)] += _nt(dt, ref[...])
        bs_s[p * 8 : (p + 1) * 8, lanes] = b
        g16 = g.astype(bf16)
        for h in range(2):
            for c in range(n):
                for a in range(2):
                    at = h * half + (c * 2 + a) * r
                    u = (h * 3 + p) * r
                    outs[a][c, u : u + r, lanes] = g16[at : at + r, :]

    go = sum(_nn(ob_ref[s], dy_ref[s * rows : (s + 1) * rows, :]) for s in range(2)).astype(bf16)
    per = 128 // (2 * r)
    for k in range(per):
        for a in range(2):
            at = (k * 2 + a) * r
            for h in range(2):
                u = (6 + h) * r
                outs[a][i * per + k, u : u + r, :] = go[at : at + r, h * half : (h + 1) * half]

    @pl.when(i == pl.num_programs(0) - 1)
    def _():
        sums = [jnp.zeros((1, width), f32) for _ in range(4)]
        for s in range(2):
            x = xo_ref[...] if s == 0 else jnp.concatenate([xg_ref[0:rows, :], xg_ref[rows:, :]], axis=1)
            xhat, _ = _norm(x)
            da = da_s[s * rows : (s + 1) * rows, :]
            dm = dm_ref[s * rows : (s + 1) * rows, :]
            e = da * n_ref[0:1, :] + dm * n_ref[2:3, :]
            if s == 0:
                eo_ref[...] = e
            else:
                ex_ref[...] = e.astype(bf16)
            for k, v in enumerate((da * xhat, da, dm * xhat, dm)):
                sums[k] = sums[k] + jnp.sum(v, axis=0, keepdims=True)
        sums.append(jnp.sum(dy_ref[0:rows, :].astype(f32), axis=0, keepdims=True))
        flat = [v[:, h * half : (h + 1) * half] for v in sums for h in range(2)]
        zero = jnp.zeros((1, half), f32)
        for p in range(3):
            flat += [jnp.where(me == k, bs_s[p * 8 : p * 8 + 1, :], zero) for k in range(2)]
        hid = gb_ref.shape[1] // half
        flat += [
            jnp.where(me == k, gb_ref[:, t * half : (t + 1) * half], zero) for k in range(2) for t in range(hid)
        ]
        flat += [zero] * (2 * n - len(flat))
        pad = jnp.zeros((6, half), f32)
        top = 8 * r
        for c in range(n):
            gb2_ref[c, top : top + 8, :] = jnp.concatenate([flat[2 * c], flat[2 * c + 1], pad], axis=0).astype(bf16)


def qkv_backward(ids, d, a, xo, got, norms, w_own, w_sib, d_mlp, ob, dy, gb_up, n):
    rows, width = xo.shape
    half = width // 2
    r = half // (2 * n)
    full = lambda v: pl.BlockSpec(v.shape, lambda i, ids: (0,) * v.ndim)
    out = [
        jax.ShapeDtypeStruct((n, 8 * r, half), bf16),
        jax.ShapeDtypeStruct((n, 8 * r + 8, half), bf16),
        jax.ShapeDtypeStruct((rows, width), f32),
        jax.ShapeDtypeStruct((rows, width), bf16),
    ]
    return pl.pallas_call(
        qkv_back_kernel,
        grid_spec=pltpu.PrefetchScalarGridSpec(
            num_scalar_prefetch=1,
            grid=(half // 128,),
            in_specs=[pl.BlockSpec((2, 2, 3 * HD, rows), lambda i, ids: (0, i, 0, 0))]
            + [full(a), full(xo), _x_got_spec(rows, half), full(norms)]
            + _wq_specs(half, width, rows)
            + [full(d_mlp), pl.BlockSpec((2, 128, rows), lambda i, ids: (0, i, 0)), full(dy), full(gb_up)],
            out_specs=tuple(full(v) for v in out),
            scratch_shapes=[
                pltpu.VMEM((width, 2 * rows), bf16),
                pltpu.VMEM((2 * rows, width), f32),
                pltpu.VMEM((24, half), f32),
            ],
        ),
        out_shape=tuple(out),
        compiler_params=_params(),
        name="qkv_backward",
    )(ids, d, a, xo, got, norms, w_own, w_own, w_own, got, got, got, w_sib, w_sib, w_sib, d_mlp, ob, dy, gb_up)


def join_kernel(ids, own_ref, got_ref, o_ref):
    mine = (pl.program_id(0) // (pl.num_programs(0) // 2)) == ids[1]

    @pl.when(mine)
    def _():
        o_ref[...] = own_ref[...].astype(f32)

    @pl.when(jnp.logical_not(mine))
    def _():
        o_ref[...] = got_ref[...].astype(f32)


def join(ids, own, got):
    n, r, w = own.shape
    src = pl.BlockSpec((1, r, w), lambda i, ids: (i % n, 0, 0))
    return pl.pallas_call(
        join_kernel,
        grid_spec=pltpu.PrefetchScalarGridSpec(
            num_scalar_prefetch=1,
            grid=(2 * n,),
            in_specs=[src, src],
            out_specs=pl.BlockSpec((1, r, w), lambda i, ids: (i, 0, 0)),
        ),
        out_shape=jax.ShapeDtypeStruct((2 * n, r, w), f32),
        compiler_params=_params(),
        name="join",
    )(ids, own, got)


def unpack_kernel(ids, ao_ref, ag_ref, bo_ref, bg_ref, q_ref, o_ref, s_ref):
    mine = (pl.program_id(0) // (pl.num_programs(0) // 2)) == ids[1]
    r = ao_ref.shape[1] // 8
    half = ao_ref.shape[2]
    for a, (own, got) in enumerate(((ao_ref, ag_ref), (bo_ref, bg_ref))):
        v = jnp.where(mine, own[0].astype(f32), got[0].astype(f32))
        for w in range(2):
            for p in range(3):
                u = (w * 3 + p) * r
                at = (p * 2 + w) * half
                q_ref[a * r : (a + 1) * r, at : at + half] = v[u : u + r, :]
            u = (6 + w) * r
            o_ref[a * r : (a + 1) * r, w * half : (w + 1) * half] = v[u : u + r, :]
        if a == 1:
            s_ref[0] = v[8 * r : 8 * r + 8, :]


def unpack(ids, a_own, a_got, b_own, b_got):
    n, ra, half = a_own.shape
    r = ra // 8
    spec = lambda v: pl.BlockSpec((1,) + v.shape[1:], lambda i, ids: (i % n, 0, 0))
    return pl.pallas_call(
        unpack_kernel,
        grid_spec=pltpu.PrefetchScalarGridSpec(
            num_scalar_prefetch=1,
            grid=(2 * n,),
            in_specs=[spec(v) for v in (a_own, a_got, b_own, b_got)],
            out_specs=(
                pl.BlockSpec((2 * r, 6 * half), lambda i, ids: (i, 0)),
                pl.BlockSpec((2 * r, 2 * half), lambda i, ids: (i, 0)),
                pl.BlockSpec((1, 8, half), lambda i, ids: (i, 0, 0)),
            ),
        ),
        out_shape=(
            jax.ShapeDtypeStruct((4 * n * r, 6 * half), f32),
            jax.ShapeDtypeStruct((4 * n * r, 2 * half), f32),
            jax.ShapeDtypeStruct((2 * n, 8, half), f32),
        ),
        compiler_params=_params(),
        name="unpack",
    )(ids, a_own, a_got, b_own, b_got)


def last_kernel(eo_ref, er_ref, x_ref, c_ref, live_ref, o_ref):
    xhat, inv = _norm(x_ref[...])
    e = eo_ref[...] + er_ref[...].astype(f32)
    dx = inv * (
        e - jnp.mean(e, axis=-1, keepdims=True) - xhat * jnp.mean(e * xhat, axis=-1, keepdims=True)
    )
    o_ref[...] = live_ref[...] * c_ref[...].astype(f32) + dx


def last(e_own, e_got, x, cot, live):
    return pl.pallas_call(
        last_kernel,
        out_shape=jax.ShapeDtypeStruct(x.shape, f32),
        compiler_params=_params(),
        name="token_grad",
    )(e_own, e_got, x, cot, live)


def fast_shards(
    tokens,
    ln1_gain,
    ln1_bias,
    ln2_gain,
    ln2_bias,
    w_qkv,
    b_qkv,
    w_out,
    b_out,
    w_up,
    b_up,
    w_down,
    b_down,
    lengths,
    block_map,
    cotangent,
):
    ctx = lax.axis_index("ctx")
    me = lax.axis_index("wsh")
    core = ctx % 2
    n_ctx = lax.axis_size("ctx")
    rows, width = tokens.shape[1:]
    half = width // 2
    seq = rows * n_ctx
    heads = H // 2
    hid = w_up.shape[1] // 2
    ids = jnp.stack([me, core]).astype(jnp.int32)
    CORE, X, ZN, ZF = 0, 1, 2, 3

    def swap(v):
        return lax.ppermute(v, "wsh", SWAP)

    def flip(v, bit):
        return lax.ppermute(v, "ctx", [(i, i ^ (1 << bit)) for i in range(n_ctx)])

    def bit_of(bit):
        return (ctx >> bit) & 1

    def halve(v, bit):
        b = bit_of(bit)
        v = v.reshape((2, v.shape[0] // 2) + v.shape[1:])
        got = flip(lax.dynamic_index_in_dim(v, 1 - b, 0, keepdims=False), bit)
        keep = lax.dynamic_index_in_dim(v, b, 0, keepdims=False)
        return (keep.astype(f32) + got.astype(f32)).astype(bf16)

    def ordered(first, a, b, axis=0):
        return jnp.where(first == 0, jnp.concatenate([a, b], axis), jnp.concatenate([b, a], axis))

    def double(v, bit):
        return ordered(bit_of(bit), v, flip(v, bit))

    half_core = lambda v: lax.dynamic_slice_in_dim(v, core * (half // 2), half // 2, 0)

    len_parts = jnp.stack([lengths[0] // 64, lengths[0] % 64]).astype(bf16)
    small = jnp.concatenate(
        [ln1_gain, ln1_bias, ln2_gain, ln2_bias, b_out, b_down, b_qkv, len_parts, jnp.zeros((126,), bf16)]
    )[None]
    small = ordered(me, small, swap(small))
    cot_own = cotangent[0]
    cot_got = swap(cot_own)
    other = (1 - me) * half
    cols = [lax.dynamic_slice_in_dim(half_core(w_qkv), p * width + other, half, 1) for p in range(3)]
    wu_send = lax.dynamic_slice_in_dim(half_core(w_up), (1 - me) * hid, hid, 1)
    x_own = tokens[0]
    pack = jnp.concatenate([x_own[:, :half], x_own[:, half:]] + cols)
    cot_got, pack = lax.optimization_barrier((cot_got, pack))
    got = swap(pack)
    wq_sib = flip(got[2 * rows :], CORE)
    got, wu_send = lax.optimization_barrier((got, wu_send))
    wu_got = swap(wu_send)
    wu_sib = flip(wu_got, CORE)

    vec = lambda i: small[:, i * half : (i + 1) * half].reshape(width).astype(f32)
    norms = jnp.stack([vec(i) for i in range(4)])
    bias_out = vec(4) + vec(5)
    qkv_bias = small[:, 6 * half : 9 * half].astype(f32).reshape(3, width)
    qkv_bias = lax.dynamic_slice_in_dim(qkv_bias, me * half, half, 1).reshape(1, 3 * half)
    lens = small[:, 9 * half : 9 * half + 2].astype(jnp.int32)
    lens = lens[:, 0] * 64 + lens[:, 1]
    other_len = lens[1 - me]

    own_blocks = lax.dynamic_slice_in_dim(block_map, 2 * ctx, 2)
    offs = jnp.arange(HB, dtype=jnp.int32)
    positions = (own_blocks[:, None] * HB + offs[None, :]).reshape(rows)
    live_own = (positions < lengths[0]).astype(f32)[:, None]
    live_got = (positions < other_len).astype(f32)[:, None]
    freq = 10000.0 ** (-jnp.arange(ROT // 2, dtype=f32) * 2.0 / ROT)
    ang = freq[:, None] * jnp.arange(seq, dtype=jnp.int32).astype(f32)[None, :]
    table = jnp.concatenate([jnp.cos(ang), jnp.sin(ang)])
    own_ang = freq[:, None] * positions.astype(f32)[None, :]
    own_table = jnp.concatenate([jnp.cos(own_ang), jnp.sin(own_ang)])

    def exchange(v):
        return lax.all_to_all(v, "ctx", 0, 0, tiled=False)

    dy = jnp.concatenate(
        [(live_own * cot_own.astype(f32)).astype(bf16), (live_got * cot_got.astype(f32)).astype(bf16)]
    )
    dctx = jnp.einsum("ed,std->set", w_out, dy.reshape(2, rows, width), preferred_element_type=f32).astype(bf16)
    do_head = exchange(dctx.reshape(2 * heads, HD, rows))

    send, attn_in, mlp_in = qkv_forward(ids, x_own, got, norms, w_qkv, wq_sib, qkv_bias, own_table)
    qkv_head = exchange(send.reshape(2 * heads, 3 * HD, rows))

    mlp_in, do_head = lax.optimization_barrier((mlp_in, do_head))

    y_mlp, d_mlp, g_up, g_down, gb_up = mlp(
        ids, mlp_in, dy, w_up, wu_got, wu_sib, w_down, b_up.astype(f32)[None, :], n_ctx
    )

    chain_a = (CORE, X, ZN, ZF)
    chain_b = (CORE, ZN, ZF, X)
    v_down = g_down.reshape(n_ctx, hid // n_ctx, width)
    v_up = g_up
    qkv_head, v_down, v_up = lax.optimization_barrier((qkv_head, v_down, v_up))
    v_down = halve(v_down, chain_a[0])
    v_up = halve(v_up, chain_b[0])
    qkv_head, v_down, v_up = lax.optimization_barrier((qkv_head, v_down, v_up))
    v_down = halve(v_down, chain_a[1])
    v_up = halve(v_up, chain_b[1])

    o_head, lse = attn_fwd(block_map, qkv_head, bq=1024, bk=1024)
    ob = exchange(o_head).reshape(2, half, rows)
    qkv_head, v_down, v_up = lax.optimization_barrier((qkv_head, v_down, v_up))
    g_head = attn_bwd(block_map, qkv_head, o_head, do_head, lse, table)
    d_qkv = exchange(g_head).reshape(2, heads, 3 * HD, rows)

    for a, b in zip(chain_a[2:], chain_b[2:]):
        v_down = halve(v_down, a)
        v_up = halve(v_up, b)
    v_up = v_up.reshape(1, 2, half // n_ctx, hid)
    up_keep = lax.dynamic_index_in_dim(v_up, me, 1, keepdims=False)
    up_got = swap(lax.dynamic_index_in_dim(v_up, 1 - me, 1, keepdims=False))
    v_up = ordered(me, up_keep, up_got, axis=2)
    for a, b in zip(chain_a[:0:-1], chain_b[:0:-1]):
        v_down = double(v_down, a)
        v_up = double(v_up, b)
    tot_down = join(ids, v_down, flip(v_down, CORE)).reshape(hid, width)
    tot_up = join(ids, v_up, flip(v_up, CORE)).reshape(half, 2 * hid)

    part = jnp.einsum("sct,cd->std", ob, w_out, preferred_element_type=f32) + y_mlp.reshape(
        2, rows, width
    )
    y_got = swap(part[1].astype(bf16)).astype(f32)
    output = (live_own * (x_own.astype(f32) + part[0] + y_got + bias_out)).astype(bf16)

    v_a, v_b, e_own, e_send = qkv_backward(
        ids, d_qkv, attn_in, x_own, got, norms, w_qkv, wq_sib, d_mlp, ob, dy, gb_up, n_ctx
    )
    for a, b in zip(chain_a, chain_b):
        v_a = halve(v_a, a)
        v_b = halve(v_b, b)
    e_got = swap(e_send)
    n3 = 3 * half // (2 * n_ctx)
    mixed = []
    for v, chain in ((v_a[0], chain_a), (v_b[0], chain_b)):
        extra = v[8 * n3 // 3 :]
        keep = lax.dynamic_slice_in_dim(v, me * n3, n3, 0)
        give = lax.dynamic_slice_in_dim(v, (1 - me) * n3, n3, 0)
        got = swap(jnp.concatenate([give, extra]))
        extra = (extra.astype(f32) + got[n3:].astype(f32)).astype(bf16)
        v = jnp.concatenate([ordered(me, keep, got[:n3]), v[2 * n3 : 8 * n3 // 3], extra])[None]
        for a in chain[:0:-1]:
            v = double(v, a)
        mixed += [v, flip(v, CORE)]
    tot_qkv, tot_out, flat = unpack(ids, *mixed)
    grad_tokens = last(e_own, e_got, x_own, cot_own, live_own)
    flat = flat[:, :2].reshape(2 * n_ctx * half)

    def own(start, size):
        return lax.dynamic_slice_in_dim(flat, start + me * size, size)

    gb_out = own(4 * width, half)
    return (
        output[None],
        grad_tokens[None],
        own(0, half),
        own(width, half),
        own(2 * width, half),
        own(3 * width, half),
        tot_qkv,
        own(5 * width, 3 * half),
        tot_out,
        gb_out,
        tot_up,
        own(8 * width, hid),
        tot_down,
        gb_out,
    )


def solution(mesh):
    placed = (
        P("wsh", "ctx", None),
        P("wsh"),
        P("wsh"),
        P("wsh"),
        P("wsh"),
        P("wsh", None),
        P("wsh"),
        P("wsh", None),
        P("wsh"),
        P("wsh", None),
        P("wsh"),
        P("wsh", None),
        P("wsh"),
        P("wsh"),
        P(),
        P("wsh", "ctx", None),
    )
    body = fast_shards if fast_fits(mesh) else shards
    return jax.shard_map(
        body,
        mesh=mesh,
        in_specs=placed,
        out_specs=(
            P("wsh", "ctx", None),
            P("wsh", "ctx", None),
            P("wsh"),
            P("wsh"),
            P("wsh"),
            P("wsh"),
            P("wsh", None),
            P("wsh"),
            P("wsh", None),
            P("wsh"),
            P("wsh", None),
            P("wsh"),
            P("wsh", None),
            P("wsh"),
        ),
        check_vma=False,
    )
```

```python
from functools import partial
import math

import jax
import jax.numpy as jnp
from jax import lax
from jax.experimental import pallas as pl
from jax.experimental.pallas import tpu as pltpu
from jax.sharding import PartitionSpec as P

H = 16
HD = 64
ROT = 16


epsilon = 1e-05


def norm_forward(values, norm_gain, norm_shift):
    average = jnp.mean(values, axis=-1, keepdims=True)
    centred = values - average
    variance = jnp.mean(centred * centred, axis=-1, keepdims=True)
    inverse = lax.rsqrt(variance + epsilon)
    normed = centred * inverse
    return (normed * norm_gain + norm_shift, normed, inverse)


def norm_backward(grad_out, normed, inverse, norm_gain):
    scaled = grad_out * norm_gain
    adjusted = (
        scaled
        - jnp.mean(scaled, axis=-1, keepdims=True)
        - normed * jnp.mean(scaled * normed, axis=-1, keepdims=True)
    )
    return (adjusted * inverse, jnp.sum(grad_out * normed, axis=0), jnp.sum(grad_out, axis=0))


def rotary_tables(positions):
    half_rot = ROT // 2
    frequency = 10000.0 ** (-jnp.arange(half_rot, dtype=jnp.float32) * 2.0 / ROT)
    angles = positions.astype(jnp.float32)[:, None] * frequency[None, :]
    return (jnp.cos(angles)[:, None, :], jnp.sin(angles)[:, None, :])


def rotate_forward(values, cosine_table, sine_table):
    half_rot = ROT // 2
    leading = values[..., :half_rot]
    trailing = values[..., half_rot:ROT]
    return jnp.concatenate(
        [
            leading * cosine_table - trailing * sine_table,
            trailing * cosine_table + leading * sine_table,
            values[..., ROT:],
        ],
        axis=-1,
    )


def rotate_backward(grads, cosine_table, sine_table):
    half_rot = ROT // 2
    leading = grads[..., :half_rot]
    trailing = grads[..., half_rot:ROT]
    return jnp.concatenate(
        [
            leading * cosine_table + trailing * sine_table,
            trailing * cosine_table - leading * sine_table,
            grads[..., ROT:],
        ],
        axis=-1,
    )


def masked_scores(query_rows, key_rows, query_pos, key_pos, key_live):
    raw_scores = jnp.einsum(
        "qhd,khd->hqk", query_rows, key_rows, preferred_element_type=jnp.float32
    )
    allowed = (key_pos[None, :] <= query_pos[:, None]) & key_live[None, :]
    return (jnp.where(allowed[None], raw_scores * (1.0 / math.sqrt(HD)), -1e30), allowed)


def score_grads(
    query_rows, key_rows, value_rows, grad_rows, query_pos, key_pos, key_live, log_total, row_dots
):
    scores = masked_scores(query_rows, key_rows, query_pos, key_pos, key_live)[0]
    probability = jnp.exp(scores - log_total[..., None])
    grad_prob = jnp.einsum(
        "qhd,khd->hqk", grad_rows, value_rows, preferred_element_type=jnp.float32
    )
    grad_score = (probability * (grad_prob - row_dots[..., None]) * (1.0 / math.sqrt(HD))).astype(
        jnp.bfloat16
    )
    return (probability.astype(jnp.bfloat16), grad_score)


def shards(
    tokens,
    ln1_gain,
    ln1_bias,
    ln2_gain,
    ln2_bias,
    w_qkv,
    b_qkv,
    w_out,
    b_out,
    w_up,
    b_up,
    w_down,
    b_down,
    lengths,
    block_map,
    cotangent,
):
    gathered = (
        lax.all_gather(ln1_gain, "wsh", axis=0, tiled=True),
        lax.all_gather(ln1_bias, "wsh", axis=0, tiled=True),
        lax.all_gather(ln2_gain, "wsh", axis=0, tiled=True),
        lax.all_gather(ln2_bias, "wsh", axis=0, tiled=True),
        lax.all_gather(w_qkv, "wsh", axis=0, tiled=True),
        lax.all_gather(b_qkv, "wsh", axis=0, tiled=True),
        lax.all_gather(w_out, "wsh", axis=0, tiled=True),
        lax.all_gather(b_out, "wsh", axis=0, tiled=True),
        lax.all_gather(w_up, "wsh", axis=0, tiled=True),
        lax.all_gather(b_up, "wsh", axis=0, tiled=True),
        lax.all_gather(w_down, "wsh", axis=0, tiled=True),
        lax.all_gather(b_down, "wsh", axis=0, tiled=True),
    )
    (
        norm1_gain,
        norm1_shift,
        norm2_gain,
        norm2_shift,
        qkv_weight,
        qkv_bias,
        out_weight,
        out_bias,
        up_weight,
        up_bias,
        down_weight,
        down_bias,
    ) = gathered
    tok_rows = tokens.shape[1]
    model_width = tokens.shape[2]
    half_rows = tok_rows // 2
    seq_rows = tok_rows * lax.axis_size("ctx")
    head_count = H
    head_size = HD
    ctx_index = lax.axis_index("ctx")
    own_blocks = lax.dynamic_slice_in_dim(block_map, 2 * ctx_index, 2)
    local_offsets = jnp.arange(half_rows, dtype=jnp.int32)
    positions = (own_blocks[:, None] * half_rows + local_offsets[None, :]).reshape(tok_rows)
    key_pos = (block_map[:, None] * half_rows + local_offsets[None, :]).reshape(seq_rows)
    length = lengths[0]
    own_live = positions < length
    live_rows = own_live.astype(jnp.float32)
    key_live = key_pos < length
    gain_first = norm1_gain.astype(jnp.float32)
    gain_second = norm2_gain.astype(jnp.float32)
    token_rows = tokens[0].astype(jnp.float32)
    normal_first, normed_first, inverse_first = norm_forward(
        token_rows, gain_first, norm1_shift.astype(jnp.float32)
    )
    normal_second, normed_second, inverse_second = norm_forward(
        token_rows, gain_second, norm2_shift.astype(jnp.float32)
    )
    attn_in = normal_first.astype(jnp.bfloat16)
    mlp_in = normal_second.astype(jnp.bfloat16)
    projected = (
        jnp.dot(attn_in, qkv_weight, preferred_element_type=jnp.float32)
        + qkv_bias.astype(jnp.float32)
    ).reshape(tok_rows, 3, head_count, head_size)
    cosine_table, sine_table = rotary_tables(positions)
    queries = rotate_forward(projected[:, 0], cosine_table, sine_table).astype(jnp.bfloat16)
    key_own = (
        rotate_forward(projected[:, 1], cosine_table, sine_table)
        .astype(jnp.bfloat16)
        .reshape(tok_rows, model_width)
    )
    value_own = projected[:, 2].astype(jnp.bfloat16).reshape(tok_rows, model_width)
    keys_all, values_all = (
        lax.all_gather(key_own, "ctx", axis=0, tiled=True),
        lax.all_gather(value_own, "ctx", axis=0, tiled=True),
    )
    block_len = math.gcd(seq_rows, 1024)
    block_count = seq_rows // block_len
    key_stack = keys_all.reshape(block_count, block_len, head_count, head_size)
    value_stack = values_all.reshape(block_count, block_len, head_count, head_size)
    pos_stack = key_pos.reshape(block_count, block_len)
    live_stack = key_live.reshape(block_count, block_len)

    def stats_step(running, key_part):
        key_block, pos_block, live_block = key_part
        scores, allowed = masked_scores(queries, key_block, positions, pos_block, live_block)
        peak_score = jnp.maximum(running[0], jnp.max(scores, axis=-1))
        exp_total = running[1] * jnp.exp(running[0] - peak_score) + jnp.sum(
            jnp.where(allowed[None], jnp.exp(scores - peak_score[..., None]), 0.0), axis=-1
        )
        return ((peak_score, exp_total), None)

    start_peak = jnp.full((head_count, tok_rows), -1e30, jnp.float32)
    final_state = lax.scan(
        stats_step, (start_peak, jnp.zeros_like(start_peak)), (key_stack, pos_stack, live_stack)
    )[0]
    log_total = final_state[0] + jnp.log(final_state[1])

    def value_step(running, key_part):
        key_block, value_block, pos_block, live_block = key_part
        scores = masked_scores(queries, key_block, positions, pos_block, live_block)[0]
        probability = jnp.exp(scores - log_total[..., None]).astype(jnp.bfloat16)
        return (
            running
            + jnp.einsum(
                "hqk,khd->qhd", probability, value_block, preferred_element_type=jnp.float32
            ),
            None,
        )

    zero_heads = jnp.zeros((tok_rows, head_count, head_size), jnp.float32)
    attended = lax.scan(value_step, zero_heads, (key_stack, value_stack, pos_stack, live_stack))[0]
    context_low = attended.reshape(tok_rows, model_width).astype(jnp.bfloat16)
    hidden = jnp.dot(mlp_in, up_weight, preferred_element_type=jnp.float32) + up_bias.astype(
        jnp.float32
    )
    activated, gelu_pull = jax.vjp(partial(jax.nn.gelu, approximate=False), hidden)
    act_low = activated.astype(jnp.bfloat16)
    branch = (
        jnp.dot(context_low, out_weight, preferred_element_type=jnp.float32)
        + out_bias.astype(jnp.float32)
        + jnp.dot(act_low, down_weight, preferred_element_type=jnp.float32)
        + down_bias.astype(jnp.float32)
    )
    output_rows = (live_rows[:, None] * (token_rows + branch)).astype(jnp.bfloat16)
    cot_rows = cotangent[0].astype(jnp.float32)
    grad_branch = (live_rows[:, None] * cot_rows).astype(jnp.bfloat16)
    grad_w_out = jnp.einsum(
        "tc,td->cd", context_low, grad_branch, preferred_element_type=jnp.float32
    )
    grad_w_down = jnp.einsum("tc,td->cd", act_low, grad_branch, preferred_element_type=jnp.float32)
    grad_branch_sum = jnp.sum(grad_branch.astype(jnp.float32), axis=0)
    grad_act = jnp.einsum("td,cd->tc", grad_branch, down_weight, preferred_element_type=jnp.float32)
    grad_hidden = gelu_pull(grad_act)[0].astype(jnp.bfloat16)
    grad_w_up = jnp.einsum("tc,td->cd", mlp_in, grad_hidden, preferred_element_type=jnp.float32)
    grad_b_up = jnp.sum(grad_hidden.astype(jnp.float32), axis=0)
    grad_mlp_in = jnp.einsum(
        "td,cd->tc", grad_hidden, up_weight, preferred_element_type=jnp.float32
    )
    grad_context = jnp.einsum(
        "td,cd->tc", grad_branch, out_weight, preferred_element_type=jnp.float32
    ).astype(jnp.bfloat16)
    grad_heads = grad_context.reshape(tok_rows, head_count, head_size)
    row_dots = jnp.sum(grad_heads.astype(jnp.float32) * attended, axis=-1).T

    def grad_step(running, key_part):
        key_block, value_block, pos_block, live_block = key_part
        prob_low, grad_score = score_grads(
            queries,
            key_block,
            value_block,
            grad_heads,
            positions,
            pos_block,
            live_block,
            log_total,
            row_dots,
        )
        query_sum = running + jnp.einsum(
            "hqk,khd->qhd", grad_score, key_block, preferred_element_type=jnp.float32
        )
        key_term = jnp.einsum(
            "hqk,qhd->khd", grad_score, queries, preferred_element_type=jnp.float32
        )
        value_term = jnp.einsum(
            "hqk,qhd->khd", prob_low, grad_heads, preferred_element_type=jnp.float32
        )
        return (query_sum, (key_term, value_term))

    query_grad, term_stacks = lax.scan(
        grad_step, zero_heads, (key_stack, value_stack, pos_stack, live_stack)
    )
    key_grad, value_grad = (
        lax.psum_scatter(
            term_stacks[0].reshape(seq_rows, model_width).astype(jnp.bfloat16),
            "ctx",
            scatter_dimension=0,
            tiled=True,
        ).astype(jnp.float32),
        lax.psum_scatter(
            term_stacks[1].reshape(seq_rows, model_width).astype(jnp.bfloat16),
            "ctx",
            scatter_dimension=0,
            tiled=True,
        ).astype(jnp.float32),
    )
    key_grad = key_grad.reshape(tok_rows, head_count, head_size)
    value_grad = value_grad.reshape(tok_rows, head_count, head_size)
    grad_projected = (
        jnp.stack(
            [
                rotate_backward(query_grad, cosine_table, sine_table),
                rotate_backward(key_grad, cosine_table, sine_table),
                value_grad,
            ],
            axis=1,
        )
        .reshape(tok_rows, 3 * model_width)
        .astype(jnp.bfloat16)
    )
    grad_w_qkv = jnp.einsum(
        "tc,td->cd", attn_in, grad_projected, preferred_element_type=jnp.float32
    )
    grad_b_qkv = jnp.sum(grad_projected.astype(jnp.float32), axis=0)
    grad_attn_in = jnp.einsum(
        "td,cd->tc", grad_projected, qkv_weight, preferred_element_type=jnp.float32
    )
    grad_input_first, grad_gain_first, grad_shift_first = norm_backward(
        grad_attn_in, normed_first, inverse_first, gain_first
    )
    grad_input_second, grad_gain_second, grad_shift_second = norm_backward(
        grad_mlp_in, normed_second, inverse_second, gain_second
    )
    grad_input = live_rows[:, None] * cot_rows + grad_input_first + grad_input_second
    shares = (
        lax.psum_scatter(
            grad_gain_first.astype(jnp.bfloat16), "wsh", scatter_dimension=0, tiled=True
        ).astype(jnp.float32),
        lax.psum_scatter(
            grad_shift_first.astype(jnp.bfloat16), "wsh", scatter_dimension=0, tiled=True
        ).astype(jnp.float32),
        lax.psum_scatter(
            grad_gain_second.astype(jnp.bfloat16), "wsh", scatter_dimension=0, tiled=True
        ).astype(jnp.float32),
        lax.psum_scatter(
            grad_shift_second.astype(jnp.bfloat16), "wsh", scatter_dimension=0, tiled=True
        ).astype(jnp.float32),
        lax.psum_scatter(
            grad_w_qkv.astype(jnp.bfloat16), "wsh", scatter_dimension=0, tiled=True
        ).astype(jnp.float32),
        lax.psum_scatter(
            grad_b_qkv.astype(jnp.bfloat16), "wsh", scatter_dimension=0, tiled=True
        ).astype(jnp.float32),
        lax.psum_scatter(
            grad_w_out.astype(jnp.bfloat16), "wsh", scatter_dimension=0, tiled=True
        ).astype(jnp.float32),
        lax.psum_scatter(
            grad_branch_sum.astype(jnp.bfloat16), "wsh", scatter_dimension=0, tiled=True
        ).astype(jnp.float32),
        lax.psum_scatter(
            grad_w_up.astype(jnp.bfloat16), "wsh", scatter_dimension=0, tiled=True
        ).astype(jnp.float32),
        lax.psum_scatter(
            grad_b_up.astype(jnp.bfloat16), "wsh", scatter_dimension=0, tiled=True
        ).astype(jnp.float32),
        lax.psum_scatter(
            grad_w_down.astype(jnp.bfloat16), "wsh", scatter_dimension=0, tiled=True
        ).astype(jnp.float32),
        lax.psum_scatter(
            grad_branch_sum.astype(jnp.bfloat16), "wsh", scatter_dimension=0, tiled=True
        ).astype(jnp.float32),
    )
    totals = (
        lax.psum(shares[0].astype(jnp.bfloat16), "ctx").astype(jnp.float32),
        lax.psum(shares[1].astype(jnp.bfloat16), "ctx").astype(jnp.float32),
        lax.psum(shares[2].astype(jnp.bfloat16), "ctx").astype(jnp.float32),
        lax.psum(shares[3].astype(jnp.bfloat16), "ctx").astype(jnp.float32),
        lax.psum(shares[4].astype(jnp.bfloat16), "ctx").astype(jnp.float32),
        lax.psum(shares[5].astype(jnp.bfloat16), "ctx").astype(jnp.float32),
        lax.psum(shares[6].astype(jnp.bfloat16), "ctx").astype(jnp.float32),
        lax.psum(shares[7].astype(jnp.bfloat16), "ctx").astype(jnp.float32),
        lax.psum(shares[8].astype(jnp.bfloat16), "ctx").astype(jnp.float32),
        lax.psum(shares[9].astype(jnp.bfloat16), "ctx").astype(jnp.float32),
        lax.psum(shares[10].astype(jnp.bfloat16), "ctx").astype(jnp.float32),
        lax.psum(shares[11].astype(jnp.bfloat16), "ctx").astype(jnp.float32),
    )
    return (
        output_rows[None],
        grad_input[None],
        totals[0],
        totals[1],
        totals[2],
        totals[3],
        totals[4],
        totals[5],
        totals[6],
        totals[7],
        totals[8],
        totals[9],
        totals[10],
        totals[11],
    )


HB = 128
NEG=-1e30
f32=jnp.float32; bf16=jnp.bfloat16

def _nn(a,b): return lax.dot_general(a,b,(((1,),(0,)),((),())),preferred_element_type=f32)
def _nt(a,b): return lax.dot_general(a,b,(((1,),(1,)),((),())),preferred_element_type=f32)

def attn_fwd_kernel(bm, x_ref, o_ref, lse_ref, q_s, kt_s, v_s, *, nblk, bq, bk):
    def perm(i,_):
        p=bm[i]; c=i//2; l=pl.multiple_of((i%2)*HB,HB); d=pl.multiple_of(p*HB,HB)
        q_s[:,pl.ds(d,HB)]=x_ref[c,0:64,pl.ds(l,HB)]*bf16(0.125)
        kt_s[pl.ds(d,HB),:]=x_ref[c,64:128,pl.ds(l,HB)].astype(f32).T.astype(bf16)
        v_s[:,pl.ds(d,HB)]=x_ref[c,128:192,pl.ds(l,HB)]
        return 0
    lax.fori_loop(0,nblk,perm,0)
    S=nblk*HB; nq=S//bq; r=bq//bk
    def step(q,qo,ko,carry,mask):
        m,l,acc=carry
        s=_nn(kt_s[pl.ds(ko,bk),:],q)
        if mask is not None: s=jnp.where(mask,s,NEG)
        mn=jnp.maximum(m,jnp.max(s,axis=0,keepdims=True))
        a=jnp.exp(m-mn); p=jnp.exp(s-mn)
        l=l*a+jnp.sum(p,axis=0,keepdims=True)
        acc=acc*a+_nn(v_s[:,pl.ds(ko,bk)],p.astype(bf16))
        return mn,l,acc
    ki=lax.broadcasted_iota(jnp.int32,(bk,bq),0); qi_=lax.broadcasted_iota(jnp.int32,(bk,bq),1)
    def qloop(i,_):
        qo=pl.multiple_of(i*bq,bq)
        q=q_s[:,pl.ds(qo,bq)]
        c=(jnp.full((1,bq),NEG,f32),jnp.zeros((1,bq),f32),jnp.zeros((64,bq),f32))
        c=lax.fori_loop(0,i*r,lambda j,c: step(q,qo,pl.multiple_of(j*bk,bk),c,None),c)
        for t in range(r):
            c=step(q,qo,pl.multiple_of(qo+t*bk,bk),c,ki+t*bk<=qi_)
        m,l,acc=c
        q_s[:,pl.ds(qo,bq)]=(acc*(1.0/l)).astype(bf16)
        lse_ref[:,pl.ds(qo,bq)]=m+jnp.log(l)
        return 0
    lax.fori_loop(0,nq,qloop,0)
    def unperm(i,_):
        p=bm[i]; c=i//2; l=pl.multiple_of((i%2)*HB,HB); d=pl.multiple_of(p*HB,HB)
        o_ref[c,:,pl.ds(l,HB)]=q_s[:,pl.ds(d,HB)]
        return 0
    lax.fori_loop(0,nblk,unperm,0)

def attn_fwd(bm,x,*,bq=512,bk=512):
    n=x.shape[0]; S=n*256; nblk=2*n
    bq=math.gcd(S,bq); bk=math.gcd(bq,bk)
    return pl.pallas_call(
        lambda *a: attn_fwd_kernel(*a,nblk=nblk,bq=bq,bk=bk),
        out_shape=(jax.ShapeDtypeStruct((n,64,256),bf16),jax.ShapeDtypeStruct((1,S),f32)),
        in_specs=[pl.BlockSpec(memory_space=pltpu.SMEM),pl.BlockSpec(memory_space=pltpu.VMEM)],
        out_specs=(pl.BlockSpec(memory_space=pltpu.VMEM),pl.BlockSpec(memory_space=pltpu.VMEM)),
        scratch_shapes=[pltpu.VMEM((64,S),bf16),pltpu.VMEM((S,64),bf16),pltpu.VMEM((64,S),bf16)],
        compiler_params=pltpu.CompilerParams(vmem_limit_bytes=56<<20),name="attn_fwd")(bm,x)

def attn_bwd_kernel(bm, x_ref, o_ref, do_ref, lse_ref, cs_ref, g_ref, q_s, kt_s, k_s, vt_s, do_s, dl_s, dq_s, dk_s, dv_s, *, nblk, bq, bk):
    def perm(i,_):
        p=bm[i]; c=i//2; l=pl.multiple_of((i%2)*HB,HB); d=pl.multiple_of(p*HB,HB)
        q_s[:,pl.ds(d,HB)]=x_ref[c,0:64,pl.ds(l,HB)]*bf16(0.125)
        k=x_ref[c,64:128,pl.ds(l,HB)]
        k_s[:,pl.ds(d,HB)]=k*bf16(0.125)
        kt_s[pl.ds(d,HB),:]=k.astype(f32).T.astype(bf16)
        vt_s[pl.ds(d,HB),:]=x_ref[c,128:192,pl.ds(l,HB)].astype(f32).T.astype(bf16)
        do=do_ref[c,:,pl.ds(l,HB)]
        do_s[:,pl.ds(d,HB)]=do
        dl_s[:,pl.ds(d,HB)]=jnp.sum(do.astype(f32)*o_ref[c,:,pl.ds(l,HB)].astype(f32),axis=0,keepdims=True)
        return 0
    lax.fori_loop(0,nblk,perm,0)
    S=nblk*HB; nq=S//bq; r=bq//bk
    dk_s[...]=jnp.zeros_like(dk_s); dv_s[...]=jnp.zeros_like(dv_s)
    def step(q,do,lse,dl,ko,dq,mask):
        s=_nn(kt_s[pl.ds(ko,bk),:],q)
        p=jnp.exp(s-lse)
        if mask is not None: p=jnp.where(mask,p,0.0)
        dp=_nn(vt_s[pl.ds(ko,bk),:],do)
        ds=(p*(dp-dl)).astype(bf16)
        pb=p.astype(bf16)
        dv_s[:,pl.ds(ko,bk)]+=_nt(do,pb)
        dk_s[:,pl.ds(ko,bk)]+=_nt(q,ds)
        return dq+_nn(k_s[:,pl.ds(ko,bk)],ds)
    ki=lax.broadcasted_iota(jnp.int32,(bk,bq),0); qi_=lax.broadcasted_iota(jnp.int32,(bk,bq),1)
    def qloop(i,_):
        qo=pl.multiple_of(i*bq,bq)
        q=q_s[:,pl.ds(qo,bq)]; do=do_s[:,pl.ds(qo,bq)]; lse=lse_ref[:,pl.ds(qo,bq)]; dl=dl_s[:,pl.ds(qo,bq)]
        dq=jnp.zeros((64,bq),f32)
        dq=lax.fori_loop(0,i*r,lambda j,c: step(q,do,lse,dl,pl.multiple_of(j*bk,bk),c,None),dq)
        for t in range(r):
            dq=step(q,do,lse,dl,pl.multiple_of(qo+t*bk,bk),dq,ki+t*bk<=qi_)
        dq_s[:,pl.ds(qo,bq)]=dq
        return 0
    lax.fori_loop(0,nq,qloop,0)
    def unperm(i,_):
        p=bm[i]; c=i//2; l=pl.multiple_of((i%2)*HB,HB); d=pl.multiple_of(p*HB,HB)
        cos=cs_ref[0:8,pl.ds(d,HB)]; sin=cs_ref[8:16,pl.ds(d,HB)]
        for n_,src in ((0,dq_s),(1,dk_s)):
            g=src[:,pl.ds(d,HB)]
            a=g[0:8]; b=g[8:16]
            full=jnp.concatenate([a*cos+b*sin,b*cos-a*sin,g[16:64]],axis=0)
            g_ref[c,64*n_:64*n_+64,pl.ds(l,HB)]=full.astype(bf16)
        g_ref[c,128:192,pl.ds(l,HB)]=dv_s[:,pl.ds(d,HB)].astype(bf16)
        return 0
    lax.fori_loop(0,nblk,unperm,0)

def attn_bwd(bm,x,o,do,lse,cs,*,bq=512,bk=512):
    n=x.shape[0]; S=n*256; nblk=2*n
    bq=math.gcd(S,bq); bk=math.gcd(bq,bk)
    vm=pl.BlockSpec(memory_space=pltpu.VMEM)
    return pl.pallas_call(
        lambda *a: attn_bwd_kernel(*a,nblk=nblk,bq=bq,bk=bk),
        out_shape=jax.ShapeDtypeStruct((n,192,256),bf16),
        in_specs=[pl.BlockSpec(memory_space=pltpu.SMEM)]+[vm]*5,
        out_specs=vm,
        scratch_shapes=[pltpu.VMEM((64,S),bf16),pltpu.VMEM((S,64),bf16),pltpu.VMEM((64,S),bf16),pltpu.VMEM((S,64),bf16),pltpu.VMEM((64,S),bf16),
                        pltpu.VMEM((1,S),f32),pltpu.VMEM((64,S),f32),pltpu.VMEM((64,S),f32),pltpu.VMEM((64,S),f32)],
        compiler_params=pltpu.CompilerParams(vmem_limit_bytes=56<<20),name="attn_bwd")(bm,x,o,do,lse,cs)


SWAP = [(0, 1), (1, 0)]


def fast_fits(mesh):
    return mesh.shape["wsh"] == 2 and mesh.shape["ctx"] == H


def _params(mb=56):
    return pltpu.CompilerParams(vmem_limit_bytes=mb << 20)


def _norm(x):
    xf = x.astype(f32)
    cen = xf - jnp.mean(xf, axis=-1, keepdims=True)
    inv = lax.rsqrt(jnp.mean(cen * cen, axis=-1, keepdims=True) + epsilon)
    return cen * inv, inv


def _pieces(ids):
    me, core = ids[0], ids[1]
    return me, core


def qkv_kernel(
    ids, xo_ref, xg_ref, n_ref, wq_ref, wk_ref, wv_ref, gq_ref, gk_ref, gv_ref, bq_ref, bk_ref, bv_ref, cs_ref,
    send_ref, ain_ref, min_ref
):
    rows, width = xo_ref.shape
    half = width // 2

    @pl.when(pl.program_id(0) == 0)
    def _():
        for s in range(2):
            x = xo_ref[...] if s == 0 else xg_ref[...]
            xhat, _ = _norm(x)
            ain_ref[s * rows : (s + 1) * rows, :] = (xhat * n_ref[0:1, :] + n_ref[1:2, :]).astype(bf16)
            min_ref[s * rows : (s + 1) * rows, :] = (xhat * n_ref[2:3, :] + n_ref[3:4, :]).astype(bf16)

    me = ids[0]
    a_own = ain_ref[:, pl.ds(pl.multiple_of(me * half, half), half)]
    a_got = ain_ref[:, pl.ds(pl.multiple_of((1 - me) * half, half), half)]
    cos = cs_ref[0:8, :]
    sin = cs_ref[8:16, :]
    for n, (w, g, b) in enumerate(((wq_ref, gq_ref, bq_ref), (wk_ref, gk_ref, bk_ref), (wv_ref, gv_ref, bv_ref))):
        t = _nn(a_own, w[...]) + _nn(a_got, g[...]) + b[...]
        t = t.T
        for s in range(2):
            for k in range(2):
                v = t[k * HD : (k + 1) * HD, s * rows : (s + 1) * rows]
                if n < 2:
                    lead = v[0:8]
                    trail = v[8:16]
                    v = jnp.concatenate([lead * cos - trail * sin, trail * cos + lead * sin, v[16:]], axis=0)
                send_ref[s, k, n * HD : (n + 1) * HD, :] = v.astype(bf16)


def _wq_specs(half, width, cols):
    own = lambda p: pl.BlockSpec((half, cols), lambda i, ids: (0, p * (width // cols) + ids[0] * (half // cols) + i))
    got = lambda p: pl.BlockSpec((half, cols), lambda i, ids: (0, p * (half // cols) + i))
    return [own(p) for p in range(3)] + [got(p) for p in range(3)]


def qkv_forward(ids, xo, xg, norms, w_own, w_got, bias, cs):
    rows, width = xo.shape
    half = width // 2
    full = lambda a: pl.BlockSpec(a.shape, lambda i, ids: (0,) * a.ndim)
    bsp = lambda p: pl.BlockSpec((1, 128), lambda i, ids: (0, p * (half // 128) + i))
    heads = half // HD
    res = lambda: pl.BlockSpec((2 * rows, width), lambda i, ids: (0, 0))
    return pl.pallas_call(
        qkv_kernel,
        grid_spec=pltpu.PrefetchScalarGridSpec(
            num_scalar_prefetch=1,
            grid=(half // 128,),
            in_specs=[full(xo), full(xg), full(norms)]
            + _wq_specs(half, width, 128)
            + [bsp(p) for p in range(3)]
            + [full(cs)],
            out_specs=(pl.BlockSpec((2, 2, 3 * HD, rows), lambda i, ids: (0, i, 0, 0)), res(), res()),
        ),
        out_shape=(
            jax.ShapeDtypeStruct((2, heads, 3 * HD, rows), bf16),
            jax.ShapeDtypeStruct((2 * rows, width), bf16),
            jax.ShapeDtypeStruct((2 * rows, width), bf16),
        ),
        compiler_params=_params(),
        cost_estimate=pl.CostEstimate(flops=1 << 20, transcendentals=0, bytes_accessed=1 << 20),
        name="qkv_forward",
    )(ids, xo, xg, norms, w_own, w_own, w_own, w_got, w_got, w_got, bias, bias, bias, cs)


def mlp_kernel(
    ids, x_ref, xt_ref, dy_ref, wo_ref, wg_ref, wd_ref, bu_ref, y0_ref, dx0_ref, y_ref, dx_ref, gu_ref,
    gd_ref, gb_ref, *, resume
):
    rows, width = x_ref.shape
    half = width // 2
    me = ids[0]
    spans = (
        (pl.multiple_of(me * half, half), half, wo_ref),
        (pl.multiple_of((1 - me) * half, half), half, wg_ref),
    )

    @pl.when(pl.program_id(0) == 0)
    def _():
        y_ref[...] = y0_ref[...] if resume else jnp.zeros_like(y_ref)
        dx_ref[...] = dx0_ref[...] if resume else jnp.zeros_like(dx_ref)

    dy = dy_ref[...]
    wd = wd_ref[...]
    u = bu_ref[...] + sum(_nn(x_ref[:, pl.ds(o, n)], w[...]) for o, n, w in spans)
    cdf = 0.5 * (1.0 + lax.erf(u * (1.0 / math.sqrt(2.0))))
    pdf = jnp.exp(-0.5 * u * u) * (1.0 / math.sqrt(2.0 * math.pi))
    act = (u * cdf).astype(bf16)
    du = (_nt(dy, wd) * (cdf + u * pdf)).astype(bf16)
    y_ref[...] += _nn(act, wd)
    for o, n, w in spans:
        dx_ref[:, pl.ds(o, n)] += _nt(du, w[...])
    gd = lax.dot_general(act, dy, (((0,), (0,)), ((), ())), preferred_element_type=f32).astype(bf16)
    k, r, _ = gd_ref.shape
    for c in range(k):
        gd_ref[c] = gd[c * r : (c + 1) * r, :]
    gu = _nn(xt_ref[...], du).astype(bf16)
    n = gu_ref.shape[0]
    r = half // n
    for h in range(2):
        for c in range(n):
            gu_ref[c, h * r : (h + 1) * r, :] = gu[h * half + c * r : h * half + (c + 1) * r, :]
    gb_ref[...] = jnp.sum(du.astype(f32), axis=0, keepdims=True)


def mlp(ids, x, xt, dy, w_own, w_got, wd, bu, n, sibling, before=None, tile=256):
    rows, width = x.shape
    half = width // 2
    steps = w_got.shape[1] // (2 * tile)
    hidden = steps * tile
    part = lambda i, ids: (1 - ids[1] if sibling else ids[1]) * steps + i
    whole = pl.BlockSpec((rows, width), lambda i, ids: (0, 0))
    sums = [jax.ShapeDtypeStruct((rows, width), f32)] * 2
    if before is None:
        before = (jnp.zeros((8, 128), f32),) * 2
        start = pl.BlockSpec((8, 128), lambda i, ids: (0, 0))
    else:
        start = whole
    per = hidden // n
    return pl.pallas_call(
        partial(mlp_kernel, resume=start is whole),
        grid_spec=pltpu.PrefetchScalarGridSpec(
            num_scalar_prefetch=1,
            grid=(steps,),
            in_specs=[
                whole,
                pl.BlockSpec((width, rows), lambda i, ids: (0, 0)),
                whole,
                pl.BlockSpec((half, tile), lambda i, ids: (0, ids[0] * 2 * steps + part(i, ids))),
                pl.BlockSpec((half, tile), lambda i, ids: (0, part(i, ids))),
                pl.BlockSpec((tile, width), lambda i, ids: (part(i, ids), 0)),
                pl.BlockSpec((1, tile), lambda i, ids: (0, part(i, ids))),
                start,
                start,
            ],
            out_specs=(
                whole,
                whole,
                pl.BlockSpec((n, width // n, tile), lambda i, ids: (0, 0, i)),
                pl.BlockSpec((tile // per, per, width), lambda i, ids: (i, 0, 0)),
                pl.BlockSpec((1, tile), lambda i, ids: (0, i)),
            ),
        ),
        out_shape=(
            *sums,
            jax.ShapeDtypeStruct((n, width // n, hidden), bf16),
            jax.ShapeDtypeStruct((n, per, width), bf16),
            jax.ShapeDtypeStruct((1, hidden), f32),
        ),
        compiler_params=_params(),
        cost_estimate=pl.CostEstimate(
            flops=12 * rows * width * hidden, transcendentals=2 * rows * hidden, bytes_accessed=24 << 20
        ),
        name="mlp",
    )(ids, x, xt, dy, w_own, w_got, wd, bu, *before)


def qkv_back_kernel(
    ids, d_ref, at_ref, xo_ref, xg_ref, n_ref, wq_ref, wk_ref, wv_ref, gq_ref, gk_ref, gv_ref, dm_ref,
    ob_ref, dy_ref, gb_ref, ak_ref, as_ref, bk_ref, bs_ref, eo_ref, ex_ref, da_s, sum_s, g_s
):
    rows, width = xo_ref.shape
    half = width // 2
    q4 = half // 2
    me = ids[0]
    core = ids[1]
    i = pl.program_id(0)
    outs = ((ak_ref, bk_ref), (as_ref, bs_ref))
    n = ak_ref.shape[0]
    r = half // (4 * n)
    nh = d_ref.shape[1]
    cols = nh * HD
    lanes = pl.ds(pl.multiple_of(i * cols, cols), cols)
    ones = jnp.ones((8, rows), bf16)
    dts = [[], []]
    for p in range(3):
        g = jnp.zeros((width, cols), f32)
        b = jnp.zeros((8, cols), f32)
        for s in range(2):
            dp = jnp.concatenate([d_ref[s, k, p * HD : (p + 1) * HD, :] for k in range(nh)], axis=0)
            g = g + _nt(at_ref[:, s * rows : (s + 1) * rows], dp)
            b = b + _nt(ones, dp)
            dts[s].append(dp.astype(f32).T.astype(bf16))
        sum_s[p * 8 : (p + 1) * 8, lanes] = b
        g_s[...] = g.astype(bf16)
        for side in range(2):
            which = core if side == 0 else 1 - core
            for h in range(2):
                for c in range(n):
                    for a in range(2):
                        at = pl.multiple_of(h * half + which * q4 + (c * 2 + a) * r, r)
                        u = (h * 3 + p) * r
                        outs[side][a][c, u : u + r, lanes] = g_s[pl.ds(at, r), :]
    for o, m, refs in (
        (pl.multiple_of(me * half, half), half, (wq_ref, wk_ref, wv_ref)),
        (pl.multiple_of((1 - me) * half, half), half, (gq_ref, gk_ref, gv_ref)),
    ):
        w = jnp.concatenate([v[...] for v in refs], axis=1)
        for s in range(2):
            v = _nt(jnp.concatenate(dts[s], axis=1), w)
            at = slice(s * rows, (s + 1) * rows)

            @pl.when(i == 0)
            def _(v=v, at=at, o=o, m=m):
                da_s[at, pl.ds(o, m)] = v

            @pl.when(i > 0)
            def _(v=v, at=at, o=o, m=m):
                da_s[at, pl.ds(o, m)] += v

    @pl.when(i == pl.num_programs(0) - 1)
    def _():
        sums = [jnp.zeros((1, width), f32) for _ in range(4)]
        for s in range(2):
            x = xo_ref[...] if s == 0 else xg_ref[...]
            xhat, _ = _norm(x)
            da = da_s[s * rows : (s + 1) * rows, :]
            dm = dm_ref[s * rows : (s + 1) * rows, :]
            e = da * n_ref[0:1, :] + dm * n_ref[2:3, :]
            if s == 0:
                eo_ref[...] = e
            else:
                ex_ref[...] = e.astype(bf16)
            for k, v in enumerate((da * xhat, da, dm * xhat, dm)):
                sums[k] = sums[k] + jnp.sum(v, axis=0, keepdims=True)
        sums.append(jnp.sum(dy_ref[0:rows, :].astype(f32), axis=0, keepdims=True))
        flat = [v[:, h * half : (h + 1) * half] for v in sums for h in range(2)]
        zero = jnp.zeros((1, half), f32)
        for p in range(3):
            flat += [jnp.where(me == k, sum_s[p * 8 : p * 8 + 1, :], zero) for k in range(2)]
        hid = gb_ref.shape[1] // half
        flat += [
            jnp.where(me == k, gb_ref[:, t * half : (t + 1) * half], zero) for k in range(2) for t in range(hid)
        ]
        flat += [zero] * (4 * n - len(flat))
        pad = jnp.zeros((6, half), f32)
        top = 8 * r
        first = core == 0
        for c in range(n):
            low = jnp.concatenate([flat[2 * c], flat[2 * c + 1], pad], axis=0).astype(bf16)
            d = c + n
            high = jnp.concatenate([flat[2 * d], flat[2 * d + 1], pad], axis=0).astype(bf16)
            bk_ref[c, top : top + 8, :] = jnp.where(first, low, high)
            bs_ref[c, top : top + 8, :] = jnp.where(first, high, low)

    rows_o = ob_ref.shape[1]
    go = sum(_nn(ob_ref[s], dy_ref[s * rows : (s + 1) * rows, :]) for s in range(2)).astype(bf16)
    same = core == i
    for k in range(rows_o // (2 * r)):
        for a in range(2):
            at = (k * 2 + a) * r
            for h in range(2):
                u = (6 + h) * r
                v = go[at : at + r, h * half : (h + 1) * half]

                @pl.when(same)
                def _(v=v, a=a, k=k, u=u):
                    outs[0][a][k, u : u + r, :] = v

                @pl.when(jnp.logical_not(same))
                def _(v=v, a=a, k=k, u=u):
                    outs[1][a][k, u : u + r, :] = v


def qkv_backward(ids, d, at, xo, xg, norms, w_own, w_got, d_mlp, ob, dy, gb_up, n):
    rows, width = xo.shape
    half = width // 2
    r = half // (4 * n)
    full = lambda v: pl.BlockSpec(v.shape, lambda i, ids: (0,) * v.ndim)
    steps = 2
    cols = half // steps
    out = [
        jax.ShapeDtypeStruct((n, 8 * r, half), bf16),
        jax.ShapeDtypeStruct((n, 8 * r, half), bf16),
        jax.ShapeDtypeStruct((n, 8 * r + 8, half), bf16),
        jax.ShapeDtypeStruct((n, 8 * r + 8, half), bf16),
        jax.ShapeDtypeStruct((rows, width), f32),
        jax.ShapeDtypeStruct((rows, width), bf16),
    ]
    return pl.pallas_call(
        qkv_back_kernel,
        grid_spec=pltpu.PrefetchScalarGridSpec(
            num_scalar_prefetch=1,
            grid=(steps,),
            in_specs=[pl.BlockSpec((2, cols // HD, 3 * HD, rows), lambda i, ids: (0, i, 0, 0))]
            + [full(at), full(xo), full(xg), full(norms)]
            + _wq_specs(half, width, cols)
            + [full(d_mlp), pl.BlockSpec((2, cols, rows), lambda i, ids: (0, i, 0)), full(dy), full(gb_up)],
            out_specs=tuple(full(v) for v in out),
            scratch_shapes=[
                pltpu.VMEM((2 * rows, width), f32),
                pltpu.VMEM((24, half), f32),
                pltpu.VMEM((width, cols), bf16),
            ],
        ),
        out_shape=tuple(out),
        compiler_params=_params(),
        name="qkv_backward",
    )(ids, d, at, xo, xg, norms, w_own, w_own, w_own, w_got, w_got, w_got, d_mlp, ob, dy, gb_up)


def _mine(ids):
    return (pl.program_id(0) // 2) == ids[1]


def _own_block(i, ids):
    return jnp.clip(i - 2 * ids[1], 0, 1)


def _got_block(i, ids):
    return jnp.clip(i - 2 * (1 - ids[1]), 0, 1)


def join_kernel(ids, own_ref, got_ref, o_ref):
    mine = _mine(ids)
    shape = o_ref.shape

    @pl.when(mine)
    def _():
        o_ref[...] = own_ref[...].astype(f32).reshape(shape)

    @pl.when(jnp.logical_not(mine))
    def _():
        o_ref[...] = got_ref[...].astype(f32).reshape(shape)


def join_rows(ids, own, got):
    n, r, w = own.shape
    src = lambda f: pl.BlockSpec((n // 2, r, w), lambda i, ids: (f(i, ids), 0, 0))
    return pl.pallas_call(
        join_kernel,
        grid_spec=pltpu.PrefetchScalarGridSpec(
            num_scalar_prefetch=1,
            grid=(4,),
            in_specs=[src(_own_block), src(_got_block)],
            out_specs=pl.BlockSpec((n * r // 2, w), lambda i, ids: (i, 0)),
        ),
        out_shape=jax.ShapeDtypeStruct((2 * n * r, w), f32),
        compiler_params=_params(),
        name="join_rows",
    )(ids, own, got)


def join_cols(ids, own, got):
    n, _, r, w = own.shape
    src = lambda f: pl.BlockSpec((n, 1, r, w), lambda i, ids: (0, f(i, ids), 0, 0))
    return pl.pallas_call(
        join_kernel,
        grid_spec=pltpu.PrefetchScalarGridSpec(
            num_scalar_prefetch=1,
            grid=(4,),
            in_specs=[src(_own_block), src(_got_block)],
            out_specs=pl.BlockSpec((n * r, w), lambda i, ids: (0, (i % 2) * 2 + i // 2)),
        ),
        out_shape=jax.ShapeDtypeStruct((n * r, 4 * w), f32),
        compiler_params=_params(),
        name="join_cols",
    )(ids, own, got)


def unpack_kernel(ids, ao_ref, ag_ref, bo_ref, bg_ref, q_ref, o_ref, s_ref):
    mine = _mine(ids)
    k = ao_ref.shape[0]
    r = ao_ref.shape[1] // 8
    half = ao_ref.shape[2]
    for a, (own, got) in enumerate(((ao_ref, ag_ref), (bo_ref, bg_ref))):
        for c in range(k):
            v = jnp.where(mine, own[c].astype(f32), got[c].astype(f32))
            to = slice((c * 2 + a) * r, (c * 2 + a + 1) * r)
            for w in range(2):
                for p in range(3):
                    u = (w * 3 + p) * r
                    at = (p * 2 + w) * half
                    q_ref[to, at : at + half] = v[u : u + r, :]
                u = (6 + w) * r
                o_ref[to, w * half : (w + 1) * half] = v[u : u + r, :]
            if a == 1:
                s_ref[c] = v[8 * r : 8 * r + 8, :]


def unpack(ids, a_own, a_got, b_own, b_got):
    n, ra, half = a_own.shape
    r = ra // 8
    k = n // 2
    spec = lambda v, f: pl.BlockSpec((k,) + v.shape[1:], lambda i, ids: (f(i, ids), 0, 0))
    return pl.pallas_call(
        unpack_kernel,
        grid_spec=pltpu.PrefetchScalarGridSpec(
            num_scalar_prefetch=1,
            grid=(4,),
            in_specs=[spec(a_own, _own_block), spec(a_got, _got_block), spec(b_own, _own_block), spec(b_got, _got_block)],
            out_specs=(
                pl.BlockSpec((2 * k * r, 6 * half), lambda i, ids: (i, 0)),
                pl.BlockSpec((2 * k * r, 2 * half), lambda i, ids: (i, 0)),
                pl.BlockSpec((k, 8, half), lambda i, ids: (i, 0, 0)),
            ),
        ),
        out_shape=(
            jax.ShapeDtypeStruct((4 * n * r, 6 * half), f32),
            jax.ShapeDtypeStruct((4 * n * r, 2 * half), f32),
            jax.ShapeDtypeStruct((2 * n, 8, half), f32),
        ),
        compiler_params=_params(),
        name="unpack",
    )(ids, a_own, a_got, b_own, b_got)


def last_kernel(eo_ref, er_ref, x_ref, c_ref, live_ref, o_ref):
    xhat, inv = _norm(x_ref[...])
    e = eo_ref[...] + er_ref[...].astype(f32)
    dx = inv * (
        e - jnp.mean(e, axis=-1, keepdims=True) - xhat * jnp.mean(e * xhat, axis=-1, keepdims=True)
    )
    o_ref[...] = live_ref[...] * c_ref[...].astype(f32) + dx


def last(e_own, e_got, x, cot, live):
    return pl.pallas_call(
        last_kernel,
        out_shape=jax.ShapeDtypeStruct(x.shape, f32),
        compiler_params=_params(),
        name="token_grad",
    )(e_own, e_got, x, cot, live)


def fast_shards(
    tokens,
    ln1_gain,
    ln1_bias,
    ln2_gain,
    ln2_bias,
    w_qkv,
    b_qkv,
    w_out,
    b_out,
    w_up,
    b_up,
    w_down,
    b_down,
    lengths,
    block_map,
    cotangent,
):
    ctx = lax.axis_index("ctx")
    me = lax.axis_index("wsh")
    core = ctx % 2
    n_ctx = lax.axis_size("ctx")
    rows, width = tokens.shape[1:]
    half = width // 2
    seq = rows * n_ctx
    heads = H // 2
    hid = w_up.shape[1] // 2
    ids = jnp.stack([me, core]).astype(jnp.int32)
    CORE, X, ZN, ZF = 0, 1, 2, 3

    def swap(v):
        return lax.ppermute(v, "wsh", SWAP)

    def flip(v, bit):
        return lax.ppermute(v, "ctx", [(i, i ^ (1 << bit)) for i in range(n_ctx)])

    def bit_of(bit):
        return (ctx >> bit) & 1

    def add(a, b):
        return (a.astype(f32) + b.astype(f32)).astype(bf16)

    def halve(pair, bit):
        b = bit_of(bit)

        def part(k):
            terms = [v.reshape((2, v.shape[0] // 2) + v.shape[1:]) for v in pair]
            return add(*[lax.dynamic_index_in_dim(v, k, 0, keepdims=False) for v in terms])

        return part(b), flip(part(1 - b), bit)

    def ordered(first, a, b, axis=0):
        return jnp.where(first == 0, jnp.concatenate([a, b], axis), jnp.concatenate([b, a], axis))

    def double(v, bit):
        return ordered(bit_of(bit), v, flip(v, bit))

    len_parts = jnp.stack([lengths[0] // 64, lengths[0] % 64]).astype(bf16)
    small = jnp.concatenate(
        [ln1_gain, ln1_bias, ln2_gain, ln2_bias, b_out, b_down, b_qkv, len_parts, jnp.zeros((126,), bf16)]
    )[None]
    small = ordered(me, small, swap(small))
    x_own = tokens[0]
    x_got = swap(x_own)
    q4 = half // 4
    rows_of = lambda v, at, n: lax.dynamic_slice_in_dim(v, at, n, 0)
    wq_rows = rows_of(w_qkv, (2 * core + bit_of(X)) * q4, q4)
    cols = [lax.dynamic_slice_in_dim(wq_rows, p * width + (1 - me) * half, half, 1) for p in range(3)]
    wq_got = swap(jnp.concatenate(cols, axis=1))
    wu_send = lax.dynamic_slice_in_dim(rows_of(w_up, core * 2 * q4, 2 * q4), (1 - me) * hid, hid, 1)
    wq_got, wu_send = lax.optimization_barrier((wq_got, wu_send))
    wq_got = double(double(wq_got, X), CORE)
    wu_got = swap(wu_send)
    cot_own = cotangent[0]

    vec = lambda i: small[:, i * half : (i + 1) * half].reshape(width).astype(f32)
    norms = jnp.stack([vec(i) for i in range(4)])
    bias_out = vec(4) + vec(5)
    qkv_bias = small[:, 6 * half : 9 * half].astype(f32).reshape(3, width)
    qkv_bias = lax.dynamic_slice_in_dim(qkv_bias, me * half, half, 1).reshape(1, 3 * half)
    lens = small[:, 9 * half : 9 * half + 2].astype(jnp.int32)
    lens = lens[:, 0] * 64 + lens[:, 1]
    other_len = lens[1 - me]

    own_blocks = lax.dynamic_slice_in_dim(block_map, 2 * ctx, 2)
    offs = jnp.arange(HB, dtype=jnp.int32)
    positions = (own_blocks[:, None] * HB + offs[None, :]).reshape(rows)
    live_own = (positions < lengths[0]).astype(f32)[:, None]
    live_got = (positions < other_len).astype(f32)[:, None]
    freq = 10000.0 ** (-jnp.arange(ROT // 2, dtype=f32) * 2.0 / ROT)
    ang = freq[:, None] * jnp.arange(seq, dtype=jnp.int32).astype(f32)[None, :]
    table = jnp.concatenate([jnp.cos(ang), jnp.sin(ang)])
    own_ang = freq[:, None] * positions.astype(f32)[None, :]
    own_table = jnp.concatenate([jnp.cos(own_ang), jnp.sin(own_ang)])

    def exchange(v):
        return lax.all_to_all(v, "ctx", 0, 0, tiled=False)

    send, attn_in, mlp_in = qkv_forward(ids, x_own, x_got, norms, w_qkv, wq_got, qkv_bias, own_table)
    qkv_head = exchange(send.reshape(2 * heads, 3 * HD, rows))
    mlp_in, wu_got, cot_send = lax.optimization_barrier((mlp_in, wu_got, cot_own))
    cot_got = swap(cot_send)
    wu_got = double(wu_got, CORE)
    dy = jnp.concatenate(
        [(live_own * cot_own.astype(f32)).astype(bf16), (live_got * cot_got.astype(f32)).astype(bf16)]
    )
    dctx = jnp.einsum("ed,std->set", w_out, dy.reshape(2, rows, width), preferred_element_type=f32).astype(bf16)
    do_head = exchange(dctx.reshape(2 * heads, HD, rows))

    mlp_t = mlp_in.T
    attn_t = attn_in.T
    run = partial(mlp, ids, mlp_in, mlp_t, dy, w_up, wu_got, w_down, b_up.astype(f32)[None, :], n_ctx // 2)
    y_mlp, d_mlp, u_send, v_send, gb_send = run(True)
    u_got = flip(u_send, CORE)
    v_got = flip(v_send, CORE)
    y_mlp, d_mlp, u_keep, v_keep, gb_keep = run(False, (y_mlp, d_mlp))
    gb_up = ordered(core, gb_keep, gb_send, axis=1)

    chain_a = (X, ZN, ZF)
    chain_b = (ZN, ZF, X)
    qkv_head, u_keep, v_keep, u_got, v_got = lax.optimization_barrier((qkv_head, u_keep, v_keep, u_got, v_got))
    down = halve((v_keep, v_got), chain_a[0])
    up = halve((u_keep, u_got), chain_b[0])

    o_head, lse = attn_fwd(block_map, qkv_head, bq=1024, bk=1024)
    qkv_head, o_head, do_head, down, up = lax.optimization_barrier((qkv_head, o_head, do_head, down, up))
    ob = exchange(o_head).reshape(2, half, rows)
    down = halve(down, chain_a[1])
    up = halve(up, chain_b[1])
    g_head = attn_bwd(block_map, qkv_head, o_head, do_head, lse, table)
    g_head, ob, down, up = lax.optimization_barrier((g_head, ob, down, up))
    d_qkv = exchange(g_head).reshape(2, heads, 3 * HD, rows)

    down = add(*halve(down, chain_a[2]))
    up = add(*halve(up, chain_b[2]))
    up = up.reshape(1, 2, up.shape[1] // 2, up.shape[2])
    up_keep = lax.dynamic_slice_in_dim(up, me, 1, 1)
    up_got = swap(lax.dynamic_slice_in_dim(up, 1 - me, 1, 1))
    up = ordered(me, up_keep, up_got, axis=1)
    down = double(down, chain_a[2])
    up = double(up, chain_b[2])
    d_qkv, down, up = lax.optimization_barrier((d_qkv, down, up))
    for a, b in zip(chain_a[1::-1], chain_b[1::-1]):
        down = double(down, a)
        up = double(up, b)
    tot_down = join_rows(ids, down, flip(down, CORE))
    tot_up = join_cols(ids, up, flip(up, CORE))

    part = jnp.einsum("sct,cd->std", ob, w_out, preferred_element_type=f32) + y_mlp.reshape(
        2, rows, width
    )
    y_got = swap(part[1].astype(bf16)).astype(f32)
    output = (live_own * (x_own.astype(f32) + part[0] + y_got + bias_out)).astype(bf16)

    a_keep, a_send, b_keep, b_send, e_own, e_send = qkv_backward(
        ids, d_qkv, attn_t, x_own, x_got, norms, w_qkv, wq_got, d_mlp, ob, dy, gb_up, n_ctx // 2
    )
    v_a = (a_keep, flip(a_send, CORE))
    v_b = (b_keep, flip(b_send, CORE))
    for a, b in zip(chain_a, chain_b):
        v_a = halve(v_a, a)
        v_b = halve(v_b, b)
    e_got = swap(e_send)
    n3 = 3 * half // (2 * n_ctx)
    mixed = []
    for v, chain in ((add(*v_a)[0], chain_a), (add(*v_b)[0], chain_b)):
        extra = v[8 * n3 // 3 :]
        keep = lax.dynamic_slice_in_dim(v, me * n3, n3, 0)
        give = lax.dynamic_slice_in_dim(v, (1 - me) * n3, n3, 0)
        back = swap(jnp.concatenate([give, extra]))
        extra = add(extra, back[n3:])
        v = jnp.concatenate([ordered(me, keep, back[:n3]), v[2 * n3 : 8 * n3 // 3], extra])[None]
        for a in chain[::-1]:
            v = double(v, a)
        mixed.append(v)
    grad_tokens = last(e_own, e_got, x_own, cot_own, live_own)
    mixed[0], mixed[1], grad_tokens, output, tot_down, tot_up = lax.optimization_barrier(
        (mixed[0], mixed[1], grad_tokens, output, tot_down, tot_up)
    )
    tot_qkv, tot_out, flat = unpack(ids, mixed[0], flip(mixed[0], CORE), mixed[1], flip(mixed[1], CORE))
    flat = flat[:, :2].reshape(2 * n_ctx * half)

    def own(start, size):
        return lax.dynamic_slice_in_dim(flat, start + me * size, size)

    gb_out = own(4 * width, half)
    return (
        output[None],
        grad_tokens[None],
        own(0, half),
        own(width, half),
        own(2 * width, half),
        own(3 * width, half),
        tot_qkv,
        own(5 * width, 3 * half),
        tot_out,
        gb_out,
        tot_up,
        own(8 * width, hid),
        tot_down,
        gb_out,
    )


def solution(mesh):
    placed = (
        P("wsh", "ctx", None),
        P("wsh"),
        P("wsh"),
        P("wsh"),
        P("wsh"),
        P("wsh", None),
        P("wsh"),
        P("wsh", None),
        P("wsh"),
        P("wsh", None),
        P("wsh"),
        P("wsh", None),
        P("wsh"),
        P("wsh"),
        P(),
        P("wsh", "ctx", None),
    )
    body = fast_shards if fast_fits(mesh) else shards
    return jax.shard_map(
        body,
        mesh=mesh,
        in_specs=placed,
        out_specs=(
            P("wsh", "ctx", None),
            P("wsh", "ctx", None),
            P("wsh"),
            P("wsh"),
            P("wsh"),
            P("wsh"),
            P("wsh", None),
            P("wsh"),
            P("wsh", None),
            P("wsh"),
            P("wsh", None),
            P("wsh"),
            P("wsh", None),
            P("wsh"),
        ),
        check_vma=False,
    )
```

```python
from functools import partial
import math

import jax
import jax.numpy as jnp
from jax import lax
from jax.experimental import pallas as pl
from jax.experimental.pallas import tpu as pltpu
from jax.sharding import PartitionSpec as P

H = 16
HD = 64
ROT = 16


epsilon = 1e-05


def norm_forward(values, norm_gain, norm_shift):
    average = jnp.mean(values, axis=-1, keepdims=True)
    centred = values - average
    variance = jnp.mean(centred * centred, axis=-1, keepdims=True)
    inverse = lax.rsqrt(variance + epsilon)
    normed = centred * inverse
    return (normed * norm_gain + norm_shift, normed, inverse)


def norm_backward(grad_out, normed, inverse, norm_gain):
    scaled = grad_out * norm_gain
    adjusted = (
        scaled
        - jnp.mean(scaled, axis=-1, keepdims=True)
        - normed * jnp.mean(scaled * normed, axis=-1, keepdims=True)
    )
    return (adjusted * inverse, jnp.sum(grad_out * normed, axis=0), jnp.sum(grad_out, axis=0))


def rotary_tables(positions):
    half_rot = ROT // 2
    frequency = 10000.0 ** (-jnp.arange(half_rot, dtype=jnp.float32) * 2.0 / ROT)
    angles = positions.astype(jnp.float32)[:, None] * frequency[None, :]
    return (jnp.cos(angles)[:, None, :], jnp.sin(angles)[:, None, :])


def rotate_forward(values, cosine_table, sine_table):
    half_rot = ROT // 2
    leading = values[..., :half_rot]
    trailing = values[..., half_rot:ROT]
    return jnp.concatenate(
        [
            leading * cosine_table - trailing * sine_table,
            trailing * cosine_table + leading * sine_table,
            values[..., ROT:],
        ],
        axis=-1,
    )


def rotate_backward(grads, cosine_table, sine_table):
    half_rot = ROT // 2
    leading = grads[..., :half_rot]
    trailing = grads[..., half_rot:ROT]
    return jnp.concatenate(
        [
            leading * cosine_table + trailing * sine_table,
            trailing * cosine_table - leading * sine_table,
            grads[..., ROT:],
        ],
        axis=-1,
    )


def masked_scores(query_rows, key_rows, query_pos, key_pos, key_live):
    raw_scores = jnp.einsum(
        "qhd,khd->hqk", query_rows, key_rows, preferred_element_type=jnp.float32
    )
    allowed = (key_pos[None, :] <= query_pos[:, None]) & key_live[None, :]
    return (jnp.where(allowed[None], raw_scores * (1.0 / math.sqrt(HD)), -1e30), allowed)


def score_grads(
    query_rows, key_rows, value_rows, grad_rows, query_pos, key_pos, key_live, log_total, row_dots
):
    scores = masked_scores(query_rows, key_rows, query_pos, key_pos, key_live)[0]
    probability = jnp.exp(scores - log_total[..., None])
    grad_prob = jnp.einsum(
        "qhd,khd->hqk", grad_rows, value_rows, preferred_element_type=jnp.float32
    )
    grad_score = (probability * (grad_prob - row_dots[..., None]) * (1.0 / math.sqrt(HD))).astype(
        jnp.bfloat16
    )
    return (probability.astype(jnp.bfloat16), grad_score)


def shards(
    tokens,
    ln1_gain,
    ln1_bias,
    ln2_gain,
    ln2_bias,
    w_qkv,
    b_qkv,
    w_out,
    b_out,
    w_up,
    b_up,
    w_down,
    b_down,
    lengths,
    block_map,
    cotangent,
):
    gathered = (
        lax.all_gather(ln1_gain, "wsh", axis=0, tiled=True),
        lax.all_gather(ln1_bias, "wsh", axis=0, tiled=True),
        lax.all_gather(ln2_gain, "wsh", axis=0, tiled=True),
        lax.all_gather(ln2_bias, "wsh", axis=0, tiled=True),
        lax.all_gather(w_qkv, "wsh", axis=0, tiled=True),
        lax.all_gather(b_qkv, "wsh", axis=0, tiled=True),
        lax.all_gather(w_out, "wsh", axis=0, tiled=True),
        lax.all_gather(b_out, "wsh", axis=0, tiled=True),
        lax.all_gather(w_up, "wsh", axis=0, tiled=True),
        lax.all_gather(b_up, "wsh", axis=0, tiled=True),
        lax.all_gather(w_down, "wsh", axis=0, tiled=True),
        lax.all_gather(b_down, "wsh", axis=0, tiled=True),
    )
    (
        norm1_gain,
        norm1_shift,
        norm2_gain,
        norm2_shift,
        qkv_weight,
        qkv_bias,
        out_weight,
        out_bias,
        up_weight,
        up_bias,
        down_weight,
        down_bias,
    ) = gathered
    tok_rows = tokens.shape[1]
    model_width = tokens.shape[2]
    half_rows = tok_rows // 2
    seq_rows = tok_rows * lax.axis_size("ctx")
    head_count = H
    head_size = HD
    ctx_index = lax.axis_index("ctx")
    own_blocks = lax.dynamic_slice_in_dim(block_map, 2 * ctx_index, 2)
    local_offsets = jnp.arange(half_rows, dtype=jnp.int32)
    positions = (own_blocks[:, None] * half_rows + local_offsets[None, :]).reshape(tok_rows)
    key_pos = (block_map[:, None] * half_rows + local_offsets[None, :]).reshape(seq_rows)
    length = lengths[0]
    own_live = positions < length
    live_rows = own_live.astype(jnp.float32)
    key_live = key_pos < length
    gain_first = norm1_gain.astype(jnp.float32)
    gain_second = norm2_gain.astype(jnp.float32)
    token_rows = tokens[0].astype(jnp.float32)
    normal_first, normed_first, inverse_first = norm_forward(
        token_rows, gain_first, norm1_shift.astype(jnp.float32)
    )
    normal_second, normed_second, inverse_second = norm_forward(
        token_rows, gain_second, norm2_shift.astype(jnp.float32)
    )
    attn_in = normal_first.astype(jnp.bfloat16)
    mlp_in = normal_second.astype(jnp.bfloat16)
    projected = (
        jnp.dot(attn_in, qkv_weight, preferred_element_type=jnp.float32)
        + qkv_bias.astype(jnp.float32)
    ).reshape(tok_rows, 3, head_count, head_size)
    cosine_table, sine_table = rotary_tables(positions)
    queries = rotate_forward(projected[:, 0], cosine_table, sine_table).astype(jnp.bfloat16)
    key_own = (
        rotate_forward(projected[:, 1], cosine_table, sine_table)
        .astype(jnp.bfloat16)
        .reshape(tok_rows, model_width)
    )
    value_own = projected[:, 2].astype(jnp.bfloat16).reshape(tok_rows, model_width)
    keys_all, values_all = (
        lax.all_gather(key_own, "ctx", axis=0, tiled=True),
        lax.all_gather(value_own, "ctx", axis=0, tiled=True),
    )
    block_len = math.gcd(seq_rows, 1024)
    block_count = seq_rows // block_len
    key_stack = keys_all.reshape(block_count, block_len, head_count, head_size)
    value_stack = values_all.reshape(block_count, block_len, head_count, head_size)
    pos_stack = key_pos.reshape(block_count, block_len)
    live_stack = key_live.reshape(block_count, block_len)

    def stats_step(running, key_part):
        key_block, pos_block, live_block = key_part
        scores, allowed = masked_scores(queries, key_block, positions, pos_block, live_block)
        peak_score = jnp.maximum(running[0], jnp.max(scores, axis=-1))
        exp_total = running[1] * jnp.exp(running[0] - peak_score) + jnp.sum(
            jnp.where(allowed[None], jnp.exp(scores - peak_score[..., None]), 0.0), axis=-1
        )
        return ((peak_score, exp_total), None)

    start_peak = jnp.full((head_count, tok_rows), -1e30, jnp.float32)
    final_state = lax.scan(
        stats_step, (start_peak, jnp.zeros_like(start_peak)), (key_stack, pos_stack, live_stack)
    )[0]
    log_total = final_state[0] + jnp.log(final_state[1])

    def value_step(running, key_part):
        key_block, value_block, pos_block, live_block = key_part
        scores = masked_scores(queries, key_block, positions, pos_block, live_block)[0]
        probability = jnp.exp(scores - log_total[..., None]).astype(jnp.bfloat16)
        return (
            running
            + jnp.einsum(
                "hqk,khd->qhd", probability, value_block, preferred_element_type=jnp.float32
            ),
            None,
        )

    zero_heads = jnp.zeros((tok_rows, head_count, head_size), jnp.float32)
    attended = lax.scan(value_step, zero_heads, (key_stack, value_stack, pos_stack, live_stack))[0]
    context_low = attended.reshape(tok_rows, model_width).astype(jnp.bfloat16)
    hidden = jnp.dot(mlp_in, up_weight, preferred_element_type=jnp.float32) + up_bias.astype(
        jnp.float32
    )
    activated, gelu_pull = jax.vjp(partial(jax.nn.gelu, approximate=False), hidden)
    act_low = activated.astype(jnp.bfloat16)
    branch = (
        jnp.dot(context_low, out_weight, preferred_element_type=jnp.float32)
        + out_bias.astype(jnp.float32)
        + jnp.dot(act_low, down_weight, preferred_element_type=jnp.float32)
        + down_bias.astype(jnp.float32)
    )
    output_rows = (live_rows[:, None] * (token_rows + branch)).astype(jnp.bfloat16)
    cot_rows = cotangent[0].astype(jnp.float32)
    grad_branch = (live_rows[:, None] * cot_rows).astype(jnp.bfloat16)
    grad_w_out = jnp.einsum(
        "tc,td->cd", context_low, grad_branch, preferred_element_type=jnp.float32
    )
    grad_w_down = jnp.einsum("tc,td->cd", act_low, grad_branch, preferred_element_type=jnp.float32)
    grad_branch_sum = jnp.sum(grad_branch.astype(jnp.float32), axis=0)
    grad_act = jnp.einsum("td,cd->tc", grad_branch, down_weight, preferred_element_type=jnp.float32)
    grad_hidden = gelu_pull(grad_act)[0].astype(jnp.bfloat16)
    grad_w_up = jnp.einsum("tc,td->cd", mlp_in, grad_hidden, preferred_element_type=jnp.float32)
    grad_b_up = jnp.sum(grad_hidden.astype(jnp.float32), axis=0)
    grad_mlp_in = jnp.einsum(
        "td,cd->tc", grad_hidden, up_weight, preferred_element_type=jnp.float32
    )
    grad_context = jnp.einsum(
        "td,cd->tc", grad_branch, out_weight, preferred_element_type=jnp.float32
    ).astype(jnp.bfloat16)
    grad_heads = grad_context.reshape(tok_rows, head_count, head_size)
    row_dots = jnp.sum(grad_heads.astype(jnp.float32) * attended, axis=-1).T

    def grad_step(running, key_part):
        key_block, value_block, pos_block, live_block = key_part
        prob_low, grad_score = score_grads(
            queries,
            key_block,
            value_block,
            grad_heads,
            positions,
            pos_block,
            live_block,
            log_total,
            row_dots,
        )
        query_sum = running + jnp.einsum(
            "hqk,khd->qhd", grad_score, key_block, preferred_element_type=jnp.float32
        )
        key_term = jnp.einsum(
            "hqk,qhd->khd", grad_score, queries, preferred_element_type=jnp.float32
        )
        value_term = jnp.einsum(
            "hqk,qhd->khd", prob_low, grad_heads, preferred_element_type=jnp.float32
        )
        return (query_sum, (key_term, value_term))

    query_grad, term_stacks = lax.scan(
        grad_step, zero_heads, (key_stack, value_stack, pos_stack, live_stack)
    )
    key_grad, value_grad = (
        lax.psum_scatter(
            term_stacks[0].reshape(seq_rows, model_width).astype(jnp.bfloat16),
            "ctx",
            scatter_dimension=0,
            tiled=True,
        ).astype(jnp.float32),
        lax.psum_scatter(
            term_stacks[1].reshape(seq_rows, model_width).astype(jnp.bfloat16),
            "ctx",
            scatter_dimension=0,
            tiled=True,
        ).astype(jnp.float32),
    )
    key_grad = key_grad.reshape(tok_rows, head_count, head_size)
    value_grad = value_grad.reshape(tok_rows, head_count, head_size)
    grad_projected = (
        jnp.stack(
            [
                rotate_backward(query_grad, cosine_table, sine_table),
                rotate_backward(key_grad, cosine_table, sine_table),
                value_grad,
            ],
            axis=1,
        )
        .reshape(tok_rows, 3 * model_width)
        .astype(jnp.bfloat16)
    )
    grad_w_qkv = jnp.einsum(
        "tc,td->cd", attn_in, grad_projected, preferred_element_type=jnp.float32
    )
    grad_b_qkv = jnp.sum(grad_projected.astype(jnp.float32), axis=0)
    grad_attn_in = jnp.einsum(
        "td,cd->tc", grad_projected, qkv_weight, preferred_element_type=jnp.float32
    )
    grad_input_first, grad_gain_first, grad_shift_first = norm_backward(
        grad_attn_in, normed_first, inverse_first, gain_first
    )
    grad_input_second, grad_gain_second, grad_shift_second = norm_backward(
        grad_mlp_in, normed_second, inverse_second, gain_second
    )
    grad_input = live_rows[:, None] * cot_rows + grad_input_first + grad_input_second
    shares = (
        lax.psum_scatter(
            grad_gain_first.astype(jnp.bfloat16), "wsh", scatter_dimension=0, tiled=True
        ).astype(jnp.float32),
        lax.psum_scatter(
            grad_shift_first.astype(jnp.bfloat16), "wsh", scatter_dimension=0, tiled=True
        ).astype(jnp.float32),
        lax.psum_scatter(
            grad_gain_second.astype(jnp.bfloat16), "wsh", scatter_dimension=0, tiled=True
        ).astype(jnp.float32),
        lax.psum_scatter(
            grad_shift_second.astype(jnp.bfloat16), "wsh", scatter_dimension=0, tiled=True
        ).astype(jnp.float32),
        lax.psum_scatter(
            grad_w_qkv.astype(jnp.bfloat16), "wsh", scatter_dimension=0, tiled=True
        ).astype(jnp.float32),
        lax.psum_scatter(
            grad_b_qkv.astype(jnp.bfloat16), "wsh", scatter_dimension=0, tiled=True
        ).astype(jnp.float32),
        lax.psum_scatter(
            grad_w_out.astype(jnp.bfloat16), "wsh", scatter_dimension=0, tiled=True
        ).astype(jnp.float32),
        lax.psum_scatter(
            grad_branch_sum.astype(jnp.bfloat16), "wsh", scatter_dimension=0, tiled=True
        ).astype(jnp.float32),
        lax.psum_scatter(
            grad_w_up.astype(jnp.bfloat16), "wsh", scatter_dimension=0, tiled=True
        ).astype(jnp.float32),
        lax.psum_scatter(
            grad_b_up.astype(jnp.bfloat16), "wsh", scatter_dimension=0, tiled=True
        ).astype(jnp.float32),
        lax.psum_scatter(
            grad_w_down.astype(jnp.bfloat16), "wsh", scatter_dimension=0, tiled=True
        ).astype(jnp.float32),
        lax.psum_scatter(
            grad_branch_sum.astype(jnp.bfloat16), "wsh", scatter_dimension=0, tiled=True
        ).astype(jnp.float32),
    )
    totals = (
        lax.psum(shares[0].astype(jnp.bfloat16), "ctx").astype(jnp.float32),
        lax.psum(shares[1].astype(jnp.bfloat16), "ctx").astype(jnp.float32),
        lax.psum(shares[2].astype(jnp.bfloat16), "ctx").astype(jnp.float32),
        lax.psum(shares[3].astype(jnp.bfloat16), "ctx").astype(jnp.float32),
        lax.psum(shares[4].astype(jnp.bfloat16), "ctx").astype(jnp.float32),
        lax.psum(shares[5].astype(jnp.bfloat16), "ctx").astype(jnp.float32),
        lax.psum(shares[6].astype(jnp.bfloat16), "ctx").astype(jnp.float32),
        lax.psum(shares[7].astype(jnp.bfloat16), "ctx").astype(jnp.float32),
        lax.psum(shares[8].astype(jnp.bfloat16), "ctx").astype(jnp.float32),
        lax.psum(shares[9].astype(jnp.bfloat16), "ctx").astype(jnp.float32),
        lax.psum(shares[10].astype(jnp.bfloat16), "ctx").astype(jnp.float32),
        lax.psum(shares[11].astype(jnp.bfloat16), "ctx").astype(jnp.float32),
    )
    return (
        output_rows[None],
        grad_input[None],
        totals[0],
        totals[1],
        totals[2],
        totals[3],
        totals[4],
        totals[5],
        totals[6],
        totals[7],
        totals[8],
        totals[9],
        totals[10],
        totals[11],
    )


HB = 128
NEG=-1e30
f32=jnp.float32; bf16=jnp.bfloat16

def _nn(a,b): return lax.dot_general(a,b,(((1,),(0,)),((),())),preferred_element_type=f32)
def _nt(a,b): return lax.dot_general(a,b,(((1,),(1,)),((),())),preferred_element_type=f32)

def attn_fwd_kernel(bm, x_ref, o_ref, lse_ref, q_s, kt_s, v_s, *, nblk, per, bq, bk):
    def perm(i,_):
        p=bm[i]; c=i//per; l=pl.multiple_of((i%per)*HB,HB); d=pl.multiple_of(p*HB,HB)
        q_s[:,pl.ds(d,HB)]=x_ref[c,0:64,pl.ds(l,HB)]*bf16(0.125)
        kt_s[pl.ds(d,HB),:]=x_ref[c,64:128,pl.ds(l,HB)].astype(f32).T.astype(bf16)
        v_s[:,pl.ds(d,HB)]=x_ref[c,128:192,pl.ds(l,HB)]
        return 0
    lax.fori_loop(0,nblk,perm,0)
    S=nblk*HB; nq=S//bq; r=bq//bk
    def step(q,qo,ko,carry,mask):
        m,l,acc=carry
        s=_nn(kt_s[pl.ds(ko,bk),:],q)
        if mask is not None: s=jnp.where(mask,s,NEG)
        mn=jnp.maximum(m,jnp.max(s,axis=0,keepdims=True))
        a=jnp.exp(m-mn); p=jnp.exp(s-mn)
        l=l*a+jnp.sum(p,axis=0,keepdims=True)
        acc=acc*a+_nn(v_s[:,pl.ds(ko,bk)],p.astype(bf16))
        return mn,l,acc
    ki=lax.broadcasted_iota(jnp.int32,(bk,bq),0); qi_=lax.broadcasted_iota(jnp.int32,(bk,bq),1)
    def qloop(i,_):
        qo=pl.multiple_of(i*bq,bq)
        q=q_s[:,pl.ds(qo,bq)]
        c=(jnp.full((1,bq),NEG,f32),jnp.zeros((1,bq),f32),jnp.zeros((64,bq),f32))
        c=lax.fori_loop(0,i*r,lambda j,c: step(q,qo,pl.multiple_of(j*bk,bk),c,None),c)
        for t in range(r):
            c=step(q,qo,pl.multiple_of(qo+t*bk,bk),c,ki+t*bk<=qi_)
        m,l,acc=c
        q_s[:,pl.ds(qo,bq)]=(acc*(1.0/l)).astype(bf16)
        lse_ref[:,pl.ds(qo,bq)]=m+jnp.log(l)
        return 0
    lax.fori_loop(0,nq,qloop,0)
    def unperm(i,_):
        p=bm[i]; c=i//per; l=pl.multiple_of((i%per)*HB,HB); d=pl.multiple_of(p*HB,HB)
        o_ref[c,:,pl.ds(l,HB)]=q_s[:,pl.ds(d,HB)]
        return 0
    lax.fori_loop(0,nblk,unperm,0)

def attn_fwd(bm,x,*,bq=512,bk=512):
    n=x.shape[0]; S=n*x.shape[2]; nblk=S//HB
    bq=math.gcd(S,bq); bk=math.gcd(bq,bk)
    return pl.pallas_call(
        lambda *a: attn_fwd_kernel(*a,nblk=nblk,per=x.shape[2]//HB,bq=bq,bk=bk),
        out_shape=(jax.ShapeDtypeStruct((n,64,x.shape[2]),bf16),jax.ShapeDtypeStruct((1,S),f32)),
        in_specs=[pl.BlockSpec(memory_space=pltpu.SMEM),pl.BlockSpec(memory_space=pltpu.VMEM)],
        out_specs=(pl.BlockSpec(memory_space=pltpu.VMEM),pl.BlockSpec(memory_space=pltpu.VMEM)),
        scratch_shapes=[pltpu.VMEM((64,S),bf16),pltpu.VMEM((S,64),bf16),pltpu.VMEM((64,S),bf16)],
        compiler_params=pltpu.CompilerParams(vmem_limit_bytes=56<<20),name="attn_fwd")(bm,x)

def attn_bwd_kernel(bm, x_ref, o_ref, do_ref, lse_ref, cs_ref, g_ref, q_s, kt_s, k_s, vt_s, do_s, dl_s, dq_s, dk_s, dv_s, *, nblk, per, bq, bk):
    def perm(i,_):
        p=bm[i]; c=i//per; l=pl.multiple_of((i%per)*HB,HB); d=pl.multiple_of(p*HB,HB)
        q_s[:,pl.ds(d,HB)]=x_ref[c,0:64,pl.ds(l,HB)]*bf16(0.125)
        k=x_ref[c,64:128,pl.ds(l,HB)]
        k_s[:,pl.ds(d,HB)]=k*bf16(0.125)
        kt_s[pl.ds(d,HB),:]=k.astype(f32).T.astype(bf16)
        vt_s[pl.ds(d,HB),:]=x_ref[c,128:192,pl.ds(l,HB)].astype(f32).T.astype(bf16)
        do=do_ref[c,:,pl.ds(l,HB)]
        do_s[:,pl.ds(d,HB)]=do
        dl_s[:,pl.ds(d,HB)]=jnp.sum(do.astype(f32)*o_ref[c,:,pl.ds(l,HB)].astype(f32),axis=0,keepdims=True)
        return 0
    lax.fori_loop(0,nblk,perm,0)
    S=nblk*HB; nq=S//bq; r=bq//bk
    dk_s[...]=jnp.zeros_like(dk_s); dv_s[...]=jnp.zeros_like(dv_s)
    def step(q,do,lse,dl,ko,dq,mask):
        s=_nn(kt_s[pl.ds(ko,bk),:],q)
        p=jnp.exp(s-lse)
        if mask is not None: p=jnp.where(mask,p,0.0)
        dp=_nn(vt_s[pl.ds(ko,bk),:],do)
        ds=(p*(dp-dl)).astype(bf16)
        pb=p.astype(bf16)
        dv_s[:,pl.ds(ko,bk)]+=_nt(do,pb)
        dk_s[:,pl.ds(ko,bk)]+=_nt(q,ds)
        return dq+_nn(k_s[:,pl.ds(ko,bk)],ds)
    ki=lax.broadcasted_iota(jnp.int32,(bk,bq),0); qi_=lax.broadcasted_iota(jnp.int32,(bk,bq),1)
    def qloop(i,_):
        qo=pl.multiple_of(i*bq,bq)
        q=q_s[:,pl.ds(qo,bq)]; do=do_s[:,pl.ds(qo,bq)]; lse=lse_ref[:,pl.ds(qo,bq)]; dl=dl_s[:,pl.ds(qo,bq)]
        dq=jnp.zeros((64,bq),f32)
        dq=lax.fori_loop(0,i*r,lambda j,c: step(q,do,lse,dl,pl.multiple_of(j*bk,bk),c,None),dq)
        for t in range(r):
            dq=step(q,do,lse,dl,pl.multiple_of(qo+t*bk,bk),dq,ki+t*bk<=qi_)
        dq_s[:,pl.ds(qo,bq)]=dq
        return 0
    lax.fori_loop(0,nq,qloop,0)
    def unperm(i,_):
        p=bm[i]; c=i//per; l=pl.multiple_of((i%per)*HB,HB); d=pl.multiple_of(p*HB,HB)
        cos=cs_ref[0:8,pl.ds(d,HB)]; sin=cs_ref[8:16,pl.ds(d,HB)]
        for n_,src in ((0,dq_s),(1,dk_s)):
            g=src[:,pl.ds(d,HB)]
            a=g[0:8]; b=g[8:16]
            full=jnp.concatenate([a*cos+b*sin,b*cos-a*sin,g[16:64]],axis=0)
            g_ref[c,64*n_:64*n_+64,pl.ds(l,HB)]=full.astype(bf16)
        g_ref[c,128:192,pl.ds(l,HB)]=dv_s[:,pl.ds(d,HB)].astype(bf16)
        return 0
    lax.fori_loop(0,nblk,unperm,0)

def attn_bwd(bm,x,o,do,lse,cs,*,bq=512,bk=512):
    n=x.shape[0]; S=n*x.shape[2]; nblk=S//HB
    bq=math.gcd(S,bq); bk=math.gcd(bq,bk)
    vm=pl.BlockSpec(memory_space=pltpu.VMEM)
    return pl.pallas_call(
        lambda *a: attn_bwd_kernel(*a,nblk=nblk,per=x.shape[2]//HB,bq=bq,bk=bk),
        out_shape=jax.ShapeDtypeStruct((n,192,x.shape[2]),bf16),
        in_specs=[pl.BlockSpec(memory_space=pltpu.SMEM)]+[vm]*5,
        out_specs=vm,
        scratch_shapes=[pltpu.VMEM((64,S),bf16),pltpu.VMEM((S,64),bf16),pltpu.VMEM((64,S),bf16),pltpu.VMEM((S,64),bf16),pltpu.VMEM((64,S),bf16),
                        pltpu.VMEM((1,S),f32),pltpu.VMEM((64,S),f32),pltpu.VMEM((64,S),f32),pltpu.VMEM((64,S),f32)],
        compiler_params=pltpu.CompilerParams(vmem_limit_bytes=56<<20),name="attn_bwd")(bm,x,o,do,lse,cs)


SWAP = [(0, 1), (1, 0)]


def fast_fits(mesh):
    return mesh.shape["wsh"] == 2 and mesh.shape["ctx"] == H


def _params(mb=56):
    return pltpu.CompilerParams(vmem_limit_bytes=mb << 20)


def _norm(x):
    xf = x.astype(f32)
    cen = xf - jnp.mean(xf, axis=-1, keepdims=True)
    inv = lax.rsqrt(jnp.mean(cen * cen, axis=-1, keepdims=True) + epsilon)
    return cen * inv, inv


def _full(v):
    return pl.BlockSpec(v.shape, lambda *a: (0,) * v.ndim)


def _wq_specs(half, width, cols, quarter, at):
    own = lambda p: pl.BlockSpec(
        (half, cols),
        lambda *a: (0, p * (width // cols) + a[-1][0] * (half // cols) + a[-1][1] * (quarter // cols) + at(*a)),
    )
    got = lambda p: pl.BlockSpec((half, cols), lambda *a: (0, p * (quarter // cols) + at(*a)))
    return [own(p) for p in range(3)] + [got(p) for p in range(3)]


def qkv_kernel(
    ids, x_ref, n_ref, wq_ref, wk_ref, wv_ref, gq_ref, gk_ref, gv_ref, bq_ref, bk_ref, bv_ref, cs_ref, send_ref,
    ain_ref, min_ref
):
    rows, width = x_ref.shape
    half = width // 2

    @pl.when(pl.program_id(1) == 0)
    def _():
        xhat, _ = _norm(x_ref[...])
        ain_ref[...] = (xhat * n_ref[0:1, :] + n_ref[1:2, :]).astype(bf16)
        min_ref[...] = (xhat * n_ref[2:3, :] + n_ref[3:4, :]).astype(bf16)

    me = ids[0]
    a_own = ain_ref[:, pl.ds(pl.multiple_of(me * half, half), half)]
    a_got = ain_ref[:, pl.ds(pl.multiple_of((1 - me) * half, half), half)]
    cos = cs_ref[0:8, :]
    sin = cs_ref[8:16, :]
    for n, (w, g, b) in enumerate(((wq_ref, gq_ref, bq_ref), (wk_ref, gk_ref, bk_ref), (wv_ref, gv_ref, bv_ref))):
        t = _nn(a_own, w[...]) + _nn(a_got, g[...]) + b[...]
        t = t.T
        for k in range(send_ref.shape[1]):
            v = t[k * HD : (k + 1) * HD]
            if n < 2:
                lead = v[0:8]
                trail = v[8:16]
                v = jnp.concatenate([lead * cos - trail * sin, trail * cos + lead * sin, v[16:]], axis=0)
            send_ref[0, k, n * HD : (n + 1) * HD, :] = v.astype(bf16)


def qkv_forward(ids, x2, norms, w_own, w_got, bias, cs, cols=128):
    rows, width = x2.shape[0] // 2, x2.shape[1]
    half = width // 2
    quarter = w_got.shape[1] // 3
    bsp = lambda p: pl.BlockSpec((1, cols), lambda s, i, ids: (0, p * (quarter // cols) + i))
    row = lambda: pl.BlockSpec((rows, width), lambda s, i, ids: (s, 0))
    return pl.pallas_call(
        qkv_kernel,
        grid_spec=pltpu.PrefetchScalarGridSpec(
            num_scalar_prefetch=1,
            grid=(2, quarter // cols),
            in_specs=[row(), _full(norms)]
            + _wq_specs(half, width, cols, quarter, lambda s, i, ids: i)
            + [bsp(p) for p in range(3)]
            + [_full(cs)],
            out_specs=(pl.BlockSpec((1, cols // HD, 3 * HD, rows), lambda s, i, ids: (s, i, 0, 0)), row(), row()),
        ),
        out_shape=(
            jax.ShapeDtypeStruct((2, quarter // HD, 3 * HD, rows), bf16),
            jax.ShapeDtypeStruct((2 * rows, width), bf16),
            jax.ShapeDtypeStruct((2 * rows, width), bf16),
        ),
        compiler_params=_params(),
        cost_estimate=pl.CostEstimate(flops=1 << 20, transcendentals=0, bytes_accessed=1 << 20),
        name="qkv_forward",
    )(ids, x2, norms, w_own, w_own, w_own, w_got, w_got, w_got, bias, bias, bias, cs)


def mlp_kernel(ids, x_ref, xt_ref, dy_ref, wo_ref, wg_ref, wd_ref, bu_ref, y_ref, dx_ref, gu_ref, gd_ref, gb_ref):
    rows, width = x_ref.shape
    half = width // 2
    me = ids[0]
    spans = (
        (pl.multiple_of(me * half, half), wo_ref),
        (pl.multiple_of((1 - me) * half, half), wg_ref),
    )

    @pl.when(pl.program_id(0) == 0)
    def _():
        y_ref[...] = jnp.zeros_like(y_ref)
        dx_ref[...] = jnp.zeros_like(dx_ref)

    dy = dy_ref[...]
    wd = wd_ref[...]
    u = bu_ref[...] + sum(_nn(x_ref[:, pl.ds(o, half)], w[...]) for o, w in spans)
    cdf = 0.5 * (1.0 + lax.erf(u * (1.0 / math.sqrt(2.0))))
    pdf = jnp.exp(-0.5 * u * u) * (1.0 / math.sqrt(2.0 * math.pi))
    act = (u * cdf).astype(bf16)
    du = (_nt(dy, wd) * (cdf + u * pdf)).astype(bf16)
    y_ref[...] += _nn(act, wd)
    for o, w in spans:
        dx_ref[:, pl.ds(o, half)] += _nt(du, w[...])
    gd = lax.dot_general(act, dy, (((0,), (0,)), ((), ())), preferred_element_type=f32).astype(bf16)
    k, r, _ = gd_ref.shape
    for c in range(k):
        gd_ref[c] = gd[c * r : (c + 1) * r, :]
    gu = _nn(xt_ref[...], du).astype(bf16)
    n = gu_ref.shape[0]
    r = half // n
    for h in range(2):
        for c in range(n):
            gu_ref[c, h * r : (h + 1) * r, :] = gu[h * half + c * r : h * half + (c + 1) * r, :]
    gb_ref[...] = jnp.sum(du.astype(f32), axis=0, keepdims=True)


def mlp(ids, x, xt, dy, w_own, w_got, wd, bu, n, tile=256):
    rows, width = x.shape
    half = width // 2
    hidden = w_got.shape[1]
    steps = hidden // tile
    whole = pl.BlockSpec((rows, width), lambda i, ids: (0, 0))
    per = hidden // n
    part = lambda i, ids: ids[1] * steps + i
    return pl.pallas_call(
        mlp_kernel,
        grid_spec=pltpu.PrefetchScalarGridSpec(
            num_scalar_prefetch=1,
            grid=(steps,),
            in_specs=[
                whole,
                pl.BlockSpec((width, rows), lambda i, ids: (0, 0)),
                whole,
                pl.BlockSpec((half, tile), lambda i, ids: (0, ids[0] * 2 * steps + part(i, ids))),
                pl.BlockSpec((half, tile), lambda i, ids: (0, i)),
                pl.BlockSpec((tile, width), lambda i, ids: (part(i, ids), 0)),
                pl.BlockSpec((1, tile), lambda i, ids: (0, part(i, ids))),
            ],
            out_specs=(
                whole,
                whole,
                pl.BlockSpec((n, width // n, tile), lambda i, ids: (0, 0, i)),
                pl.BlockSpec((tile // per, per, width), lambda i, ids: (i, 0, 0)),
                pl.BlockSpec((1, tile), lambda i, ids: (0, i)),
            ),
        ),
        out_shape=(
            jax.ShapeDtypeStruct((rows, width), f32),
            jax.ShapeDtypeStruct((rows, width), f32),
            jax.ShapeDtypeStruct((n, width // n, hidden), bf16),
            jax.ShapeDtypeStruct((n, per, width), bf16),
            jax.ShapeDtypeStruct((1, hidden), f32),
        ),
        compiler_params=_params(),
        cost_estimate=pl.CostEstimate(
            flops=12 * rows * width * hidden, transcendentals=2 * rows * hidden, bytes_accessed=24 << 20
        ),
        name="mlp",
    )(ids, x, xt, dy, w_own, w_got, wd, bu)


def qkv_back_kernel(
    ids, d_ref, at_ref, x_ref, n_ref, wq_ref, wk_ref, wv_ref, gq_ref, gk_ref, gv_ref, dm_ref, ob_ref, dy_ref, gb_ref,
    a_ref, b_ref, e_ref, g_s, go_s, bias_s, sum_s
):
    rows, width = x_ref.shape
    half = width // 2
    me = ids[0]
    core = ids[1]
    s = pl.program_id(0)
    outs = (a_ref, b_ref)
    n = a_ref.shape[0]
    nh = d_ref.shape[1]
    cols = nh * HD
    r = half // (2 * n)

    @pl.when(s == 0)
    def _():
        g_s[...] = jnp.zeros_like(g_s)
        go_s[...] = jnp.zeros_like(go_s)
        bias_s[...] = jnp.zeros_like(bias_s)
        sum_s[...] = jnp.zeros_like(sum_s)

    ones = jnp.ones((8, rows), bf16)
    at = at_ref[...]
    dts = []
    for p in range(3):
        dp = jnp.concatenate([d_ref[0, k, p * HD : (p + 1) * HD, :] for k in range(nh)], axis=0)
        g_s[p] += _nt(at, dp)
        bias_s[p * 8 : (p + 1) * 8, :] += _nt(ones, dp)
        dts.append(dp.astype(f32).T.astype(bf16))
    go_s[...] += _nn(ob_ref[0], dy_ref[...])
    dt = jnp.concatenate(dts, axis=1)
    w_own = jnp.concatenate([wq_ref[...], wk_ref[...], wv_ref[...]], axis=1)
    w_got = jnp.concatenate([gq_ref[...], gk_ref[...], gv_ref[...]], axis=1)
    d_own = _nt(dt, w_own)
    d_got = _nt(dt, w_got)
    first = me == 0
    xhat, _ = _norm(x_ref[...])
    for h in range(2):
        lanes = slice(h * half, (h + 1) * half)
        da = jnp.where(first, d_own, d_got) if h == 0 else jnp.where(first, d_got, d_own)
        dm = dm_ref[:, lanes]
        xh = xhat[:, lanes]
        e_ref[0, :, lanes] = da * n_ref[0:1, lanes] + dm * n_ref[2:3, lanes]
        for k, v in enumerate((da * xh, da, dm * xh, dm)):
            sum_s[k : k + 1, lanes] += jnp.sum(v, axis=0, keepdims=True)

    @pl.when(s == 0)
    def _():
        mine = dy_ref[pl.ds(pl.multiple_of(core * (rows // 2), rows // 2), rows // 2), :]
        sum_s[4:5, :] = jnp.sum(mine.astype(f32), axis=0, keepdims=True)

    @pl.when(s == pl.num_programs(0) - 1)
    def _():
        for p in range(3):
            g = g_s[p].astype(bf16)
            for h in range(2):
                for c in range(n):
                    for a in range(2):
                        row = h * half + (c * 2 + a) * r
                        u = (h * 3 + p) * r
                        outs[a][c, u : u + r, :] = g[row : row + r, :]
        go = go_s[...].astype(bf16)
        q = cols // (2 * n)
        for c in range(n):
            for a in range(2):
                row = (c * 2 + a) * q
                for k in range(width // cols):
                    u = 6 * r + k * q
                    outs[a][c, u : u + q, :] = go[row : row + q, k * cols : (k + 1) * cols]
        flat = [sum_s[k : k + 1, t * cols : (t + 1) * cols] for k in range(5) for t in range(width // cols)]
        zero = jnp.zeros((1, cols), f32)
        for p in range(3):
            flat += [
                jnp.where((me == k) & (core == j), bias_s[p * 8 : p * 8 + 1, :], zero) for k in range(2) for j in range(2)
            ]
        flat += [
            jnp.where((me == k) & (core == j), gb_ref[:, t * cols : (t + 1) * cols], zero)
            for k in range(2)
            for j in range(2)
            for t in range(gb_ref.shape[1] // cols)
        ]
        top = 6 * r + (width // cols) * q
        per = len(flat) // n
        pad = [zero] * (8 - per)
        for c in range(n):
            b_ref[c, top : top + 8, :] = jnp.concatenate(flat[c * per : (c + 1) * per] + pad, axis=0).astype(bf16)


def qkv_backward(ids, d, at, x2, norms, w_own, w_got, d_mlp, ob, dy, gb_up, n):
    rows, width = x2.shape[0] // 2, x2.shape[1]
    half = width // 2
    cols = w_got.shape[1] // 3
    size = 6 * (half // (2 * n)) + width // (2 * n)
    row = lambda: pl.BlockSpec((rows, width), lambda s, ids: (s, 0))
    out = [
        jax.ShapeDtypeStruct((n, size, cols), bf16),
        jax.ShapeDtypeStruct((n, size + 8, cols), bf16),
    ]
    return pl.pallas_call(
        qkv_back_kernel,
        grid_spec=pltpu.PrefetchScalarGridSpec(
            num_scalar_prefetch=1,
            grid=(2,),
            in_specs=[
                pl.BlockSpec((1, cols // HD, 3 * HD, rows), lambda s, ids: (s, 0, 0, 0)),
                pl.BlockSpec((width, rows), lambda s, ids: (0, s)),
                row(),
                _full(norms),
            ]
            + _wq_specs(half, width, cols, cols, lambda s, ids: 0)
            + [row(), pl.BlockSpec((1, cols, rows), lambda s, ids: (s, 0, 0)), row(), _full(gb_up)],
            out_specs=(*[_full(v) for v in out], pl.BlockSpec((1, rows, width), lambda s, ids: (s, 0, 0))),
            scratch_shapes=[
                pltpu.VMEM((3, width, cols), f32),
                pltpu.VMEM((cols, width), f32),
                pltpu.VMEM((24, cols), f32),
                pltpu.VMEM((8, width), f32),
            ],
        ),
        out_shape=(*out, jax.ShapeDtypeStruct((2, rows, width), f32)),
        compiler_params=_params(),
        name="qkv_backward",
    )(ids, d, at, x2, norms, w_own, w_own, w_own, w_got, w_got, w_got, d_mlp, ob, dy, gb_up)


def _mine(ids):
    return (pl.program_id(0) // 2) == ids[1]


def _own_block(i, ids):
    return jnp.clip(i - 2 * ids[1], 0, 1)


def _got_block(i, ids):
    return jnp.clip(i - 2 * (1 - ids[1]), 0, 1)


def join_kernel(ids, own_ref, got_ref, o_ref):
    mine = _mine(ids)
    shape = o_ref.shape

    @pl.when(mine)
    def _():
        o_ref[...] = own_ref[...].astype(f32).reshape(shape)

    @pl.when(jnp.logical_not(mine))
    def _():
        o_ref[...] = got_ref[...].astype(f32).reshape(shape)


def join_rows(ids, own, got):
    n, r, w = own.shape
    src = lambda f: pl.BlockSpec((n // 2, r, w), lambda i, ids: (f(i, ids), 0, 0))
    return pl.pallas_call(
        join_kernel,
        grid_spec=pltpu.PrefetchScalarGridSpec(
            num_scalar_prefetch=1,
            grid=(4,),
            in_specs=[src(_own_block), src(_got_block)],
            out_specs=pl.BlockSpec((n * r // 2, w), lambda i, ids: (i, 0)),
        ),
        out_shape=jax.ShapeDtypeStruct((2 * n * r, w), f32),
        compiler_params=_params(),
        name="join_rows",
    )(ids, own, got)


def join_cols(ids, own, got):
    n, _, r, w = own.shape
    src = lambda f: pl.BlockSpec((n, 1, r, w), lambda i, ids: (0, f(i, ids), 0, 0))
    return pl.pallas_call(
        join_kernel,
        grid_spec=pltpu.PrefetchScalarGridSpec(
            num_scalar_prefetch=1,
            grid=(4,),
            in_specs=[src(_own_block), src(_got_block)],
            out_specs=pl.BlockSpec((n * r, w), lambda i, ids: (0, (i % 2) * 2 + i // 2)),
        ),
        out_shape=jax.ShapeDtypeStruct((n * r, 4 * w), f32),
        compiler_params=_params(),
        name="join_cols",
    )(ids, own, got)


def unpack_kernel(ids, ao_ref, ag_ref, bo_ref, bg_ref, q_ref, o_ref, s_ref):
    first = ids[1] == 0
    k, _, cols = ao_ref.shape
    r = q_ref.shape[0] // (2 * k)
    q = o_ref.shape[1] // (2 * k)
    for a, (own, got) in enumerate(((ao_ref, ag_ref), (bo_ref, bg_ref))):
        for c in range(k):
            x = own[c].astype(f32)
            y = got[c].astype(f32)
            to = slice((c * 2 + a) * r, (c * 2 + a + 1) * r)
            tq = slice((c * 2 + a) * q, (c * 2 + a + 1) * q)
            for j in range(2):
                v = jnp.where(first, x, y) if j == 0 else jnp.where(first, y, x)
                for w in range(2):
                    for p in range(3):
                        u = (w * 3 + p) * r
                        at = ((p * 2 + w) * 2 + j) * cols
                        q_ref[to, at : at + cols] = v[u : u + r, :]
                for t in range(o_ref.shape[2] // cols):
                    u = 6 * r + t * q
                    o_ref[j, tq, t * cols : (t + 1) * cols] = v[u : u + q, :]
            if a == 1:
                s_ref[c] = (x + y)[-8:, :]


def unpack(ids, a_own, a_got, b_own, b_got, width, steps=4):
    n, _, cols = a_own.shape
    half = width // 2
    k = n // steps
    spec = lambda v: pl.BlockSpec((k,) + v.shape[1:], lambda i, ids: (i, 0, 0))
    return pl.pallas_call(
        unpack_kernel,
        grid_spec=pltpu.PrefetchScalarGridSpec(
            num_scalar_prefetch=1,
            grid=(steps,),
            in_specs=[spec(v) for v in (a_own, a_got, b_own, b_got)],
            out_specs=(
                pl.BlockSpec((half // steps, 3 * width), lambda i, ids: (i, 0)),
                pl.BlockSpec((2, cols // steps, width), lambda i, ids: (0, i, 0)),
                pl.BlockSpec((k, 8, cols), lambda i, ids: (i, 0, 0)),
            ),
        ),
        out_shape=(
            jax.ShapeDtypeStruct((half, 3 * width), f32),
            jax.ShapeDtypeStruct((2, cols, width), f32),
            jax.ShapeDtypeStruct((n, 8, cols), f32),
        ),
        compiler_params=_params(),
        name="unpack",
    )(ids, a_own, a_got, b_own, b_got)


def last_kernel(eo_ref, er_ref, x_ref, c_ref, live_ref, o_ref):
    xhat, inv = _norm(x_ref[...])
    e = eo_ref[...] + er_ref[...].astype(f32)
    dx = inv * (
        e - jnp.mean(e, axis=-1, keepdims=True) - xhat * jnp.mean(e * xhat, axis=-1, keepdims=True)
    )
    o_ref[...] = live_ref[...] * c_ref[...].astype(f32) + dx


def last(e_own, e_got, x, cot, live):
    return pl.pallas_call(
        last_kernel,
        out_shape=jax.ShapeDtypeStruct(x.shape, f32),
        compiler_params=_params(),
        name="token_grad",
    )(e_own, e_got, x, cot, live)


def fast_shards(
    tokens,
    ln1_gain,
    ln1_bias,
    ln2_gain,
    ln2_bias,
    w_qkv,
    b_qkv,
    w_out,
    b_out,
    w_up,
    b_up,
    w_down,
    b_down,
    lengths,
    block_map,
    cotangent,
):
    ctx = lax.axis_index("ctx")
    me = lax.axis_index("wsh")
    core = ctx % 2
    n_ctx = lax.axis_size("ctx")
    chips = n_ctx // 2
    own_rows, width = tokens.shape[1:]
    rows = 2 * own_rows
    half = width // 2
    quarter = half // 2
    seq = own_rows * n_ctx
    heads = H // 4
    hid = w_up.shape[1] // 4
    ids = jnp.stack([me, core]).astype(jnp.int32)
    CORE, X, ZN, ZF = 0, 1, 2, 3

    def swap(v):
        return lax.ppermute(v, "wsh", SWAP)

    def flip(v, bit):
        return lax.ppermute(v, "ctx", [(i, i ^ (1 << bit)) for i in range(n_ctx)])

    def bit_of(bit):
        return (ctx >> bit) & 1

    def add(*terms):
        return sum(v.astype(f32) for v in terms).astype(bf16) if len(terms) > 1 else terms[0]

    def halve(terms, bit):
        b = bit_of(bit)

        def part(k):
            cut = [v.reshape((2, v.shape[0] // 2) + v.shape[1:]) for v in terms]
            return add(*[lax.dynamic_index_in_dim(v, k, 0, keepdims=False) for v in cut])

        return part(b), flip(part(1 - b), bit)

    def ordered(first, a, b, axis=0):
        return jnp.where(first == 0, jnp.concatenate([a, b], axis), jnp.concatenate([b, a], axis))

    def double(v, bit):
        return ordered(bit_of(bit), v, flip(v, bit))

    def exchange(v):
        groups = [[2 * i + c for i in range(chips)] for c in range(2)]
        return lax.all_to_all(v, "ctx", 0, 0, axis_index_groups=groups, tiled=False)

    def rows_of(v, at, n, axis=0):
        return lax.dynamic_slice_in_dim(v, at, n, axis)

    len_parts = jnp.stack([lengths[0] // 64, lengths[0] % 64]).astype(bf16)
    small = jnp.concatenate(
        [ln1_gain, ln1_bias, ln2_gain, ln2_bias, b_out, b_down, b_qkv, len_parts, jnp.zeros((126,), bf16)]
    )[None]
    small = ordered(me, small, swap(small))
    x_own = tokens[0]
    x_got = swap(x_own)
    mine = me * half + core * quarter
    other = (1 - me) * half + core * quarter
    wq_rows = rows_of(w_qkv, bit_of(X) * quarter, quarter)
    wq_got = swap(jnp.concatenate([rows_of(wq_rows, p * width + other, quarter, 1) for p in range(3)], axis=1))
    wu_send = rows_of(w_up, ((1 - me) * 2 + core) * hid, hid, 1)
    wq_got, wu_send = lax.optimization_barrier((wq_got, wu_send))
    wq_got = double(wq_got, X)
    wu_got = swap(wu_send)
    x_sib = flip(x_own, CORE)
    x2 = jnp.concatenate([ordered(core, x_own, x_sib), double(x_got, CORE)])
    cot_own = cotangent[0]
    cot_sib = flip(cot_own, CORE)

    vec = lambda i: small[:, i * half : (i + 1) * half].reshape(width).astype(f32)
    norms = jnp.stack([vec(i) for i in range(4)])
    bias_out = vec(4) + vec(5)
    qkv_bias = small[:, 6 * half : 9 * half].astype(f32).reshape(3, width)
    qkv_bias = rows_of(qkv_bias, mine, quarter, 1).reshape(1, 3 * quarter)
    lens = small[:, 9 * half : 9 * half + 2].astype(jnp.int32)
    lens = lens[:, 0] * 64 + lens[:, 1]
    other_len = lens[1 - me]

    blocks = rows_of(block_map, (rows // HB) * (ctx // 2), rows // HB)
    offs = jnp.arange(HB, dtype=jnp.int32)
    positions = (blocks[:, None] * HB + offs[None, :]).reshape(rows)
    live2 = jnp.concatenate([positions < lengths[0], positions < other_len]).astype(f32)[:, None]
    live_own = rows_of(live2, core * own_rows, own_rows)
    freq = 10000.0 ** (-jnp.arange(ROT // 2, dtype=f32) * 2.0 / ROT)
    ang = freq[:, None] * jnp.arange(seq, dtype=jnp.int32).astype(f32)[None, :]
    table = jnp.concatenate([jnp.cos(ang), jnp.sin(ang)])
    own_ang = freq[:, None] * positions.astype(f32)[None, :]
    own_table = jnp.concatenate([jnp.cos(own_ang), jnp.sin(own_ang)])

    send, attn_in, mlp_in = qkv_forward(ids, x2, norms, w_qkv, wq_got, qkv_bias, own_table)
    qkv_head = exchange(send.reshape(2 * heads, 3 * HD, rows))
    mlp_in, wu_got, cot_send = lax.optimization_barrier((mlp_in, wu_got, cot_own))
    cot_got = swap(cot_send)
    cot2 = jnp.concatenate([ordered(core, cot_own, cot_sib), double(cot_got, CORE)])
    dy = (live2 * cot2.astype(f32)).astype(bf16)
    dy2 = dy.reshape(2, rows, width)
    w_out_mine = rows_of(w_out, core * quarter, quarter)
    dctx = jnp.einsum("ed,std->set", w_out_mine, dy2, preferred_element_type=f32).astype(bf16)
    do_head = exchange(dctx.reshape(2 * heads, HD, rows))

    attn_t = attn_in.T
    y_mlp, d_mlp, g_up, g_down, gb_up = mlp(
        ids, mlp_in, mlp_in.T, dy, w_up, wu_got, w_down, b_up.astype(f32)[None, :], chips
    )

    chain_a = (X, ZN, ZF)
    chain_b = (ZN, ZF, X)
    qkv_head, g_up, g_down = lax.optimization_barrier((qkv_head, g_up, g_down))
    down = halve((g_down,), chain_a[0])
    up = halve((g_up,), chain_b[0])

    o_head, lse = attn_fwd(block_map, qkv_head, bq=1024, bk=1024)
    qkv_head, o_head, do_head, down, up = lax.optimization_barrier((qkv_head, o_head, do_head, down, up))
    ob = exchange(o_head).reshape(2, quarter, rows)
    down = halve(down, chain_a[1])
    up = halve(up, chain_b[1])
    g_head = attn_bwd(block_map, qkv_head, o_head, do_head, lse, table)
    g_head, ob, down, up = lax.optimization_barrier((g_head, ob, down, up))
    d_qkv = exchange(g_head).reshape(2, heads, 3 * HD, rows)

    down = add(*halve(down, chain_a[2]))
    up = add(*halve(up, chain_b[2]))
    up = up.reshape(1, 2, up.shape[1] // 2, up.shape[2])
    up_keep = rows_of(up, me, 1, 1)
    up_got = swap(rows_of(up, 1 - me, 1, 1))
    up = ordered(me, up_keep, up_got, axis=1)
    for a, b in zip(chain_a[::-1], chain_b[::-1]):
        down = double(down, a)
        up = double(up, b)
    tot_down = join_rows(ids, down, flip(down, CORE))
    tot_up = join_cols(ids, up, flip(up, CORE))

    def settle(v):
        give = rows_of(v, (1 - core) * own_rows, own_rows, 1).astype(bf16)
        v = rows_of(v, core * own_rows, own_rows, 1) + flip(give, CORE).astype(f32)
        return v[0], swap(v[1].astype(bf16))

    part = jnp.einsum("sct,cd->std", ob, w_out_mine, preferred_element_type=f32) + y_mlp.reshape(2, rows, width)
    part, part_got = settle(part)
    output = (live_own * (x_own.astype(f32) + part + part_got.astype(f32) + bias_out)).astype(bf16)

    v_a, v_b, e = qkv_backward(
        ids, d_qkv, attn_t, x2, norms, w_qkv, wq_got, d_mlp, ob, dy, gb_up, chips
    )
    v_a = (v_a,)
    v_b = (v_b,)
    for a, b in zip(chain_a, chain_b):
        v_a = halve(v_a, a)
        v_b = halve(v_b, b)
    e_own, e_got = settle(e)
    n3 = 3 * half // (2 * chips)
    size = 2 * n3 + width // (2 * chips)
    mixed = []
    for v, chain in ((add(*v_a)[0], chain_a), (add(*v_b)[0], chain_b)):
        extra = v[size:]
        back = swap(jnp.concatenate([rows_of(v, (1 - me) * n3, n3), extra]))
        extra = add(extra, back[n3:])
        v = jnp.concatenate([ordered(me, rows_of(v, me * n3, n3), back[:n3]), v[2 * n3 : size], extra])[None]
        for a in chain[::-1]:
            v = double(v, a)
        mixed.append(v)
    grad_tokens = last(e_own, e_got, x_own, cot_own, live_own)
    mixed[0], mixed[1], grad_tokens, output, tot_down, tot_up = lax.optimization_barrier(
        (mixed[0], mixed[1], grad_tokens, output, tot_down, tot_up)
    )
    tot_qkv, tot_out, flat = unpack(ids, mixed[0], flip(mixed[0], CORE), mixed[1], flip(mixed[1], CORE), width)
    flat = flat[:, :6].reshape(12 * width)

    def own(start, size):
        return lax.dynamic_slice_in_dim(flat, start + me * size, size)

    gb_out = own(4 * width, half)
    return (
        output[None],
        grad_tokens[None],
        own(0, half),
        own(width, half),
        own(2 * width, half),
        own(3 * width, half),
        tot_qkv,
        own(5 * width, 3 * half),
        tot_out.reshape(half, width),
        gb_out,
        tot_up,
        own(8 * width, 2 * hid),
        tot_down,
        gb_out,
    )


def solution(mesh):
    placed = (
        P("wsh", "ctx", None),
        P("wsh"),
        P("wsh"),
        P("wsh"),
        P("wsh"),
        P("wsh", None),
        P("wsh"),
        P("wsh", None),
        P("wsh"),
        P("wsh", None),
        P("wsh"),
        P("wsh", None),
        P("wsh"),
        P("wsh"),
        P(),
        P("wsh", "ctx", None),
    )
    body = fast_shards if fast_fits(mesh) else shards
    return jax.shard_map(
        body,
        mesh=mesh,
        in_specs=placed,
        out_specs=(
            P("wsh", "ctx", None),
            P("wsh", "ctx", None),
            P("wsh"),
            P("wsh"),
            P("wsh"),
            P("wsh"),
            P("wsh", None),
            P("wsh"),
            P("wsh", None),
            P("wsh"),
            P("wsh", None),
            P("wsh"),
            P("wsh", None),
            P("wsh"),
        ),
        check_vma=False,
    )
```

```python
from functools import partial
import math

import jax
import jax.numpy as jnp
from jax import lax
from jax.experimental import pallas as pl
from jax.experimental.pallas import tpu as pltpu
from jax.sharding import PartitionSpec as P

H = 16
HD = 64
ROT = 16


epsilon = 1e-05


def norm_forward(values, norm_gain, norm_shift):
    average = jnp.mean(values, axis=-1, keepdims=True)
    centred = values - average
    variance = jnp.mean(centred * centred, axis=-1, keepdims=True)
    inverse = lax.rsqrt(variance + epsilon)
    normed = centred * inverse
    return (normed * norm_gain + norm_shift, normed, inverse)


def norm_backward(grad_out, normed, inverse, norm_gain):
    scaled = grad_out * norm_gain
    adjusted = (
        scaled
        - jnp.mean(scaled, axis=-1, keepdims=True)
        - normed * jnp.mean(scaled * normed, axis=-1, keepdims=True)
    )
    return (adjusted * inverse, jnp.sum(grad_out * normed, axis=0), jnp.sum(grad_out, axis=0))


def rotary_tables(positions):
    half_rot = ROT // 2
    frequency = 10000.0 ** (-jnp.arange(half_rot, dtype=jnp.float32) * 2.0 / ROT)
    angles = positions.astype(jnp.float32)[:, None] * frequency[None, :]
    return (jnp.cos(angles)[:, None, :], jnp.sin(angles)[:, None, :])


def rotate_forward(values, cosine_table, sine_table):
    half_rot = ROT // 2
    leading = values[..., :half_rot]
    trailing = values[..., half_rot:ROT]
    return jnp.concatenate(
        [
            leading * cosine_table - trailing * sine_table,
            trailing * cosine_table + leading * sine_table,
            values[..., ROT:],
        ],
        axis=-1,
    )


def rotate_backward(grads, cosine_table, sine_table):
    half_rot = ROT // 2
    leading = grads[..., :half_rot]
    trailing = grads[..., half_rot:ROT]
    return jnp.concatenate(
        [
            leading * cosine_table + trailing * sine_table,
            trailing * cosine_table - leading * sine_table,
            grads[..., ROT:],
        ],
        axis=-1,
    )


def masked_scores(query_rows, key_rows, query_pos, key_pos, key_live):
    raw_scores = jnp.einsum(
        "qhd,khd->hqk", query_rows, key_rows, preferred_element_type=jnp.float32
    )
    allowed = (key_pos[None, :] <= query_pos[:, None]) & key_live[None, :]
    return (jnp.where(allowed[None], raw_scores * (1.0 / math.sqrt(HD)), -1e30), allowed)


def score_grads(
    query_rows, key_rows, value_rows, grad_rows, query_pos, key_pos, key_live, log_total, row_dots
):
    scores = masked_scores(query_rows, key_rows, query_pos, key_pos, key_live)[0]
    probability = jnp.exp(scores - log_total[..., None])
    grad_prob = jnp.einsum(
        "qhd,khd->hqk", grad_rows, value_rows, preferred_element_type=jnp.float32
    )
    grad_score = (probability * (grad_prob - row_dots[..., None]) * (1.0 / math.sqrt(HD))).astype(
        jnp.bfloat16
    )
    return (probability.astype(jnp.bfloat16), grad_score)


def shards(
    tokens,
    ln1_gain,
    ln1_bias,
    ln2_gain,
    ln2_bias,
    w_qkv,
    b_qkv,
    w_out,
    b_out,
    w_up,
    b_up,
    w_down,
    b_down,
    lengths,
    block_map,
    cotangent,
):
    gathered = (
        lax.all_gather(ln1_gain, "wsh", axis=0, tiled=True),
        lax.all_gather(ln1_bias, "wsh", axis=0, tiled=True),
        lax.all_gather(ln2_gain, "wsh", axis=0, tiled=True),
        lax.all_gather(ln2_bias, "wsh", axis=0, tiled=True),
        lax.all_gather(w_qkv, "wsh", axis=0, tiled=True),
        lax.all_gather(b_qkv, "wsh", axis=0, tiled=True),
        lax.all_gather(w_out, "wsh", axis=0, tiled=True),
        lax.all_gather(b_out, "wsh", axis=0, tiled=True),
        lax.all_gather(w_up, "wsh", axis=0, tiled=True),
        lax.all_gather(b_up, "wsh", axis=0, tiled=True),
        lax.all_gather(w_down, "wsh", axis=0, tiled=True),
        lax.all_gather(b_down, "wsh", axis=0, tiled=True),
    )
    (
        norm1_gain,
        norm1_shift,
        norm2_gain,
        norm2_shift,
        qkv_weight,
        qkv_bias,
        out_weight,
        out_bias,
        up_weight,
        up_bias,
        down_weight,
        down_bias,
    ) = gathered
    tok_rows = tokens.shape[1]
    model_width = tokens.shape[2]
    half_rows = tok_rows // 2
    seq_rows = tok_rows * lax.axis_size("ctx")
    head_count = H
    head_size = HD
    ctx_index = lax.axis_index("ctx")
    own_blocks = lax.dynamic_slice_in_dim(block_map, 2 * ctx_index, 2)
    local_offsets = jnp.arange(half_rows, dtype=jnp.int32)
    positions = (own_blocks[:, None] * half_rows + local_offsets[None, :]).reshape(tok_rows)
    key_pos = (block_map[:, None] * half_rows + local_offsets[None, :]).reshape(seq_rows)
    length = lengths[0]
    own_live = positions < length
    live_rows = own_live.astype(jnp.float32)
    key_live = key_pos < length
    gain_first = norm1_gain.astype(jnp.float32)
    gain_second = norm2_gain.astype(jnp.float32)
    token_rows = tokens[0].astype(jnp.float32)
    normal_first, normed_first, inverse_first = norm_forward(
        token_rows, gain_first, norm1_shift.astype(jnp.float32)
    )
    normal_second, normed_second, inverse_second = norm_forward(
        token_rows, gain_second, norm2_shift.astype(jnp.float32)
    )
    attn_in = normal_first.astype(jnp.bfloat16)
    mlp_in = normal_second.astype(jnp.bfloat16)
    projected = (
        jnp.dot(attn_in, qkv_weight, preferred_element_type=jnp.float32)
        + qkv_bias.astype(jnp.float32)
    ).reshape(tok_rows, 3, head_count, head_size)
    cosine_table, sine_table = rotary_tables(positions)
    queries = rotate_forward(projected[:, 0], cosine_table, sine_table).astype(jnp.bfloat16)
    key_own = (
        rotate_forward(projected[:, 1], cosine_table, sine_table)
        .astype(jnp.bfloat16)
        .reshape(tok_rows, model_width)
    )
    value_own = projected[:, 2].astype(jnp.bfloat16).reshape(tok_rows, model_width)
    keys_all, values_all = (
        lax.all_gather(key_own, "ctx", axis=0, tiled=True),
        lax.all_gather(value_own, "ctx", axis=0, tiled=True),
    )
    block_len = math.gcd(seq_rows, 1024)
    block_count = seq_rows // block_len
    key_stack = keys_all.reshape(block_count, block_len, head_count, head_size)
    value_stack = values_all.reshape(block_count, block_len, head_count, head_size)
    pos_stack = key_pos.reshape(block_count, block_len)
    live_stack = key_live.reshape(block_count, block_len)

    def stats_step(running, key_part):
        key_block, pos_block, live_block = key_part
        scores, allowed = masked_scores(queries, key_block, positions, pos_block, live_block)
        peak_score = jnp.maximum(running[0], jnp.max(scores, axis=-1))
        exp_total = running[1] * jnp.exp(running[0] - peak_score) + jnp.sum(
            jnp.where(allowed[None], jnp.exp(scores - peak_score[..., None]), 0.0), axis=-1
        )
        return ((peak_score, exp_total), None)

    start_peak = jnp.full((head_count, tok_rows), -1e30, jnp.float32)
    final_state = lax.scan(
        stats_step, (start_peak, jnp.zeros_like(start_peak)), (key_stack, pos_stack, live_stack)
    )[0]
    log_total = final_state[0] + jnp.log(final_state[1])

    def value_step(running, key_part):
        key_block, value_block, pos_block, live_block = key_part
        scores = masked_scores(queries, key_block, positions, pos_block, live_block)[0]
        probability = jnp.exp(scores - log_total[..., None]).astype(jnp.bfloat16)
        return (
            running
            + jnp.einsum(
                "hqk,khd->qhd", probability, value_block, preferred_element_type=jnp.float32
            ),
            None,
        )

    zero_heads = jnp.zeros((tok_rows, head_count, head_size), jnp.float32)
    attended = lax.scan(value_step, zero_heads, (key_stack, value_stack, pos_stack, live_stack))[0]
    context_low = attended.reshape(tok_rows, model_width).astype(jnp.bfloat16)
    hidden = jnp.dot(mlp_in, up_weight, preferred_element_type=jnp.float32) + up_bias.astype(
        jnp.float32
    )
    activated, gelu_pull = jax.vjp(partial(jax.nn.gelu, approximate=False), hidden)
    act_low = activated.astype(jnp.bfloat16)
    branch = (
        jnp.dot(context_low, out_weight, preferred_element_type=jnp.float32)
        + out_bias.astype(jnp.float32)
        + jnp.dot(act_low, down_weight, preferred_element_type=jnp.float32)
        + down_bias.astype(jnp.float32)
    )
    output_rows = (live_rows[:, None] * (token_rows + branch)).astype(jnp.bfloat16)
    cot_rows = cotangent[0].astype(jnp.float32)
    grad_branch = (live_rows[:, None] * cot_rows).astype(jnp.bfloat16)
    grad_w_out = jnp.einsum(
        "tc,td->cd", context_low, grad_branch, preferred_element_type=jnp.float32
    )
    grad_w_down = jnp.einsum("tc,td->cd", act_low, grad_branch, preferred_element_type=jnp.float32)
    grad_branch_sum = jnp.sum(grad_branch.astype(jnp.float32), axis=0)
    grad_act = jnp.einsum("td,cd->tc", grad_branch, down_weight, preferred_element_type=jnp.float32)
    grad_hidden = gelu_pull(grad_act)[0].astype(jnp.bfloat16)
    grad_w_up = jnp.einsum("tc,td->cd", mlp_in, grad_hidden, preferred_element_type=jnp.float32)
    grad_b_up = jnp.sum(grad_hidden.astype(jnp.float32), axis=0)
    grad_mlp_in = jnp.einsum(
        "td,cd->tc", grad_hidden, up_weight, preferred_element_type=jnp.float32
    )
    grad_context = jnp.einsum(
        "td,cd->tc", grad_branch, out_weight, preferred_element_type=jnp.float32
    ).astype(jnp.bfloat16)
    grad_heads = grad_context.reshape(tok_rows, head_count, head_size)
    row_dots = jnp.sum(grad_heads.astype(jnp.float32) * attended, axis=-1).T

    def grad_step(running, key_part):
        key_block, value_block, pos_block, live_block = key_part
        prob_low, grad_score = score_grads(
            queries,
            key_block,
            value_block,
            grad_heads,
            positions,
            pos_block,
            live_block,
            log_total,
            row_dots,
        )
        query_sum = running + jnp.einsum(
            "hqk,khd->qhd", grad_score, key_block, preferred_element_type=jnp.float32
        )
        key_term = jnp.einsum(
            "hqk,qhd->khd", grad_score, queries, preferred_element_type=jnp.float32
        )
        value_term = jnp.einsum(
            "hqk,qhd->khd", prob_low, grad_heads, preferred_element_type=jnp.float32
        )
        return (query_sum, (key_term, value_term))

    query_grad, term_stacks = lax.scan(
        grad_step, zero_heads, (key_stack, value_stack, pos_stack, live_stack)
    )
    key_grad, value_grad = (
        lax.psum_scatter(
            term_stacks[0].reshape(seq_rows, model_width).astype(jnp.bfloat16),
            "ctx",
            scatter_dimension=0,
            tiled=True,
        ).astype(jnp.float32),
        lax.psum_scatter(
            term_stacks[1].reshape(seq_rows, model_width).astype(jnp.bfloat16),
            "ctx",
            scatter_dimension=0,
            tiled=True,
        ).astype(jnp.float32),
    )
    key_grad = key_grad.reshape(tok_rows, head_count, head_size)
    value_grad = value_grad.reshape(tok_rows, head_count, head_size)
    grad_projected = (
        jnp.stack(
            [
                rotate_backward(query_grad, cosine_table, sine_table),
                rotate_backward(key_grad, cosine_table, sine_table),
                value_grad,
            ],
            axis=1,
        )
        .reshape(tok_rows, 3 * model_width)
        .astype(jnp.bfloat16)
    )
    grad_w_qkv = jnp.einsum(
        "tc,td->cd", attn_in, grad_projected, preferred_element_type=jnp.float32
    )
    grad_b_qkv = jnp.sum(grad_projected.astype(jnp.float32), axis=0)
    grad_attn_in = jnp.einsum(
        "td,cd->tc", grad_projected, qkv_weight, preferred_element_type=jnp.float32
    )
    grad_input_first, grad_gain_first, grad_shift_first = norm_backward(
        grad_attn_in, normed_first, inverse_first, gain_first
    )
    grad_input_second, grad_gain_second, grad_shift_second = norm_backward(
        grad_mlp_in, normed_second, inverse_second, gain_second
    )
    grad_input = live_rows[:, None] * cot_rows + grad_input_first + grad_input_second
    shares = (
        lax.psum_scatter(
            grad_gain_first.astype(jnp.bfloat16), "wsh", scatter_dimension=0, tiled=True
        ).astype(jnp.float32),
        lax.psum_scatter(
            grad_shift_first.astype(jnp.bfloat16), "wsh", scatter_dimension=0, tiled=True
        ).astype(jnp.float32),
        lax.psum_scatter(
            grad_gain_second.astype(jnp.bfloat16), "wsh", scatter_dimension=0, tiled=True
        ).astype(jnp.float32),
        lax.psum_scatter(
            grad_shift_second.astype(jnp.bfloat16), "wsh", scatter_dimension=0, tiled=True
        ).astype(jnp.float32),
        lax.psum_scatter(
            grad_w_qkv.astype(jnp.bfloat16), "wsh", scatter_dimension=0, tiled=True
        ).astype(jnp.float32),
        lax.psum_scatter(
            grad_b_qkv.astype(jnp.bfloat16), "wsh", scatter_dimension=0, tiled=True
        ).astype(jnp.float32),
        lax.psum_scatter(
            grad_w_out.astype(jnp.bfloat16), "wsh", scatter_dimension=0, tiled=True
        ).astype(jnp.float32),
        lax.psum_scatter(
            grad_branch_sum.astype(jnp.bfloat16), "wsh", scatter_dimension=0, tiled=True
        ).astype(jnp.float32),
        lax.psum_scatter(
            grad_w_up.astype(jnp.bfloat16), "wsh", scatter_dimension=0, tiled=True
        ).astype(jnp.float32),
        lax.psum_scatter(
            grad_b_up.astype(jnp.bfloat16), "wsh", scatter_dimension=0, tiled=True
        ).astype(jnp.float32),
        lax.psum_scatter(
            grad_w_down.astype(jnp.bfloat16), "wsh", scatter_dimension=0, tiled=True
        ).astype(jnp.float32),
        lax.psum_scatter(
            grad_branch_sum.astype(jnp.bfloat16), "wsh", scatter_dimension=0, tiled=True
        ).astype(jnp.float32),
    )
    totals = (
        lax.psum(shares[0].astype(jnp.bfloat16), "ctx").astype(jnp.float32),
        lax.psum(shares[1].astype(jnp.bfloat16), "ctx").astype(jnp.float32),
        lax.psum(shares[2].astype(jnp.bfloat16), "ctx").astype(jnp.float32),
        lax.psum(shares[3].astype(jnp.bfloat16), "ctx").astype(jnp.float32),
        lax.psum(shares[4].astype(jnp.bfloat16), "ctx").astype(jnp.float32),
        lax.psum(shares[5].astype(jnp.bfloat16), "ctx").astype(jnp.float32),
        lax.psum(shares[6].astype(jnp.bfloat16), "ctx").astype(jnp.float32),
        lax.psum(shares[7].astype(jnp.bfloat16), "ctx").astype(jnp.float32),
        lax.psum(shares[8].astype(jnp.bfloat16), "ctx").astype(jnp.float32),
        lax.psum(shares[9].astype(jnp.bfloat16), "ctx").astype(jnp.float32),
        lax.psum(shares[10].astype(jnp.bfloat16), "ctx").astype(jnp.float32),
        lax.psum(shares[11].astype(jnp.bfloat16), "ctx").astype(jnp.float32),
    )
    return (
        output_rows[None],
        grad_input[None],
        totals[0],
        totals[1],
        totals[2],
        totals[3],
        totals[4],
        totals[5],
        totals[6],
        totals[7],
        totals[8],
        totals[9],
        totals[10],
        totals[11],
    )


HB = 128
NEG=-1e30
f32=jnp.float32; bf16=jnp.bfloat16

def _nn(a,b): return lax.dot_general(a,b,(((1,),(0,)),((),())),preferred_element_type=f32)
def _nt(a,b): return lax.dot_general(a,b,(((1,),(1,)),((),())),preferred_element_type=f32)

def attn_fwd_kernel(bm, x_ref, o_ref, lse_ref, q_s, kt_s, v_s, *, nblk, per, bq, bk):
    def perm(i,_):
        p=bm[i]; c=i//per; l=pl.multiple_of((i%per)*HB,HB); d=pl.multiple_of(p*HB,HB)
        q_s[:,pl.ds(d,HB)]=x_ref[c,0:64,pl.ds(l,HB)]*bf16(0.125)
        kt_s[pl.ds(d,HB),:]=x_ref[c,64:128,pl.ds(l,HB)].astype(f32).T.astype(bf16)
        v_s[:,pl.ds(d,HB)]=x_ref[c,128:192,pl.ds(l,HB)]
        return 0
    lax.fori_loop(0,nblk,perm,0)
    S=nblk*HB; nq=S//bq; r=bq//bk
    def step(q,qo,ko,carry,mask):
        m,l,acc=carry
        s=_nn(kt_s[pl.ds(ko,bk),:],q)
        if mask is not None: s=jnp.where(mask,s,NEG)
        mn=jnp.maximum(m,jnp.max(s,axis=0,keepdims=True))
        a=jnp.exp(m-mn); p=jnp.exp(s-mn)
        l=l*a+jnp.sum(p,axis=0,keepdims=True)
        acc=acc*a+_nn(v_s[:,pl.ds(ko,bk)],p.astype(bf16))
        return mn,l,acc
    ki=lax.broadcasted_iota(jnp.int32,(bk,bq),0); qi_=lax.broadcasted_iota(jnp.int32,(bk,bq),1)
    def qloop(i,_):
        qo=pl.multiple_of(i*bq,bq)
        q=q_s[:,pl.ds(qo,bq)]
        c=(jnp.full((1,bq),NEG,f32),jnp.zeros((1,bq),f32),jnp.zeros((64,bq),f32))
        c=lax.fori_loop(0,i*r,lambda j,c: step(q,qo,pl.multiple_of(j*bk,bk),c,None),c)
        for t in range(r):
            c=step(q,qo,pl.multiple_of(qo+t*bk,bk),c,ki+t*bk<=qi_)
        m,l,acc=c
        q_s[:,pl.ds(qo,bq)]=(acc*(1.0/l)).astype(bf16)
        lse_ref[:,pl.ds(qo,bq)]=m+jnp.log(l)
        return 0
    lax.fori_loop(0,nq,qloop,0)
    def unperm(i,_):
        p=bm[i]; c=i//per; l=pl.multiple_of((i%per)*HB,HB); d=pl.multiple_of(p*HB,HB)
        o_ref[c,:,pl.ds(l,HB)]=q_s[:,pl.ds(d,HB)]
        return 0
    lax.fori_loop(0,nblk,unperm,0)

def attn_fwd(bm,x,*,bq=512,bk=512):
    n=x.shape[0]; S=n*x.shape[2]; nblk=S//HB
    bq=math.gcd(S,bq); bk=math.gcd(bq,bk)
    return pl.pallas_call(
        lambda *a: attn_fwd_kernel(*a,nblk=nblk,per=x.shape[2]//HB,bq=bq,bk=bk),
        out_shape=(jax.ShapeDtypeStruct((n,64,x.shape[2]),bf16),jax.ShapeDtypeStruct((1,S),f32)),
        in_specs=[pl.BlockSpec(memory_space=pltpu.SMEM),pl.BlockSpec(memory_space=pltpu.VMEM)],
        out_specs=(pl.BlockSpec(memory_space=pltpu.VMEM),pl.BlockSpec(memory_space=pltpu.VMEM)),
        scratch_shapes=[pltpu.VMEM((64,S),bf16),pltpu.VMEM((S,64),bf16),pltpu.VMEM((64,S),bf16)],
        compiler_params=pltpu.CompilerParams(vmem_limit_bytes=56<<20),name="attn_fwd")(bm,x)

def attn_bwd_kernel(bm, x_ref, o_ref, do_ref, lse_ref, cs_ref, g_ref, q_s, kt_s, k_s, vt_s, do_s, dl_s, dq_s, dk_s, dv_s, *, nblk, per, bq, bk):
    def perm(i,_):
        p=bm[i]; c=i//per; l=pl.multiple_of((i%per)*HB,HB); d=pl.multiple_of(p*HB,HB)
        q_s[:,pl.ds(d,HB)]=x_ref[c,0:64,pl.ds(l,HB)]*bf16(0.125)
        k=x_ref[c,64:128,pl.ds(l,HB)]
        k_s[:,pl.ds(d,HB)]=k*bf16(0.125)
        kt_s[pl.ds(d,HB),:]=k.astype(f32).T.astype(bf16)
        vt_s[pl.ds(d,HB),:]=x_ref[c,128:192,pl.ds(l,HB)].astype(f32).T.astype(bf16)
        do=do_ref[c,:,pl.ds(l,HB)]
        do_s[:,pl.ds(d,HB)]=do
        dl_s[:,pl.ds(d,HB)]=jnp.sum(do.astype(f32)*o_ref[c,:,pl.ds(l,HB)].astype(f32),axis=0,keepdims=True)
        return 0
    lax.fori_loop(0,nblk,perm,0)
    S=nblk*HB; nq=S//bq; r=bq//bk
    dk_s[...]=jnp.zeros_like(dk_s); dv_s[...]=jnp.zeros_like(dv_s)
    def step(q,do,lse,dl,ko,dq,mask):
        s=_nn(kt_s[pl.ds(ko,bk),:],q)
        p=jnp.exp(s-lse)
        if mask is not None: p=jnp.where(mask,p,0.0)
        dp=_nn(vt_s[pl.ds(ko,bk),:],do)
        ds=(p*(dp-dl)).astype(bf16)
        pb=p.astype(bf16)
        dv_s[:,pl.ds(ko,bk)]+=_nt(do,pb)
        dk_s[:,pl.ds(ko,bk)]+=_nt(q,ds)
        return dq+_nn(k_s[:,pl.ds(ko,bk)],ds)
    ki=lax.broadcasted_iota(jnp.int32,(bk,bq),0); qi_=lax.broadcasted_iota(jnp.int32,(bk,bq),1)
    def qloop(i,_):
        qo=pl.multiple_of(i*bq,bq)
        q=q_s[:,pl.ds(qo,bq)]; do=do_s[:,pl.ds(qo,bq)]; lse=lse_ref[:,pl.ds(qo,bq)]; dl=dl_s[:,pl.ds(qo,bq)]
        dq=jnp.zeros((64,bq),f32)
        dq=lax.fori_loop(0,i*r,lambda j,c: step(q,do,lse,dl,pl.multiple_of(j*bk,bk),c,None),dq)
        for t in range(r):
            dq=step(q,do,lse,dl,pl.multiple_of(qo+t*bk,bk),dq,ki+t*bk<=qi_)
        dq_s[:,pl.ds(qo,bq)]=dq
        return 0
    lax.fori_loop(0,nq,qloop,0)
    def unperm(i,_):
        p=bm[i]; c=i//per; l=pl.multiple_of((i%per)*HB,HB); d=pl.multiple_of(p*HB,HB)
        cos=cs_ref[0:8,pl.ds(d,HB)]; sin=cs_ref[8:16,pl.ds(d,HB)]
        for n_,src in ((0,dq_s),(1,dk_s)):
            g=src[:,pl.ds(d,HB)]
            a=g[0:8]; b=g[8:16]
            full=jnp.concatenate([a*cos+b*sin,b*cos-a*sin,g[16:64]],axis=0)
            g_ref[c,64*n_:64*n_+64,pl.ds(l,HB)]=full.astype(bf16)
        g_ref[c,128:192,pl.ds(l,HB)]=dv_s[:,pl.ds(d,HB)].astype(bf16)
        return 0
    lax.fori_loop(0,nblk,unperm,0)

def attn_bwd(bm,x,o,do,lse,cs,*,bq=512,bk=512):
    n=x.shape[0]; S=n*x.shape[2]; nblk=S//HB
    bq=math.gcd(S,bq); bk=math.gcd(bq,bk)
    vm=pl.BlockSpec(memory_space=pltpu.VMEM)
    return pl.pallas_call(
        lambda *a: attn_bwd_kernel(*a,nblk=nblk,per=x.shape[2]//HB,bq=bq,bk=bk),
        out_shape=jax.ShapeDtypeStruct((n,192,x.shape[2]),bf16),
        in_specs=[pl.BlockSpec(memory_space=pltpu.SMEM)]+[vm]*5,
        out_specs=vm,
        scratch_shapes=[pltpu.VMEM((64,S),bf16),pltpu.VMEM((S,64),bf16),pltpu.VMEM((64,S),bf16),pltpu.VMEM((S,64),bf16),pltpu.VMEM((64,S),bf16),
                        pltpu.VMEM((1,S),f32),pltpu.VMEM((64,S),f32),pltpu.VMEM((64,S),f32),pltpu.VMEM((64,S),f32)],
        compiler_params=pltpu.CompilerParams(vmem_limit_bytes=56<<20),name="attn_bwd")(bm,x,o,do,lse,cs)


SWAP = [(0, 1), (1, 0)]


def fast_fits(mesh):
    return mesh.shape["wsh"] == 2 and mesh.shape["ctx"] == H


def _params(mb=56):
    return pltpu.CompilerParams(vmem_limit_bytes=mb << 20)


def _norm(x):
    xf = x.astype(f32)
    cen = xf - jnp.mean(xf, axis=-1, keepdims=True)
    inv = lax.rsqrt(jnp.mean(cen * cen, axis=-1, keepdims=True) + epsilon)
    return cen * inv, inv


def _full(v):
    return pl.BlockSpec(v.shape, lambda *a: (0,) * v.ndim)


def _wq_specs(half, width, cols, quarter, at):
    own = lambda p: pl.BlockSpec(
        (half, cols),
        lambda *a: (0, p * (width // cols) + a[-1][0] * (half // cols) + a[-1][1] * (quarter // cols) + at(*a)),
    )
    got = lambda p: pl.BlockSpec((half, cols), lambda *a: (0, p * (quarter // cols) + at(*a)))
    return [own(p) for p in range(3)] + [got(p) for p in range(3)]


def norm_kernel(ids, a_ref, b_ref, n_ref, *refs):
    x_ref, ain_ref, min_ref = refs[-3:]
    mine = pl.program_id(0) == ids[1]
    x = jnp.where(mine, a_ref[...].astype(f32), b_ref[...].astype(f32))
    x_ref[...] = x.astype(bf16)
    xhat, _ = _norm(x)
    ain_ref[...] = (xhat * n_ref[0:1, :] + n_ref[1:2, :]).astype(bf16)
    min_ref[...] = (xhat * n_ref[2:3, :] + n_ref[3:4, :]).astype(bf16)


def norm_rows(ids, a, b, norms, before=()):
    rows, width = a.shape
    slot = 2 if before else 0
    out = jax.ShapeDtypeStruct((4 * rows, width), bf16)
    return pl.pallas_call(
        norm_kernel,
        grid_spec=pltpu.PrefetchScalarGridSpec(
            num_scalar_prefetch=1,
            grid=(2,),
            in_specs=[_full(a), _full(b), _full(norms)] + [pl.BlockSpec(memory_space=pl.ANY)] * len(before),
            out_specs=(pl.BlockSpec((rows, width), lambda i, ids: (slot + i, 0)),) * 3,
        ),
        out_shape=(out,) * 3,
        input_output_aliases={4 + k: k for k in range(len(before))},
        compiler_params=_params(),
        cost_estimate=pl.CostEstimate(flops=0, transcendentals=0, bytes_accessed=1 << 20),
        name="norm_rows",
    )(ids, a, b, norms, *before)


def mask_kernel(ids, a_ref, b_ref, c_ref, d_ref, live_ref, o_ref):
    i = pl.program_id(0)
    mine = (i % 2) == ids[1]
    for slot, (own, sib) in enumerate(((a_ref, b_ref), (c_ref, d_ref))):
        @pl.when((i // 2) == slot)
        def _(own=own, sib=sib):
            v = jnp.where(mine, own[...].astype(f32), sib[...].astype(f32))
            o_ref[...] = (live_ref[...] * v).astype(bf16)


def mask_rows(ids, own, own_sib, got, got_sib, live):
    rows, width = own.shape
    return pl.pallas_call(
        mask_kernel,
        grid_spec=pltpu.PrefetchScalarGridSpec(
            num_scalar_prefetch=1,
            grid=(4,),
            in_specs=[_full(v) for v in (own, own_sib, got, got_sib)] + [pl.BlockSpec((rows, 1), lambda i, ids: (i, 0))],
            out_specs=pl.BlockSpec((rows, width), lambda i, ids: (i, 0)),
        ),
        out_shape=jax.ShapeDtypeStruct((4 * rows, width), bf16),
        compiler_params=_params(),
        cost_estimate=pl.CostEstimate(flops=0, transcendentals=0, bytes_accessed=1 << 20),
        name="mask_rows",
    )(ids, own, own_sib, got, got_sib, live)


def qkv_kernel(
    ids, ain_ref, wq_ref, wk_ref, wv_ref, gq_ref, gk_ref, gv_ref, bq_ref, bk_ref, bv_ref, cs_ref, send_ref
):
    width = ain_ref.shape[1]
    half = width // 2
    me = ids[0]
    a_own = ain_ref[:, pl.ds(pl.multiple_of(me * half, half), half)]
    a_got = ain_ref[:, pl.ds(pl.multiple_of((1 - me) * half, half), half)]
    cos = cs_ref[0:8, :]
    sin = cs_ref[8:16, :]
    for n, (w, g, b) in enumerate(((wq_ref, gq_ref, bq_ref), (wk_ref, gk_ref, bk_ref), (wv_ref, gv_ref, bv_ref))):
        t = _nn(a_own, w[...]) + _nn(a_got, g[...]) + b[...]
        t = t.T
        for k in range(send_ref.shape[1]):
            v = t[k * HD : (k + 1) * HD]
            if n < 2:
                lead = v[0:8]
                trail = v[8:16]
                v = jnp.concatenate([lead * cos - trail * sin, trail * cos + lead * sin, v[16:]], axis=0)
            send_ref[0, k, n * HD : (n + 1) * HD, :] = v.astype(bf16)


def qkv_forward(ids, attn_in, w_own, w_got, bias, cs, cols=256):
    rows, width = attn_in.shape[0] // 2, attn_in.shape[1]
    half = width // 2
    quarter = w_got.shape[1] // 3
    bsp = lambda p: pl.BlockSpec((1, cols), lambda s, i, ids: (0, p * (quarter // cols) + i))
    return pl.pallas_call(
        qkv_kernel,
        grid_spec=pltpu.PrefetchScalarGridSpec(
            num_scalar_prefetch=1,
            grid=(2, quarter // cols),
            in_specs=[pl.BlockSpec((rows, width), lambda s, i, ids: (s, 0))]
            + _wq_specs(half, width, cols, quarter, lambda s, i, ids: i)
            + [bsp(p) for p in range(3)]
            + [_full(cs)],
            out_specs=pl.BlockSpec((1, cols // HD, 3 * HD, rows), lambda s, i, ids: (s, i, 0, 0)),
        ),
        out_shape=jax.ShapeDtypeStruct((2, quarter // HD, 3 * HD, rows), bf16),
        compiler_params=_params(),
        cost_estimate=pl.CostEstimate(flops=1 << 20, transcendentals=0, bytes_accessed=1 << 20),
        name="qkv_forward",
    )(ids, attn_in, w_own, w_own, w_own, w_got, w_got, w_got, bias, bias, bias, cs)


MLP_CHUNKS = 2


def mlp_kernel(ids, x_ref, xt_ref, dy_ref, wo_ref, wg_ref, wd_ref, bu_ref, y_ref, dx_ref, uk_ref, us_ref, dk_ref, ds_ref, gb_ref,
    g_s, act_s, du_s, y_s, dx_s
):
    rows, width = x_ref.shape
    half = width // 2
    me = ids[0]
    spans = (
        (pl.multiple_of(me * half, half), wo_ref[...]),
        (pl.multiple_of((1 - me) * half, half), wg_ref[...]),
    )

    @pl.when(pl.program_id(0) == 0)
    def _():
        y_s[...] = jnp.zeros_like(y_s)
        dx_s[...] = jnp.zeros_like(dx_s)

    wd = wd_ref[...]
    bias = bu_ref[...]
    step = rows // MLP_CHUNKS
    for c in range(MLP_CHUNKS):
        at = slice(c * step, (c + 1) * step)
        u = bias + sum(_nn(x_ref[at, pl.ds(o, half)], w) for o, w in spans)
        cdf = 0.5 * (1.0 + lax.erf(u * (1.0 / math.sqrt(2.0))))
        pdf = jnp.exp(-0.5 * u * u) * (1.0 / math.sqrt(2.0 * math.pi))
        act = (u * cdf).astype(bf16)
        du = (_nt(dy_ref[at, :], wd) * (cdf + u * pdf)).astype(bf16)
        y_s[at, :] += _nn(act, wd)
        for o, w in spans:
            dx_s[at, pl.ds(o, half)] += _nt(du, w)
        act_s[at, :] = act
        du_s[at, :] = du
    du = du_s[...]
    gd = lax.dot_general(
        act_s[...], dy_ref[...], (((0,), (0,)), ((), ())), preferred_element_type=f32
    ).astype(bf16)
    k, r, _ = dk_ref.shape
    k = gd.shape[0] // r
    early = pl.program_id(0) < pl.num_programs(0) // 2
    for c in range(k):
        v = gd[c * r : (c + 1) * r, :]

        @pl.when(early)
        def _(v=v, c=c):
            ds_ref[c] = v

        @pl.when(jnp.logical_not(early))
        def _(v=v, c=c):
            dk_ref[c] = v

    g_s[...] = _nn(xt_ref[...], du).astype(bf16)
    n = uk_ref.shape[0]
    r = uk_ref.shape[1] // 2
    for ref, side in ((uk_ref, ids[3]), (us_ref, 1 - ids[3])):
        for h in range(2):
            for c in range(n):
                at = pl.multiple_of(h * half + (side * n + c) * r, r)
                ref[c, h * r : (h + 1) * r, :] = g_s[pl.ds(at, r), :]
    gb_ref[...] = jnp.sum(du.astype(f32), axis=0, keepdims=True)

    @pl.when(pl.program_id(0) == pl.num_programs(0) - 1)
    def _():
        y_ref[...] = y_s[...].astype(bf16)
        dx_ref[...] = dx_s[...].astype(bf16)


def mlp(ids, x, xt, dy, w_own, w_got, wd, bu, n, tile=512):
    rows, width = x.shape
    half = width // 2
    hidden = w_got.shape[1]
    steps = hidden // tile
    mid = steps // 2
    whole = pl.BlockSpec((rows, width), lambda i, ids: (0, 0))
    per = hidden // n
    order = lambda i, ids: i % mid + mid * jnp.where(i < mid, 1 - ids[2], ids[2])
    part = lambda i, ids: ids[1] * steps + order(i, ids)
    up_spec = pl.BlockSpec((n // 2, width // n, tile), lambda i, ids: (0, 0, order(i, ids)))
    down_spec = lambda f: pl.BlockSpec((tile // per, per, width), lambda i, ids: (f(i), 0, 0))
    up_shape = jax.ShapeDtypeStruct((n // 2, width // n, hidden), bf16)
    down_shape = jax.ShapeDtypeStruct((n // 2, per, width), bf16)
    return pl.pallas_call(
        mlp_kernel,
        grid_spec=pltpu.PrefetchScalarGridSpec(
            num_scalar_prefetch=1,
            grid=(steps,),
            in_specs=[
                whole,
                pl.BlockSpec((width, rows), lambda i, ids: (0, 0)),
                whole,
                pl.BlockSpec((half, tile), lambda i, ids: (0, ids[0] * 2 * steps + part(i, ids))),
                pl.BlockSpec((half, tile), lambda i, ids: (0, order(i, ids))),
                pl.BlockSpec((tile, width), lambda i, ids: (part(i, ids), 0)),
                pl.BlockSpec((1, tile), lambda i, ids: (0, part(i, ids))),
            ],
            out_specs=(
                whole,
                whole,
                up_spec,
                up_spec,
                down_spec(lambda i: jnp.maximum(i - mid, 0)),
                down_spec(lambda i: jnp.minimum(i, mid - 1)),
                pl.BlockSpec((1, tile), lambda i, ids: (0, order(i, ids))),
            ),
            scratch_shapes=[pltpu.VMEM((width, tile), bf16), pltpu.VMEM((rows, tile), bf16), pltpu.VMEM((rows, tile), bf16)]
            + [pltpu.VMEM((rows, width), f32)] * 2,
        ),
        out_shape=(
            jax.ShapeDtypeStruct((rows, width), bf16),
            jax.ShapeDtypeStruct((rows, width), bf16),
            up_shape,
            up_shape,
            down_shape,
            down_shape,
            jax.ShapeDtypeStruct((1, hidden), f32),
        ),
        compiler_params=_params(),
        cost_estimate=pl.CostEstimate(
            flops=12 * rows * width * hidden, transcendentals=2 * rows * hidden, bytes_accessed=24 << 20
        ),
        name="mlp",
    )(ids, x, xt, dy, w_own, w_got, wd, bu)


def qkv_back_kernel(
    ids, d_ref, at_ref, x_ref, n_ref, wq_ref, wk_ref, wv_ref, gq_ref, gk_ref, gv_ref, dm_ref, ob_ref, dy_ref, gb_ref,
    a_ref, b_ref, e_ref, g_s, go_s, bias_s, sum_s
):
    rows, width = x_ref.shape
    half = width // 2
    me = ids[0]
    core = ids[1]
    s = pl.program_id(0)
    outs = (a_ref, b_ref)
    n = a_ref.shape[0]
    nh = d_ref.shape[1]
    cols = nh * HD
    r = half // (2 * n)

    @pl.when(s == 0)
    def _():
        g_s[...] = jnp.zeros_like(g_s)
        go_s[...] = jnp.zeros_like(go_s)
        bias_s[...] = jnp.zeros_like(bias_s)
        sum_s[...] = jnp.zeros_like(sum_s)

    ones = jnp.ones((8, rows), bf16)
    at = at_ref[...]
    dts = []
    for p in range(3):
        dp = jnp.concatenate([d_ref[0, k, p * HD : (p + 1) * HD, :] for k in range(nh)], axis=0)
        g_s[p] += _nt(at, dp)
        bias_s[p * 8 : (p + 1) * 8, :] += _nt(ones, dp)
        dts.append(dp.astype(f32).T.astype(bf16))
    go_s[...] += _nn(ob_ref[0], dy_ref[...])
    dt = jnp.concatenate(dts, axis=1)
    w_own = jnp.concatenate([wq_ref[...], wk_ref[...], wv_ref[...]], axis=1)
    w_got = jnp.concatenate([gq_ref[...], gk_ref[...], gv_ref[...]], axis=1)
    d_own = _nt(dt, w_own)
    d_got = _nt(dt, w_got)
    first = me == 0
    xhat, _ = _norm(x_ref[...])
    for h in range(2):
        lanes = slice(h * half, (h + 1) * half)
        da = jnp.where(first, d_own, d_got) if h == 0 else jnp.where(first, d_got, d_own)
        dm = dm_ref[:, lanes].astype(f32)
        xh = xhat[:, lanes]
        e_ref[0, :, lanes] = da * n_ref[0:1, lanes] + dm * n_ref[2:3, lanes]
        for k, v in enumerate((da * xh, da, dm * xh, dm)):
            sum_s[k : k + 1, lanes] += jnp.sum(v, axis=0, keepdims=True)

    @pl.when(s == 0)
    def _():
        mine = dy_ref[pl.ds(pl.multiple_of(core * (rows // 2), rows // 2), rows // 2), :]
        sum_s[4:5, :] = jnp.sum(mine.astype(f32), axis=0, keepdims=True)

    @pl.when(s == pl.num_programs(0) - 1)
    def _():
        for p in range(3):
            g = g_s[p].astype(bf16)
            for h in range(2):
                for c in range(n):
                    for a in range(2):
                        row = h * half + (c * 2 + a) * r
                        u = (h * 3 + p) * r
                        outs[a][c, u : u + r, :] = g[row : row + r, :]
        go = go_s[...].astype(bf16)
        q = cols // (2 * n)
        for c in range(n):
            for a in range(2):
                row = (c * 2 + a) * q
                for k in range(width // cols):
                    u = 6 * r + k * q
                    outs[a][c, u : u + q, :] = go[row : row + q, k * cols : (k + 1) * cols]
        flat = [sum_s[k : k + 1, t * cols : (t + 1) * cols] for k in range(5) for t in range(width // cols)]
        zero = jnp.zeros((1, cols), f32)
        for p in range(3):
            flat += [
                jnp.where((me == k) & (core == j), bias_s[p * 8 : p * 8 + 1, :], zero) for k in range(2) for j in range(2)
            ]
        flat += [
            jnp.where((me == k) & (core == j), gb_ref[:, t * cols : (t + 1) * cols], zero)
            for k in range(2)
            for j in range(2)
            for t in range(gb_ref.shape[1] // cols)
        ]
        top = 6 * r + (width // cols) * q
        per = len(flat) // n
        pad = [zero] * (8 - per)
        for c in range(n):
            b_ref[c, top : top + 8, :] = jnp.concatenate(flat[c * per : (c + 1) * per] + pad, axis=0).astype(bf16)


def qkv_backward(ids, d, at, x2, norms, w_own, w_got, d_mlp, ob, dy, gb_up, n):
    rows, width = x2.shape[0] // 2, x2.shape[1]
    half = width // 2
    cols = w_got.shape[1] // 3
    size = 6 * (half // (2 * n)) + width // (2 * n)
    row = lambda: pl.BlockSpec((rows, width), lambda s, ids: (s, 0))
    out = [
        jax.ShapeDtypeStruct((n, size, cols), bf16),
        jax.ShapeDtypeStruct((n, size + 8, cols), bf16),
    ]
    return pl.pallas_call(
        qkv_back_kernel,
        grid_spec=pltpu.PrefetchScalarGridSpec(
            num_scalar_prefetch=1,
            grid=(2,),
            in_specs=[
                pl.BlockSpec((1, cols // HD, 3 * HD, rows), lambda s, ids: (s, 0, 0, 0)),
                pl.BlockSpec((width, rows), lambda s, ids: (0, s)),
                row(),
                _full(norms),
            ]
            + _wq_specs(half, width, cols, cols, lambda s, ids: 0)
            + [row(), pl.BlockSpec((1, cols, rows), lambda s, ids: (s, 0, 0)), row(), _full(gb_up)],
            out_specs=(*[_full(v) for v in out], pl.BlockSpec((1, rows, width), lambda s, ids: (s, 0, 0))),
            scratch_shapes=[
                pltpu.VMEM((3, width, cols), f32),
                pltpu.VMEM((cols, width), f32),
                pltpu.VMEM((24, cols), f32),
                pltpu.VMEM((8, width), f32),
            ],
        ),
        out_shape=(*out, jax.ShapeDtypeStruct((2, rows, width), f32)),
        compiler_params=_params(),
        name="qkv_backward",
    )(ids, d, at, x2, norms, w_own, w_own, w_own, w_got, w_got, w_got, d_mlp, ob, dy, gb_up)


def _mine(ids):
    return (pl.program_id(0) // 2) == ids[1]


def _own_block(i, ids):
    return jnp.clip(i - 2 * ids[1], 0, 1)


def _got_block(i, ids):
    return jnp.clip(i - 2 * (1 - ids[1]), 0, 1)


def join_kernel(ids, own_ref, got_ref, o_ref):
    mine = _mine(ids)
    shape = o_ref.shape

    @pl.when(mine)
    def _():
        o_ref[...] = own_ref[...].astype(f32).reshape(shape)

    @pl.when(jnp.logical_not(mine))
    def _():
        o_ref[...] = got_ref[...].astype(f32).reshape(shape)


def join_rows(ids, own, got):
    n, r, w = own.shape
    src = lambda f: pl.BlockSpec((n // 2, r, w), lambda i, ids: (f(i, ids), 0, 0))
    return pl.pallas_call(
        join_kernel,
        grid_spec=pltpu.PrefetchScalarGridSpec(
            num_scalar_prefetch=1,
            grid=(4,),
            in_specs=[src(_own_block), src(_got_block)],
            out_specs=pl.BlockSpec((n * r // 2, w), lambda i, ids: (i, 0)),
        ),
        out_shape=jax.ShapeDtypeStruct((2 * n * r, w), f32),
        compiler_params=_params(),
        name="join_rows",
    )(ids, own, got)


def join_cols(ids, own, got):
    n, _, r, w = own.shape
    src = lambda f: pl.BlockSpec((n, 1, r, w), lambda i, ids: (0, f(i, ids), 0, 0))
    return pl.pallas_call(
        join_kernel,
        grid_spec=pltpu.PrefetchScalarGridSpec(
            num_scalar_prefetch=1,
            grid=(4,),
            in_specs=[src(_own_block), src(_got_block)],
            out_specs=pl.BlockSpec((n * r, w), lambda i, ids: (0, (i % 2) * 2 + i // 2)),
        ),
        out_shape=jax.ShapeDtypeStruct((n * r, 4 * w), f32),
        compiler_params=_params(),
        name="join_cols",
    )(ids, own, got)


def unpack_kernel(ids, ao_ref, ag_ref, bo_ref, bg_ref, q_ref, o_ref, s_ref):
    first = ids[1] == 0
    k, _, cols = ao_ref.shape
    r = q_ref.shape[0] // (2 * k)
    q = o_ref.shape[1] // (2 * k)
    for a, (own, got) in enumerate(((ao_ref, ag_ref), (bo_ref, bg_ref))):
        for c in range(k):
            x = own[c].astype(f32)
            y = got[c].astype(f32)
            to = slice((c * 2 + a) * r, (c * 2 + a + 1) * r)
            tq = slice((c * 2 + a) * q, (c * 2 + a + 1) * q)
            for j in range(2):
                v = jnp.where(first, x, y) if j == 0 else jnp.where(first, y, x)
                for w in range(2):
                    for p in range(3):
                        u = (w * 3 + p) * r
                        at = ((p * 2 + w) * 2 + j) * cols
                        q_ref[to, at : at + cols] = v[u : u + r, :]
                for t in range(o_ref.shape[2] // cols):
                    u = 6 * r + t * q
                    o_ref[j, tq, t * cols : (t + 1) * cols] = v[u : u + q, :]
            if a == 1:
                s_ref[c] = (x + y)[-8:, :]


def unpack(ids, a_own, a_got, b_own, b_got, width, steps=4):
    n, _, cols = a_own.shape
    half = width // 2
    k = n // steps
    spec = lambda v: pl.BlockSpec((k,) + v.shape[1:], lambda i, ids: (i, 0, 0))
    return pl.pallas_call(
        unpack_kernel,
        grid_spec=pltpu.PrefetchScalarGridSpec(
            num_scalar_prefetch=1,
            grid=(steps,),
            in_specs=[spec(v) for v in (a_own, a_got, b_own, b_got)],
            out_specs=(
                pl.BlockSpec((half // steps, 3 * width), lambda i, ids: (i, 0)),
                pl.BlockSpec((2, cols // steps, width), lambda i, ids: (0, i, 0)),
                pl.BlockSpec((k, 8, cols), lambda i, ids: (i, 0, 0)),
            ),
        ),
        out_shape=(
            jax.ShapeDtypeStruct((half, 3 * width), f32),
            jax.ShapeDtypeStruct((2, cols, width), f32),
            jax.ShapeDtypeStruct((n, 8, cols), f32),
        ),
        compiler_params=_params(),
        name="unpack",
    )(ids, a_own, a_got, b_own, b_got)


def last_kernel(eo_ref, er_ref, x_ref, c_ref, live_ref, o_ref):
    xhat, inv = _norm(x_ref[...])
    e = eo_ref[...] + er_ref[...].astype(f32)
    dx = inv * (
        e - jnp.mean(e, axis=-1, keepdims=True) - xhat * jnp.mean(e * xhat, axis=-1, keepdims=True)
    )
    o_ref[...] = live_ref[...] * c_ref[...].astype(f32) + dx


def last(e_own, e_got, x, cot, live):
    return pl.pallas_call(
        last_kernel,
        out_shape=jax.ShapeDtypeStruct(x.shape, f32),
        compiler_params=_params(),
        name="token_grad",
    )(e_own, e_got, x, cot, live)


def fast_shards(
    tokens,
    ln1_gain,
    ln1_bias,
    ln2_gain,
    ln2_bias,
    w_qkv,
    b_qkv,
    w_out,
    b_out,
    w_up,
    b_up,
    w_down,
    b_down,
    lengths,
    block_map,
    cotangent,
):
    ctx = lax.axis_index("ctx")
    me = lax.axis_index("wsh")
    core = ctx % 2
    n_ctx = lax.axis_size("ctx")
    chips = n_ctx // 2
    own_rows, width = tokens.shape[1:]
    rows = 2 * own_rows
    half = width // 2
    quarter = half // 2
    seq = own_rows * n_ctx
    heads = H // 4
    hid = w_up.shape[1] // 4
    CORE, X, ZN, ZF = 0, 1, 2, 3

    def swap(v):
        return lax.ppermute(v, "wsh", SWAP)

    def flip(v, bit):
        return lax.ppermute(v, "ctx", [(i, i ^ (1 << bit)) for i in range(n_ctx)])

    def bit_of(bit):
        return (ctx >> bit) & 1

    ids = jnp.stack([me, core, bit_of(X), bit_of(ZN)]).astype(jnp.int32)

    def add(*terms):
        return sum(v.astype(f32) for v in terms).astype(bf16) if len(terms) > 1 else terms[0]

    def halve(terms, bit):
        b = bit_of(bit)
        cut = [v.reshape((2, v.shape[0] // 2) + v.shape[1:]) for v in terms]
        part = lambda k: [lax.dynamic_index_in_dim(v, k, 0, keepdims=False) for v in cut]
        return part(b) + [flip(add(*part(1 - b)), bit)]

    def ordered(first, a, b, axis=0):
        return jnp.where(first == 0, jnp.concatenate([a, b], axis), jnp.concatenate([b, a], axis))

    def double(v, bit):
        return ordered(bit_of(bit), v, flip(v, bit))

    def exchange(v):
        groups = [[2 * i + c for i in range(chips)] for c in range(2)]
        return lax.all_to_all(v, "ctx", 0, 0, axis_index_groups=groups, tiled=False)

    def rows_of(v, at, n, axis=0):
        return lax.dynamic_slice_in_dim(v, at, n, axis)

    x_own = tokens[0]
    x_got = swap(x_own)
    x_sib = flip(x_own, CORE)
    mine = me * half + core * quarter
    other = (1 - me) * half + core * quarter
    wq_send = jnp.concatenate([rows_of(w_qkv, p * width + other, quarter, 1) for p in range(3)], axis=1)
    wq_send, ln1_gain = lax.optimization_barrier((wq_send, ln1_gain))
    len_parts = jnp.stack([lengths[0] // 64, lengths[0] % 64]).astype(bf16)
    parts = [ln1_gain, ln1_bias, ln2_gain, ln2_bias, b_out, b_down, b_qkv, jnp.pad(len_parts, (0, half - 2))]
    small = jnp.concatenate([v.reshape(-1, half) for v in parts])
    small = ordered(me, small[None], swap(small)[None])
    wq_got = swap(wq_send)
    vec = lambda i: small[:, i].reshape(width).astype(f32)
    norms = jnp.stack([vec(i) for i in range(4)])
    bias_out = vec(4) + vec(5)
    qkv_bias = small[:, 6:9].astype(f32).reshape(3, width)
    qkv_bias = rows_of(qkv_bias, mine, quarter, 1).reshape(1, 3 * quarter)
    lens = small[:, 9, :2].astype(jnp.int32)
    lens = lens[:, 0] * 64 + lens[:, 1]
    other_len = lens[1 - me]

    normed = norm_rows(ids, x_own, x_sib, norms)
    cot_own = cotangent[0]
    wu_send = rows_of(w_up, ((1 - me) * 2 + core) * hid, hid, 1)
    wq_got, cot_send, normed = lax.optimization_barrier((wq_got, cot_own, normed))
    cot_got = swap(cot_send)
    cot_got, wu_send = lax.optimization_barrier((cot_got, wu_send))
    wu_got = swap(wu_send)
    normed = norm_rows(ids, x_got, flip(x_got, CORE), norms, normed)
    x2, attn_in, mlp_in = normed
    cot_sib = flip(cot_own, CORE)

    blocks = rows_of(block_map, (rows // HB) * (ctx // 2), rows // HB)
    offs = jnp.arange(HB, dtype=jnp.int32)
    positions = (blocks[:, None] * HB + offs[None, :]).reshape(rows)
    live2 = jnp.concatenate([positions < lengths[0], positions < other_len]).astype(f32)[:, None]
    live_own = rows_of(live2, core * own_rows, own_rows)
    freq = 10000.0 ** (-jnp.arange(ROT // 2, dtype=f32) * 2.0 / ROT)
    ang = freq[:, None] * jnp.arange(seq, dtype=jnp.int32).astype(f32)[None, :]
    table = jnp.concatenate([jnp.cos(ang), jnp.sin(ang)])
    own_ang = freq[:, None] * positions.astype(f32)[None, :]
    own_table = jnp.concatenate([jnp.cos(own_ang), jnp.sin(own_ang)])

    attn_in, table = lax.optimization_barrier((attn_in, table))
    send = qkv_forward(ids, attn_in, w_qkv, wq_got, qkv_bias, own_table)
    qkv_head = exchange(send.reshape(2 * heads, 3 * HD, rows))
    dy = mask_rows(ids, cot_own, cot_sib, cot_got, flip(cot_got, CORE), live2)
    dy2 = dy.reshape(2, rows, width)
    w_out_mine = rows_of(w_out, core * quarter, quarter)
    dctx = jnp.einsum("ed,std->set", w_out_mine, dy2, preferred_element_type=f32).astype(bf16)
    attn_t = attn_in.T
    do_head = exchange(dctx.reshape(2 * heads, HD, rows))
    y_mlp, d_mlp, up_keep, up_send, down_keep, down_send, gb_up = mlp(
        ids, mlp_in, mlp_in.T, dy, w_up, wu_got, w_down, b_up.astype(f32)[None, :], chips
    )

    chain_a = (X, ZN, ZF)
    chain_b = (ZN, ZF, X)
    qkv_head, up_send, down_send = lax.optimization_barrier((qkv_head, up_send, down_send))
    down = [down_keep, flip(down_send, chain_a[0])]
    up = [up_keep, flip(up_send, chain_b[0])]

    o_head, lse = attn_fwd(block_map, qkv_head, bq=1024, bk=1024)
    qkv_head, o_head, do_head, down[-1], up[-1] = lax.optimization_barrier((qkv_head, o_head, do_head, down[-1], up[-1]))
    ob = exchange(o_head).reshape(2, quarter, rows)
    down = halve(down, chain_a[1])
    up = halve(up, chain_b[1])
    g_head = attn_bwd(block_map, qkv_head, o_head, do_head, lse, table)
    g_head, ob, down[-1], up[-1] = lax.optimization_barrier((g_head, ob, down[-1], up[-1]))
    d_qkv = exchange(g_head).reshape(2, heads, 3 * HD, rows)

    down = add(*halve(down, chain_a[2]))
    up = add(*halve(up, chain_b[2]))
    up = up.reshape(1, 2, up.shape[1] // 2, up.shape[2])
    up_keep = rows_of(up, me, 1, 1)
    up_got = swap(rows_of(up, 1 - me, 1, 1))
    up = ordered(me, up_keep, up_got, axis=1)
    for a, b in zip(chain_a[::-1], chain_b[::-1]):
        down = double(down, a)
        up = double(up, b)
    tot_down = join_rows(ids, down, flip(down, CORE))
    tot_up = join_cols(ids, up, flip(up, CORE))

    def settle(v):
        give = rows_of(v, (1 - core) * own_rows, own_rows, 1).astype(bf16)
        v = rows_of(v, core * own_rows, own_rows, 1) + flip(give, CORE).astype(f32)
        return v[0], swap(v[1].astype(bf16))

    part = jnp.einsum("sct,cd->std", ob, w_out_mine, preferred_element_type=f32) + y_mlp.reshape(2, rows, width).astype(f32)
    part, part_got = settle(part)
    output = (live_own * (x_own.astype(f32) + part + part_got.astype(f32) + bias_out)).astype(bf16)

    v_a, v_b, e = qkv_backward(
        ids, d_qkv, attn_t, x2, norms, w_qkv, wq_got, d_mlp, ob, dy, gb_up, chips
    )
    v_a = [v_a]
    v_b = [v_b]
    for a, b in zip(chain_a, chain_b):
        v_a = halve(v_a, a)
        v_b = halve(v_b, b)
    e_own, e_got = settle(e)
    n3 = 3 * half // (2 * chips)
    size = 2 * n3 + width // (2 * chips)
    tail = []
    for v in (add(*v_a)[0], add(*v_b)[0]):
        extra = v[size:]
        back = swap(jnp.concatenate([rows_of(v, (1 - me) * n3, n3), extra]))
        extra = add(extra, back[n3:])
        tail.append(jnp.concatenate([ordered(me, rows_of(v, me * n3, n3), back[:n3]), v[2 * n3 : size], extra])[None])
    grad_tokens = last(e_own, e_got, x_own, cot_own, live_own)
    cover = [[tot_down], [tot_up], [grad_tokens, output]]
    for k, (a, b) in enumerate(zip(chain_a[::-1], chain_b[::-1])):
        tail = [double(tail[0], a), double(tail[1], b)]
        tail, cover[k] = lax.optimization_barrier((tail, cover[k]))
    mixed = tail
    (tot_down,), (tot_up,), (grad_tokens, output) = cover
    tot_qkv, tot_out, flat = unpack(ids, mixed[0], flip(mixed[0], CORE), mixed[1], flip(mixed[1], CORE), width)
    flat = flat[:, :6].reshape(12 * width)

    def own(start, size):
        return lax.dynamic_slice_in_dim(flat, start + me * size, size)

    gb_out = own(4 * width, half)
    return (
        output[None],
        grad_tokens[None],
        own(0, half),
        own(width, half),
        own(2 * width, half),
        own(3 * width, half),
        tot_qkv,
        own(5 * width, 3 * half),
        tot_out.reshape(half, width),
        gb_out,
        tot_up,
        own(8 * width, 2 * hid),
        tot_down,
        gb_out,
    )


def solution(mesh):
    placed = (
        P("wsh", "ctx", None),
        P("wsh"),
        P("wsh"),
        P("wsh"),
        P("wsh"),
        P("wsh", None),
        P("wsh"),
        P("wsh", None),
        P("wsh"),
        P("wsh", None),
        P("wsh"),
        P("wsh", None),
        P("wsh"),
        P("wsh"),
        P(),
        P("wsh", "ctx", None),
    )
    body = fast_shards if fast_fits(mesh) else shards
    return jax.shard_map(
        body,
        mesh=mesh,
        in_specs=placed,
        out_specs=(
            P("wsh", "ctx", None),
            P("wsh", "ctx", None),
            P("wsh"),
            P("wsh"),
            P("wsh"),
            P("wsh"),
            P("wsh", None),
            P("wsh"),
            P("wsh", None),
            P("wsh"),
            P("wsh", None),
            P("wsh"),
            P("wsh", None),
            P("wsh"),
        ),
        check_vma=False,
    )
```

```python
from functools import partial
import math

import jax
import jax.numpy as jnp
from jax import lax
from jax.experimental import pallas as pl
from jax.experimental.pallas import tpu as pltpu
from jax.sharding import PartitionSpec as P

H = 16
HD = 64
ROT = 16


epsilon = 1e-05


def norm_forward(values, norm_gain, norm_shift):
    average = jnp.mean(values, axis=-1, keepdims=True)
    centred = values - average
    variance = jnp.mean(centred * centred, axis=-1, keepdims=True)
    inverse = lax.rsqrt(variance + epsilon)
    normed = centred * inverse
    return (normed * norm_gain + norm_shift, normed, inverse)


def norm_backward(grad_out, normed, inverse, norm_gain):
    scaled = grad_out * norm_gain
    adjusted = (
        scaled
        - jnp.mean(scaled, axis=-1, keepdims=True)
        - normed * jnp.mean(scaled * normed, axis=-1, keepdims=True)
    )
    return (adjusted * inverse, jnp.sum(grad_out * normed, axis=0), jnp.sum(grad_out, axis=0))


def rotary_tables(positions):
    half_rot = ROT // 2
    frequency = 10000.0 ** (-jnp.arange(half_rot, dtype=jnp.float32) * 2.0 / ROT)
    angles = positions.astype(jnp.float32)[:, None] * frequency[None, :]
    return (jnp.cos(angles)[:, None, :], jnp.sin(angles)[:, None, :])


def rotate_forward(values, cosine_table, sine_table):
    half_rot = ROT // 2
    leading = values[..., :half_rot]
    trailing = values[..., half_rot:ROT]
    return jnp.concatenate(
        [
            leading * cosine_table - trailing * sine_table,
            trailing * cosine_table + leading * sine_table,
            values[..., ROT:],
        ],
        axis=-1,
    )


def rotate_backward(grads, cosine_table, sine_table):
    half_rot = ROT // 2
    leading = grads[..., :half_rot]
    trailing = grads[..., half_rot:ROT]
    return jnp.concatenate(
        [
            leading * cosine_table + trailing * sine_table,
            trailing * cosine_table - leading * sine_table,
            grads[..., ROT:],
        ],
        axis=-1,
    )


def masked_scores(query_rows, key_rows, query_pos, key_pos, key_live):
    raw_scores = jnp.einsum(
        "qhd,khd->hqk", query_rows, key_rows, preferred_element_type=jnp.float32
    )
    allowed = (key_pos[None, :] <= query_pos[:, None]) & key_live[None, :]
    return (jnp.where(allowed[None], raw_scores * (1.0 / math.sqrt(HD)), -1e30), allowed)


def score_grads(
    query_rows, key_rows, value_rows, grad_rows, query_pos, key_pos, key_live, log_total, row_dots
):
    scores = masked_scores(query_rows, key_rows, query_pos, key_pos, key_live)[0]
    probability = jnp.exp(scores - log_total[..., None])
    grad_prob = jnp.einsum(
        "qhd,khd->hqk", grad_rows, value_rows, preferred_element_type=jnp.float32
    )
    grad_score = (probability * (grad_prob - row_dots[..., None]) * (1.0 / math.sqrt(HD))).astype(
        jnp.bfloat16
    )
    return (probability.astype(jnp.bfloat16), grad_score)


def shards(
    tokens,
    ln1_gain,
    ln1_bias,
    ln2_gain,
    ln2_bias,
    w_qkv,
    b_qkv,
    w_out,
    b_out,
    w_up,
    b_up,
    w_down,
    b_down,
    lengths,
    block_map,
    cotangent,
):
    gathered = (
        lax.all_gather(ln1_gain, "wsh", axis=0, tiled=True),
        lax.all_gather(ln1_bias, "wsh", axis=0, tiled=True),
        lax.all_gather(ln2_gain, "wsh", axis=0, tiled=True),
        lax.all_gather(ln2_bias, "wsh", axis=0, tiled=True),
        lax.all_gather(w_qkv, "wsh", axis=0, tiled=True),
        lax.all_gather(b_qkv, "wsh", axis=0, tiled=True),
        lax.all_gather(w_out, "wsh", axis=0, tiled=True),
        lax.all_gather(b_out, "wsh", axis=0, tiled=True),
        lax.all_gather(w_up, "wsh", axis=0, tiled=True),
        lax.all_gather(b_up, "wsh", axis=0, tiled=True),
        lax.all_gather(w_down, "wsh", axis=0, tiled=True),
        lax.all_gather(b_down, "wsh", axis=0, tiled=True),
    )
    (
        norm1_gain,
        norm1_shift,
        norm2_gain,
        norm2_shift,
        qkv_weight,
        qkv_bias,
        out_weight,
        out_bias,
        up_weight,
        up_bias,
        down_weight,
        down_bias,
    ) = gathered
    tok_rows = tokens.shape[1]
    model_width = tokens.shape[2]
    half_rows = tok_rows // 2
    seq_rows = tok_rows * lax.axis_size("ctx")
    head_count = H
    head_size = HD
    ctx_index = lax.axis_index("ctx")
    own_blocks = lax.dynamic_slice_in_dim(block_map, 2 * ctx_index, 2)
    local_offsets = jnp.arange(half_rows, dtype=jnp.int32)
    positions = (own_blocks[:, None] * half_rows + local_offsets[None, :]).reshape(tok_rows)
    key_pos = (block_map[:, None] * half_rows + local_offsets[None, :]).reshape(seq_rows)
    length = lengths[0]
    own_live = positions < length
    live_rows = own_live.astype(jnp.float32)
    key_live = key_pos < length
    gain_first = norm1_gain.astype(jnp.float32)
    gain_second = norm2_gain.astype(jnp.float32)
    token_rows = tokens[0].astype(jnp.float32)
    normal_first, normed_first, inverse_first = norm_forward(
        token_rows, gain_first, norm1_shift.astype(jnp.float32)
    )
    normal_second, normed_second, inverse_second = norm_forward(
        token_rows, gain_second, norm2_shift.astype(jnp.float32)
    )
    attn_in = normal_first.astype(jnp.bfloat16)
    mlp_in = normal_second.astype(jnp.bfloat16)
    projected = (
        jnp.dot(attn_in, qkv_weight, preferred_element_type=jnp.float32)
        + qkv_bias.astype(jnp.float32)
    ).reshape(tok_rows, 3, head_count, head_size)
    cosine_table, sine_table = rotary_tables(positions)
    queries = rotate_forward(projected[:, 0], cosine_table, sine_table).astype(jnp.bfloat16)
    key_own = (
        rotate_forward(projected[:, 1], cosine_table, sine_table)
        .astype(jnp.bfloat16)
        .reshape(tok_rows, model_width)
    )
    value_own = projected[:, 2].astype(jnp.bfloat16).reshape(tok_rows, model_width)
    keys_all, values_all = (
        lax.all_gather(key_own, "ctx", axis=0, tiled=True),
        lax.all_gather(value_own, "ctx", axis=0, tiled=True),
    )
    block_len = math.gcd(seq_rows, 1024)
    block_count = seq_rows // block_len
    key_stack = keys_all.reshape(block_count, block_len, head_count, head_size)
    value_stack = values_all.reshape(block_count, block_len, head_count, head_size)
    pos_stack = key_pos.reshape(block_count, block_len)
    live_stack = key_live.reshape(block_count, block_len)

    def stats_step(running, key_part):
        key_block, pos_block, live_block = key_part
        scores, allowed = masked_scores(queries, key_block, positions, pos_block, live_block)
        peak_score = jnp.maximum(running[0], jnp.max(scores, axis=-1))
        exp_total = running[1] * jnp.exp(running[0] - peak_score) + jnp.sum(
            jnp.where(allowed[None], jnp.exp(scores - peak_score[..., None]), 0.0), axis=-1
        )
        return ((peak_score, exp_total), None)

    start_peak = jnp.full((head_count, tok_rows), -1e30, jnp.float32)
    final_state = lax.scan(
        stats_step, (start_peak, jnp.zeros_like(start_peak)), (key_stack, pos_stack, live_stack)
    )[0]
    log_total = final_state[0] + jnp.log(final_state[1])

    def value_step(running, key_part):
        key_block, value_block, pos_block, live_block = key_part
        scores = masked_scores(queries, key_block, positions, pos_block, live_block)[0]
        probability = jnp.exp(scores - log_total[..., None]).astype(jnp.bfloat16)
        return (
            running
            + jnp.einsum(
                "hqk,khd->qhd", probability, value_block, preferred_element_type=jnp.float32
            ),
            None,
        )

    zero_heads = jnp.zeros((tok_rows, head_count, head_size), jnp.float32)
    attended = lax.scan(value_step, zero_heads, (key_stack, value_stack, pos_stack, live_stack))[0]
    context_low = attended.reshape(tok_rows, model_width).astype(jnp.bfloat16)
    hidden = jnp.dot(mlp_in, up_weight, preferred_element_type=jnp.float32) + up_bias.astype(
        jnp.float32
    )
    activated, gelu_pull = jax.vjp(partial(jax.nn.gelu, approximate=False), hidden)
    act_low = activated.astype(jnp.bfloat16)
    branch = (
        jnp.dot(context_low, out_weight, preferred_element_type=jnp.float32)
        + out_bias.astype(jnp.float32)
        + jnp.dot(act_low, down_weight, preferred_element_type=jnp.float32)
        + down_bias.astype(jnp.float32)
    )
    output_rows = (live_rows[:, None] * (token_rows + branch)).astype(jnp.bfloat16)
    cot_rows = cotangent[0].astype(jnp.float32)
    grad_branch = (live_rows[:, None] * cot_rows).astype(jnp.bfloat16)
    grad_w_out = jnp.einsum(
        "tc,td->cd", context_low, grad_branch, preferred_element_type=jnp.float32
    )
    grad_w_down = jnp.einsum("tc,td->cd", act_low, grad_branch, preferred_element_type=jnp.float32)
    grad_branch_sum = jnp.sum(grad_branch.astype(jnp.float32), axis=0)
    grad_act = jnp.einsum("td,cd->tc", grad_branch, down_weight, preferred_element_type=jnp.float32)
    grad_hidden = gelu_pull(grad_act)[0].astype(jnp.bfloat16)
    grad_w_up = jnp.einsum("tc,td->cd", mlp_in, grad_hidden, preferred_element_type=jnp.float32)
    grad_b_up = jnp.sum(grad_hidden.astype(jnp.float32), axis=0)
    grad_mlp_in = jnp.einsum(
        "td,cd->tc", grad_hidden, up_weight, preferred_element_type=jnp.float32
    )
    grad_context = jnp.einsum(
        "td,cd->tc", grad_branch, out_weight, preferred_element_type=jnp.float32
    ).astype(jnp.bfloat16)
    grad_heads = grad_context.reshape(tok_rows, head_count, head_size)
    row_dots = jnp.sum(grad_heads.astype(jnp.float32) * attended, axis=-1).T

    def grad_step(running, key_part):
        key_block, value_block, pos_block, live_block = key_part
        prob_low, grad_score = score_grads(
            queries,
            key_block,
            value_block,
            grad_heads,
            positions,
            pos_block,
            live_block,
            log_total,
            row_dots,
        )
        query_sum = running + jnp.einsum(
            "hqk,khd->qhd", grad_score, key_block, preferred_element_type=jnp.float32
        )
        key_term = jnp.einsum(
            "hqk,qhd->khd", grad_score, queries, preferred_element_type=jnp.float32
        )
        value_term = jnp.einsum(
            "hqk,qhd->khd", prob_low, grad_heads, preferred_element_type=jnp.float32
        )
        return (query_sum, (key_term, value_term))

    query_grad, term_stacks = lax.scan(
        grad_step, zero_heads, (key_stack, value_stack, pos_stack, live_stack)
    )
    key_grad, value_grad = (
        lax.psum_scatter(
            term_stacks[0].reshape(seq_rows, model_width).astype(jnp.bfloat16),
            "ctx",
            scatter_dimension=0,
            tiled=True,
        ).astype(jnp.float32),
        lax.psum_scatter(
            term_stacks[1].reshape(seq_rows, model_width).astype(jnp.bfloat16),
            "ctx",
            scatter_dimension=0,
            tiled=True,
        ).astype(jnp.float32),
    )
    key_grad = key_grad.reshape(tok_rows, head_count, head_size)
    value_grad = value_grad.reshape(tok_rows, head_count, head_size)
    grad_projected = (
        jnp.stack(
            [
                rotate_backward(query_grad, cosine_table, sine_table),
                rotate_backward(key_grad, cosine_table, sine_table),
                value_grad,
            ],
            axis=1,
        )
        .reshape(tok_rows, 3 * model_width)
        .astype(jnp.bfloat16)
    )
    grad_w_qkv = jnp.einsum(
        "tc,td->cd", attn_in, grad_projected, preferred_element_type=jnp.float32
    )
    grad_b_qkv = jnp.sum(grad_projected.astype(jnp.float32), axis=0)
    grad_attn_in = jnp.einsum(
        "td,cd->tc", grad_projected, qkv_weight, preferred_element_type=jnp.float32
    )
    grad_input_first, grad_gain_first, grad_shift_first = norm_backward(
        grad_attn_in, normed_first, inverse_first, gain_first
    )
    grad_input_second, grad_gain_second, grad_shift_second = norm_backward(
        grad_mlp_in, normed_second, inverse_second, gain_second
    )
    grad_input = live_rows[:, None] * cot_rows + grad_input_first + grad_input_second
    shares = (
        lax.psum_scatter(
            grad_gain_first.astype(jnp.bfloat16), "wsh", scatter_dimension=0, tiled=True
        ).astype(jnp.float32),
        lax.psum_scatter(
            grad_shift_first.astype(jnp.bfloat16), "wsh", scatter_dimension=0, tiled=True
        ).astype(jnp.float32),
        lax.psum_scatter(
            grad_gain_second.astype(jnp.bfloat16), "wsh", scatter_dimension=0, tiled=True
        ).astype(jnp.float32),
        lax.psum_scatter(
            grad_shift_second.astype(jnp.bfloat16), "wsh", scatter_dimension=0, tiled=True
        ).astype(jnp.float32),
        lax.psum_scatter(
            grad_w_qkv.astype(jnp.bfloat16), "wsh", scatter_dimension=0, tiled=True
        ).astype(jnp.float32),
        lax.psum_scatter(
            grad_b_qkv.astype(jnp.bfloat16), "wsh", scatter_dimension=0, tiled=True
        ).astype(jnp.float32),
        lax.psum_scatter(
            grad_w_out.astype(jnp.bfloat16), "wsh", scatter_dimension=0, tiled=True
        ).astype(jnp.float32),
        lax.psum_scatter(
            grad_branch_sum.astype(jnp.bfloat16), "wsh", scatter_dimension=0, tiled=True
        ).astype(jnp.float32),
        lax.psum_scatter(
            grad_w_up.astype(jnp.bfloat16), "wsh", scatter_dimension=0, tiled=True
        ).astype(jnp.float32),
        lax.psum_scatter(
            grad_b_up.astype(jnp.bfloat16), "wsh", scatter_dimension=0, tiled=True
        ).astype(jnp.float32),
        lax.psum_scatter(
            grad_w_down.astype(jnp.bfloat16), "wsh", scatter_dimension=0, tiled=True
        ).astype(jnp.float32),
        lax.psum_scatter(
            grad_branch_sum.astype(jnp.bfloat16), "wsh", scatter_dimension=0, tiled=True
        ).astype(jnp.float32),
    )
    totals = (
        lax.psum(shares[0].astype(jnp.bfloat16), "ctx").astype(jnp.float32),
        lax.psum(shares[1].astype(jnp.bfloat16), "ctx").astype(jnp.float32),
        lax.psum(shares[2].astype(jnp.bfloat16), "ctx").astype(jnp.float32),
        lax.psum(shares[3].astype(jnp.bfloat16), "ctx").astype(jnp.float32),
        lax.psum(shares[4].astype(jnp.bfloat16), "ctx").astype(jnp.float32),
        lax.psum(shares[5].astype(jnp.bfloat16), "ctx").astype(jnp.float32),
        lax.psum(shares[6].astype(jnp.bfloat16), "ctx").astype(jnp.float32),
        lax.psum(shares[7].astype(jnp.bfloat16), "ctx").astype(jnp.float32),
        lax.psum(shares[8].astype(jnp.bfloat16), "ctx").astype(jnp.float32),
        lax.psum(shares[9].astype(jnp.bfloat16), "ctx").astype(jnp.float32),
        lax.psum(shares[10].astype(jnp.bfloat16), "ctx").astype(jnp.float32),
        lax.psum(shares[11].astype(jnp.bfloat16), "ctx").astype(jnp.float32),
    )
    return (
        output_rows[None],
        grad_input[None],
        totals[0],
        totals[1],
        totals[2],
        totals[3],
        totals[4],
        totals[5],
        totals[6],
        totals[7],
        totals[8],
        totals[9],
        totals[10],
        totals[11],
    )


HB = 128
NEG=-1e30
f32=jnp.float32; bf16=jnp.bfloat16

def _nn(a,b): return lax.dot_general(a,b,(((1,),(0,)),((),())),preferred_element_type=f32)
def _nt(a,b): return lax.dot_general(a,b,(((1,),(1,)),((),())),preferred_element_type=f32)

def attn_fwd_kernel(bm, x_ref, o_ref, lse_ref, q_s, kt_s, v_s, *, nblk, per, bq, bk):
    def perm(i,_):
        p=bm[i]; c=i//per; l=pl.multiple_of((i%per)*HB,HB); d=pl.multiple_of(p*HB,HB)
        q_s[:,pl.ds(d,HB)]=x_ref[c,0:64,pl.ds(l,HB)]*bf16(0.125)
        kt_s[pl.ds(d,HB),:]=x_ref[c,64:128,pl.ds(l,HB)].astype(f32).T.astype(bf16)
        v_s[:,pl.ds(d,HB)]=x_ref[c,128:192,pl.ds(l,HB)]
        return 0
    lax.fori_loop(0,nblk,perm,0,unroll=32)
    S=nblk*HB; nq=S//bq; r=bq//bk
    def step(q,qo,ko,carry,mask):
        m,l,acc=carry
        s=_nn(kt_s[pl.ds(ko,bk),:],q)
        if mask is not None: s=jnp.where(mask,s,NEG)
        mn=jnp.maximum(m,jnp.max(s,axis=0,keepdims=True))
        a=jnp.exp(m-mn); p=jnp.exp(s-mn)
        l=l*a+jnp.sum(p,axis=0,keepdims=True)
        acc=acc*a+_nn(v_s[:,pl.ds(ko,bk)],p.astype(bf16))
        return mn,l,acc
    ki=lax.broadcasted_iota(jnp.int32,(bk,bq),0); qi_=lax.broadcasted_iota(jnp.int32,(bk,bq),1)
    def qloop(i,_):
        qo=pl.multiple_of(i*bq,bq)
        q=q_s[:,pl.ds(qo,bq)]
        c=(jnp.full((1,bq),NEG,f32),jnp.zeros((1,bq),f32),jnp.zeros((64,bq),f32))
        c=lax.fori_loop(0,i*r,lambda j,c: step(q,qo,pl.multiple_of(j*bk,bk),c,None),c)
        for t in range(r):
            c=step(q,qo,pl.multiple_of(qo+t*bk,bk),c,ki+t*bk<=qi_)
        m,l,acc=c
        q_s[:,pl.ds(qo,bq)]=(acc*(1.0/l)).astype(bf16)
        lse_ref[:,pl.ds(qo,bq)]=m+jnp.log(l)
        return 0
    lax.fori_loop(0,nq,qloop,0)
    def unperm(i,_):
        p=bm[i]; c=i//per; l=pl.multiple_of((i%per)*HB,HB); d=pl.multiple_of(p*HB,HB)
        o_ref[c,:,pl.ds(l,HB)]=q_s[:,pl.ds(d,HB)]
        return 0
    lax.fori_loop(0,nblk,unperm,0,unroll=32)

def attn_fwd(bm,x,*,bq=512,bk=512):
    n=x.shape[0]; S=n*x.shape[2]; nblk=S//HB
    bq=math.gcd(S,bq); bk=math.gcd(bq,bk)
    return pl.pallas_call(
        lambda *a: attn_fwd_kernel(*a,nblk=nblk,per=x.shape[2]//HB,bq=bq,bk=bk),
        out_shape=(jax.ShapeDtypeStruct((n,64,x.shape[2]),bf16),jax.ShapeDtypeStruct((1,S),f32)),
        in_specs=[pl.BlockSpec(memory_space=pltpu.SMEM),pl.BlockSpec(memory_space=pltpu.VMEM)],
        out_specs=(pl.BlockSpec(memory_space=pltpu.VMEM),pl.BlockSpec(memory_space=pltpu.VMEM)),
        scratch_shapes=[pltpu.VMEM((64,S),bf16),pltpu.VMEM((S,64),bf16),pltpu.VMEM((64,S),bf16)],
        compiler_params=pltpu.CompilerParams(vmem_limit_bytes=56<<20),name="attn_fwd")(bm,x)

def attn_bwd_kernel(bm, x_ref, o_ref, do_ref, lse_ref, cs_ref, g_ref, q_s, kt_s, k_s, vt_s, do_s, dl_s, dq_s, dk_s, dv_s, *, nblk, per, bq, bk):
    def perm(i,_):
        p=bm[i]; c=i//per; l=pl.multiple_of((i%per)*HB,HB); d=pl.multiple_of(p*HB,HB)
        q_s[:,pl.ds(d,HB)]=x_ref[c,0:64,pl.ds(l,HB)]*bf16(0.125)
        k=x_ref[c,64:128,pl.ds(l,HB)]
        k_s[:,pl.ds(d,HB)]=k*bf16(0.125)
        kt_s[pl.ds(d,HB),:]=k.astype(f32).T.astype(bf16)
        vt_s[pl.ds(d,HB),:]=x_ref[c,128:192,pl.ds(l,HB)].astype(f32).T.astype(bf16)
        do=do_ref[c,:,pl.ds(l,HB)]
        do_s[:,pl.ds(d,HB)]=do
        dl_s[:,pl.ds(d,HB)]=jnp.sum(do.astype(f32)*o_ref[c,:,pl.ds(l,HB)].astype(f32),axis=0,keepdims=True)
        return 0
    lax.fori_loop(0,nblk,perm,0,unroll=32)
    S=nblk*HB; nq=S//bq; r=bq//bk
    dk_s[...]=jnp.zeros_like(dk_s); dv_s[...]=jnp.zeros_like(dv_s)
    def step(q,do,lse,dl,ko,dq,mask):
        s=_nn(kt_s[pl.ds(ko,bk),:],q)
        p=jnp.exp(s-lse)
        if mask is not None: p=jnp.where(mask,p,0.0)
        dp=_nn(vt_s[pl.ds(ko,bk),:],do)
        ds=(p*(dp-dl)).astype(bf16)
        pb=p.astype(bf16)
        dv_s[:,pl.ds(ko,bk)]+=_nt(do,pb)
        dk_s[:,pl.ds(ko,bk)]+=_nt(q,ds)
        return dq+_nn(k_s[:,pl.ds(ko,bk)],ds)
    ki=lax.broadcasted_iota(jnp.int32,(bk,bq),0); qi_=lax.broadcasted_iota(jnp.int32,(bk,bq),1)
    def qloop(i,_):
        qo=pl.multiple_of(i*bq,bq)
        q=q_s[:,pl.ds(qo,bq)]; do=do_s[:,pl.ds(qo,bq)]; lse=lse_ref[:,pl.ds(qo,bq)]; dl=dl_s[:,pl.ds(qo,bq)]
        dq=jnp.zeros((64,bq),f32)
        dq=lax.fori_loop(0,i*r,lambda j,c: step(q,do,lse,dl,pl.multiple_of(j*bk,bk),c,None),dq)
        for t in range(r):
            dq=step(q,do,lse,dl,pl.multiple_of(qo+t*bk,bk),dq,ki+t*bk<=qi_)
        dq_s[:,pl.ds(qo,bq)]=dq
        return 0
    lax.fori_loop(0,nq,qloop,0)
    def unperm(i,_):
        p=bm[i]; c=i//per; l=pl.multiple_of((i%per)*HB,HB); d=pl.multiple_of(p*HB,HB)
        cos=cs_ref[0:8,pl.ds(d,HB)]; sin=cs_ref[8:16,pl.ds(d,HB)]
        for n_,src in ((0,dq_s),(1,dk_s)):
            g=src[:,pl.ds(d,HB)]
            a=g[0:8]; b=g[8:16]
            full=jnp.concatenate([a*cos+b*sin,b*cos-a*sin,g[16:64]],axis=0)
            g_ref[c,64*n_:64*n_+64,pl.ds(l,HB)]=full.astype(bf16)
        g_ref[c,128:192,pl.ds(l,HB)]=dv_s[:,pl.ds(d,HB)].astype(bf16)
        return 0
    lax.fori_loop(0,nblk,unperm,0,unroll=32)

def attn_bwd(bm,x,o,do,lse,cs,*,bq=512,bk=512):
    n=x.shape[0]; S=n*x.shape[2]; nblk=S//HB
    bq=math.gcd(S,bq); bk=math.gcd(bq,bk)
    vm=pl.BlockSpec(memory_space=pltpu.VMEM)
    return pl.pallas_call(
        lambda *a: attn_bwd_kernel(*a,nblk=nblk,per=x.shape[2]//HB,bq=bq,bk=bk),
        out_shape=jax.ShapeDtypeStruct((n,192,x.shape[2]),bf16),
        in_specs=[pl.BlockSpec(memory_space=pltpu.SMEM)]+[vm]*5,
        out_specs=vm,
        scratch_shapes=[pltpu.VMEM((64,S),bf16),pltpu.VMEM((S,64),bf16),pltpu.VMEM((64,S),bf16),pltpu.VMEM((S,64),bf16),pltpu.VMEM((64,S),bf16),
                        pltpu.VMEM((1,S),f32),pltpu.VMEM((64,S),f32),pltpu.VMEM((64,S),f32),pltpu.VMEM((64,S),f32)],
        compiler_params=pltpu.CompilerParams(vmem_limit_bytes=56<<20),name="attn_bwd")(bm,x,o,do,lse,cs)


SWAP = [(0, 1), (1, 0)]


def fast_fits(mesh):
    return mesh.shape["wsh"] == 2 and mesh.shape["ctx"] == H


def _params(mb=56):
    return pltpu.CompilerParams(vmem_limit_bytes=mb << 20)


def _norm(x):
    xf = x.astype(f32)
    cen = xf - jnp.mean(xf, axis=-1, keepdims=True)
    inv = lax.rsqrt(jnp.mean(cen * cen, axis=-1, keepdims=True) + epsilon)
    return cen * inv, inv


def _full(v):
    return pl.BlockSpec(v.shape, lambda *a: (0,) * v.ndim)


def _wq_specs(half, width, cols, quarter, at):
    own = lambda p: pl.BlockSpec(
        (half, cols),
        lambda *a: (0, p * (width // cols) + a[-1][0] * (half // cols) + a[-1][1] * (quarter // cols) + at(*a)),
    )
    got = lambda p: pl.BlockSpec((half, cols), lambda *a: (0, p * (quarter // cols) + at(*a)))
    return [own(p) for p in range(3)] + [got(p) for p in range(3)]


def norm_kernel(ids, a_ref, b_ref, n_ref, *refs):
    x_ref, ain_ref, min_ref = refs[-3:]
    mine = pl.program_id(0) == ids[1]
    x = jnp.where(mine, a_ref[...].astype(f32), b_ref[...].astype(f32))
    x_ref[...] = x.astype(bf16)
    xhat, _ = _norm(x)
    ain_ref[...] = (xhat * n_ref[0:1, :] + n_ref[1:2, :]).astype(bf16)
    min_ref[...] = (xhat * n_ref[2:3, :] + n_ref[3:4, :]).astype(bf16)


def norm_rows(ids, a, b, norms, before=()):
    rows, width = a.shape
    slot = 2 if before else 0
    out = jax.ShapeDtypeStruct((4 * rows, width), bf16)
    return pl.pallas_call(
        norm_kernel,
        grid_spec=pltpu.PrefetchScalarGridSpec(
            num_scalar_prefetch=1,
            grid=(2,),
            in_specs=[_full(a), _full(b), _full(norms)] + [pl.BlockSpec(memory_space=pl.ANY)] * len(before),
            out_specs=(pl.BlockSpec((rows, width), lambda i, ids: (slot + i, 0)),) * 3,
        ),
        out_shape=(out,) * 3,
        input_output_aliases={4 + k: k for k in range(len(before))},
        compiler_params=_params(),
        cost_estimate=pl.CostEstimate(flops=0, transcendentals=0, bytes_accessed=1 << 20),
        name="norm_rows",
    )(ids, a, b, norms, *before)


def turn_kernel(a_ref, b_ref, at_ref, bt_ref):
    at_ref[...] = a_ref[...].astype(f32).T.astype(bf16)
    bt_ref[...] = b_ref[...].astype(f32).T.astype(bf16)


def turn(a, b, steps=4):
    rows, width = a.shape
    src = pl.BlockSpec((rows // steps, width), lambda i: (i, 0))
    dst = pl.BlockSpec((width, rows // steps), lambda i: (0, i))
    return pl.pallas_call(
        turn_kernel,
        grid=(steps,),
        in_specs=[src, src],
        out_specs=(dst, dst),
        out_shape=(jax.ShapeDtypeStruct((width, rows), a.dtype),) * 2,
        compiler_params=_params(),
        cost_estimate=pl.CostEstimate(flops=0, transcendentals=0, bytes_accessed=1 << 20),
        name="turn",
    )(a, b)


def mask_kernel(ids, a_ref, b_ref, c_ref, d_ref, live_ref, o_ref):
    i = pl.program_id(0)
    mine = (i % 2) == ids[1]
    for slot, (own, sib) in enumerate(((a_ref, b_ref), (c_ref, d_ref))):
        @pl.when((i // 2) == slot)
        def _(own=own, sib=sib):
            v = jnp.where(mine, own[...].astype(f32), sib[...].astype(f32))
            o_ref[...] = (live_ref[...] * v).astype(bf16)


def mask_rows(ids, own, own_sib, got, got_sib, live):
    rows, width = own.shape
    return pl.pallas_call(
        mask_kernel,
        grid_spec=pltpu.PrefetchScalarGridSpec(
            num_scalar_prefetch=1,
            grid=(4,),
            in_specs=[_full(v) for v in (own, own_sib, got, got_sib)] + [pl.BlockSpec((rows, 1), lambda i, ids: (i, 0))],
            out_specs=pl.BlockSpec((rows, width), lambda i, ids: (i, 0)),
        ),
        out_shape=jax.ShapeDtypeStruct((4 * rows, width), bf16),
        compiler_params=_params(),
        cost_estimate=pl.CostEstimate(flops=0, transcendentals=0, bytes_accessed=1 << 20),
        name="mask_rows",
    )(ids, own, own_sib, got, got_sib, live)


def qkv_kernel(
    ids, ain_ref, wq_ref, wk_ref, wv_ref, gq_ref, gk_ref, gv_ref, bq_ref, bk_ref, bv_ref, cs_ref, send_ref
):
    width = ain_ref.shape[1]
    half = width // 2
    me = ids[0]
    a_own = ain_ref[:, pl.ds(pl.multiple_of(me * half, half), half)]
    a_got = ain_ref[:, pl.ds(pl.multiple_of((1 - me) * half, half), half)]
    cos = cs_ref[0:8, :]
    sin = cs_ref[8:16, :]
    for n, (w, g, b) in enumerate(((wq_ref, gq_ref, bq_ref), (wk_ref, gk_ref, bk_ref), (wv_ref, gv_ref, bv_ref))):
        t = _nn(a_own, w[...]) + _nn(a_got, g[...]) + b[...]
        t = t.T
        for k in range(send_ref.shape[1]):
            v = t[k * HD : (k + 1) * HD]
            if n < 2:
                lead = v[0:8]
                trail = v[8:16]
                v = jnp.concatenate([lead * cos - trail * sin, trail * cos + lead * sin, v[16:]], axis=0)
            send_ref[0, k, n * HD : (n + 1) * HD, :] = v.astype(bf16)


def qkv_forward(ids, attn_in, w_own, w_got, bias, cs, cols=256):
    rows, width = attn_in.shape[0] // 2, attn_in.shape[1]
    half = width // 2
    quarter = w_got.shape[1] // 3
    bsp = lambda p: pl.BlockSpec((1, cols), lambda s, i, ids: (0, p * (quarter // cols) + i))
    return pl.pallas_call(
        qkv_kernel,
        grid_spec=pltpu.PrefetchScalarGridSpec(
            num_scalar_prefetch=1,
            grid=(2, quarter // cols),
            in_specs=[pl.BlockSpec((rows, width), lambda s, i, ids: (s, 0))]
            + _wq_specs(half, width, cols, quarter, lambda s, i, ids: i)
            + [bsp(p) for p in range(3)]
            + [_full(cs)],
            out_specs=pl.BlockSpec((1, cols // HD, 3 * HD, rows), lambda s, i, ids: (s, i, 0, 0)),
        ),
        out_shape=jax.ShapeDtypeStruct((2, quarter // HD, 3 * HD, rows), bf16),
        compiler_params=_params(),
        cost_estimate=pl.CostEstimate(flops=1 << 20, transcendentals=0, bytes_accessed=1 << 20),
        name="qkv_forward",
    )(ids, attn_in, w_own, w_own, w_own, w_got, w_got, w_got, bias, bias, bias, cs)


MLP_CHUNKS = 2


def mlp_kernel(ids, x_ref, xt_ref, dy_ref, wo_ref, wg_ref, wd_ref, bu_ref, y_ref, dx_ref, uk_ref, us_ref, dk_ref, ds_ref, gb_ref,
    g_s, act_s, du_s, y_s, dx_s
):
    rows, width = x_ref.shape
    half = width // 2
    me = ids[0]
    spans = (
        (pl.multiple_of(me * half, half), wo_ref[...]),
        (pl.multiple_of((1 - me) * half, half), wg_ref[...]),
    )

    @pl.when(pl.program_id(0) == 0)
    def _():
        y_s[...] = jnp.zeros_like(y_s)
        dx_s[...] = jnp.zeros_like(dx_s)

    wd = wd_ref[...]
    bias = bu_ref[...]
    step = rows // MLP_CHUNKS
    for c in range(MLP_CHUNKS):
        at = slice(c * step, (c + 1) * step)
        u = bias + sum(_nn(x_ref[at, pl.ds(o, half)], w) for o, w in spans)
        cdf = 0.5 * (1.0 + lax.erf(u * (1.0 / math.sqrt(2.0))))
        pdf = jnp.exp(-0.5 * u * u) * (1.0 / math.sqrt(2.0 * math.pi))
        act = (u * cdf).astype(bf16)
        du = (_nt(dy_ref[at, :], wd) * (cdf + u * pdf)).astype(bf16)
        y_s[at, :] += _nn(act, wd)
        for o, w in spans:
            dx_s[at, pl.ds(o, half)] += _nt(du, w)
        act_s[at, :] = act
        du_s[at, :] = du
    du = du_s[...]
    gd = lax.dot_general(
        act_s[...], dy_ref[...], (((0,), (0,)), ((), ())), preferred_element_type=f32
    ).astype(bf16)
    k, r, _ = dk_ref.shape
    k = gd.shape[0] // r
    early = pl.program_id(0) < pl.num_programs(0) // 2
    for c in range(k):
        v = gd[c * r : (c + 1) * r, :]

        @pl.when(early)
        def _(v=v, c=c):
            ds_ref[c] = v

        @pl.when(jnp.logical_not(early))
        def _(v=v, c=c):
            dk_ref[c] = v

    g_s[...] = _nn(xt_ref[...], du).astype(bf16)
    n = uk_ref.shape[0]
    r = uk_ref.shape[1] // 2
    for ref, side in ((uk_ref, ids[3]), (us_ref, 1 - ids[3])):
        for h in range(2):
            for c in range(n):
                at = pl.multiple_of(h * half + (side * n + c) * r, r)
                ref[c, h * r : (h + 1) * r, :] = g_s[pl.ds(at, r), :]
    gb_ref[...] = jnp.sum(du.astype(f32), axis=0, keepdims=True)

    @pl.when(pl.program_id(0) == pl.num_programs(0) - 1)
    def _():
        y_ref[...] = y_s[...].astype(bf16)
        dx_ref[...] = dx_s[...].astype(bf16)


def mlp(ids, x, xt, dy, w_own, w_got, wd, bu, n, tile=512):
    rows, width = x.shape
    half = width // 2
    hidden = w_got.shape[1]
    steps = hidden // tile
    mid = steps // 2
    whole = pl.BlockSpec((rows, width), lambda i, ids: (0, 0))
    per = hidden // n
    order = lambda i, ids: i % mid + mid * jnp.where(i < mid, 1 - ids[2], ids[2])
    part = lambda i, ids: ids[1] * steps + order(i, ids)
    up_spec = pl.BlockSpec((n // 2, width // n, tile), lambda i, ids: (0, 0, order(i, ids)))
    down_spec = lambda f: pl.BlockSpec((tile // per, per, width), lambda i, ids: (f(i), 0, 0))
    up_shape = jax.ShapeDtypeStruct((n // 2, width // n, hidden), bf16)
    down_shape = jax.ShapeDtypeStruct((n // 2, per, width), bf16)
    return pl.pallas_call(
        mlp_kernel,
        grid_spec=pltpu.PrefetchScalarGridSpec(
            num_scalar_prefetch=1,
            grid=(steps,),
            in_specs=[
                whole,
                pl.BlockSpec((width, rows), lambda i, ids: (0, 0)),
                whole,
                pl.BlockSpec((half, tile), lambda i, ids: (0, ids[0] * 2 * steps + part(i, ids))),
                pl.BlockSpec((half, tile), lambda i, ids: (0, order(i, ids))),
                pl.BlockSpec((tile, width), lambda i, ids: (part(i, ids), 0)),
                pl.BlockSpec((1, tile), lambda i, ids: (0, part(i, ids))),
            ],
            out_specs=(
                whole,
                whole,
                up_spec,
                up_spec,
                down_spec(lambda i: jnp.maximum(i - mid, 0)),
                down_spec(lambda i: jnp.minimum(i, mid - 1)),
                pl.BlockSpec((1, tile), lambda i, ids: (0, order(i, ids))),
            ),
            scratch_shapes=[pltpu.VMEM((width, tile), bf16), pltpu.VMEM((rows, tile), bf16), pltpu.VMEM((rows, tile), bf16)]
            + [pltpu.VMEM((rows, width), f32)] * 2,
        ),
        out_shape=(
            jax.ShapeDtypeStruct((rows, width), bf16),
            jax.ShapeDtypeStruct((rows, width), bf16),
            up_shape,
            up_shape,
            down_shape,
            down_shape,
            jax.ShapeDtypeStruct((1, hidden), f32),
        ),
        compiler_params=_params(),
        cost_estimate=pl.CostEstimate(
            flops=12 * rows * width * hidden, transcendentals=2 * rows * hidden, bytes_accessed=24 << 20
        ),
        name="mlp",
    )(ids, x, xt, dy, w_own, w_got, wd, bu)


def qkv_back_kernel(
    ids, d_ref, at_ref, x_ref, n_ref, wq_ref, wk_ref, wv_ref, gq_ref, gk_ref, gv_ref, dm_ref, ob_ref, dy_ref, gb_ref,
    a_ref, b_ref, e_ref, g_s, go_s, bias_s, sum_s
):
    rows, width = x_ref.shape
    half = width // 2
    me = ids[0]
    core = ids[1]
    s = pl.program_id(0)
    outs = (a_ref, b_ref)
    n = a_ref.shape[0]
    nh = d_ref.shape[1]
    cols = nh * HD
    r = half // (2 * n)

    @pl.when(s == 0)
    def _():
        g_s[...] = jnp.zeros_like(g_s)
        go_s[...] = jnp.zeros_like(go_s)
        bias_s[...] = jnp.zeros_like(bias_s)
        sum_s[...] = jnp.zeros_like(sum_s)

    ones = jnp.ones((8, rows), bf16)
    at = at_ref[...]
    dts = []
    for p in range(3):
        dp = jnp.concatenate([d_ref[0, k, p * HD : (p + 1) * HD, :] for k in range(nh)], axis=0)
        g_s[p] += _nt(at, dp)
        bias_s[p * 8 : (p + 1) * 8, :] += _nt(ones, dp)
        dts.append(dp.astype(f32).T.astype(bf16))
    go_s[...] += _nn(ob_ref[0], dy_ref[...])
    dt = jnp.concatenate(dts, axis=1)
    w_own = jnp.concatenate([wq_ref[...], wk_ref[...], wv_ref[...]], axis=1)
    w_got = jnp.concatenate([gq_ref[...], gk_ref[...], gv_ref[...]], axis=1)
    d_own = _nt(dt, w_own)
    d_got = _nt(dt, w_got)
    first = me == 0
    xhat, _ = _norm(x_ref[...])
    for h in range(2):
        lanes = slice(h * half, (h + 1) * half)
        da = jnp.where(first, d_own, d_got) if h == 0 else jnp.where(first, d_got, d_own)
        dm = dm_ref[:, lanes].astype(f32)
        xh = xhat[:, lanes]
        e_ref[0, :, lanes] = da * n_ref[0:1, lanes] + dm * n_ref[2:3, lanes]
        for k, v in enumerate((da * xh, da, dm * xh, dm)):
            sum_s[k : k + 1, lanes] += jnp.sum(v, axis=0, keepdims=True)

    @pl.when(s == 0)
    def _():
        mine = dy_ref[pl.ds(pl.multiple_of(core * (rows // 2), rows // 2), rows // 2), :]
        sum_s[4:5, :] = jnp.sum(mine.astype(f32), axis=0, keepdims=True)

    @pl.when(s == pl.num_programs(0) - 1)
    def _():
        for p in range(3):
            g = g_s[p].astype(bf16)
            for h in range(2):
                for c in range(n):
                    for a in range(2):
                        row = h * half + (c * 2 + a) * r
                        u = (h * 3 + p) * r
                        outs[a][c, u : u + r, :] = g[row : row + r, :]
        go = go_s[...].astype(bf16)
        q = cols // (2 * n)
        for c in range(n):
            for a in range(2):
                row = (c * 2 + a) * q
                for k in range(width // cols):
                    u = 6 * r + k * q
                    outs[a][c, u : u + q, :] = go[row : row + q, k * cols : (k + 1) * cols]
        flat = [sum_s[k : k + 1, t * cols : (t + 1) * cols] for k in range(5) for t in range(width // cols)]
        zero = jnp.zeros((1, cols), f32)
        for p in range(3):
            flat += [
                jnp.where((me == k) & (core == j), bias_s[p * 8 : p * 8 + 1, :], zero) for k in range(2) for j in range(2)
            ]
        flat += [
            jnp.where((me == k) & (core == j), gb_ref[:, t * cols : (t + 1) * cols], zero)
            for k in range(2)
            for j in range(2)
            for t in range(gb_ref.shape[1] // cols)
        ]
        top = 6 * r + (width // cols) * q
        per = len(flat) // n
        pad = [zero] * (8 - per)
        for c in range(n):
            b_ref[c, top : top + 8, :] = jnp.concatenate(flat[c * per : (c + 1) * per] + pad, axis=0).astype(bf16)


def qkv_backward(ids, d, at, x2, norms, w_own, w_got, d_mlp, ob, dy, gb_up, n):
    rows, width = x2.shape[0] // 2, x2.shape[1]
    half = width // 2
    cols = w_got.shape[1] // 3
    size = 6 * (half // (2 * n)) + width // (2 * n)
    row = lambda: pl.BlockSpec((rows, width), lambda s, ids: (s, 0))
    out = [
        jax.ShapeDtypeStruct((n, size, cols), bf16),
        jax.ShapeDtypeStruct((n, size + 8, cols), bf16),
    ]
    return pl.pallas_call(
        qkv_back_kernel,
        grid_spec=pltpu.PrefetchScalarGridSpec(
            num_scalar_prefetch=1,
            grid=(2,),
            in_specs=[
                pl.BlockSpec((1, cols // HD, 3 * HD, rows), lambda s, ids: (s, 0, 0, 0)),
                pl.BlockSpec((width, rows), lambda s, ids: (0, s)),
                row(),
                _full(norms),
            ]
            + _wq_specs(half, width, cols, cols, lambda s, ids: 0)
            + [row(), pl.BlockSpec((1, cols, rows), lambda s, ids: (s, 0, 0)), row(), _full(gb_up)],
            out_specs=(*[_full(v) for v in out], pl.BlockSpec((1, rows, width), lambda s, ids: (s, 0, 0))),
            scratch_shapes=[
                pltpu.VMEM((3, width, cols), f32),
                pltpu.VMEM((cols, width), f32),
                pltpu.VMEM((24, cols), f32),
                pltpu.VMEM((8, width), f32),
            ],
        ),
        out_shape=(*out, jax.ShapeDtypeStruct((2, rows, width), f32)),
        compiler_params=_params(),
        name="qkv_backward",
    )(ids, d, at, x2, norms, w_own, w_own, w_own, w_got, w_got, w_got, d_mlp, ob, dy, gb_up)


def _mine(ids):
    return (pl.program_id(0) // 2) == ids[1]


def _own_block(i, ids):
    return jnp.clip(i - 2 * ids[1], 0, 1)


def _got_block(i, ids):
    return jnp.clip(i - 2 * (1 - ids[1]), 0, 1)


def join_kernel(ids, own_ref, got_ref, o_ref):
    mine = _mine(ids)
    shape = o_ref.shape

    @pl.when(mine)
    def _():
        o_ref[...] = own_ref[...].astype(f32).reshape(shape)

    @pl.when(jnp.logical_not(mine))
    def _():
        o_ref[...] = got_ref[...].astype(f32).reshape(shape)


def join_rows(ids, own, got):
    n, r, w = own.shape
    src = lambda f: pl.BlockSpec((n // 2, r, w), lambda i, ids: (f(i, ids), 0, 0))
    return pl.pallas_call(
        join_kernel,
        grid_spec=pltpu.PrefetchScalarGridSpec(
            num_scalar_prefetch=1,
            grid=(4,),
            in_specs=[src(_own_block), src(_got_block)],
            out_specs=pl.BlockSpec((n * r // 2, w), lambda i, ids: (i, 0)),
        ),
        out_shape=jax.ShapeDtypeStruct((2 * n * r, w), f32),
        compiler_params=_params(),
        name="join_rows",
    )(ids, own, got)


def join_cols(ids, own, got):
    n, _, r, w = own.shape
    src = lambda f: pl.BlockSpec((n, 1, r, w), lambda i, ids: (0, f(i, ids), 0, 0))
    return pl.pallas_call(
        join_kernel,
        grid_spec=pltpu.PrefetchScalarGridSpec(
            num_scalar_prefetch=1,
            grid=(4,),
            in_specs=[src(_own_block), src(_got_block)],
            out_specs=pl.BlockSpec((n * r, w), lambda i, ids: (0, (i % 2) * 2 + i // 2)),
        ),
        out_shape=jax.ShapeDtypeStruct((n * r, 4 * w), f32),
        compiler_params=_params(),
        name="join_cols",
    )(ids, own, got)


def unpack_kernel(ids, ao_ref, ag_ref, bo_ref, bg_ref, q_ref, o_ref, s_ref):
    first = ids[1] == 0
    k, _, cols = ao_ref.shape
    r = q_ref.shape[0] // (2 * k)
    q = o_ref.shape[1] // (2 * k)
    for a, (own, got) in enumerate(((ao_ref, ag_ref), (bo_ref, bg_ref))):
        for c in range(k):
            x = own[c].astype(f32)
            y = got[c].astype(f32)
            to = slice((c * 2 + a) * r, (c * 2 + a + 1) * r)
            tq = slice((c * 2 + a) * q, (c * 2 + a + 1) * q)
            for j in range(2):
                v = jnp.where(first, x, y) if j == 0 else jnp.where(first, y, x)
                for w in range(2):
                    for p in range(3):
                        u = (w * 3 + p) * r
                        at = ((p * 2 + w) * 2 + j) * cols
                        q_ref[to, at : at + cols] = v[u : u + r, :]
                for t in range(o_ref.shape[2] // cols):
                    u = 6 * r + t * q
                    o_ref[j, tq, t * cols : (t + 1) * cols] = v[u : u + q, :]
            if a == 1:
                s_ref[c] = (x + y)[-8:, :]


def unpack(ids, a_own, a_got, b_own, b_got, width, steps=4):
    n, _, cols = a_own.shape
    half = width // 2
    k = n // steps
    spec = lambda v: pl.BlockSpec((k,) + v.shape[1:], lambda i, ids: (i, 0, 0))
    return pl.pallas_call(
        unpack_kernel,
        grid_spec=pltpu.PrefetchScalarGridSpec(
            num_scalar_prefetch=1,
            grid=(steps,),
            in_specs=[spec(v) for v in (a_own, a_got, b_own, b_got)],
            out_specs=(
                pl.BlockSpec((half // steps, 3 * width), lambda i, ids: (i, 0)),
                pl.BlockSpec((2, cols // steps, width), lambda i, ids: (0, i, 0)),
                pl.BlockSpec((k, 8, cols), lambda i, ids: (i, 0, 0)),
            ),
        ),
        out_shape=(
            jax.ShapeDtypeStruct((half, 3 * width), f32),
            jax.ShapeDtypeStruct((2, cols, width), f32),
            jax.ShapeDtypeStruct((n, 8, cols), f32),
        ),
        compiler_params=_params(),
        name="unpack",
    )(ids, a_own, a_got, b_own, b_got)


def last_kernel(eo_ref, er_ref, x_ref, c_ref, live_ref, o_ref):
    xhat, inv = _norm(x_ref[...])
    e = eo_ref[...] + er_ref[...].astype(f32)
    dx = inv * (
        e - jnp.mean(e, axis=-1, keepdims=True) - xhat * jnp.mean(e * xhat, axis=-1, keepdims=True)
    )
    o_ref[...] = live_ref[...] * c_ref[...].astype(f32) + dx


def last(e_own, e_got, x, cot, live):
    return pl.pallas_call(
        last_kernel,
        out_shape=jax.ShapeDtypeStruct(x.shape, f32),
        compiler_params=_params(),
        name="token_grad",
    )(e_own, e_got, x, cot, live)


def fast_shards(
    tokens,
    ln1_gain,
    ln1_bias,
    ln2_gain,
    ln2_bias,
    w_qkv,
    b_qkv,
    w_out,
    b_out,
    w_up,
    b_up,
    w_down,
    b_down,
    lengths,
    block_map,
    cotangent,
):
    ctx = lax.axis_index("ctx")
    me = lax.axis_index("wsh")
    core = ctx % 2
    n_ctx = lax.axis_size("ctx")
    chips = n_ctx // 2
    own_rows, width = tokens.shape[1:]
    rows = 2 * own_rows
    half = width // 2
    quarter = half // 2
    seq = own_rows * n_ctx
    heads = H // 4
    hid = w_up.shape[1] // 4
    CORE, X, ZN, ZF = 0, 1, 2, 3

    def swap(v):
        return lax.ppermute(v, "wsh", SWAP)

    def flip(v, bit):
        return lax.ppermute(v, "ctx", [(i, i ^ (1 << bit)) for i in range(n_ctx)])

    def bit_of(bit):
        return (ctx >> bit) & 1

    ids = jnp.stack([me, core, bit_of(X), bit_of(ZN)]).astype(jnp.int32)

    def add(*terms):
        return sum(v.astype(f32) for v in terms).astype(bf16) if len(terms) > 1 else terms[0]

    def halve(terms, bit):
        b = bit_of(bit)
        cut = [v.reshape((2, v.shape[0] // 2) + v.shape[1:]) for v in terms]
        part = lambda k: [lax.dynamic_index_in_dim(v, k, 0, keepdims=False) for v in cut]
        return part(b) + [flip(add(*part(1 - b)), bit)]

    def ordered(first, a, b, axis=0):
        return jnp.where(first == 0, jnp.concatenate([a, b], axis), jnp.concatenate([b, a], axis))

    def double(v, bit):
        return ordered(bit_of(bit), v, flip(v, bit))

    def exchange(v):
        groups = [[2 * i + c for i in range(chips)] for c in range(2)]
        return lax.all_to_all(v, "ctx", 0, 0, axis_index_groups=groups, tiled=False)

    def rows_of(v, at, n, axis=0):
        return lax.dynamic_slice_in_dim(v, at, n, axis)

    x_own = tokens[0]
    x_got = swap(x_own)
    x_sib = flip(x_own, CORE)
    mine = me * half + core * quarter
    other = (1 - me) * half + core * quarter
    wq_send = jnp.concatenate([rows_of(w_qkv, p * width + other, quarter, 1) for p in range(3)], axis=1)
    wq_send, ln1_gain = lax.optimization_barrier((wq_send, ln1_gain))
    len_parts = jnp.stack([lengths[0] // 64, lengths[0] % 64]).astype(bf16)
    parts = [ln1_gain, ln1_bias, ln2_gain, ln2_bias, b_out, b_down, b_qkv, jnp.pad(len_parts, (0, half - 2))]
    small = jnp.concatenate([v.reshape(-1, half) for v in parts])
    small = ordered(me, small[None], swap(small)[None])
    wq_got = swap(wq_send)
    vec = lambda i: small[:, i].reshape(width).astype(f32)
    norms = jnp.stack([vec(i) for i in range(4)])
    bias_out = vec(4) + vec(5)
    qkv_bias = small[:, 6:9].astype(f32).reshape(3, width)
    qkv_bias = rows_of(qkv_bias, mine, quarter, 1).reshape(1, 3 * quarter)
    lens = small[:, 9, :2].astype(jnp.int32)
    lens = lens[:, 0] * 64 + lens[:, 1]
    other_len = lens[1 - me]

    normed = norm_rows(ids, x_own, x_sib, norms)
    cot_own = cotangent[0]
    wu_send = rows_of(w_up, ((1 - me) * 2 + core) * hid, hid, 1)
    wq_got, cot_send, normed = lax.optimization_barrier((wq_got, cot_own, normed))
    cot_got = swap(cot_send)
    cot_got, wu_send = lax.optimization_barrier((cot_got, wu_send))
    wu_got = swap(wu_send)
    normed = norm_rows(ids, x_got, flip(x_got, CORE), norms, normed)
    x2, attn_in, mlp_in = normed
    cot_sib = flip(cot_own, CORE)

    blocks = rows_of(block_map, (rows // HB) * (ctx // 2), rows // HB)
    offs = jnp.arange(HB, dtype=jnp.int32)
    positions = (blocks[:, None] * HB + offs[None, :]).reshape(rows)
    live2 = jnp.concatenate([positions < lengths[0], positions < other_len]).astype(f32)[:, None]
    live_own = rows_of(live2, core * own_rows, own_rows)
    freq = 10000.0 ** (-jnp.arange(ROT // 2, dtype=f32) * 2.0 / ROT)
    ang = freq[:, None] * jnp.arange(seq, dtype=jnp.int32).astype(f32)[None, :]
    table = jnp.concatenate([jnp.cos(ang), jnp.sin(ang)])
    own_ang = freq[:, None] * positions.astype(f32)[None, :]
    own_table = jnp.concatenate([jnp.cos(own_ang), jnp.sin(own_ang)])

    attn_in, table = lax.optimization_barrier((attn_in, table))
    send = qkv_forward(ids, attn_in, w_qkv, wq_got, qkv_bias, own_table)
    qkv_head = exchange(send.reshape(2 * heads, 3 * HD, rows))
    dy = mask_rows(ids, cot_own, cot_sib, cot_got, flip(cot_got, CORE), live2)
    dy2 = dy.reshape(2, rows, width)
    w_out_mine = rows_of(w_out, core * quarter, quarter)
    dctx = jnp.einsum("ed,std->set", w_out_mine, dy2, preferred_element_type=f32).astype(bf16)
    attn_t, mlp_t = turn(attn_in, mlp_in)
    do_head = exchange(dctx.reshape(2 * heads, HD, rows))
    y_mlp, d_mlp, up_keep, up_send, down_keep, down_send, gb_up = mlp(
        ids, mlp_in, mlp_t, dy, w_up, wu_got, w_down, b_up.astype(f32)[None, :], chips
    )

    chain_a = (X, ZN, ZF)
    chain_b = (ZN, ZF, X)
    qkv_head, up_send, down_send = lax.optimization_barrier((qkv_head, up_send, down_send))
    down = [down_keep, flip(down_send, chain_a[0])]
    up = [up_keep, flip(up_send, chain_b[0])]

    o_head, lse = attn_fwd(block_map, qkv_head, bq=1024, bk=1024)
    qkv_head, o_head, do_head, down[-1], up[-1] = lax.optimization_barrier((qkv_head, o_head, do_head, down[-1], up[-1]))
    ob = exchange(o_head).reshape(2, quarter, rows)
    down = halve(down, chain_a[1])
    up = halve(up, chain_b[1])
    g_head = attn_bwd(block_map, qkv_head, o_head, do_head, lse, table)
    g_head, ob, down[-1], up[-1] = lax.optimization_barrier((g_head, ob, down[-1], up[-1]))
    d_qkv = exchange(g_head).reshape(2, heads, 3 * HD, rows)

    down = add(*halve(down, chain_a[2]))
    up = add(*halve(up, chain_b[2]))
    up = up.reshape(1, 2, up.shape[1] // 2, up.shape[2])
    up_keep = rows_of(up, me, 1, 1)
    up_got = swap(rows_of(up, 1 - me, 1, 1))
    up = ordered(me, up_keep, up_got, axis=1)
    for a, b in zip(chain_a[::-1], chain_b[::-1]):
        down = double(down, a)
        up = double(up, b)
    tot_down = join_rows(ids, down, flip(down, CORE))
    tot_up = join_cols(ids, up, flip(up, CORE))

    def settle(v):
        give = rows_of(v, (1 - core) * own_rows, own_rows, 1).astype(bf16)
        v = rows_of(v, core * own_rows, own_rows, 1) + flip(give, CORE).astype(f32)
        return v[0], swap(v[1].astype(bf16))

    part = jnp.einsum("sct,cd->std", ob, w_out_mine, preferred_element_type=f32) + y_mlp.reshape(2, rows, width).astype(f32)
    part, part_got = settle(part)
    output = (live_own * (x_own.astype(f32) + part + part_got.astype(f32) + bias_out)).astype(bf16)

    v_a, v_b, e = qkv_backward(
        ids, d_qkv, attn_t, x2, norms, w_qkv, wq_got, d_mlp, ob, dy, gb_up, chips
    )
    v_a = [v_a]
    v_b = [v_b]
    for a, b in zip(chain_a, chain_b):
        v_a = halve(v_a, a)
        v_b = halve(v_b, b)
    e_own, e_got = settle(e)
    n3 = 3 * half // (2 * chips)
    size = 2 * n3 + width // (2 * chips)
    tail = []
    for v in (add(*v_a)[0], add(*v_b)[0]):
        extra = v[size:]
        back = swap(jnp.concatenate([rows_of(v, (1 - me) * n3, n3), extra]))
        extra = add(extra, back[n3:])
        tail.append(jnp.concatenate([ordered(me, rows_of(v, me * n3, n3), back[:n3]), v[2 * n3 : size], extra])[None])
    grad_tokens = last(e_own, e_got, x_own, cot_own, live_own)
    cover = [[tot_down], [tot_up], [grad_tokens, output]]
    for k, (a, b) in enumerate(zip(chain_a[::-1], chain_b[::-1])):
        tail = [double(tail[0], a), double(tail[1], b)]
        tail, cover[k] = lax.optimization_barrier((tail, cover[k]))
    mixed = tail
    (tot_down,), (tot_up,), (grad_tokens, output) = cover
    tot_qkv, tot_out, flat = unpack(ids, mixed[0], flip(mixed[0], CORE), mixed[1], flip(mixed[1], CORE), width)
    flat = flat[:, :6].reshape(12 * width)

    def own(start, size):
        return lax.dynamic_slice_in_dim(flat, start + me * size, size)

    gb_out = own(4 * width, half)
    return (
        output[None],
        grad_tokens[None],
        own(0, half),
        own(width, half),
        own(2 * width, half),
        own(3 * width, half),
        tot_qkv,
        own(5 * width, 3 * half),
        tot_out.reshape(half, width),
        gb_out,
        tot_up,
        own(8 * width, 2 * hid),
        tot_down,
        gb_out,
    )


def solution(mesh):
    placed = (
        P("wsh", "ctx", None),
        P("wsh"),
        P("wsh"),
        P("wsh"),
        P("wsh"),
        P("wsh", None),
        P("wsh"),
        P("wsh", None),
        P("wsh"),
        P("wsh", None),
        P("wsh"),
        P("wsh", None),
        P("wsh"),
        P("wsh"),
        P(),
        P("wsh", "ctx", None),
    )
    body = fast_shards if fast_fits(mesh) else shards
    return jax.shard_map(
        body,
        mesh=mesh,
        in_specs=placed,
        out_specs=(
            P("wsh", "ctx", None),
            P("wsh", "ctx", None),
            P("wsh"),
            P("wsh"),
            P("wsh"),
            P("wsh"),
            P("wsh", None),
            P("wsh"),
            P("wsh", None),
            P("wsh"),
            P("wsh", None),
            P("wsh"),
            P("wsh", None),
            P("wsh"),
        ),
        check_vma=False,
    )
```

```python
from functools import partial
import math

import jax
import jax.numpy as jnp
from jax import lax
from jax.experimental import pallas as pl
from jax.experimental.pallas import tpu as pltpu
from jax.sharding import PartitionSpec as P

H = 16
HD = 64
ROT = 16


epsilon = 1e-05


def norm_forward(values, norm_gain, norm_shift):
    average = jnp.mean(values, axis=-1, keepdims=True)
    centred = values - average
    variance = jnp.mean(centred * centred, axis=-1, keepdims=True)
    inverse = lax.rsqrt(variance + epsilon)
    normed = centred * inverse
    return (normed * norm_gain + norm_shift, normed, inverse)


def norm_backward(grad_out, normed, inverse, norm_gain):
    scaled = grad_out * norm_gain
    adjusted = (
        scaled
        - jnp.mean(scaled, axis=-1, keepdims=True)
        - normed * jnp.mean(scaled * normed, axis=-1, keepdims=True)
    )
    return (adjusted * inverse, jnp.sum(grad_out * normed, axis=0), jnp.sum(grad_out, axis=0))


def rotary_tables(positions):
    half_rot = ROT // 2
    frequency = 10000.0 ** (-jnp.arange(half_rot, dtype=jnp.float32) * 2.0 / ROT)
    angles = positions.astype(jnp.float32)[:, None] * frequency[None, :]
    return (jnp.cos(angles)[:, None, :], jnp.sin(angles)[:, None, :])


def rotate_forward(values, cosine_table, sine_table):
    half_rot = ROT // 2
    leading = values[..., :half_rot]
    trailing = values[..., half_rot:ROT]
    return jnp.concatenate(
        [
            leading * cosine_table - trailing * sine_table,
            trailing * cosine_table + leading * sine_table,
            values[..., ROT:],
        ],
        axis=-1,
    )


def rotate_backward(grads, cosine_table, sine_table):
    half_rot = ROT // 2
    leading = grads[..., :half_rot]
    trailing = grads[..., half_rot:ROT]
    return jnp.concatenate(
        [
            leading * cosine_table + trailing * sine_table,
            trailing * cosine_table - leading * sine_table,
            grads[..., ROT:],
        ],
        axis=-1,
    )


def masked_scores(query_rows, key_rows, query_pos, key_pos, key_live):
    raw_scores = jnp.einsum(
        "qhd,khd->hqk", query_rows, key_rows, preferred_element_type=jnp.float32
    )
    allowed = (key_pos[None, :] <= query_pos[:, None]) & key_live[None, :]
    return (jnp.where(allowed[None], raw_scores * (1.0 / math.sqrt(HD)), -1e30), allowed)


def score_grads(
    query_rows, key_rows, value_rows, grad_rows, query_pos, key_pos, key_live, log_total, row_dots
):
    scores = masked_scores(query_rows, key_rows, query_pos, key_pos, key_live)[0]
    probability = jnp.exp(scores - log_total[..., None])
    grad_prob = jnp.einsum(
        "qhd,khd->hqk", grad_rows, value_rows, preferred_element_type=jnp.float32
    )
    grad_score = (probability * (grad_prob - row_dots[..., None]) * (1.0 / math.sqrt(HD))).astype(
        jnp.bfloat16
    )
    return (probability.astype(jnp.bfloat16), grad_score)


def shards(
    tokens,
    ln1_gain,
    ln1_bias,
    ln2_gain,
    ln2_bias,
    w_qkv,
    b_qkv,
    w_out,
    b_out,
    w_up,
    b_up,
    w_down,
    b_down,
    lengths,
    block_map,
    cotangent,
):
    gathered = (
        lax.all_gather(ln1_gain, "wsh", axis=0, tiled=True),
        lax.all_gather(ln1_bias, "wsh", axis=0, tiled=True),
        lax.all_gather(ln2_gain, "wsh", axis=0, tiled=True),
        lax.all_gather(ln2_bias, "wsh", axis=0, tiled=True),
        lax.all_gather(w_qkv, "wsh", axis=0, tiled=True),
        lax.all_gather(b_qkv, "wsh", axis=0, tiled=True),
        lax.all_gather(w_out, "wsh", axis=0, tiled=True),
        lax.all_gather(b_out, "wsh", axis=0, tiled=True),
        lax.all_gather(w_up, "wsh", axis=0, tiled=True),
        lax.all_gather(b_up, "wsh", axis=0, tiled=True),
        lax.all_gather(w_down, "wsh", axis=0, tiled=True),
        lax.all_gather(b_down, "wsh", axis=0, tiled=True),
    )
    (
        norm1_gain,
        norm1_shift,
        norm2_gain,
        norm2_shift,
        qkv_weight,
        qkv_bias,
        out_weight,
        out_bias,
        up_weight,
        up_bias,
        down_weight,
        down_bias,
    ) = gathered
    tok_rows = tokens.shape[1]
    model_width = tokens.shape[2]
    half_rows = tok_rows // 2
    seq_rows = tok_rows * lax.axis_size("ctx")
    head_count = H
    head_size = HD
    ctx_index = lax.axis_index("ctx")
    own_blocks = lax.dynamic_slice_in_dim(block_map, 2 * ctx_index, 2)
    local_offsets = jnp.arange(half_rows, dtype=jnp.int32)
    positions = (own_blocks[:, None] * half_rows + local_offsets[None, :]).reshape(tok_rows)
    key_pos = (block_map[:, None] * half_rows + local_offsets[None, :]).reshape(seq_rows)
    length = lengths[0]
    own_live = positions < length
    live_rows = own_live.astype(jnp.float32)
    key_live = key_pos < length
    gain_first = norm1_gain.astype(jnp.float32)
    gain_second = norm2_gain.astype(jnp.float32)
    token_rows = tokens[0].astype(jnp.float32)
    normal_first, normed_first, inverse_first = norm_forward(
        token_rows, gain_first, norm1_shift.astype(jnp.float32)
    )
    normal_second, normed_second, inverse_second = norm_forward(
        token_rows, gain_second, norm2_shift.astype(jnp.float32)
    )
    attn_in = normal_first.astype(jnp.bfloat16)
    mlp_in = normal_second.astype(jnp.bfloat16)
    projected = (
        jnp.dot(attn_in, qkv_weight, preferred_element_type=jnp.float32)
        + qkv_bias.astype(jnp.float32)
    ).reshape(tok_rows, 3, head_count, head_size)
    cosine_table, sine_table = rotary_tables(positions)
    queries = rotate_forward(projected[:, 0], cosine_table, sine_table).astype(jnp.bfloat16)
    key_own = (
        rotate_forward(projected[:, 1], cosine_table, sine_table)
        .astype(jnp.bfloat16)
        .reshape(tok_rows, model_width)
    )
    value_own = projected[:, 2].astype(jnp.bfloat16).reshape(tok_rows, model_width)
    keys_all, values_all = (
        lax.all_gather(key_own, "ctx", axis=0, tiled=True),
        lax.all_gather(value_own, "ctx", axis=0, tiled=True),
    )
    block_len = math.gcd(seq_rows, 1024)
    block_count = seq_rows // block_len
    key_stack = keys_all.reshape(block_count, block_len, head_count, head_size)
    value_stack = values_all.reshape(block_count, block_len, head_count, head_size)
    pos_stack = key_pos.reshape(block_count, block_len)
    live_stack = key_live.reshape(block_count, block_len)

    def stats_step(running, key_part):
        key_block, pos_block, live_block = key_part
        scores, allowed = masked_scores(queries, key_block, positions, pos_block, live_block)
        peak_score = jnp.maximum(running[0], jnp.max(scores, axis=-1))
        exp_total = running[1] * jnp.exp(running[0] - peak_score) + jnp.sum(
            jnp.where(allowed[None], jnp.exp(scores - peak_score[..., None]), 0.0), axis=-1
        )
        return ((peak_score, exp_total), None)

    start_peak = jnp.full((head_count, tok_rows), -1e30, jnp.float32)
    final_state = lax.scan(
        stats_step, (start_peak, jnp.zeros_like(start_peak)), (key_stack, pos_stack, live_stack)
    )[0]
    log_total = final_state[0] + jnp.log(final_state[1])

    def value_step(running, key_part):
        key_block, value_block, pos_block, live_block = key_part
        scores = masked_scores(queries, key_block, positions, pos_block, live_block)[0]
        probability = jnp.exp(scores - log_total[..., None]).astype(jnp.bfloat16)
        return (
            running
            + jnp.einsum(
                "hqk,khd->qhd", probability, value_block, preferred_element_type=jnp.float32
            ),
            None,
        )

    zero_heads = jnp.zeros((tok_rows, head_count, head_size), jnp.float32)
    attended = lax.scan(value_step, zero_heads, (key_stack, value_stack, pos_stack, live_stack))[0]
    context_low = attended.reshape(tok_rows, model_width).astype(jnp.bfloat16)
    hidden = jnp.dot(mlp_in, up_weight, preferred_element_type=jnp.float32) + up_bias.astype(
        jnp.float32
    )
    activated, gelu_pull = jax.vjp(partial(jax.nn.gelu, approximate=False), hidden)
    act_low = activated.astype(jnp.bfloat16)
    branch = (
        jnp.dot(context_low, out_weight, preferred_element_type=jnp.float32)
        + out_bias.astype(jnp.float32)
        + jnp.dot(act_low, down_weight, preferred_element_type=jnp.float32)
        + down_bias.astype(jnp.float32)
    )
    output_rows = (live_rows[:, None] * (token_rows + branch)).astype(jnp.bfloat16)
    cot_rows = cotangent[0].astype(jnp.float32)
    grad_branch = (live_rows[:, None] * cot_rows).astype(jnp.bfloat16)
    grad_w_out = jnp.einsum(
        "tc,td->cd", context_low, grad_branch, preferred_element_type=jnp.float32
    )
    grad_w_down = jnp.einsum("tc,td->cd", act_low, grad_branch, preferred_element_type=jnp.float32)
    grad_branch_sum = jnp.sum(grad_branch.astype(jnp.float32), axis=0)
    grad_act = jnp.einsum("td,cd->tc", grad_branch, down_weight, preferred_element_type=jnp.float32)
    grad_hidden = gelu_pull(grad_act)[0].astype(jnp.bfloat16)
    grad_w_up = jnp.einsum("tc,td->cd", mlp_in, grad_hidden, preferred_element_type=jnp.float32)
    grad_b_up = jnp.sum(grad_hidden.astype(jnp.float32), axis=0)
    grad_mlp_in = jnp.einsum(
        "td,cd->tc", grad_hidden, up_weight, preferred_element_type=jnp.float32
    )
    grad_context = jnp.einsum(
        "td,cd->tc", grad_branch, out_weight, preferred_element_type=jnp.float32
    ).astype(jnp.bfloat16)
    grad_heads = grad_context.reshape(tok_rows, head_count, head_size)
    row_dots = jnp.sum(grad_heads.astype(jnp.float32) * attended, axis=-1).T

    def grad_step(running, key_part):
        key_block, value_block, pos_block, live_block = key_part
        prob_low, grad_score = score_grads(
            queries,
            key_block,
            value_block,
            grad_heads,
            positions,
            pos_block,
            live_block,
            log_total,
            row_dots,
        )
        query_sum = running + jnp.einsum(
            "hqk,khd->qhd", grad_score, key_block, preferred_element_type=jnp.float32
        )
        key_term = jnp.einsum(
            "hqk,qhd->khd", grad_score, queries, preferred_element_type=jnp.float32
        )
        value_term = jnp.einsum(
            "hqk,qhd->khd", prob_low, grad_heads, preferred_element_type=jnp.float32
        )
        return (query_sum, (key_term, value_term))

    query_grad, term_stacks = lax.scan(
        grad_step, zero_heads, (key_stack, value_stack, pos_stack, live_stack)
    )
    key_grad, value_grad = (
        lax.psum_scatter(
            term_stacks[0].reshape(seq_rows, model_width).astype(jnp.bfloat16),
            "ctx",
            scatter_dimension=0,
            tiled=True,
        ).astype(jnp.float32),
        lax.psum_scatter(
            term_stacks[1].reshape(seq_rows, model_width).astype(jnp.bfloat16),
            "ctx",
            scatter_dimension=0,
            tiled=True,
        ).astype(jnp.float32),
    )
    key_grad = key_grad.reshape(tok_rows, head_count, head_size)
    value_grad = value_grad.reshape(tok_rows, head_count, head_size)
    grad_projected = (
        jnp.stack(
            [
                rotate_backward(query_grad, cosine_table, sine_table),
                rotate_backward(key_grad, cosine_table, sine_table),
                value_grad,
            ],
            axis=1,
        )
        .reshape(tok_rows, 3 * model_width)
        .astype(jnp.bfloat16)
    )
    grad_w_qkv = jnp.einsum(
        "tc,td->cd", attn_in, grad_projected, preferred_element_type=jnp.float32
    )
    grad_b_qkv = jnp.sum(grad_projected.astype(jnp.float32), axis=0)
    grad_attn_in = jnp.einsum(
        "td,cd->tc", grad_projected, qkv_weight, preferred_element_type=jnp.float32
    )
    grad_input_first, grad_gain_first, grad_shift_first = norm_backward(
        grad_attn_in, normed_first, inverse_first, gain_first
    )
    grad_input_second, grad_gain_second, grad_shift_second = norm_backward(
        grad_mlp_in, normed_second, inverse_second, gain_second
    )
    grad_input = live_rows[:, None] * cot_rows + grad_input_first + grad_input_second
    shares = (
        lax.psum_scatter(
            grad_gain_first.astype(jnp.bfloat16), "wsh", scatter_dimension=0, tiled=True
        ).astype(jnp.float32),
        lax.psum_scatter(
            grad_shift_first.astype(jnp.bfloat16), "wsh", scatter_dimension=0, tiled=True
        ).astype(jnp.float32),
        lax.psum_scatter(
            grad_gain_second.astype(jnp.bfloat16), "wsh", scatter_dimension=0, tiled=True
        ).astype(jnp.float32),
        lax.psum_scatter(
            grad_shift_second.astype(jnp.bfloat16), "wsh", scatter_dimension=0, tiled=True
        ).astype(jnp.float32),
        lax.psum_scatter(
            grad_w_qkv.astype(jnp.bfloat16), "wsh", scatter_dimension=0, tiled=True
        ).astype(jnp.float32),
        lax.psum_scatter(
            grad_b_qkv.astype(jnp.bfloat16), "wsh", scatter_dimension=0, tiled=True
        ).astype(jnp.float32),
        lax.psum_scatter(
            grad_w_out.astype(jnp.bfloat16), "wsh", scatter_dimension=0, tiled=True
        ).astype(jnp.float32),
        lax.psum_scatter(
            grad_branch_sum.astype(jnp.bfloat16), "wsh", scatter_dimension=0, tiled=True
        ).astype(jnp.float32),
        lax.psum_scatter(
            grad_w_up.astype(jnp.bfloat16), "wsh", scatter_dimension=0, tiled=True
        ).astype(jnp.float32),
        lax.psum_scatter(
            grad_b_up.astype(jnp.bfloat16), "wsh", scatter_dimension=0, tiled=True
        ).astype(jnp.float32),
        lax.psum_scatter(
            grad_w_down.astype(jnp.bfloat16), "wsh", scatter_dimension=0, tiled=True
        ).astype(jnp.float32),
        lax.psum_scatter(
            grad_branch_sum.astype(jnp.bfloat16), "wsh", scatter_dimension=0, tiled=True
        ).astype(jnp.float32),
    )
    totals = (
        lax.psum(shares[0].astype(jnp.bfloat16), "ctx").astype(jnp.float32),
        lax.psum(shares[1].astype(jnp.bfloat16), "ctx").astype(jnp.float32),
        lax.psum(shares[2].astype(jnp.bfloat16), "ctx").astype(jnp.float32),
        lax.psum(shares[3].astype(jnp.bfloat16), "ctx").astype(jnp.float32),
        lax.psum(shares[4].astype(jnp.bfloat16), "ctx").astype(jnp.float32),
        lax.psum(shares[5].astype(jnp.bfloat16), "ctx").astype(jnp.float32),
        lax.psum(shares[6].astype(jnp.bfloat16), "ctx").astype(jnp.float32),
        lax.psum(shares[7].astype(jnp.bfloat16), "ctx").astype(jnp.float32),
        lax.psum(shares[8].astype(jnp.bfloat16), "ctx").astype(jnp.float32),
        lax.psum(shares[9].astype(jnp.bfloat16), "ctx").astype(jnp.float32),
        lax.psum(shares[10].astype(jnp.bfloat16), "ctx").astype(jnp.float32),
        lax.psum(shares[11].astype(jnp.bfloat16), "ctx").astype(jnp.float32),
    )
    return (
        output_rows[None],
        grad_input[None],
        totals[0],
        totals[1],
        totals[2],
        totals[3],
        totals[4],
        totals[5],
        totals[6],
        totals[7],
        totals[8],
        totals[9],
        totals[10],
        totals[11],
    )


HB = 128
NEG=-1e30
f32=jnp.float32; bf16=jnp.bfloat16

def _nn(a,b): return lax.dot_general(a,b,(((1,),(0,)),((),())),preferred_element_type=f32)
def _nt(a,b): return lax.dot_general(a,b,(((1,),(1,)),((),())),preferred_element_type=f32)

def attn_fwd_kernel(bm, x_ref, o_ref, lse_ref, q_s, kt_s, v_s, *, nblk, per, bq, bk):
    def perm(i,_):
        p=bm[i]; c=i//per; l=pl.multiple_of((i%per)*HB,HB); d=pl.multiple_of(p*HB,HB)
        q_s[:,pl.ds(d,HB)]=x_ref[c,0:64,pl.ds(l,HB)]*bf16(0.125)
        kt_s[pl.ds(d,HB),:]=x_ref[c,64:128,pl.ds(l,HB)].astype(f32).T.astype(bf16)
        v_s[:,pl.ds(d,HB)]=x_ref[c,128:192,pl.ds(l,HB)]
        return 0
    lax.fori_loop(0,nblk,perm,0,unroll=32)
    S=nblk*HB; nq=S//bq; r=bq//bk
    def step(q,qo,ko,carry,mask):
        m,l,acc=carry
        s=_nn(kt_s[pl.ds(ko,bk),:],q)
        if mask is not None: s=jnp.where(mask,s,NEG)
        mn=jnp.maximum(m,jnp.max(s,axis=0,keepdims=True))
        a=jnp.exp(m-mn); p=jnp.exp(s-mn)
        l=l*a+jnp.sum(p,axis=0,keepdims=True)
        acc=acc*a+_nn(v_s[:,pl.ds(ko,bk)],p.astype(bf16))
        return mn,l,acc
    ki=lax.broadcasted_iota(jnp.int32,(bk,bq),0); qi_=lax.broadcasted_iota(jnp.int32,(bk,bq),1)
    def qloop(i,_):
        qo=pl.multiple_of(i*bq,bq)
        q=q_s[:,pl.ds(qo,bq)]
        c=(jnp.full((1,bq),NEG,f32),jnp.zeros((1,bq),f32),jnp.zeros((64,bq),f32))
        c=lax.fori_loop(0,i*r,lambda j,c: step(q,qo,pl.multiple_of(j*bk,bk),c,None),c)
        for t in range(r):
            c=step(q,qo,pl.multiple_of(qo+t*bk,bk),c,ki+t*bk<=qi_)
        m,l,acc=c
        q_s[:,pl.ds(qo,bq)]=(acc*(1.0/l)).astype(bf16)
        lse_ref[:,pl.ds(qo,bq)]=m+jnp.log(l)
        return 0
    lax.fori_loop(0,nq,qloop,0)
    def unperm(i,_):
        p=bm[i]; c=i//per; l=pl.multiple_of((i%per)*HB,HB); d=pl.multiple_of(p*HB,HB)
        o_ref[c,:,pl.ds(l,HB)]=q_s[:,pl.ds(d,HB)]
        return 0
    lax.fori_loop(0,nblk,unperm,0,unroll=32)

def attn_fwd(bm,x,*,bq=512,bk=512):
    n=x.shape[0]; S=n*x.shape[2]; nblk=S//HB
    bq=math.gcd(S,bq); bk=math.gcd(bq,bk)
    return pl.pallas_call(
        lambda *a: attn_fwd_kernel(*a,nblk=nblk,per=x.shape[2]//HB,bq=bq,bk=bk),
        out_shape=(jax.ShapeDtypeStruct((n,64,x.shape[2]),bf16),jax.ShapeDtypeStruct((1,S),f32)),
        in_specs=[pl.BlockSpec(memory_space=pltpu.SMEM),pl.BlockSpec(memory_space=pltpu.VMEM)],
        out_specs=(pl.BlockSpec(memory_space=pltpu.VMEM),pl.BlockSpec(memory_space=pltpu.VMEM)),
        scratch_shapes=[pltpu.VMEM((64,S),bf16),pltpu.VMEM((S,64),bf16),pltpu.VMEM((64,S),bf16)],
        compiler_params=pltpu.CompilerParams(vmem_limit_bytes=56<<20),name="attn_fwd")(bm,x)

def attn_bwd_kernel(bm, x_ref, o_ref, do_ref, lse_ref, cs_ref, g_ref, q_s, kt_s, k_s, vt_s, do_s, dl_s, dq_s, dk_s, dv_s, *, nblk, per, bq, bk):
    def perm(i,_):
        p=bm[i]; c=i//per; l=pl.multiple_of((i%per)*HB,HB); d=pl.multiple_of(p*HB,HB)
        q_s[:,pl.ds(d,HB)]=x_ref[c,0:64,pl.ds(l,HB)]*bf16(0.125)
        k=x_ref[c,64:128,pl.ds(l,HB)]
        k_s[:,pl.ds(d,HB)]=k*bf16(0.125)
        kt_s[pl.ds(d,HB),:]=k.astype(f32).T.astype(bf16)
        vt_s[pl.ds(d,HB),:]=x_ref[c,128:192,pl.ds(l,HB)].astype(f32).T.astype(bf16)
        do=do_ref[c,:,pl.ds(l,HB)]
        do_s[:,pl.ds(d,HB)]=do
        dl_s[:,pl.ds(d,HB)]=jnp.sum(do.astype(f32)*o_ref[c,:,pl.ds(l,HB)].astype(f32),axis=0,keepdims=True)
        return 0
    lax.fori_loop(0,nblk,perm,0,unroll=32)
    S=nblk*HB; nq=S//bq; r=bq//bk
    dk_s[...]=jnp.zeros_like(dk_s); dv_s[...]=jnp.zeros_like(dv_s)
    def step(q,do,lse,dl,ko,dq,mask):
        s=_nn(kt_s[pl.ds(ko,bk),:],q)
        p=jnp.exp(s-lse)
        if mask is not None: p=jnp.where(mask,p,0.0)
        dp=_nn(vt_s[pl.ds(ko,bk),:],do)
        ds=(p*(dp-dl)).astype(bf16)
        pb=p.astype(bf16)
        dv_s[:,pl.ds(ko,bk)]+=_nt(do,pb)
        dk_s[:,pl.ds(ko,bk)]+=_nt(q,ds)
        return dq+_nn(k_s[:,pl.ds(ko,bk)],ds)
    ki=lax.broadcasted_iota(jnp.int32,(bk,bq),0); qi_=lax.broadcasted_iota(jnp.int32,(bk,bq),1)
    def qloop(i,_):
        qo=pl.multiple_of(i*bq,bq)
        q=q_s[:,pl.ds(qo,bq)]; do=do_s[:,pl.ds(qo,bq)]; lse=lse_ref[:,pl.ds(qo,bq)]; dl=dl_s[:,pl.ds(qo,bq)]
        dq=jnp.zeros((64,bq),f32)
        dq=lax.fori_loop(0,i*r,lambda j,c: step(q,do,lse,dl,pl.multiple_of(j*bk,bk),c,None),dq)
        for t in range(r):
            dq=step(q,do,lse,dl,pl.multiple_of(qo+t*bk,bk),dq,ki+t*bk<=qi_)
        dq_s[:,pl.ds(qo,bq)]=dq
        return 0
    lax.fori_loop(0,nq,qloop,0)
    def unperm(i,_):
        p=bm[i]; c=i//per; l=pl.multiple_of((i%per)*HB,HB); d=pl.multiple_of(p*HB,HB)
        cos=cs_ref[0:8,pl.ds(d,HB)]; sin=cs_ref[8:16,pl.ds(d,HB)]
        for n_,src in ((0,dq_s),(1,dk_s)):
            g=src[:,pl.ds(d,HB)]
            a=g[0:8]; b=g[8:16]
            full=jnp.concatenate([a*cos+b*sin,b*cos-a*sin,g[16:64]],axis=0)
            g_ref[c,64*n_:64*n_+64,pl.ds(l,HB)]=full.astype(bf16)
        g_ref[c,128:192,pl.ds(l,HB)]=dv_s[:,pl.ds(d,HB)].astype(bf16)
        return 0
    lax.fori_loop(0,nblk,unperm,0,unroll=32)

def attn_bwd(bm,x,o,do,lse,cs,*,bq=512,bk=512):
    n=x.shape[0]; S=n*x.shape[2]; nblk=S//HB
    bq=math.gcd(S,bq); bk=math.gcd(bq,bk)
    vm=pl.BlockSpec(memory_space=pltpu.VMEM)
    return pl.pallas_call(
        lambda *a: attn_bwd_kernel(*a,nblk=nblk,per=x.shape[2]//HB,bq=bq,bk=bk),
        out_shape=jax.ShapeDtypeStruct((n,192,x.shape[2]),bf16),
        in_specs=[pl.BlockSpec(memory_space=pltpu.SMEM)]+[vm]*5,
        out_specs=vm,
        scratch_shapes=[pltpu.VMEM((64,S),bf16),pltpu.VMEM((S,64),bf16),pltpu.VMEM((64,S),bf16),pltpu.VMEM((S,64),bf16),pltpu.VMEM((64,S),bf16),
                        pltpu.VMEM((1,S),f32),pltpu.VMEM((64,S),f32),pltpu.VMEM((64,S),f32),pltpu.VMEM((64,S),f32)],
        compiler_params=pltpu.CompilerParams(vmem_limit_bytes=56<<20),name="attn_bwd")(bm,x,o,do,lse,cs)


SWAP = [(0, 1), (1, 0)]


def fast_fits(mesh):
    return mesh.shape["wsh"] == 2 and mesh.shape["ctx"] == H


def _params(mb=56):
    return pltpu.CompilerParams(vmem_limit_bytes=mb << 20)


def _norm(x):
    xf = x.astype(f32)
    cen = xf - jnp.mean(xf, axis=-1, keepdims=True)
    inv = lax.rsqrt(jnp.mean(cen * cen, axis=-1, keepdims=True) + epsilon)
    return cen * inv, inv


def _full(v):
    return pl.BlockSpec(v.shape, lambda *a: (0,) * v.ndim)


def _wq_specs(half, width, cols, quarter, at):
    own = lambda p: pl.BlockSpec(
        (half, cols),
        lambda *a: (0, p * (width // cols) + a[-1][0] * (half // cols) + a[-1][1] * (quarter // cols) + at(*a)),
    )
    got = lambda p: pl.BlockSpec((half, cols), lambda *a: (0, p * (quarter // cols) + at(*a)))
    return [own(p) for p in range(3)] + [got(p) for p in range(3)]


def norm_kernel(ids, a_ref, b_ref, n_ref, *refs):
    x_ref, ain_ref, min_ref = refs[-3:]
    mine = pl.program_id(0) == ids[1]
    x = jnp.where(mine, a_ref[...].astype(f32), b_ref[...].astype(f32))
    x_ref[...] = x.astype(bf16)
    xhat, _ = _norm(x)
    ain_ref[...] = (xhat * n_ref[0:1, :] + n_ref[1:2, :]).astype(bf16)
    min_ref[...] = (xhat * n_ref[2:3, :] + n_ref[3:4, :]).astype(bf16)


def norm_rows(ids, a, b, norms, before=()):
    rows, width = a.shape
    slot = 2 if before else 0
    out = jax.ShapeDtypeStruct((4 * rows, width), bf16)
    return pl.pallas_call(
        norm_kernel,
        grid_spec=pltpu.PrefetchScalarGridSpec(
            num_scalar_prefetch=1,
            grid=(2,),
            in_specs=[_full(a), _full(b), _full(norms)] + [pl.BlockSpec(memory_space=pl.ANY)] * len(before),
            out_specs=(pl.BlockSpec((rows, width), lambda i, ids: (slot + i, 0)),) * 3,
        ),
        out_shape=(out,) * 3,
        input_output_aliases={4 + k: k for k in range(len(before))},
        compiler_params=_params(),
        cost_estimate=pl.CostEstimate(flops=0, transcendentals=0, bytes_accessed=1 << 20),
        name="norm_rows",
    )(ids, a, b, norms, *before)


def turn_kernel(a_ref, b_ref, at_ref, bt_ref):
    at_ref[...] = a_ref[...].astype(f32).T.astype(bf16)
    bt_ref[...] = b_ref[...].astype(f32).T.astype(bf16)


def turn(a, b, steps=4):
    rows, width = a.shape
    src = pl.BlockSpec((rows // steps, width), lambda i: (i, 0))
    dst = pl.BlockSpec((width, rows // steps), lambda i: (0, i))
    return pl.pallas_call(
        turn_kernel,
        grid=(steps,),
        in_specs=[src, src],
        out_specs=(dst, dst),
        out_shape=(jax.ShapeDtypeStruct((width, rows), a.dtype),) * 2,
        compiler_params=_params(),
        cost_estimate=pl.CostEstimate(flops=0, transcendentals=0, bytes_accessed=1 << 20),
        name="turn",
    )(a, b)


def mask_kernel(ids, a_ref, b_ref, c_ref, d_ref, live_ref, w_ref, o_ref, f_ref):
    i = pl.program_id(0)
    mine = (i % 2) == ids[1]
    for slot, (own, sib) in enumerate(((a_ref, b_ref), (c_ref, d_ref))):
        @pl.when((i // 2) == slot)
        def _(own=own, sib=sib):
            v = jnp.where(mine, own[...].astype(f32), sib[...].astype(f32))
            o_ref[...] = (live_ref[...] * v).astype(bf16)

    f = _nt(w_ref[...], o_ref[...]).astype(bf16)
    for k in range(f_ref.shape[0]):
        f_ref[k] = f[k * HD : (k + 1) * HD, :]


def mask_rows(ids, own, own_sib, got, got_sib, live, w_out, quarter):
    rows, width = own.shape
    heads = quarter // HD
    return pl.pallas_call(
        mask_kernel,
        grid_spec=pltpu.PrefetchScalarGridSpec(
            num_scalar_prefetch=1,
            grid=(4,),
            in_specs=[_full(v) for v in (own, own_sib, got, got_sib)]
            + [
                pl.BlockSpec((rows, 1), lambda i, ids: (i, 0)),
                pl.BlockSpec((quarter, width), lambda i, ids: (ids[1], 0)),
            ],
            out_specs=(
                pl.BlockSpec((rows, width), lambda i, ids: (i, 0)),
                pl.BlockSpec((heads, HD, rows), lambda i, ids: (i // 2, 0, i % 2)),
            ),
        ),
        out_shape=(
            jax.ShapeDtypeStruct((4 * rows, width), bf16),
            jax.ShapeDtypeStruct((2 * heads, HD, 2 * rows), bf16),
        ),
        compiler_params=_params(),
        cost_estimate=pl.CostEstimate(flops=0, transcendentals=0, bytes_accessed=1 << 20),
        name="mask_rows",
    )(ids, own, own_sib, got, got_sib, live, w_out)


def qkv_kernel(
    ids, ain_ref, wq_ref, wk_ref, wv_ref, gq_ref, gk_ref, gv_ref, bq_ref, bk_ref, bv_ref, cs_ref, send_ref
):
    width = ain_ref.shape[1]
    half = width // 2
    me = ids[0]
    a_own = ain_ref[:, pl.ds(pl.multiple_of(me * half, half), half)]
    a_got = ain_ref[:, pl.ds(pl.multiple_of((1 - me) * half, half), half)]
    cos = cs_ref[0:8, :]
    sin = cs_ref[8:16, :]
    for n, (w, g, b) in enumerate(((wq_ref, gq_ref, bq_ref), (wk_ref, gk_ref, bk_ref), (wv_ref, gv_ref, bv_ref))):
        t = _nn(a_own, w[...]) + _nn(a_got, g[...]) + b[...]
        t = t.T
        for k in range(send_ref.shape[1]):
            v = t[k * HD : (k + 1) * HD]
            if n < 2:
                lead = v[0:8]
                trail = v[8:16]
                v = jnp.concatenate([lead * cos - trail * sin, trail * cos + lead * sin, v[16:]], axis=0)
            send_ref[0, k, n * HD : (n + 1) * HD, :] = v.astype(bf16)


def qkv_forward(ids, attn_in, w_own, w_got, bias, cs, cols=256):
    rows, width = attn_in.shape[0] // 2, attn_in.shape[1]
    half = width // 2
    quarter = w_got.shape[1] // 3
    bsp = lambda p: pl.BlockSpec((1, cols), lambda s, i, ids: (0, p * (quarter // cols) + i))
    return pl.pallas_call(
        qkv_kernel,
        grid_spec=pltpu.PrefetchScalarGridSpec(
            num_scalar_prefetch=1,
            grid=(2, quarter // cols),
            in_specs=[pl.BlockSpec((rows, width), lambda s, i, ids: (s, 0))]
            + _wq_specs(half, width, cols, quarter, lambda s, i, ids: i)
            + [bsp(p) for p in range(3)]
            + [_full(cs)],
            out_specs=pl.BlockSpec((1, cols // HD, 3 * HD, rows), lambda s, i, ids: (s, i, 0, 0)),
        ),
        out_shape=jax.ShapeDtypeStruct((2, quarter // HD, 3 * HD, rows), bf16),
        compiler_params=_params(),
        cost_estimate=pl.CostEstimate(flops=1 << 20, transcendentals=0, bytes_accessed=1 << 20),
        name="qkv_forward",
    )(ids, attn_in, w_own, w_own, w_own, w_got, w_got, w_got, bias, bias, bias, cs)


MLP_CHUNKS = 2


def mlp_kernel(ids, x_ref, xt_ref, dy_ref, wo_ref, wg_ref, wd_ref, bu_ref, y_ref, dx_ref, uk_ref, us_ref, dk_ref, ds_ref, gb_ref,
    g_s, act_s, du_s, y_s, dx_s
):
    rows, width = x_ref.shape
    half = width // 2
    me = ids[0]
    spans = (
        (pl.multiple_of(me * half, half), wo_ref[...]),
        (pl.multiple_of((1 - me) * half, half), wg_ref[...]),
    )

    @pl.when(pl.program_id(0) == 0)
    def _():
        y_s[...] = jnp.zeros_like(y_s)
        dx_s[...] = jnp.zeros_like(dx_s)

    wd = wd_ref[...]
    bias = bu_ref[...]
    step = rows // MLP_CHUNKS
    for c in range(MLP_CHUNKS):
        at = slice(c * step, (c + 1) * step)
        u = bias + sum(_nn(x_ref[at, pl.ds(o, half)], w) for o, w in spans)
        cdf = 0.5 * (1.0 + lax.erf(u * (1.0 / math.sqrt(2.0))))
        pdf = jnp.exp(-0.5 * u * u) * (1.0 / math.sqrt(2.0 * math.pi))
        act = (u * cdf).astype(bf16)
        du = (_nt(dy_ref[at, :], wd) * (cdf + u * pdf)).astype(bf16)
        y_s[at, :] += _nn(act, wd)
        for o, w in spans:
            dx_s[at, pl.ds(o, half)] += _nt(du, w)
        act_s[at, :] = act
        du_s[at, :] = du
    du = du_s[...]
    gd = lax.dot_general(
        act_s[...], dy_ref[...], (((0,), (0,)), ((), ())), preferred_element_type=f32
    ).astype(bf16)
    k, r, _ = dk_ref.shape
    k = gd.shape[0] // r
    early = pl.program_id(0) < pl.num_programs(0) // 2
    for c in range(k):
        v = gd[c * r : (c + 1) * r, :]

        @pl.when(early)
        def _(v=v, c=c):
            ds_ref[c] = v

        @pl.when(jnp.logical_not(early))
        def _(v=v, c=c):
            dk_ref[c] = v

    g_s[...] = _nn(xt_ref[...], du).astype(bf16)
    n = uk_ref.shape[0]
    r = uk_ref.shape[1] // 2
    for ref, side in ((uk_ref, ids[3]), (us_ref, 1 - ids[3])):
        for h in range(2):
            for c in range(n):
                at = pl.multiple_of(h * half + (side * n + c) * r, r)
                ref[c, h * r : (h + 1) * r, :] = g_s[pl.ds(at, r), :]
    gb_ref[...] = jnp.sum(du.astype(f32), axis=0, keepdims=True)

    @pl.when(pl.program_id(0) == pl.num_programs(0) - 1)
    def _():
        y_ref[...] = y_s[...].astype(bf16)
        dx_ref[...] = dx_s[...].astype(bf16)


def mlp(ids, x, xt, dy, w_own, w_got, wd, bu, n, tile=512):
    rows, width = x.shape
    half = width // 2
    hidden = w_got.shape[1]
    steps = hidden // tile
    mid = steps // 2
    whole = pl.BlockSpec((rows, width), lambda i, ids: (0, 0))
    per = hidden // n
    order = lambda i, ids: i % mid + mid * jnp.where(i < mid, 1 - ids[2], ids[2])
    part = lambda i, ids: ids[1] * steps + order(i, ids)
    up_spec = pl.BlockSpec((n // 2, width // n, tile), lambda i, ids: (0, 0, order(i, ids)))
    down_spec = lambda f: pl.BlockSpec((tile // per, per, width), lambda i, ids: (f(i), 0, 0))
    up_shape = jax.ShapeDtypeStruct((n // 2, width // n, hidden), bf16)
    down_shape = jax.ShapeDtypeStruct((n // 2, per, width), bf16)
    return pl.pallas_call(
        mlp_kernel,
        grid_spec=pltpu.PrefetchScalarGridSpec(
            num_scalar_prefetch=1,
            grid=(steps,),
            in_specs=[
                whole,
                pl.BlockSpec((width, rows), lambda i, ids: (0, 0)),
                whole,
                pl.BlockSpec((half, tile), lambda i, ids: (0, ids[0] * 2 * steps + part(i, ids))),
                pl.BlockSpec((half, tile), lambda i, ids: (0, order(i, ids))),
                pl.BlockSpec((tile, width), lambda i, ids: (part(i, ids), 0)),
                pl.BlockSpec((1, tile), lambda i, ids: (0, part(i, ids))),
            ],
            out_specs=(
                whole,
                whole,
                up_spec,
                up_spec,
                down_spec(lambda i: jnp.maximum(i - mid, 0)),
                down_spec(lambda i: jnp.minimum(i, mid - 1)),
                pl.BlockSpec((1, tile), lambda i, ids: (0, order(i, ids))),
            ),
            scratch_shapes=[pltpu.VMEM((width, tile), bf16), pltpu.VMEM((rows, tile), bf16), pltpu.VMEM((rows, tile), bf16)]
            + [pltpu.VMEM((rows, width), f32)] * 2,
        ),
        out_shape=(
            jax.ShapeDtypeStruct((rows, width), bf16),
            jax.ShapeDtypeStruct((rows, width), bf16),
            up_shape,
            up_shape,
            down_shape,
            down_shape,
            jax.ShapeDtypeStruct((1, hidden), f32),
        ),
        compiler_params=_params(),
        cost_estimate=pl.CostEstimate(
            flops=12 * rows * width * hidden, transcendentals=2 * rows * hidden, bytes_accessed=24 << 20
        ),
        name="mlp",
    )(ids, x, xt, dy, w_own, w_got, wd, bu)


def qkv_back_kernel(
    ids, d_ref, at_ref, x_ref, n_ref, wq_ref, wk_ref, wv_ref, gq_ref, gk_ref, gv_ref, dm_ref, ob_ref, dy_ref, gb_ref,
    a_ref, b_ref, e_ref, g_s, go_s, bias_s, sum_s
):
    rows, width = x_ref.shape
    half = width // 2
    me = ids[0]
    core = ids[1]
    s = pl.program_id(0)
    outs = (a_ref, b_ref)
    n = a_ref.shape[0]
    nh = d_ref.shape[1]
    cols = nh * HD
    r = half // (2 * n)

    @pl.when(s == 0)
    def _():
        g_s[...] = jnp.zeros_like(g_s)
        go_s[...] = jnp.zeros_like(go_s)
        bias_s[...] = jnp.zeros_like(bias_s)
        sum_s[...] = jnp.zeros_like(sum_s)

    ones = jnp.ones((8, rows), bf16)
    at = at_ref[...]
    dts = []
    for p in range(3):
        dp = jnp.concatenate([d_ref[0, k, p * HD : (p + 1) * HD, :] for k in range(nh)], axis=0)
        g_s[p] += _nt(at, dp)
        bias_s[p * 8 : (p + 1) * 8, :] += _nt(ones, dp)
        dts.append(dp.astype(f32).T.astype(bf16))
    go_s[...] += _nn(ob_ref[0], dy_ref[...])
    dt = jnp.concatenate(dts, axis=1)
    w_own = jnp.concatenate([wq_ref[...], wk_ref[...], wv_ref[...]], axis=1)
    w_got = jnp.concatenate([gq_ref[...], gk_ref[...], gv_ref[...]], axis=1)
    d_own = _nt(dt, w_own)
    d_got = _nt(dt, w_got)
    first = me == 0
    xhat, _ = _norm(x_ref[...])
    for h in range(2):
        lanes = slice(h * half, (h + 1) * half)
        da = jnp.where(first, d_own, d_got) if h == 0 else jnp.where(first, d_got, d_own)
        dm = dm_ref[:, lanes].astype(f32)
        xh = xhat[:, lanes]
        e_ref[0, :, lanes] = da * n_ref[0:1, lanes] + dm * n_ref[2:3, lanes]
        for k, v in enumerate((da * xh, da, dm * xh, dm)):
            sum_s[k : k + 1, lanes] += jnp.sum(v, axis=0, keepdims=True)

    @pl.when(s == 0)
    def _():
        mine = dy_ref[pl.ds(pl.multiple_of(core * (rows // 2), rows // 2), rows // 2), :]
        sum_s[4:5, :] = jnp.sum(mine.astype(f32), axis=0, keepdims=True)

    @pl.when(s == pl.num_programs(0) - 1)
    def _():
        for p in range(3):
            g = g_s[p].astype(bf16)
            for h in range(2):
                for c in range(n):
                    for a in range(2):
                        row = h * half + (c * 2 + a) * r
                        u = (h * 3 + p) * r
                        outs[a][c, u : u + r, :] = g[row : row + r, :]
        go = go_s[...].astype(bf16)
        q = cols // (2 * n)
        for c in range(n):
            for a in range(2):
                row = (c * 2 + a) * q
                for k in range(width // cols):
                    u = 6 * r + k * q
                    outs[a][c, u : u + q, :] = go[row : row + q, k * cols : (k + 1) * cols]
        flat = [sum_s[k : k + 1, t * cols : (t + 1) * cols] for k in range(5) for t in range(width // cols)]
        zero = jnp.zeros((1, cols), f32)
        for p in range(3):
            flat += [
                jnp.where((me == k) & (core == j), bias_s[p * 8 : p * 8 + 1, :], zero) for k in range(2) for j in range(2)
            ]
        flat += [
            jnp.where((me == k) & (core == j), gb_ref[:, t * cols : (t + 1) * cols], zero)
            for k in range(2)
            for j in range(2)
            for t in range(gb_ref.shape[1] // cols)
        ]
        top = 6 * r + (width // cols) * q
        per = len(flat) // n
        pad = [zero] * (8 - per)
        for c in range(n):
            b_ref[c, top : top + 8, :] = jnp.concatenate(flat[c * per : (c + 1) * per] + pad, axis=0).astype(bf16)


def qkv_backward(ids, d, at, x2, norms, w_own, w_got, d_mlp, ob, dy, gb_up, n):
    rows, width = x2.shape[0] // 2, x2.shape[1]
    half = width // 2
    cols = w_got.shape[1] // 3
    size = 6 * (half // (2 * n)) + width // (2 * n)
    row = lambda: pl.BlockSpec((rows, width), lambda s, ids: (s, 0))
    out = [
        jax.ShapeDtypeStruct((n, size, cols), bf16),
        jax.ShapeDtypeStruct((n, size + 8, cols), bf16),
    ]
    return pl.pallas_call(
        qkv_back_kernel,
        grid_spec=pltpu.PrefetchScalarGridSpec(
            num_scalar_prefetch=1,
            grid=(2,),
            in_specs=[
                pl.BlockSpec((1, cols // HD, 3 * HD, rows), lambda s, ids: (s, 0, 0, 0)),
                pl.BlockSpec((width, rows), lambda s, ids: (0, s)),
                row(),
                _full(norms),
            ]
            + _wq_specs(half, width, cols, cols, lambda s, ids: 0)
            + [row(), pl.BlockSpec((1, cols, rows), lambda s, ids: (s, 0, 0)), row(), _full(gb_up)],
            out_specs=(*[_full(v) for v in out], pl.BlockSpec((1, rows, width), lambda s, ids: (s, 0, 0))),
            scratch_shapes=[
                pltpu.VMEM((3, width, cols), f32),
                pltpu.VMEM((cols, width), f32),
                pltpu.VMEM((24, cols), f32),
                pltpu.VMEM((8, width), f32),
            ],
        ),
        out_shape=(*out, jax.ShapeDtypeStruct((2, rows, width), f32)),
        compiler_params=_params(),
        name="qkv_backward",
    )(ids, d, at, x2, norms, w_own, w_own, w_own, w_got, w_got, w_got, d_mlp, ob, dy, gb_up)


def _mine(ids):
    return (pl.program_id(0) // 2) == ids[1]


def _own_block(i, ids):
    return jnp.clip(i - 2 * ids[1], 0, 1)


def _got_block(i, ids):
    return jnp.clip(i - 2 * (1 - ids[1]), 0, 1)


def join_kernel(ids, own_ref, got_ref, o_ref):
    mine = _mine(ids)
    shape = o_ref.shape

    @pl.when(mine)
    def _():
        o_ref[...] = own_ref[...].astype(f32).reshape(shape)

    @pl.when(jnp.logical_not(mine))
    def _():
        o_ref[...] = got_ref[...].astype(f32).reshape(shape)


def join_rows(ids, own, got):
    n, r, w = own.shape
    src = lambda f: pl.BlockSpec((n // 2, r, w), lambda i, ids: (f(i, ids), 0, 0))
    return pl.pallas_call(
        join_kernel,
        grid_spec=pltpu.PrefetchScalarGridSpec(
            num_scalar_prefetch=1,
            grid=(4,),
            in_specs=[src(_own_block), src(_got_block)],
            out_specs=pl.BlockSpec((n * r // 2, w), lambda i, ids: (i, 0)),
        ),
        out_shape=jax.ShapeDtypeStruct((2 * n * r, w), f32),
        compiler_params=_params(),
        name="join_rows",
    )(ids, own, got)


def join_cols(ids, own, got):
    n, _, r, w = own.shape
    src = lambda f: pl.BlockSpec((n, 1, r, w), lambda i, ids: (0, f(i, ids), 0, 0))
    return pl.pallas_call(
        join_kernel,
        grid_spec=pltpu.PrefetchScalarGridSpec(
            num_scalar_prefetch=1,
            grid=(4,),
            in_specs=[src(_own_block), src(_got_block)],
            out_specs=pl.BlockSpec((n * r, w), lambda i, ids: (0, (i % 2) * 2 + i // 2)),
        ),
        out_shape=jax.ShapeDtypeStruct((n * r, 4 * w), f32),
        compiler_params=_params(),
        name="join_cols",
    )(ids, own, got)


def unpack_kernel(ids, ao_ref, ag_ref, bo_ref, bg_ref, q_ref, o_ref, s_ref):
    first = ids[1] == 0
    k, _, cols = ao_ref.shape
    r = q_ref.shape[0] // (2 * k)
    q = o_ref.shape[1] // (2 * k)
    for a, (own, got) in enumerate(((ao_ref, ag_ref), (bo_ref, bg_ref))):
        for c in range(k):
            x = own[c].astype(f32)
            y = got[c].astype(f32)
            to = slice((c * 2 + a) * r, (c * 2 + a + 1) * r)
            tq = slice((c * 2 + a) * q, (c * 2 + a + 1) * q)
            for j in range(2):
                v = jnp.where(first, x, y) if j == 0 else jnp.where(first, y, x)
                for w in range(2):
                    for p in range(3):
                        u = (w * 3 + p) * r
                        at = ((p * 2 + w) * 2 + j) * cols
                        q_ref[to, at : at + cols] = v[u : u + r, :]
                for t in range(o_ref.shape[2] // cols):
                    u = 6 * r + t * q
                    o_ref[j, tq, t * cols : (t + 1) * cols] = v[u : u + q, :]
            if a == 1:
                s_ref[c] = (x + y)[-8:, :]


def unpack(ids, a_own, a_got, b_own, b_got, width, steps=4):
    n, _, cols = a_own.shape
    half = width // 2
    k = n // steps
    spec = lambda v: pl.BlockSpec((k,) + v.shape[1:], lambda i, ids: (i, 0, 0))
    return pl.pallas_call(
        unpack_kernel,
        grid_spec=pltpu.PrefetchScalarGridSpec(
            num_scalar_prefetch=1,
            grid=(steps,),
            in_specs=[spec(v) for v in (a_own, a_got, b_own, b_got)],
            out_specs=(
                pl.BlockSpec((half // steps, 3 * width), lambda i, ids: (i, 0)),
                pl.BlockSpec((2, cols // steps, width), lambda i, ids: (0, i, 0)),
                pl.BlockSpec((k, 8, cols), lambda i, ids: (i, 0, 0)),
            ),
        ),
        out_shape=(
            jax.ShapeDtypeStruct((half, 3 * width), f32),
            jax.ShapeDtypeStruct((2, cols, width), f32),
            jax.ShapeDtypeStruct((n, 8, cols), f32),
        ),
        compiler_params=_params(),
        name="unpack",
    )(ids, a_own, a_got, b_own, b_got)


def last_kernel(eo_ref, er_ref, x_ref, c_ref, live_ref, o_ref):
    xhat, inv = _norm(x_ref[...])
    e = eo_ref[...] + er_ref[...].astype(f32)
    dx = inv * (
        e - jnp.mean(e, axis=-1, keepdims=True) - xhat * jnp.mean(e * xhat, axis=-1, keepdims=True)
    )
    o_ref[...] = live_ref[...] * c_ref[...].astype(f32) + dx


def last(e_own, e_got, x, cot, live):
    return pl.pallas_call(
        last_kernel,
        out_shape=jax.ShapeDtypeStruct(x.shape, f32),
        compiler_params=_params(),
        name="token_grad",
    )(e_own, e_got, x, cot, live)


def fast_shards(
    tokens,
    ln1_gain,
    ln1_bias,
    ln2_gain,
    ln2_bias,
    w_qkv,
    b_qkv,
    w_out,
    b_out,
    w_up,
    b_up,
    w_down,
    b_down,
    lengths,
    block_map,
    cotangent,
):
    ctx = lax.axis_index("ctx")
    me = lax.axis_index("wsh")
    core = ctx % 2
    n_ctx = lax.axis_size("ctx")
    chips = n_ctx // 2
    own_rows, width = tokens.shape[1:]
    rows = 2 * own_rows
    half = width // 2
    quarter = half // 2
    seq = own_rows * n_ctx
    heads = H // 4
    hid = w_up.shape[1] // 4
    CORE, X, ZN, ZF = 0, 1, 2, 3

    def swap(v):
        return lax.ppermute(v, "wsh", SWAP)

    def flip(v, bit):
        return lax.ppermute(v, "ctx", [(i, i ^ (1 << bit)) for i in range(n_ctx)])

    def bit_of(bit):
        return (ctx >> bit) & 1

    ids = jnp.stack([me, core, bit_of(X), bit_of(ZN)]).astype(jnp.int32)

    def add(*terms):
        return sum(v.astype(f32) for v in terms).astype(bf16) if len(terms) > 1 else terms[0]

    def halve(terms, bit):
        b = bit_of(bit)
        cut = [v.reshape((2, v.shape[0] // 2) + v.shape[1:]) for v in terms]
        part = lambda k: [lax.dynamic_index_in_dim(v, k, 0, keepdims=False) for v in cut]
        return part(b) + [flip(add(*part(1 - b)), bit)]

    def ordered(first, a, b, axis=0):
        return jnp.where(first == 0, jnp.concatenate([a, b], axis), jnp.concatenate([b, a], axis))

    def double(v, bit):
        return ordered(bit_of(bit), v, flip(v, bit))

    def exchange(v):
        groups = [[2 * i + c for i in range(chips)] for c in range(2)]
        return lax.all_to_all(v, "ctx", 0, 0, axis_index_groups=groups, tiled=False)

    def rows_of(v, at, n, axis=0):
        return lax.dynamic_slice_in_dim(v, at, n, axis)

    x_own = tokens[0]
    x_got = swap(x_own)
    x_sib = flip(x_own, CORE)
    mine = me * half + core * quarter
    other = (1 - me) * half + core * quarter
    wq_send = jnp.concatenate([rows_of(w_qkv, p * width + other, quarter, 1) for p in range(3)], axis=1)
    wq_send, ln1_gain = lax.optimization_barrier((wq_send, ln1_gain))
    len_parts = jnp.stack([lengths[0] // 64, lengths[0] % 64]).astype(bf16)
    parts = [ln1_gain, ln1_bias, ln2_gain, ln2_bias, b_out, b_down, b_qkv, jnp.pad(len_parts, (0, half - 2))]
    small = jnp.concatenate([v.reshape(-1, half) for v in parts])
    small = ordered(me, small[None], swap(small)[None])
    wq_got = swap(wq_send)
    vec = lambda i: small[:, i].reshape(width).astype(f32)
    norms = jnp.stack([vec(i) for i in range(4)])
    bias_out = vec(4) + vec(5)
    qkv_bias = small[:, 6:9].astype(f32).reshape(3, width)
    qkv_bias = rows_of(qkv_bias, mine, quarter, 1).reshape(1, 3 * quarter)
    lens = small[:, 9, :2].astype(jnp.int32)
    lens = lens[:, 0] * 64 + lens[:, 1]
    other_len = lens[1 - me]

    normed = norm_rows(ids, x_own, x_sib, norms)
    cot_own = cotangent[0]
    wu_send = rows_of(w_up, ((1 - me) * 2 + core) * hid, hid, 1)
    wq_got, cot_send, normed = lax.optimization_barrier((wq_got, cot_own, normed))
    cot_got = swap(cot_send)
    cot_got, wu_send = lax.optimization_barrier((cot_got, wu_send))
    wu_got = swap(wu_send)
    normed = norm_rows(ids, x_got, flip(x_got, CORE), norms, normed)
    x2, attn_in, mlp_in = normed
    cot_sib = flip(cot_own, CORE)

    blocks = rows_of(block_map, (rows // HB) * (ctx // 2), rows // HB)
    offs = jnp.arange(HB, dtype=jnp.int32)
    positions = (blocks[:, None] * HB + offs[None, :]).reshape(rows)
    live2 = jnp.concatenate([positions < lengths[0], positions < other_len]).astype(f32)[:, None]
    live_own = rows_of(live2, core * own_rows, own_rows)
    freq = 10000.0 ** (-jnp.arange(ROT // 2, dtype=f32) * 2.0 / ROT)
    ang = freq[:, None] * jnp.arange(seq, dtype=jnp.int32).astype(f32)[None, :]
    table = jnp.concatenate([jnp.cos(ang), jnp.sin(ang)])
    own_ang = freq[:, None] * positions.astype(f32)[None, :]
    own_table = jnp.concatenate([jnp.cos(own_ang), jnp.sin(own_ang)])

    attn_in, table = lax.optimization_barrier((attn_in, table))
    send = qkv_forward(ids, attn_in, w_qkv, wq_got, qkv_bias, own_table)
    qkv_head = exchange(send.reshape(2 * heads, 3 * HD, rows))
    dy, dctx = mask_rows(ids, cot_own, cot_sib, cot_got, flip(cot_got, CORE), live2, w_out, quarter)
    w_out_mine = rows_of(w_out, core * quarter, quarter)
    do_head = exchange(dctx)

    attn_t, mlp_t = turn(attn_in, mlp_in)
    do_head = exchange(dctx.reshape(2 * heads, HD, rows))
    y_mlp, d_mlp, up_keep, up_send, down_keep, down_send, gb_up = mlp(
        ids, mlp_in, mlp_t, dy, w_up, wu_got, w_down, b_up.astype(f32)[None, :], chips
    )

    chain_a = (X, ZN, ZF)
    chain_b = (ZN, ZF, X)
    qkv_head, up_send, down_send = lax.optimization_barrier((qkv_head, up_send, down_send))
    down = [down_keep, flip(down_send, chain_a[0])]
    up = [up_keep, flip(up_send, chain_b[0])]

    o_head, lse = attn_fwd(block_map, qkv_head, bq=1024, bk=1024)
    qkv_head, o_head, do_head, down[-1], up[-1] = lax.optimization_barrier((qkv_head, o_head, do_head, down[-1], up[-1]))
    ob = exchange(o_head).reshape(2, quarter, rows)
    down = halve(down, chain_a[1])
    up = halve(up, chain_b[1])
    g_head = attn_bwd(block_map, qkv_head, o_head, do_head, lse, table)
    g_head, ob, down[-1], up[-1] = lax.optimization_barrier((g_head, ob, down[-1], up[-1]))
    d_qkv = exchange(g_head).reshape(2, heads, 3 * HD, rows)

    down = add(*halve(down, chain_a[2]))
    up = add(*halve(up, chain_b[2]))
    up = up.reshape(1, 2, up.shape[1] // 2, up.shape[2])
    up_keep = rows_of(up, me, 1, 1)
    up_got = swap(rows_of(up, 1 - me, 1, 1))
    up = ordered(me, up_keep, up_got, axis=1)
    for a, b in zip(chain_a[::-1], chain_b[::-1]):
        down = double(down, a)
        up = double(up, b)
    tot_down = join_rows(ids, down, flip(down, CORE))
    tot_up = join_cols(ids, up, flip(up, CORE))

    def settle(v):
        give = rows_of(v, (1 - core) * own_rows, own_rows, 1).astype(bf16)
        v = rows_of(v, core * own_rows, own_rows, 1) + flip(give, CORE).astype(f32)
        return v[0], swap(v[1].astype(bf16))

    part = jnp.einsum("sct,cd->std", ob, w_out_mine, preferred_element_type=f32) + y_mlp.reshape(2, rows, width).astype(f32)
    part, part_got = settle(part)
    output = (live_own * (x_own.astype(f32) + part + part_got.astype(f32) + bias_out)).astype(bf16)

    v_a, v_b, e = qkv_backward(
        ids, d_qkv, attn_t, x2, norms, w_qkv, wq_got, d_mlp, ob, dy, gb_up, chips
    )
    v_a = [v_a]
    v_b = [v_b]
    for a, b in zip(chain_a, chain_b):
        v_a = halve(v_a, a)
        v_b = halve(v_b, b)
    e_own, e_got = settle(e)
    n3 = 3 * half // (2 * chips)
    size = 2 * n3 + width // (2 * chips)
    tail = []
    for v in (add(*v_a)[0], add(*v_b)[0]):
        extra = v[size:]
        back = swap(jnp.concatenate([rows_of(v, (1 - me) * n3, n3), extra]))
        extra = add(extra, back[n3:])
        tail.append(jnp.concatenate([ordered(me, rows_of(v, me * n3, n3), back[:n3]), v[2 * n3 : size], extra])[None])
    grad_tokens = last(e_own, e_got, x_own, cot_own, live_own)
    cover = [[grad_tokens, output], [tot_down], [tot_up]]
    for k, (a, b) in enumerate(zip(chain_a[::-1], chain_b[::-1])):
        tail = [double(tail[0], a), double(tail[1], b)]
        tail, cover[k] = lax.optimization_barrier((tail, cover[k]))
    mixed = tail
    (grad_tokens, output), (tot_down,), (tot_up,) = cover
    tot_qkv, tot_out, flat = unpack(ids, mixed[0], flip(mixed[0], CORE), mixed[1], flip(mixed[1], CORE), width)
    flat = flat[:, :6].reshape(12 * width)

    def own(start, size):
        return lax.dynamic_slice_in_dim(flat, start + me * size, size)

    gb_out = own(4 * width, half)
    return (
        output[None],
        grad_tokens[None],
        own(0, half),
        own(width, half),
        own(2 * width, half),
        own(3 * width, half),
        tot_qkv,
        own(5 * width, 3 * half),
        tot_out.reshape(half, width),
        gb_out,
        tot_up,
        own(8 * width, 2 * hid),
        tot_down,
        gb_out,
    )


def solution(mesh):
    placed = (
        P("wsh", "ctx", None),
        P("wsh"),
        P("wsh"),
        P("wsh"),
        P("wsh"),
        P("wsh", None),
        P("wsh"),
        P("wsh", None),
        P("wsh"),
        P("wsh", None),
        P("wsh"),
        P("wsh", None),
        P("wsh"),
        P("wsh"),
        P(),
        P("wsh", "ctx", None),
    )
    body = fast_shards if fast_fits(mesh) else shards
    return jax.shard_map(
        body,
        mesh=mesh,
        in_specs=placed,
        out_specs=(
            P("wsh", "ctx", None),
            P("wsh", "ctx", None),
            P("wsh"),
            P("wsh"),
            P("wsh"),
            P("wsh"),
            P("wsh", None),
            P("wsh"),
            P("wsh", None),
            P("wsh"),
            P("wsh", None),
            P("wsh"),
            P("wsh", None),
            P("wsh"),
        ),
        check_vma=False,
    )
```

```python
from functools import partial
import math

import jax
import jax.numpy as jnp
from jax import lax
from jax.experimental import pallas as pl
from jax.experimental.pallas import tpu as pltpu
from jax.sharding import PartitionSpec as P

H = 16
HD = 64
ROT = 16


epsilon = 1e-05


def norm_forward(values, norm_gain, norm_shift):
    average = jnp.mean(values, axis=-1, keepdims=True)
    centred = values - average
    variance = jnp.mean(centred * centred, axis=-1, keepdims=True)
    inverse = lax.rsqrt(variance + epsilon)
    normed = centred * inverse
    return (normed * norm_gain + norm_shift, normed, inverse)


def norm_backward(grad_out, normed, inverse, norm_gain):
    scaled = grad_out * norm_gain
    adjusted = (
        scaled
        - jnp.mean(scaled, axis=-1, keepdims=True)
        - normed * jnp.mean(scaled * normed, axis=-1, keepdims=True)
    )
    return (adjusted * inverse, jnp.sum(grad_out * normed, axis=0), jnp.sum(grad_out, axis=0))


def rotary_tables(positions):
    half_rot = ROT // 2
    frequency = 10000.0 ** (-jnp.arange(half_rot, dtype=jnp.float32) * 2.0 / ROT)
    angles = positions.astype(jnp.float32)[:, None] * frequency[None, :]
    return (jnp.cos(angles)[:, None, :], jnp.sin(angles)[:, None, :])


def rotate_forward(values, cosine_table, sine_table):
    half_rot = ROT // 2
    leading = values[..., :half_rot]
    trailing = values[..., half_rot:ROT]
    return jnp.concatenate(
        [
            leading * cosine_table - trailing * sine_table,
            trailing * cosine_table + leading * sine_table,
            values[..., ROT:],
        ],
        axis=-1,
    )


def rotate_backward(grads, cosine_table, sine_table):
    half_rot = ROT // 2
    leading = grads[..., :half_rot]
    trailing = grads[..., half_rot:ROT]
    return jnp.concatenate(
        [
            leading * cosine_table + trailing * sine_table,
            trailing * cosine_table - leading * sine_table,
            grads[..., ROT:],
        ],
        axis=-1,
    )


def masked_scores(query_rows, key_rows, query_pos, key_pos, key_live):
    raw_scores = jnp.einsum(
        "qhd,khd->hqk", query_rows, key_rows, preferred_element_type=jnp.float32
    )
    allowed = (key_pos[None, :] <= query_pos[:, None]) & key_live[None, :]
    return (jnp.where(allowed[None], raw_scores * (1.0 / math.sqrt(HD)), -1e30), allowed)


def score_grads(
    query_rows, key_rows, value_rows, grad_rows, query_pos, key_pos, key_live, log_total, row_dots
):
    scores = masked_scores(query_rows, key_rows, query_pos, key_pos, key_live)[0]
    probability = jnp.exp(scores - log_total[..., None])
    grad_prob = jnp.einsum(
        "qhd,khd->hqk", grad_rows, value_rows, preferred_element_type=jnp.float32
    )
    grad_score = (probability * (grad_prob - row_dots[..., None]) * (1.0 / math.sqrt(HD))).astype(
        jnp.bfloat16
    )
    return (probability.astype(jnp.bfloat16), grad_score)


def shards(
    tokens,
    ln1_gain,
    ln1_bias,
    ln2_gain,
    ln2_bias,
    w_qkv,
    b_qkv,
    w_out,
    b_out,
    w_up,
    b_up,
    w_down,
    b_down,
    lengths,
    block_map,
    cotangent,
):
    gathered = (
        lax.all_gather(ln1_gain, "wsh", axis=0, tiled=True),
        lax.all_gather(ln1_bias, "wsh", axis=0, tiled=True),
        lax.all_gather(ln2_gain, "wsh", axis=0, tiled=True),
        lax.all_gather(ln2_bias, "wsh", axis=0, tiled=True),
        lax.all_gather(w_qkv, "wsh", axis=0, tiled=True),
        lax.all_gather(b_qkv, "wsh", axis=0, tiled=True),
        lax.all_gather(w_out, "wsh", axis=0, tiled=True),
        lax.all_gather(b_out, "wsh", axis=0, tiled=True),
        lax.all_gather(w_up, "wsh", axis=0, tiled=True),
        lax.all_gather(b_up, "wsh", axis=0, tiled=True),
        lax.all_gather(w_down, "wsh", axis=0, tiled=True),
        lax.all_gather(b_down, "wsh", axis=0, tiled=True),
    )
    (
        norm1_gain,
        norm1_shift,
        norm2_gain,
        norm2_shift,
        qkv_weight,
        qkv_bias,
        out_weight,
        out_bias,
        up_weight,
        up_bias,
        down_weight,
        down_bias,
    ) = gathered
    tok_rows = tokens.shape[1]
    model_width = tokens.shape[2]
    half_rows = tok_rows // 2
    seq_rows = tok_rows * lax.axis_size("ctx")
    head_count = H
    head_size = HD
    ctx_index = lax.axis_index("ctx")
    own_blocks = lax.dynamic_slice_in_dim(block_map, 2 * ctx_index, 2)
    local_offsets = jnp.arange(half_rows, dtype=jnp.int32)
    positions = (own_blocks[:, None] * half_rows + local_offsets[None, :]).reshape(tok_rows)
    key_pos = (block_map[:, None] * half_rows + local_offsets[None, :]).reshape(seq_rows)
    length = lengths[0]
    own_live = positions < length
    live_rows = own_live.astype(jnp.float32)
    key_live = key_pos < length
    gain_first = norm1_gain.astype(jnp.float32)
    gain_second = norm2_gain.astype(jnp.float32)
    token_rows = tokens[0].astype(jnp.float32)
    normal_first, normed_first, inverse_first = norm_forward(
        token_rows, gain_first, norm1_shift.astype(jnp.float32)
    )
    normal_second, normed_second, inverse_second = norm_forward(
        token_rows, gain_second, norm2_shift.astype(jnp.float32)
    )
    attn_in = normal_first.astype(jnp.bfloat16)
    mlp_in = normal_second.astype(jnp.bfloat16)
    projected = (
        jnp.dot(attn_in, qkv_weight, preferred_element_type=jnp.float32)
        + qkv_bias.astype(jnp.float32)
    ).reshape(tok_rows, 3, head_count, head_size)
    cosine_table, sine_table = rotary_tables(positions)
    queries = rotate_forward(projected[:, 0], cosine_table, sine_table).astype(jnp.bfloat16)
    key_own = (
        rotate_forward(projected[:, 1], cosine_table, sine_table)
        .astype(jnp.bfloat16)
        .reshape(tok_rows, model_width)
    )
    value_own = projected[:, 2].astype(jnp.bfloat16).reshape(tok_rows, model_width)
    keys_all, values_all = (
        lax.all_gather(key_own, "ctx", axis=0, tiled=True),
        lax.all_gather(value_own, "ctx", axis=0, tiled=True),
    )
    block_len = math.gcd(seq_rows, 1024)
    block_count = seq_rows // block_len
    key_stack = keys_all.reshape(block_count, block_len, head_count, head_size)
    value_stack = values_all.reshape(block_count, block_len, head_count, head_size)
    pos_stack = key_pos.reshape(block_count, block_len)
    live_stack = key_live.reshape(block_count, block_len)

    def stats_step(running, key_part):
        key_block, pos_block, live_block = key_part
        scores, allowed = masked_scores(queries, key_block, positions, pos_block, live_block)
        peak_score = jnp.maximum(running[0], jnp.max(scores, axis=-1))
        exp_total = running[1] * jnp.exp(running[0] - peak_score) + jnp.sum(
            jnp.where(allowed[None], jnp.exp(scores - peak_score[..., None]), 0.0), axis=-1
        )
        return ((peak_score, exp_total), None)

    start_peak = jnp.full((head_count, tok_rows), -1e30, jnp.float32)
    final_state = lax.scan(
        stats_step, (start_peak, jnp.zeros_like(start_peak)), (key_stack, pos_stack, live_stack)
    )[0]
    log_total = final_state[0] + jnp.log(final_state[1])

    def value_step(running, key_part):
        key_block, value_block, pos_block, live_block = key_part
        scores = masked_scores(queries, key_block, positions, pos_block, live_block)[0]
        probability = jnp.exp(scores - log_total[..., None]).astype(jnp.bfloat16)
        return (
            running
            + jnp.einsum(
                "hqk,khd->qhd", probability, value_block, preferred_element_type=jnp.float32
            ),
            None,
        )

    zero_heads = jnp.zeros((tok_rows, head_count, head_size), jnp.float32)
    attended = lax.scan(value_step, zero_heads, (key_stack, value_stack, pos_stack, live_stack))[0]
    context_low = attended.reshape(tok_rows, model_width).astype(jnp.bfloat16)
    hidden = jnp.dot(mlp_in, up_weight, preferred_element_type=jnp.float32) + up_bias.astype(
        jnp.float32
    )
    activated, gelu_pull = jax.vjp(partial(jax.nn.gelu, approximate=False), hidden)
    act_low = activated.astype(jnp.bfloat16)
    branch = (
        jnp.dot(context_low, out_weight, preferred_element_type=jnp.float32)
        + out_bias.astype(jnp.float32)
        + jnp.dot(act_low, down_weight, preferred_element_type=jnp.float32)
        + down_bias.astype(jnp.float32)
    )
    output_rows = (live_rows[:, None] * (token_rows + branch)).astype(jnp.bfloat16)
    cot_rows = cotangent[0].astype(jnp.float32)
    grad_branch = (live_rows[:, None] * cot_rows).astype(jnp.bfloat16)
    grad_w_out = jnp.einsum(
        "tc,td->cd", context_low, grad_branch, preferred_element_type=jnp.float32
    )
    grad_w_down = jnp.einsum("tc,td->cd", act_low, grad_branch, preferred_element_type=jnp.float32)
    grad_branch_sum = jnp.sum(grad_branch.astype(jnp.float32), axis=0)
    grad_act = jnp.einsum("td,cd->tc", grad_branch, down_weight, preferred_element_type=jnp.float32)
    grad_hidden = gelu_pull(grad_act)[0].astype(jnp.bfloat16)
    grad_w_up = jnp.einsum("tc,td->cd", mlp_in, grad_hidden, preferred_element_type=jnp.float32)
    grad_b_up = jnp.sum(grad_hidden.astype(jnp.float32), axis=0)
    grad_mlp_in = jnp.einsum(
        "td,cd->tc", grad_hidden, up_weight, preferred_element_type=jnp.float32
    )
    grad_context = jnp.einsum(
        "td,cd->tc", grad_branch, out_weight, preferred_element_type=jnp.float32
    ).astype(jnp.bfloat16)
    grad_heads = grad_context.reshape(tok_rows, head_count, head_size)
    row_dots = jnp.sum(grad_heads.astype(jnp.float32) * attended, axis=-1).T

    def grad_step(running, key_part):
        key_block, value_block, pos_block, live_block = key_part
        prob_low, grad_score = score_grads(
            queries,
            key_block,
            value_block,
            grad_heads,
            positions,
            pos_block,
            live_block,
            log_total,
            row_dots,
        )
        query_sum = running + jnp.einsum(
            "hqk,khd->qhd", grad_score, key_block, preferred_element_type=jnp.float32
        )
        key_term = jnp.einsum(
            "hqk,qhd->khd", grad_score, queries, preferred_element_type=jnp.float32
        )
        value_term = jnp.einsum(
            "hqk,qhd->khd", prob_low, grad_heads, preferred_element_type=jnp.float32
        )
        return (query_sum, (key_term, value_term))

    query_grad, term_stacks = lax.scan(
        grad_step, zero_heads, (key_stack, value_stack, pos_stack, live_stack)
    )
    key_grad, value_grad = (
        lax.psum_scatter(
            term_stacks[0].reshape(seq_rows, model_width).astype(jnp.bfloat16),
            "ctx",
            scatter_dimension=0,
            tiled=True,
        ).astype(jnp.float32),
        lax.psum_scatter(
            term_stacks[1].reshape(seq_rows, model_width).astype(jnp.bfloat16),
            "ctx",
            scatter_dimension=0,
            tiled=True,
        ).astype(jnp.float32),
    )
    key_grad = key_grad.reshape(tok_rows, head_count, head_size)
    value_grad = value_grad.reshape(tok_rows, head_count, head_size)
    grad_projected = (
        jnp.stack(
            [
                rotate_backward(query_grad, cosine_table, sine_table),
                rotate_backward(key_grad, cosine_table, sine_table),
                value_grad,
            ],
            axis=1,
        )
        .reshape(tok_rows, 3 * model_width)
        .astype(jnp.bfloat16)
    )
    grad_w_qkv = jnp.einsum(
        "tc,td->cd", attn_in, grad_projected, preferred_element_type=jnp.float32
    )
    grad_b_qkv = jnp.sum(grad_projected.astype(jnp.float32), axis=0)
    grad_attn_in = jnp.einsum(
        "td,cd->tc", grad_projected, qkv_weight, preferred_element_type=jnp.float32
    )
    grad_input_first, grad_gain_first, grad_shift_first = norm_backward(
        grad_attn_in, normed_first, inverse_first, gain_first
    )
    grad_input_second, grad_gain_second, grad_shift_second = norm_backward(
        grad_mlp_in, normed_second, inverse_second, gain_second
    )
    grad_input = live_rows[:, None] * cot_rows + grad_input_first + grad_input_second
    shares = (
        lax.psum_scatter(
            grad_gain_first.astype(jnp.bfloat16), "wsh", scatter_dimension=0, tiled=True
        ).astype(jnp.float32),
        lax.psum_scatter(
            grad_shift_first.astype(jnp.bfloat16), "wsh", scatter_dimension=0, tiled=True
        ).astype(jnp.float32),
        lax.psum_scatter(
            grad_gain_second.astype(jnp.bfloat16), "wsh", scatter_dimension=0, tiled=True
        ).astype(jnp.float32),
        lax.psum_scatter(
            grad_shift_second.astype(jnp.bfloat16), "wsh", scatter_dimension=0, tiled=True
        ).astype(jnp.float32),
        lax.psum_scatter(
            grad_w_qkv.astype(jnp.bfloat16), "wsh", scatter_dimension=0, tiled=True
        ).astype(jnp.float32),
        lax.psum_scatter(
            grad_b_qkv.astype(jnp.bfloat16), "wsh", scatter_dimension=0, tiled=True
        ).astype(jnp.float32),
        lax.psum_scatter(
            grad_w_out.astype(jnp.bfloat16), "wsh", scatter_dimension=0, tiled=True
        ).astype(jnp.float32),
        lax.psum_scatter(
            grad_branch_sum.astype(jnp.bfloat16), "wsh", scatter_dimension=0, tiled=True
        ).astype(jnp.float32),
        lax.psum_scatter(
            grad_w_up.astype(jnp.bfloat16), "wsh", scatter_dimension=0, tiled=True
        ).astype(jnp.float32),
        lax.psum_scatter(
            grad_b_up.astype(jnp.bfloat16), "wsh", scatter_dimension=0, tiled=True
        ).astype(jnp.float32),
        lax.psum_scatter(
            grad_w_down.astype(jnp.bfloat16), "wsh", scatter_dimension=0, tiled=True
        ).astype(jnp.float32),
        lax.psum_scatter(
            grad_branch_sum.astype(jnp.bfloat16), "wsh", scatter_dimension=0, tiled=True
        ).astype(jnp.float32),
    )
    totals = (
        lax.psum(shares[0].astype(jnp.bfloat16), "ctx").astype(jnp.float32),
        lax.psum(shares[1].astype(jnp.bfloat16), "ctx").astype(jnp.float32),
        lax.psum(shares[2].astype(jnp.bfloat16), "ctx").astype(jnp.float32),
        lax.psum(shares[3].astype(jnp.bfloat16), "ctx").astype(jnp.float32),
        lax.psum(shares[4].astype(jnp.bfloat16), "ctx").astype(jnp.float32),
        lax.psum(shares[5].astype(jnp.bfloat16), "ctx").astype(jnp.float32),
        lax.psum(shares[6].astype(jnp.bfloat16), "ctx").astype(jnp.float32),
        lax.psum(shares[7].astype(jnp.bfloat16), "ctx").astype(jnp.float32),
        lax.psum(shares[8].astype(jnp.bfloat16), "ctx").astype(jnp.float32),
        lax.psum(shares[9].astype(jnp.bfloat16), "ctx").astype(jnp.float32),
        lax.psum(shares[10].astype(jnp.bfloat16), "ctx").astype(jnp.float32),
        lax.psum(shares[11].astype(jnp.bfloat16), "ctx").astype(jnp.float32),
    )
    return (
        output_rows[None],
        grad_input[None],
        totals[0],
        totals[1],
        totals[2],
        totals[3],
        totals[4],
        totals[5],
        totals[6],
        totals[7],
        totals[8],
        totals[9],
        totals[10],
        totals[11],
    )


HB = 128
NEG=-1e30
f32=jnp.float32; bf16=jnp.bfloat16

def _nn(a,b): return lax.dot_general(a,b,(((1,),(0,)),((),())),preferred_element_type=f32)
def _nt(a,b): return lax.dot_general(a,b,(((1,),(1,)),((),())),preferred_element_type=f32)

def attn_fwd_kernel(bm, x_ref, o_ref, lse_ref, q_s, kt_s, v_s, *, nblk, per, bq, bk):
    def perm(i,_):
        p=bm[i]; c=i//per; l=pl.multiple_of((i%per)*HB,HB); d=pl.multiple_of(p*HB,HB)
        q_s[:,pl.ds(d,HB)]=x_ref[c,0:64,pl.ds(l,HB)]*bf16(0.125)
        kt_s[pl.ds(d,HB),:]=x_ref[c,64:128,pl.ds(l,HB)].astype(f32).T.astype(bf16)
        v_s[:,pl.ds(d,HB)]=x_ref[c,128:192,pl.ds(l,HB)]
        return 0
    lax.fori_loop(0,nblk,perm,0,unroll=32)
    S=nblk*HB; nq=S//bq; r=bq//bk
    def step(q,qo,ko,carry,mask):
        m,l,acc=carry
        s=_nn(kt_s[pl.ds(ko,bk),:],q)
        if mask is not None: s=jnp.where(mask,s,NEG)
        mn=jnp.maximum(m,jnp.max(s,axis=0,keepdims=True))
        a=jnp.exp(m-mn); p=jnp.exp(s-mn)
        l=l*a+jnp.sum(p,axis=0,keepdims=True)
        acc=acc*a+_nn(v_s[:,pl.ds(ko,bk)],p.astype(bf16))
        return mn,l,acc
    ki=lax.broadcasted_iota(jnp.int32,(bk,bq),0); qi_=lax.broadcasted_iota(jnp.int32,(bk,bq),1)
    def qloop(i,_):
        qo=pl.multiple_of(i*bq,bq)
        q=q_s[:,pl.ds(qo,bq)]
        c=(jnp.full((1,bq),NEG,f32),jnp.zeros((1,bq),f32),jnp.zeros((64,bq),f32))
        c=lax.fori_loop(0,i*r,lambda j,c: step(q,qo,pl.multiple_of(j*bk,bk),c,None),c)
        for t in range(r):
            c=step(q,qo,pl.multiple_of(qo+t*bk,bk),c,ki+t*bk<=qi_)
        m,l,acc=c
        q_s[:,pl.ds(qo,bq)]=(acc*(1.0/l)).astype(bf16)
        lse_ref[:,pl.ds(qo,bq)]=m+jnp.log(l)
        return 0
    lax.fori_loop(0,nq,qloop,0)
    def unperm(i,_):
        p=bm[i]; c=i//per; l=pl.multiple_of((i%per)*HB,HB); d=pl.multiple_of(p*HB,HB)
        o_ref[c,:,pl.ds(l,HB)]=q_s[:,pl.ds(d,HB)]
        return 0
    lax.fori_loop(0,nblk,unperm,0,unroll=32)

def attn_fwd(bm,x,*,bq=512,bk=512):
    n=x.shape[0]; S=n*x.shape[2]; nblk=S//HB
    bq=math.gcd(S,bq); bk=math.gcd(bq,bk)
    return pl.pallas_call(
        lambda *a: attn_fwd_kernel(*a,nblk=nblk,per=x.shape[2]//HB,bq=bq,bk=bk),
        out_shape=(jax.ShapeDtypeStruct((n,64,x.shape[2]),bf16),jax.ShapeDtypeStruct((1,S),f32)),
        in_specs=[pl.BlockSpec(memory_space=pltpu.SMEM),pl.BlockSpec(memory_space=pltpu.VMEM)],
        out_specs=(pl.BlockSpec(memory_space=pltpu.VMEM),pl.BlockSpec(memory_space=pltpu.VMEM)),
        scratch_shapes=[pltpu.VMEM((64,S),bf16),pltpu.VMEM((S,64),bf16),pltpu.VMEM((64,S),bf16)],
        compiler_params=pltpu.CompilerParams(vmem_limit_bytes=56<<20),name="attn_fwd")(bm,x)

def attn_bwd_kernel(bm, x_ref, o_ref, do_ref, lse_ref, cs_ref, g_ref, q_s, kt_s, k_s, vt_s, do_s, dl_s, dq_s, dk_s, dv_s, *, nblk, per, bq, bk):
    def perm(i,_):
        p=bm[i]; c=i//per; l=pl.multiple_of((i%per)*HB,HB); d=pl.multiple_of(p*HB,HB)
        q_s[:,pl.ds(d,HB)]=x_ref[c,0:64,pl.ds(l,HB)]*bf16(0.125)
        k=x_ref[c,64:128,pl.ds(l,HB)]
        k_s[:,pl.ds(d,HB)]=k*bf16(0.125)
        kt_s[pl.ds(d,HB),:]=k.astype(f32).T.astype(bf16)
        vt_s[pl.ds(d,HB),:]=x_ref[c,128:192,pl.ds(l,HB)].astype(f32).T.astype(bf16)
        do=do_ref[c,:,pl.ds(l,HB)]
        do_s[:,pl.ds(d,HB)]=do
        dl_s[:,pl.ds(d,HB)]=jnp.sum(do.astype(f32)*o_ref[c,:,pl.ds(l,HB)].astype(f32),axis=0,keepdims=True)
        return 0
    lax.fori_loop(0,nblk,perm,0,unroll=32)
    S=nblk*HB; nq=S//bq; r=bq//bk
    dk_s[...]=jnp.zeros_like(dk_s); dv_s[...]=jnp.zeros_like(dv_s)
    def step(q,do,lse,dl,ko,dq,mask):
        s=_nn(kt_s[pl.ds(ko,bk),:],q)
        p=jnp.exp(s-lse)
        if mask is not None: p=jnp.where(mask,p,0.0)
        dp=_nn(vt_s[pl.ds(ko,bk),:],do)
        ds=(p*(dp-dl)).astype(bf16)
        pb=p.astype(bf16)
        dv_s[:,pl.ds(ko,bk)]+=_nt(do,pb)
        dk_s[:,pl.ds(ko,bk)]+=_nt(q,ds)
        return dq+_nn(k_s[:,pl.ds(ko,bk)],ds)
    ki=lax.broadcasted_iota(jnp.int32,(bk,bq),0); qi_=lax.broadcasted_iota(jnp.int32,(bk,bq),1)
    def qloop(i,_):
        qo=pl.multiple_of(i*bq,bq)
        q=q_s[:,pl.ds(qo,bq)]; do=do_s[:,pl.ds(qo,bq)]; lse=lse_ref[:,pl.ds(qo,bq)]; dl=dl_s[:,pl.ds(qo,bq)]
        dq=jnp.zeros((64,bq),f32)
        dq=lax.fori_loop(0,i*r,lambda j,c: step(q,do,lse,dl,pl.multiple_of(j*bk,bk),c,None),dq)
        for t in range(r):
            dq=step(q,do,lse,dl,pl.multiple_of(qo+t*bk,bk),dq,ki+t*bk<=qi_)
        dq_s[:,pl.ds(qo,bq)]=dq
        return 0
    lax.fori_loop(0,nq,qloop,0)
    def unperm(i,_):
        p=bm[i]; c=i//per; l=pl.multiple_of((i%per)*HB,HB); d=pl.multiple_of(p*HB,HB)
        cos=cs_ref[0:8,pl.ds(d,HB)]; sin=cs_ref[8:16,pl.ds(d,HB)]
        for n_,src in ((0,dq_s),(1,dk_s)):
            g=src[:,pl.ds(d,HB)]
            a=g[0:8]; b=g[8:16]
            full=jnp.concatenate([a*cos+b*sin,b*cos-a*sin,g[16:64]],axis=0)
            g_ref[c,64*n_:64*n_+64,pl.ds(l,HB)]=full.astype(bf16)
        g_ref[c,128:192,pl.ds(l,HB)]=dv_s[:,pl.ds(d,HB)].astype(bf16)
        return 0
    lax.fori_loop(0,nblk,unperm,0,unroll=32)

def attn_bwd(bm,x,o,do,lse,cs,*,bq=512,bk=512):
    n=x.shape[0]; S=n*x.shape[2]; nblk=S//HB
    bq=math.gcd(S,bq); bk=math.gcd(bq,bk)
    vm=pl.BlockSpec(memory_space=pltpu.VMEM)
    return pl.pallas_call(
        lambda *a: attn_bwd_kernel(*a,nblk=nblk,per=x.shape[2]//HB,bq=bq,bk=bk),
        out_shape=jax.ShapeDtypeStruct((n,192,x.shape[2]),bf16),
        in_specs=[pl.BlockSpec(memory_space=pltpu.SMEM)]+[vm]*5,
        out_specs=vm,
        scratch_shapes=[pltpu.VMEM((64,S),bf16),pltpu.VMEM((S,64),bf16),pltpu.VMEM((64,S),bf16),pltpu.VMEM((S,64),bf16),pltpu.VMEM((64,S),bf16),
                        pltpu.VMEM((1,S),f32),pltpu.VMEM((64,S),f32),pltpu.VMEM((64,S),f32),pltpu.VMEM((64,S),f32)],
        compiler_params=pltpu.CompilerParams(vmem_limit_bytes=56<<20),name="attn_bwd")(bm,x,o,do,lse,cs)


SWAP = [(0, 1), (1, 0)]


def fast_fits(mesh):
    return mesh.shape["wsh"] == 2 and mesh.shape["ctx"] == H


def _params(mb=56):
    return pltpu.CompilerParams(vmem_limit_bytes=mb << 20)


def _norm(x):
    xf = x.astype(f32)
    cen = xf - jnp.mean(xf, axis=-1, keepdims=True)
    inv = lax.rsqrt(jnp.mean(cen * cen, axis=-1, keepdims=True) + epsilon)
    return cen * inv, inv


def _full(v):
    return pl.BlockSpec(v.shape, lambda *a: (0,) * v.ndim)


def _wq_specs(half, width, cols, quarter, at):
    own = lambda p: pl.BlockSpec(
        (half, cols),
        lambda *a: (0, p * (width // cols) + a[-1][0] * (half // cols) + a[-1][1] * (quarter // cols) + at(*a)),
    )
    got = lambda p: pl.BlockSpec((half, cols), lambda *a: (0, p * (quarter // cols) + at(*a)))
    return [own(p) for p in range(3)] + [got(p) for p in range(3)]


def norm_kernel(ids, a_ref, b_ref, n_ref, *refs):
    x_ref, ain_ref, min_ref = refs[-3:]
    mine = pl.program_id(0) == ids[1]
    x = jnp.where(mine, a_ref[...].astype(f32), b_ref[...].astype(f32))
    x_ref[...] = x.astype(bf16)
    xhat, _ = _norm(x)
    ain_ref[...] = (xhat * n_ref[0:1, :] + n_ref[1:2, :]).astype(bf16)
    min_ref[...] = (xhat * n_ref[2:3, :] + n_ref[3:4, :]).astype(bf16)


def norm_rows(ids, a, b, norms, before=()):
    rows, width = a.shape
    slot = 2 if before else 0
    out = jax.ShapeDtypeStruct((4 * rows, width), bf16)
    return pl.pallas_call(
        norm_kernel,
        grid_spec=pltpu.PrefetchScalarGridSpec(
            num_scalar_prefetch=1,
            grid=(2,),
            in_specs=[_full(a), _full(b), _full(norms)] + [pl.BlockSpec(memory_space=pl.ANY)] * len(before),
            out_specs=(pl.BlockSpec((rows, width), lambda i, ids: (slot + i, 0)),) * 3,
        ),
        out_shape=(out,) * 3,
        input_output_aliases={4 + k: k for k in range(len(before))},
        compiler_params=_params(),
        cost_estimate=pl.CostEstimate(flops=0, transcendentals=0, bytes_accessed=1 << 20),
        name="norm_rows",
    )(ids, a, b, norms, *before)


def turn_kernel(a_ref, b_ref, at_ref, bt_ref):
    at_ref[...] = a_ref[...].astype(f32).T.astype(bf16)
    bt_ref[...] = b_ref[...].astype(f32).T.astype(bf16)


def turn(a, b, steps=4):
    rows, width = a.shape
    src = pl.BlockSpec((rows // steps, width), lambda i: (i, 0))
    dst = pl.BlockSpec((width, rows // steps), lambda i: (0, i))
    return pl.pallas_call(
        turn_kernel,
        grid=(steps,),
        in_specs=[src, src],
        out_specs=(dst, dst),
        out_shape=(jax.ShapeDtypeStruct((width, rows), a.dtype),) * 2,
        compiler_params=_params(),
        cost_estimate=pl.CostEstimate(flops=0, transcendentals=0, bytes_accessed=1 << 20),
        name="turn",
    )(a, b)


def mask_kernel(ids, a_ref, b_ref, c_ref, d_ref, live_ref, w_ref, o_ref, f_ref):
    i = pl.program_id(0)
    mine = (i % 2) == ids[1]
    for slot, (own, sib) in enumerate(((a_ref, b_ref), (c_ref, d_ref))):
        @pl.when((i // 2) == slot)
        def _(own=own, sib=sib):
            v = jnp.where(mine, own[...].astype(f32), sib[...].astype(f32))
            o_ref[...] = (live_ref[...] * v).astype(bf16)

    f = _nt(w_ref[...], o_ref[...]).astype(bf16)
    for k in range(f_ref.shape[0]):
        f_ref[k] = f[k * HD : (k + 1) * HD, :]


def mask_rows(ids, own, own_sib, got, got_sib, live, w_out, quarter):
    rows, width = own.shape
    heads = quarter // HD
    return pl.pallas_call(
        mask_kernel,
        grid_spec=pltpu.PrefetchScalarGridSpec(
            num_scalar_prefetch=1,
            grid=(4,),
            in_specs=[_full(v) for v in (own, own_sib, got, got_sib)]
            + [
                pl.BlockSpec((rows, 1), lambda i, ids: (i, 0)),
                pl.BlockSpec((quarter, width), lambda i, ids: (ids[1], 0)),
            ],
            out_specs=(
                pl.BlockSpec((rows, width), lambda i, ids: (i, 0)),
                pl.BlockSpec((heads, HD, rows), lambda i, ids: (i // 2, 0, i % 2)),
            ),
        ),
        out_shape=(
            jax.ShapeDtypeStruct((4 * rows, width), bf16),
            jax.ShapeDtypeStruct((2 * heads, HD, 2 * rows), bf16),
        ),
        compiler_params=_params(),
        cost_estimate=pl.CostEstimate(flops=0, transcendentals=0, bytes_accessed=1 << 20),
        name="mask_rows",
    )(ids, own, own_sib, got, got_sib, live, w_out)


def qkv_kernel(
    ids, ain_ref, wq_ref, wk_ref, wv_ref, gq_ref, gk_ref, gv_ref, bq_ref, bk_ref, bv_ref, cs_ref, send_ref
):
    width = ain_ref.shape[1]
    half = width // 2
    me = ids[0]
    a_own = ain_ref[:, pl.ds(pl.multiple_of(me * half, half), half)]
    a_got = ain_ref[:, pl.ds(pl.multiple_of((1 - me) * half, half), half)]
    cos = cs_ref[0:8, :]
    sin = cs_ref[8:16, :]
    for n, (w, g, b) in enumerate(((wq_ref, gq_ref, bq_ref), (wk_ref, gk_ref, bk_ref), (wv_ref, gv_ref, bv_ref))):
        t = _nn(a_own, w[...]) + _nn(a_got, g[...]) + b[...]
        t = t.T
        for k in range(send_ref.shape[1]):
            v = t[k * HD : (k + 1) * HD]
            if n < 2:
                lead = v[0:8]
                trail = v[8:16]
                v = jnp.concatenate([lead * cos - trail * sin, trail * cos + lead * sin, v[16:]], axis=0)
            send_ref[0, k, n * HD : (n + 1) * HD, :] = v.astype(bf16)


def qkv_forward(ids, attn_in, w_own, w_got, bias, cs, cols=256):
    rows, width = attn_in.shape[0] // 2, attn_in.shape[1]
    half = width // 2
    quarter = w_got.shape[1] // 3
    bsp = lambda p: pl.BlockSpec((1, cols), lambda s, i, ids: (0, p * (quarter // cols) + i))
    return pl.pallas_call(
        qkv_kernel,
        grid_spec=pltpu.PrefetchScalarGridSpec(
            num_scalar_prefetch=1,
            grid=(2, quarter // cols),
            in_specs=[pl.BlockSpec((rows, width), lambda s, i, ids: (s, 0))]
            + _wq_specs(half, width, cols, quarter, lambda s, i, ids: i)
            + [bsp(p) for p in range(3)]
            + [_full(cs)],
            out_specs=pl.BlockSpec((1, cols // HD, 3 * HD, rows), lambda s, i, ids: (s, i, 0, 0)),
        ),
        out_shape=jax.ShapeDtypeStruct((2, quarter // HD, 3 * HD, rows), bf16),
        compiler_params=_params(),
        cost_estimate=pl.CostEstimate(flops=1 << 20, transcendentals=0, bytes_accessed=1 << 20),
        name="qkv_forward",
    )(ids, attn_in, w_own, w_own, w_own, w_got, w_got, w_got, bias, bias, bias, cs)


MLP_CHUNKS = 2


def mlp_kernel(ids, x_ref, xt_ref, dy_ref, wo_ref, wg_ref, wd_ref, bu_ref, y_ref, dx_ref, uk_ref, us_ref, dk_ref, ds_ref, gb_ref,
    g_s, act_s, du_s, y_s, dx_s
):
    rows, width = x_ref.shape
    half = width // 2
    me = ids[0]
    spans = (
        (pl.multiple_of(me * half, half), wo_ref[...]),
        (pl.multiple_of((1 - me) * half, half), wg_ref[...]),
    )

    @pl.when(pl.program_id(0) == 0)
    def _():
        y_s[...] = jnp.zeros_like(y_s)
        dx_s[...] = jnp.zeros_like(dx_s)

    wd = wd_ref[...]
    bias = bu_ref[...]
    step = rows // MLP_CHUNKS
    for c in range(MLP_CHUNKS):
        at = slice(c * step, (c + 1) * step)
        u = bias + sum(_nn(x_ref[at, pl.ds(o, half)], w) for o, w in spans)
        cdf = 0.5 * (1.0 + lax.erf(u * (1.0 / math.sqrt(2.0))))
        pdf = jnp.exp(-0.5 * u * u) * (1.0 / math.sqrt(2.0 * math.pi))
        act = (u * cdf).astype(bf16)
        du = (_nt(dy_ref[at, :], wd) * (cdf + u * pdf)).astype(bf16)
        y_s[at, :] += _nn(act, wd)
        for o, w in spans:
            dx_s[at, pl.ds(o, half)] += _nt(du, w)
        act_s[at, :] = act
        du_s[at, :] = du
    du = du_s[...]
    gd = lax.dot_general(
        act_s[...], dy_ref[...], (((0,), (0,)), ((), ())), preferred_element_type=f32
    ).astype(bf16)
    k, r, _ = dk_ref.shape
    k = gd.shape[0] // r
    early = pl.program_id(0) < pl.num_programs(0) // 2
    for c in range(k):
        v = gd[c * r : (c + 1) * r, :]

        @pl.when(early)
        def _(v=v, c=c):
            ds_ref[c] = v

        @pl.when(jnp.logical_not(early))
        def _(v=v, c=c):
            dk_ref[c] = v

    g_s[...] = _nn(xt_ref[...], du).astype(bf16)
    n = uk_ref.shape[0]
    r = uk_ref.shape[1] // 2
    for ref, side in ((uk_ref, ids[3]), (us_ref, 1 - ids[3])):
        for h in range(2):
            for c in range(n):
                at = pl.multiple_of(h * half + (side * n + c) * r, r)
                ref[c, h * r : (h + 1) * r, :] = g_s[pl.ds(at, r), :]
    gb_ref[...] = jnp.sum(du.astype(f32), axis=0, keepdims=True)

    @pl.when(pl.program_id(0) == pl.num_programs(0) - 1)
    def _():
        y_ref[...] = y_s[...].astype(bf16)
        dx_ref[...] = dx_s[...].astype(bf16)


def mlp(ids, x, xt, dy, w_own, w_got, wd, bu, n, tile=512):
    rows, width = x.shape
    half = width // 2
    hidden = w_got.shape[1]
    steps = hidden // tile
    mid = steps // 2
    whole = pl.BlockSpec((rows, width), lambda i, ids: (0, 0))
    per = hidden // n
    order = lambda i, ids: i % mid + mid * jnp.where(i < mid, 1 - ids[2], ids[2])
    part = lambda i, ids: ids[1] * steps + order(i, ids)
    up_spec = pl.BlockSpec((n // 2, width // n, tile), lambda i, ids: (0, 0, order(i, ids)))
    down_spec = lambda f: pl.BlockSpec((tile // per, per, width), lambda i, ids: (f(i), 0, 0))
    up_shape = jax.ShapeDtypeStruct((n // 2, width // n, hidden), bf16)
    down_shape = jax.ShapeDtypeStruct((n // 2, per, width), bf16)
    return pl.pallas_call(
        mlp_kernel,
        grid_spec=pltpu.PrefetchScalarGridSpec(
            num_scalar_prefetch=1,
            grid=(steps,),
            in_specs=[
                whole,
                pl.BlockSpec((width, rows), lambda i, ids: (0, 0)),
                whole,
                pl.BlockSpec((half, tile), lambda i, ids: (0, ids[0] * 2 * steps + part(i, ids))),
                pl.BlockSpec((half, tile), lambda i, ids: (0, order(i, ids))),
                pl.BlockSpec((tile, width), lambda i, ids: (part(i, ids), 0)),
                pl.BlockSpec((1, tile), lambda i, ids: (0, part(i, ids))),
            ],
            out_specs=(
                whole,
                whole,
                up_spec,
                up_spec,
                down_spec(lambda i: jnp.maximum(i - mid, 0)),
                down_spec(lambda i: jnp.minimum(i, mid - 1)),
                pl.BlockSpec((1, tile), lambda i, ids: (0, order(i, ids))),
            ),
            scratch_shapes=[pltpu.VMEM((width, tile), bf16), pltpu.VMEM((rows, tile), bf16), pltpu.VMEM((rows, tile), bf16)]
            + [pltpu.VMEM((rows, width), f32)] * 2,
        ),
        out_shape=(
            jax.ShapeDtypeStruct((rows, width), bf16),
            jax.ShapeDtypeStruct((rows, width), bf16),
            up_shape,
            up_shape,
            down_shape,
            down_shape,
            jax.ShapeDtypeStruct((1, hidden), f32),
        ),
        compiler_params=_params(),
        cost_estimate=pl.CostEstimate(
            flops=12 * rows * width * hidden, transcendentals=2 * rows * hidden, bytes_accessed=24 << 20
        ),
        name="mlp",
    )(ids, x, xt, dy, w_own, w_got, wd, bu)


def qkv_back_kernel(
    ids, d_ref, at_ref, x_ref, n_ref, wq_ref, wk_ref, wv_ref, gq_ref, gk_ref, gv_ref, dm_ref, ob_ref, dy_ref, gb_ref,
    a_ref, b_ref, e_ref, g_s, go_s, bias_s, sum_s
):
    rows, width = x_ref.shape
    half = width // 2
    me = ids[0]
    core = ids[1]
    s = pl.program_id(0)
    outs = (a_ref, b_ref)
    n = a_ref.shape[0]
    nh = d_ref.shape[1]
    cols = nh * HD
    r = half // (2 * n)

    @pl.when(s == 0)
    def _():
        g_s[...] = jnp.zeros_like(g_s)
        go_s[...] = jnp.zeros_like(go_s)
        bias_s[...] = jnp.zeros_like(bias_s)
        sum_s[...] = jnp.zeros_like(sum_s)

    ones = jnp.ones((8, rows), bf16)
    at = at_ref[...]
    dts = []
    for p in range(3):
        dp = jnp.concatenate([d_ref[0, k, p * HD : (p + 1) * HD, :] for k in range(nh)], axis=0)
        g_s[p] += _nt(at, dp)
        bias_s[p * 8 : (p + 1) * 8, :] += _nt(ones, dp)
        dts.append(dp.astype(f32).T.astype(bf16))
    go_s[...] += _nn(ob_ref[0], dy_ref[...])
    dt = jnp.concatenate(dts, axis=1)
    w_own = jnp.concatenate([wq_ref[...], wk_ref[...], wv_ref[...]], axis=1)
    w_got = jnp.concatenate([gq_ref[...], gk_ref[...], gv_ref[...]], axis=1)
    d_own = _nt(dt, w_own)
    d_got = _nt(dt, w_got)
    first = me == 0
    xhat, _ = _norm(x_ref[...])
    for h in range(2):
        lanes = slice(h * half, (h + 1) * half)
        da = jnp.where(first, d_own, d_got) if h == 0 else jnp.where(first, d_got, d_own)
        dm = dm_ref[:, lanes].astype(f32)
        xh = xhat[:, lanes]
        e_ref[0, :, lanes] = da * n_ref[0:1, lanes] + dm * n_ref[2:3, lanes]
        for k, v in enumerate((da * xh, da, dm * xh, dm)):
            sum_s[k : k + 1, lanes] += jnp.sum(v, axis=0, keepdims=True)

    @pl.when(s == 0)
    def _():
        mine = dy_ref[pl.ds(pl.multiple_of(core * (rows // 2), rows // 2), rows // 2), :]
        sum_s[4:5, :] = jnp.sum(mine.astype(f32), axis=0, keepdims=True)

    @pl.when(s == pl.num_programs(0) - 1)
    def _():
        for p in range(3):
            g = g_s[p].astype(bf16)
            for h in range(2):
                for c in range(n):
                    for a in range(2):
                        row = h * half + (c * 2 + a) * r
                        u = (h * 3 + p) * r
                        outs[a][c, u : u + r, :] = g[row : row + r, :]
        go = go_s[...].astype(bf16)
        q = cols // (2 * n)
        for c in range(n):
            for a in range(2):
                row = (c * 2 + a) * q
                for k in range(width // cols):
                    u = 6 * r + k * q
                    outs[a][c, u : u + q, :] = go[row : row + q, k * cols : (k + 1) * cols]
        flat = [sum_s[k : k + 1, t * cols : (t + 1) * cols] for k in range(5) for t in range(width // cols)]
        zero = jnp.zeros((1, cols), f32)
        for p in range(3):
            flat += [
                jnp.where((me == k) & (core == j), bias_s[p * 8 : p * 8 + 1, :], zero) for k in range(2) for j in range(2)
            ]
        flat += [
            jnp.where((me == k) & (core == j), gb_ref[:, t * cols : (t + 1) * cols], zero)
            for k in range(2)
            for j in range(2)
            for t in range(gb_ref.shape[1] // cols)
        ]
        top = 6 * r + (width // cols) * q
        per = len(flat) // n
        pad = [zero] * (8 - per)
        for c in range(n):
            b_ref[c, top : top + 8, :] = jnp.concatenate(flat[c * per : (c + 1) * per] + pad, axis=0).astype(bf16)


def qkv_backward(ids, d, at, x2, norms, w_own, w_got, d_mlp, ob, dy, gb_up, n):
    rows, width = x2.shape[0] // 2, x2.shape[1]
    half = width // 2
    cols = w_got.shape[1] // 3
    size = 6 * (half // (2 * n)) + width // (2 * n)
    row = lambda: pl.BlockSpec((rows, width), lambda s, ids: (s, 0))
    out = [
        jax.ShapeDtypeStruct((n, size, cols), bf16),
        jax.ShapeDtypeStruct((n, size + 8, cols), bf16),
    ]
    return pl.pallas_call(
        qkv_back_kernel,
        grid_spec=pltpu.PrefetchScalarGridSpec(
            num_scalar_prefetch=1,
            grid=(2,),
            in_specs=[
                pl.BlockSpec((1, cols // HD, 3 * HD, rows), lambda s, ids: (s, 0, 0, 0)),
                pl.BlockSpec((width, rows), lambda s, ids: (0, s)),
                row(),
                _full(norms),
            ]
            + _wq_specs(half, width, cols, cols, lambda s, ids: 0)
            + [row(), pl.BlockSpec((1, cols, rows), lambda s, ids: (s, 0, 0)), row(), _full(gb_up)],
            out_specs=(*[_full(v) for v in out], pl.BlockSpec((1, rows, width), lambda s, ids: (s, 0, 0))),
            scratch_shapes=[
                pltpu.VMEM((3, width, cols), f32),
                pltpu.VMEM((cols, width), f32),
                pltpu.VMEM((24, cols), f32),
                pltpu.VMEM((8, width), f32),
            ],
        ),
        out_shape=(*out, jax.ShapeDtypeStruct((2, rows, width), f32)),
        compiler_params=_params(),
        name="qkv_backward",
    )(ids, d, at, x2, norms, w_own, w_own, w_own, w_got, w_got, w_got, d_mlp, ob, dy, gb_up)


def _mine(ids):
    return (pl.program_id(0) // 2) == ids[1]


def _own_block(i, ids):
    return jnp.clip(i - 2 * ids[1], 0, 1)


def _got_block(i, ids):
    return jnp.clip(i - 2 * (1 - ids[1]), 0, 1)


def join_kernel(ids, own_ref, got_ref, o_ref):
    mine = _mine(ids)
    shape = o_ref.shape

    @pl.when(mine)
    def _():
        o_ref[...] = own_ref[...].astype(f32).reshape(shape)

    @pl.when(jnp.logical_not(mine))
    def _():
        o_ref[...] = got_ref[...].astype(f32).reshape(shape)


def join_rows(ids, own, got):
    n, r, w = own.shape
    src = lambda f: pl.BlockSpec((n // 2, r, w), lambda i, ids: (f(i, ids), 0, 0))
    return pl.pallas_call(
        join_kernel,
        grid_spec=pltpu.PrefetchScalarGridSpec(
            num_scalar_prefetch=1,
            grid=(4,),
            in_specs=[src(_own_block), src(_got_block)],
            out_specs=pl.BlockSpec((n * r // 2, w), lambda i, ids: (i, 0)),
        ),
        out_shape=jax.ShapeDtypeStruct((2 * n * r, w), f32),
        compiler_params=_params(),
        name="join_rows",
    )(ids, own, got)


def join_cols(ids, own, got):
    n, _, r, w = own.shape
    src = lambda f: pl.BlockSpec((n, 1, r, w), lambda i, ids: (0, f(i, ids), 0, 0))
    return pl.pallas_call(
        join_kernel,
        grid_spec=pltpu.PrefetchScalarGridSpec(
            num_scalar_prefetch=1,
            grid=(4,),
            in_specs=[src(_own_block), src(_got_block)],
            out_specs=pl.BlockSpec((n * r, w), lambda i, ids: (0, (i % 2) * 2 + i // 2)),
        ),
        out_shape=jax.ShapeDtypeStruct((n * r, 4 * w), f32),
        compiler_params=_params(),
        name="join_cols",
    )(ids, own, got)


def unpack_kernel(ids, ao_ref, ag_ref, bo_ref, bg_ref, q_ref, o_ref, s_ref):
    first = ids[1] == 0
    k, _, cols = ao_ref.shape
    r = q_ref.shape[0] // (2 * k)
    q = o_ref.shape[1] // (2 * k)
    for a, (own, got) in enumerate(((ao_ref, ag_ref), (bo_ref, bg_ref))):
        for c in range(k):
            x = own[c].astype(f32)
            y = got[c].astype(f32)
            to = slice((c * 2 + a) * r, (c * 2 + a + 1) * r)
            tq = slice((c * 2 + a) * q, (c * 2 + a + 1) * q)
            for j in range(2):
                v = jnp.where(first, x, y) if j == 0 else jnp.where(first, y, x)
                for w in range(2):
                    for p in range(3):
                        u = (w * 3 + p) * r
                        at = ((p * 2 + w) * 2 + j) * cols
                        q_ref[to, at : at + cols] = v[u : u + r, :]
                for t in range(o_ref.shape[2] // cols):
                    u = 6 * r + t * q
                    o_ref[j, tq, t * cols : (t + 1) * cols] = v[u : u + q, :]
            if a == 1:
                s_ref[c] = (x + y)[-8:, :]


def unpack(ids, a_own, a_got, b_own, b_got, width, steps=4):
    n, _, cols = a_own.shape
    half = width // 2
    k = n // steps
    spec = lambda v: pl.BlockSpec((k,) + v.shape[1:], lambda i, ids: (i, 0, 0))
    return pl.pallas_call(
        unpack_kernel,
        grid_spec=pltpu.PrefetchScalarGridSpec(
            num_scalar_prefetch=1,
            grid=(steps,),
            in_specs=[spec(v) for v in (a_own, a_got, b_own, b_got)],
            out_specs=(
                pl.BlockSpec((half // steps, 3 * width), lambda i, ids: (i, 0)),
                pl.BlockSpec((2, cols // steps, width), lambda i, ids: (0, i, 0)),
                pl.BlockSpec((k, 8, cols), lambda i, ids: (i, 0, 0)),
            ),
        ),
        out_shape=(
            jax.ShapeDtypeStruct((half, 3 * width), f32),
            jax.ShapeDtypeStruct((2, cols, width), f32),
            jax.ShapeDtypeStruct((n, 8, cols), f32),
        ),
        compiler_params=_params(),
        name="unpack",
    )(ids, a_own, a_got, b_own, b_got)


def last_kernel(eo_ref, er_ref, x_ref, c_ref, live_ref, o_ref):
    xhat, inv = _norm(x_ref[...])
    e = eo_ref[...] + er_ref[...].astype(f32)
    dx = inv * (
        e - jnp.mean(e, axis=-1, keepdims=True) - xhat * jnp.mean(e * xhat, axis=-1, keepdims=True)
    )
    o_ref[...] = live_ref[...] * c_ref[...].astype(f32) + dx


def last(e_own, e_got, x, cot, live):
    return pl.pallas_call(
        last_kernel,
        out_shape=jax.ShapeDtypeStruct(x.shape, f32),
        compiler_params=_params(),
        name="token_grad",
    )(e_own, e_got, x, cot, live)


def fast_shards(
    tokens,
    ln1_gain,
    ln1_bias,
    ln2_gain,
    ln2_bias,
    w_qkv,
    b_qkv,
    w_out,
    b_out,
    w_up,
    b_up,
    w_down,
    b_down,
    lengths,
    block_map,
    cotangent,
):
    ctx = lax.axis_index("ctx")
    me = lax.axis_index("wsh")
    core = ctx % 2
    n_ctx = lax.axis_size("ctx")
    chips = n_ctx // 2
    own_rows, width = tokens.shape[1:]
    rows = 2 * own_rows
    half = width // 2
    quarter = half // 2
    seq = own_rows * n_ctx
    heads = H // 4
    hid = w_up.shape[1] // 4
    CORE, X, ZN, ZF = 0, 1, 2, 3

    def swap(v):
        return lax.ppermute(v, "wsh", SWAP)

    def flip(v, bit):
        return lax.ppermute(v, "ctx", [(i, i ^ (1 << bit)) for i in range(n_ctx)])

    def bit_of(bit):
        return (ctx >> bit) & 1

    ids = jnp.stack([me, core, bit_of(X), bit_of(ZN)]).astype(jnp.int32)

    def add(*terms):
        return sum(v.astype(f32) for v in terms).astype(bf16) if len(terms) > 1 else terms[0]

    def halve(terms, bit):
        b = bit_of(bit)
        cut = [v.reshape((2, v.shape[0] // 2) + v.shape[1:]) for v in terms]
        part = lambda k: [lax.dynamic_index_in_dim(v, k, 0, keepdims=False) for v in cut]
        return part(b) + [flip(add(*part(1 - b)), bit)]

    def ordered(first, a, b, axis=0):
        return jnp.where(first == 0, jnp.concatenate([a, b], axis), jnp.concatenate([b, a], axis))

    def double(v, bit):
        return ordered(bit_of(bit), v, flip(v, bit))

    def exchange(v):
        groups = [[2 * i + c for i in range(chips)] for c in range(2)]
        return lax.all_to_all(v, "ctx", 0, 0, axis_index_groups=groups, tiled=False)

    def rows_of(v, at, n, axis=0):
        return lax.dynamic_slice_in_dim(v, at, n, axis)

    x_own = tokens[0]
    x_got = swap(x_own)
    x_sib = flip(x_own, CORE)
    mine = me * half + core * quarter
    other = (1 - me) * half + core * quarter
    wq_send = jnp.concatenate([rows_of(w_qkv, p * width + other, quarter, 1) for p in range(3)], axis=1)
    wq_send, ln1_gain = lax.optimization_barrier((wq_send, ln1_gain))
    len_parts = jnp.stack([lengths[0] // 64, lengths[0] % 64]).astype(bf16)
    parts = [ln1_gain, ln1_bias, ln2_gain, ln2_bias, b_out, b_down, b_qkv, jnp.pad(len_parts, (0, half - 2))]
    small = jnp.concatenate([v.reshape(-1, half) for v in parts])
    small = ordered(me, small[None], swap(small)[None])
    wq_got = swap(wq_send)
    vec = lambda i: small[:, i].reshape(width).astype(f32)
    norms = jnp.stack([vec(i) for i in range(4)])
    bias_out = vec(4) + vec(5)
    qkv_bias = small[:, 6:9].astype(f32).reshape(3, width)
    qkv_bias = rows_of(qkv_bias, mine, quarter, 1).reshape(1, 3 * quarter)
    lens = small[:, 9, :2].astype(jnp.int32)
    lens = lens[:, 0] * 64 + lens[:, 1]
    other_len = lens[1 - me]

    normed = norm_rows(ids, x_own, x_sib, norms)
    cot_own = cotangent[0]
    wu_send = rows_of(w_up, ((1 - me) * 2 + core) * hid, hid, 1)
    wq_got, cot_send, normed = lax.optimization_barrier((wq_got, cot_own, normed))
    cot_got = swap(cot_send)
    cot_got, wu_send = lax.optimization_barrier((cot_got, wu_send))
    wu_got = swap(wu_send)
    normed = norm_rows(ids, x_got, flip(x_got, CORE), norms, normed)
    x2, attn_in, mlp_in = normed
    cot_sib = flip(cot_own, CORE)

    blocks = rows_of(block_map, (rows // HB) * (ctx // 2), rows // HB)
    offs = jnp.arange(HB, dtype=jnp.int32)
    positions = (blocks[:, None] * HB + offs[None, :]).reshape(rows)
    live2 = jnp.concatenate([positions < lengths[0], positions < other_len]).astype(f32)[:, None]
    live_own = rows_of(live2, core * own_rows, own_rows)
    freq = 10000.0 ** (-jnp.arange(ROT // 2, dtype=f32) * 2.0 / ROT)
    ang = freq[:, None] * jnp.arange(seq, dtype=jnp.int32).astype(f32)[None, :]
    table = jnp.concatenate([jnp.cos(ang), jnp.sin(ang)])
    own_ang = freq[:, None] * positions.astype(f32)[None, :]
    own_table = jnp.concatenate([jnp.cos(own_ang), jnp.sin(own_ang)])

    attn_in, table = lax.optimization_barrier((attn_in, table))
    send = qkv_forward(ids, attn_in, w_qkv, wq_got, qkv_bias, own_table)
    qkv_head = exchange(send.reshape(2 * heads, 3 * HD, rows))
    dy, dctx = mask_rows(ids, cot_own, cot_sib, cot_got, flip(cot_got, CORE), live2, w_out, quarter)
    w_out_mine = rows_of(w_out, core * quarter, quarter)
    do_head = exchange(dctx)

    attn_t, mlp_t = turn(attn_in, mlp_in)
    do_head = exchange(dctx.reshape(2 * heads, HD, rows))
    y_mlp, d_mlp, up_keep, up_send, down_keep, down_send, gb_up = mlp(
        ids, mlp_in, mlp_t, dy, w_up, wu_got, w_down, b_up.astype(f32)[None, :], chips
    )

    chain_a = (X, ZN, ZF)
    chain_b = (ZN, ZF, X)
    qkv_head, up_send, down_send = lax.optimization_barrier((qkv_head, up_send, down_send))
    down = [down_keep, flip(down_send, chain_a[0])]
    up = [up_keep, flip(up_send, chain_b[0])]

    o_head, lse = attn_fwd(block_map, qkv_head, bq=1024, bk=1024)
    qkv_head, o_head, do_head, down[-1], up[-1] = lax.optimization_barrier((qkv_head, o_head, do_head, down[-1], up[-1]))
    ob = exchange(o_head).reshape(2, quarter, rows)
    down = halve(down, chain_a[1])
    up = halve(up, chain_b[1])
    g_head = attn_bwd(block_map, qkv_head, o_head, do_head, lse, table)
    g_head, ob = lax.optimization_barrier((g_head, ob))
    d_qkv = exchange(g_head).reshape(2, heads, 3 * HD, rows)

    down = add(*halve(down, chain_a[2]))
    up = add(*halve(up, chain_b[2]))
    up = up.reshape(1, 2, up.shape[1] // 2, up.shape[2])
    up_keep = rows_of(up, me, 1, 1)
    up_got = swap(rows_of(up, 1 - me, 1, 1))
    up = ordered(me, up_keep, up_got, axis=1)
    for a, b in zip(chain_a[::-1], chain_b[::-1]):
        down = double(down, a)
        up = double(up, b)
    tot_down = join_rows(ids, down, flip(down, CORE))
    tot_up = join_cols(ids, up, flip(up, CORE))

    def settle(v):
        give = rows_of(v, (1 - core) * own_rows, own_rows, 1).astype(bf16)
        v = rows_of(v, core * own_rows, own_rows, 1) + flip(give, CORE).astype(f32)
        return v[0], swap(v[1].astype(bf16))

    part = jnp.einsum("sct,cd->std", ob, w_out_mine, preferred_element_type=f32) + y_mlp.reshape(2, rows, width).astype(f32)
    part, part_got = settle(part)
    output = (live_own * (x_own.astype(f32) + part + part_got.astype(f32) + bias_out)).astype(bf16)

    v_a, v_b, e = qkv_backward(
        ids, d_qkv, attn_t, x2, norms, w_qkv, wq_got, d_mlp, ob, dy, gb_up, chips
    )
    v_a = [v_a]
    v_b = [v_b]
    for a, b in zip(chain_a, chain_b):
        v_a = halve(v_a, a)
        v_b = halve(v_b, b)
    e_own, e_got = settle(e)
    n3 = 3 * half // (2 * chips)
    size = 2 * n3 + width // (2 * chips)
    tail = []
    for v in (add(*v_a)[0], add(*v_b)[0]):
        extra = v[size:]
        back = swap(jnp.concatenate([rows_of(v, (1 - me) * n3, n3), extra]))
        extra = add(extra, back[n3:])
        tail.append(jnp.concatenate([ordered(me, rows_of(v, me * n3, n3), back[:n3]), v[2 * n3 : size], extra])[None])
    grad_tokens = last(e_own, e_got, x_own, cot_own, live_own)
    cover = [[grad_tokens, output], [tot_down], [tot_up]]
    for k, (a, b) in enumerate(zip(chain_a[::-1], chain_b[::-1])):
        tail = [double(tail[0], a), double(tail[1], b)]
        tail, cover[k] = lax.optimization_barrier((tail, cover[k]))
    mixed = tail
    (grad_tokens, output), (tot_down,), (tot_up,) = cover
    tot_qkv, tot_out, flat = unpack(ids, mixed[0], flip(mixed[0], CORE), mixed[1], flip(mixed[1], CORE), width)
    flat = flat[:, :6].reshape(12 * width)

    def own(start, size):
        return lax.dynamic_slice_in_dim(flat, start + me * size, size)

    gb_out = own(4 * width, half)
    return (
        output[None],
        grad_tokens[None],
        own(0, half),
        own(width, half),
        own(2 * width, half),
        own(3 * width, half),
        tot_qkv,
        own(5 * width, 3 * half),
        tot_out.reshape(half, width),
        gb_out,
        tot_up,
        own(8 * width, 2 * hid),
        tot_down,
        gb_out,
    )


def solution(mesh):
    placed = (
        P("wsh", "ctx", None),
        P("wsh"),
        P("wsh"),
        P("wsh"),
        P("wsh"),
        P("wsh", None),
        P("wsh"),
        P("wsh", None),
        P("wsh"),
        P("wsh", None),
        P("wsh"),
        P("wsh", None),
        P("wsh"),
        P("wsh"),
        P(),
        P("wsh", "ctx", None),
    )
    body = fast_shards if fast_fits(mesh) else shards
    return jax.shard_map(
        body,
        mesh=mesh,
        in_specs=placed,
        out_specs=(
            P("wsh", "ctx", None),
            P("wsh", "ctx", None),
            P("wsh"),
            P("wsh"),
            P("wsh"),
            P("wsh"),
            P("wsh", None),
            P("wsh"),
            P("wsh", None),
            P("wsh"),
            P("wsh", None),
            P("wsh"),
            P("wsh", None),
            P("wsh"),
        ),
        check_vma=False,
    )
```

```python
from functools import partial
import math

import jax
import jax.numpy as jnp
from jax import lax
from jax.experimental import pallas as pl
from jax.experimental.pallas import tpu as pltpu
from jax.sharding import PartitionSpec as P

H = 16
HD = 64
ROT = 16


epsilon = 1e-05


def norm_forward(values, norm_gain, norm_shift):
    average = jnp.mean(values, axis=-1, keepdims=True)
    centred = values - average
    variance = jnp.mean(centred * centred, axis=-1, keepdims=True)
    inverse = lax.rsqrt(variance + epsilon)
    normed = centred * inverse
    return (normed * norm_gain + norm_shift, normed, inverse)


def norm_backward(grad_out, normed, inverse, norm_gain):
    scaled = grad_out * norm_gain
    adjusted = (
        scaled
        - jnp.mean(scaled, axis=-1, keepdims=True)
        - normed * jnp.mean(scaled * normed, axis=-1, keepdims=True)
    )
    return (adjusted * inverse, jnp.sum(grad_out * normed, axis=0), jnp.sum(grad_out, axis=0))


def rotary_tables(positions):
    half_rot = ROT // 2
    frequency = 10000.0 ** (-jnp.arange(half_rot, dtype=jnp.float32) * 2.0 / ROT)
    angles = positions.astype(jnp.float32)[:, None] * frequency[None, :]
    return (jnp.cos(angles)[:, None, :], jnp.sin(angles)[:, None, :])


def rotate_forward(values, cosine_table, sine_table):
    half_rot = ROT // 2
    leading = values[..., :half_rot]
    trailing = values[..., half_rot:ROT]
    return jnp.concatenate(
        [
            leading * cosine_table - trailing * sine_table,
            trailing * cosine_table + leading * sine_table,
            values[..., ROT:],
        ],
        axis=-1,
    )


def rotate_backward(grads, cosine_table, sine_table):
    half_rot = ROT // 2
    leading = grads[..., :half_rot]
    trailing = grads[..., half_rot:ROT]
    return jnp.concatenate(
        [
            leading * cosine_table + trailing * sine_table,
            trailing * cosine_table - leading * sine_table,
            grads[..., ROT:],
        ],
        axis=-1,
    )


def masked_scores(query_rows, key_rows, query_pos, key_pos, key_live):
    raw_scores = jnp.einsum(
        "qhd,khd->hqk", query_rows, key_rows, preferred_element_type=jnp.float32
    )
    allowed = (key_pos[None, :] <= query_pos[:, None]) & key_live[None, :]
    return (jnp.where(allowed[None], raw_scores * (1.0 / math.sqrt(HD)), -1e30), allowed)


def score_grads(
    query_rows, key_rows, value_rows, grad_rows, query_pos, key_pos, key_live, log_total, row_dots
):
    scores = masked_scores(query_rows, key_rows, query_pos, key_pos, key_live)[0]
    probability = jnp.exp(scores - log_total[..., None])
    grad_prob = jnp.einsum(
        "qhd,khd->hqk", grad_rows, value_rows, preferred_element_type=jnp.float32
    )
    grad_score = (probability * (grad_prob - row_dots[..., None]) * (1.0 / math.sqrt(HD))).astype(
        jnp.bfloat16
    )
    return (probability.astype(jnp.bfloat16), grad_score)


def shards(
    tokens,
    ln1_gain,
    ln1_bias,
    ln2_gain,
    ln2_bias,
    w_qkv,
    b_qkv,
    w_out,
    b_out,
    w_up,
    b_up,
    w_down,
    b_down,
    lengths,
    block_map,
    cotangent,
):
    gathered = (
        lax.all_gather(ln1_gain, "wsh", axis=0, tiled=True),
        lax.all_gather(ln1_bias, "wsh", axis=0, tiled=True),
        lax.all_gather(ln2_gain, "wsh", axis=0, tiled=True),
        lax.all_gather(ln2_bias, "wsh", axis=0, tiled=True),
        lax.all_gather(w_qkv, "wsh", axis=0, tiled=True),
        lax.all_gather(b_qkv, "wsh", axis=0, tiled=True),
        lax.all_gather(w_out, "wsh", axis=0, tiled=True),
        lax.all_gather(b_out, "wsh", axis=0, tiled=True),
        lax.all_gather(w_up, "wsh", axis=0, tiled=True),
        lax.all_gather(b_up, "wsh", axis=0, tiled=True),
        lax.all_gather(w_down, "wsh", axis=0, tiled=True),
        lax.all_gather(b_down, "wsh", axis=0, tiled=True),
    )
    (
        norm1_gain,
        norm1_shift,
        norm2_gain,
        norm2_shift,
        qkv_weight,
        qkv_bias,
        out_weight,
        out_bias,
        up_weight,
        up_bias,
        down_weight,
        down_bias,
    ) = gathered
    tok_rows = tokens.shape[1]
    model_width = tokens.shape[2]
    half_rows = tok_rows // 2
    seq_rows = tok_rows * lax.axis_size("ctx")
    head_count = H
    head_size = HD
    ctx_index = lax.axis_index("ctx")
    own_blocks = lax.dynamic_slice_in_dim(block_map, 2 * ctx_index, 2)
    local_offsets = jnp.arange(half_rows, dtype=jnp.int32)
    positions = (own_blocks[:, None] * half_rows + local_offsets[None, :]).reshape(tok_rows)
    key_pos = (block_map[:, None] * half_rows + local_offsets[None, :]).reshape(seq_rows)
    length = lengths[0]
    own_live = positions < length
    live_rows = own_live.astype(jnp.float32)
    key_live = key_pos < length
    gain_first = norm1_gain.astype(jnp.float32)
    gain_second = norm2_gain.astype(jnp.float32)
    token_rows = tokens[0].astype(jnp.float32)
    normal_first, normed_first, inverse_first = norm_forward(
        token_rows, gain_first, norm1_shift.astype(jnp.float32)
    )
    normal_second, normed_second, inverse_second = norm_forward(
        token_rows, gain_second, norm2_shift.astype(jnp.float32)
    )
    attn_in = normal_first.astype(jnp.bfloat16)
    mlp_in = normal_second.astype(jnp.bfloat16)
    projected = (
        jnp.dot(attn_in, qkv_weight, preferred_element_type=jnp.float32)
        + qkv_bias.astype(jnp.float32)
    ).reshape(tok_rows, 3, head_count, head_size)
    cosine_table, sine_table = rotary_tables(positions)
    queries = rotate_forward(projected[:, 0], cosine_table, sine_table).astype(jnp.bfloat16)
    key_own = (
        rotate_forward(projected[:, 1], cosine_table, sine_table)
        .astype(jnp.bfloat16)
        .reshape(tok_rows, model_width)
    )
    value_own = projected[:, 2].astype(jnp.bfloat16).reshape(tok_rows, model_width)
    keys_all, values_all = (
        lax.all_gather(key_own, "ctx", axis=0, tiled=True),
        lax.all_gather(value_own, "ctx", axis=0, tiled=True),
    )
    block_len = math.gcd(seq_rows, 1024)
    block_count = seq_rows // block_len
    key_stack = keys_all.reshape(block_count, block_len, head_count, head_size)
    value_stack = values_all.reshape(block_count, block_len, head_count, head_size)
    pos_stack = key_pos.reshape(block_count, block_len)
    live_stack = key_live.reshape(block_count, block_len)

    def stats_step(running, key_part):
        key_block, pos_block, live_block = key_part
        scores, allowed = masked_scores(queries, key_block, positions, pos_block, live_block)
        peak_score = jnp.maximum(running[0], jnp.max(scores, axis=-1))
        exp_total = running[1] * jnp.exp(running[0] - peak_score) + jnp.sum(
            jnp.where(allowed[None], jnp.exp(scores - peak_score[..., None]), 0.0), axis=-1
        )
        return ((peak_score, exp_total), None)

    start_peak = jnp.full((head_count, tok_rows), -1e30, jnp.float32)
    final_state = lax.scan(
        stats_step, (start_peak, jnp.zeros_like(start_peak)), (key_stack, pos_stack, live_stack)
    )[0]
    log_total = final_state[0] + jnp.log(final_state[1])

    def value_step(running, key_part):
        key_block, value_block, pos_block, live_block = key_part
        scores = masked_scores(queries, key_block, positions, pos_block, live_block)[0]
        probability = jnp.exp(scores - log_total[..., None]).astype(jnp.bfloat16)
        return (
            running
            + jnp.einsum(
                "hqk,khd->qhd", probability, value_block, preferred_element_type=jnp.float32
            ),
            None,
        )

    zero_heads = jnp.zeros((tok_rows, head_count, head_size), jnp.float32)
    attended = lax.scan(value_step, zero_heads, (key_stack, value_stack, pos_stack, live_stack))[0]
    context_low = attended.reshape(tok_rows, model_width).astype(jnp.bfloat16)
    hidden = jnp.dot(mlp_in, up_weight, preferred_element_type=jnp.float32) + up_bias.astype(
        jnp.float32
    )
    activated, gelu_pull = jax.vjp(partial(jax.nn.gelu, approximate=False), hidden)
    act_low = activated.astype(jnp.bfloat16)
    branch = (
        jnp.dot(context_low, out_weight, preferred_element_type=jnp.float32)
        + out_bias.astype(jnp.float32)
        + jnp.dot(act_low, down_weight, preferred_element_type=jnp.float32)
        + down_bias.astype(jnp.float32)
    )
    output_rows = (live_rows[:, None] * (token_rows + branch)).astype(jnp.bfloat16)
    cot_rows = cotangent[0].astype(jnp.float32)
    grad_branch = (live_rows[:, None] * cot_rows).astype(jnp.bfloat16)
    grad_w_out = jnp.einsum(
        "tc,td->cd", context_low, grad_branch, preferred_element_type=jnp.float32
    )
    grad_w_down = jnp.einsum("tc,td->cd", act_low, grad_branch, preferred_element_type=jnp.float32)
    grad_branch_sum = jnp.sum(grad_branch.astype(jnp.float32), axis=0)
    grad_act = jnp.einsum("td,cd->tc", grad_branch, down_weight, preferred_element_type=jnp.float32)
    grad_hidden = gelu_pull(grad_act)[0].astype(jnp.bfloat16)
    grad_w_up = jnp.einsum("tc,td->cd", mlp_in, grad_hidden, preferred_element_type=jnp.float32)
    grad_b_up = jnp.sum(grad_hidden.astype(jnp.float32), axis=0)
    grad_mlp_in = jnp.einsum(
        "td,cd->tc", grad_hidden, up_weight, preferred_element_type=jnp.float32
    )
    grad_context = jnp.einsum(
        "td,cd->tc", grad_branch, out_weight, preferred_element_type=jnp.float32
    ).astype(jnp.bfloat16)
    grad_heads = grad_context.reshape(tok_rows, head_count, head_size)
    row_dots = jnp.sum(grad_heads.astype(jnp.float32) * attended, axis=-1).T

    def grad_step(running, key_part):
        key_block, value_block, pos_block, live_block = key_part
        prob_low, grad_score = score_grads(
            queries,
            key_block,
            value_block,
            grad_heads,
            positions,
            pos_block,
            live_block,
            log_total,
            row_dots,
        )
        query_sum = running + jnp.einsum(
            "hqk,khd->qhd", grad_score, key_block, preferred_element_type=jnp.float32
        )
        key_term = jnp.einsum(
            "hqk,qhd->khd", grad_score, queries, preferred_element_type=jnp.float32
        )
        value_term = jnp.einsum(
            "hqk,qhd->khd", prob_low, grad_heads, preferred_element_type=jnp.float32
        )
        return (query_sum, (key_term, value_term))

    query_grad, term_stacks = lax.scan(
        grad_step, zero_heads, (key_stack, value_stack, pos_stack, live_stack)
    )
    key_grad, value_grad = (
        lax.psum_scatter(
            term_stacks[0].reshape(seq_rows, model_width).astype(jnp.bfloat16),
            "ctx",
            scatter_dimension=0,
            tiled=True,
        ).astype(jnp.float32),
        lax.psum_scatter(
            term_stacks[1].reshape(seq_rows, model_width).astype(jnp.bfloat16),
            "ctx",
            scatter_dimension=0,
            tiled=True,
        ).astype(jnp.float32),
    )
    key_grad = key_grad.reshape(tok_rows, head_count, head_size)
    value_grad = value_grad.reshape(tok_rows, head_count, head_size)
    grad_projected = (
        jnp.stack(
            [
                rotate_backward(query_grad, cosine_table, sine_table),
                rotate_backward(key_grad, cosine_table, sine_table),
                value_grad,
            ],
            axis=1,
        )
        .reshape(tok_rows, 3 * model_width)
        .astype(jnp.bfloat16)
    )
    grad_w_qkv = jnp.einsum(
        "tc,td->cd", attn_in, grad_projected, preferred_element_type=jnp.float32
    )
    grad_b_qkv = jnp.sum(grad_projected.astype(jnp.float32), axis=0)
    grad_attn_in = jnp.einsum(
        "td,cd->tc", grad_projected, qkv_weight, preferred_element_type=jnp.float32
    )
    grad_input_first, grad_gain_first, grad_shift_first = norm_backward(
        grad_attn_in, normed_first, inverse_first, gain_first
    )
    grad_input_second, grad_gain_second, grad_shift_second = norm_backward(
        grad_mlp_in, normed_second, inverse_second, gain_second
    )
    grad_input = live_rows[:, None] * cot_rows + grad_input_first + grad_input_second
    shares = (
        lax.psum_scatter(
            grad_gain_first.astype(jnp.bfloat16), "wsh", scatter_dimension=0, tiled=True
        ).astype(jnp.float32),
        lax.psum_scatter(
            grad_shift_first.astype(jnp.bfloat16), "wsh", scatter_dimension=0, tiled=True
        ).astype(jnp.float32),
        lax.psum_scatter(
            grad_gain_second.astype(jnp.bfloat16), "wsh", scatter_dimension=0, tiled=True
        ).astype(jnp.float32),
        lax.psum_scatter(
            grad_shift_second.astype(jnp.bfloat16), "wsh", scatter_dimension=0, tiled=True
        ).astype(jnp.float32),
        lax.psum_scatter(
            grad_w_qkv.astype(jnp.bfloat16), "wsh", scatter_dimension=0, tiled=True
        ).astype(jnp.float32),
        lax.psum_scatter(
            grad_b_qkv.astype(jnp.bfloat16), "wsh", scatter_dimension=0, tiled=True
        ).astype(jnp.float32),
        lax.psum_scatter(
            grad_w_out.astype(jnp.bfloat16), "wsh", scatter_dimension=0, tiled=True
        ).astype(jnp.float32),
        lax.psum_scatter(
            grad_branch_sum.astype(jnp.bfloat16), "wsh", scatter_dimension=0, tiled=True
        ).astype(jnp.float32),
        lax.psum_scatter(
            grad_w_up.astype(jnp.bfloat16), "wsh", scatter_dimension=0, tiled=True
        ).astype(jnp.float32),
        lax.psum_scatter(
            grad_b_up.astype(jnp.bfloat16), "wsh", scatter_dimension=0, tiled=True
        ).astype(jnp.float32),
        lax.psum_scatter(
            grad_w_down.astype(jnp.bfloat16), "wsh", scatter_dimension=0, tiled=True
        ).astype(jnp.float32),
        lax.psum_scatter(
            grad_branch_sum.astype(jnp.bfloat16), "wsh", scatter_dimension=0, tiled=True
        ).astype(jnp.float32),
    )
    totals = (
        lax.psum(shares[0].astype(jnp.bfloat16), "ctx").astype(jnp.float32),
        lax.psum(shares[1].astype(jnp.bfloat16), "ctx").astype(jnp.float32),
        lax.psum(shares[2].astype(jnp.bfloat16), "ctx").astype(jnp.float32),
        lax.psum(shares[3].astype(jnp.bfloat16), "ctx").astype(jnp.float32),
        lax.psum(shares[4].astype(jnp.bfloat16), "ctx").astype(jnp.float32),
        lax.psum(shares[5].astype(jnp.bfloat16), "ctx").astype(jnp.float32),
        lax.psum(shares[6].astype(jnp.bfloat16), "ctx").astype(jnp.float32),
        lax.psum(shares[7].astype(jnp.bfloat16), "ctx").astype(jnp.float32),
        lax.psum(shares[8].astype(jnp.bfloat16), "ctx").astype(jnp.float32),
        lax.psum(shares[9].astype(jnp.bfloat16), "ctx").astype(jnp.float32),
        lax.psum(shares[10].astype(jnp.bfloat16), "ctx").astype(jnp.float32),
        lax.psum(shares[11].astype(jnp.bfloat16), "ctx").astype(jnp.float32),
    )
    return (
        output_rows[None],
        grad_input[None],
        totals[0],
        totals[1],
        totals[2],
        totals[3],
        totals[4],
        totals[5],
        totals[6],
        totals[7],
        totals[8],
        totals[9],
        totals[10],
        totals[11],
    )


HB = 128
NEG=-1e30
f32=jnp.float32; bf16=jnp.bfloat16

def _nn(a,b): return lax.dot_general(a,b,(((1,),(0,)),((),())),preferred_element_type=f32)
def _nt(a,b): return lax.dot_general(a,b,(((1,),(1,)),((),())),preferred_element_type=f32)

def attn_fwd_kernel(bm, x_ref, o_ref, lse_ref, q_s, kt_s, v_s, *, nblk, per, bq, bk):
    def perm(i,_):
        p=bm[i]; c=i//per; l=pl.multiple_of((i%per)*HB,HB); d=pl.multiple_of(p*HB,HB)
        q_s[:,pl.ds(d,HB)]=x_ref[c,0:64,pl.ds(l,HB)]*bf16(0.125)
        kt_s[pl.ds(d,HB),:]=x_ref[c,64:128,pl.ds(l,HB)].astype(f32).T.astype(bf16)
        v_s[:,pl.ds(d,HB)]=x_ref[c,128:192,pl.ds(l,HB)]
        return 0
    lax.fori_loop(0,nblk,perm,0,unroll=32)
    S=nblk*HB; nq=S//bq; r=bq//bk
    def step(q,qo,ko,carry,mask):
        m,l,acc=carry
        s=_nn(kt_s[pl.ds(ko,bk),:],q)
        if mask is not None: s=jnp.where(mask,s,NEG)
        mn=jnp.maximum(m,jnp.max(s,axis=0,keepdims=True))
        a=jnp.exp(m-mn); p=jnp.exp(s-mn)
        l=l*a+jnp.sum(p,axis=0,keepdims=True)
        acc=acc*a+_nn(v_s[:,pl.ds(ko,bk)],p.astype(bf16))
        return mn,l,acc
    ki=lax.broadcasted_iota(jnp.int32,(bk,bq),0); qi_=lax.broadcasted_iota(jnp.int32,(bk,bq),1)
    def qloop(i,_):
        qo=pl.multiple_of(i*bq,bq)
        q=q_s[:,pl.ds(qo,bq)]
        c=(jnp.full((1,bq),NEG,f32),jnp.zeros((1,bq),f32),jnp.zeros((64,bq),f32))
        c=lax.fori_loop(0,i*r,lambda j,c: step(q,qo,pl.multiple_of(j*bk,bk),c,None),c)
        for t in range(r):
            c=step(q,qo,pl.multiple_of(qo+t*bk,bk),c,ki+t*bk<=qi_)
        m,l,acc=c
        q_s[:,pl.ds(qo,bq)]=(acc*(1.0/l)).astype(bf16)
        lse_ref[:,pl.ds(qo,bq)]=m+jnp.log(l)
        return 0
    lax.fori_loop(0,nq,qloop,0)
    def unperm(i,_):
        p=bm[i]; c=i//per; l=pl.multiple_of((i%per)*HB,HB); d=pl.multiple_of(p*HB,HB)
        o_ref[c,:,pl.ds(l,HB)]=q_s[:,pl.ds(d,HB)]
        return 0
    lax.fori_loop(0,nblk,unperm,0,unroll=32)

def attn_fwd(bm,x,*,bq=512,bk=512):
    n=x.shape[0]; S=n*x.shape[2]; nblk=S//HB
    bq=math.gcd(S,bq); bk=math.gcd(bq,bk)
    return pl.pallas_call(
        lambda *a: attn_fwd_kernel(*a,nblk=nblk,per=x.shape[2]//HB,bq=bq,bk=bk),
        out_shape=(jax.ShapeDtypeStruct((n,64,x.shape[2]),bf16),jax.ShapeDtypeStruct((1,S),f32)),
        in_specs=[pl.BlockSpec(memory_space=pltpu.SMEM),pl.BlockSpec(memory_space=pltpu.VMEM)],
        out_specs=(pl.BlockSpec(memory_space=pltpu.VMEM),pl.BlockSpec(memory_space=pltpu.VMEM)),
        scratch_shapes=[pltpu.VMEM((64,S),bf16),pltpu.VMEM((S,64),bf16),pltpu.VMEM((64,S),bf16)],
        compiler_params=pltpu.CompilerParams(vmem_limit_bytes=56<<20),name="attn_fwd")(bm,x)

def attn_bwd_kernel(bm, x_ref, o_ref, do_ref, lse_ref, cs_ref, g_ref, q_s, kt_s, k_s, vt_s, do_s, dl_s, dq_s, dk_s, dv_s, *, nblk, per, bq, bk):
    def perm(i,_):
        p=bm[i]; c=i//per; l=pl.multiple_of((i%per)*HB,HB); d=pl.multiple_of(p*HB,HB)
        q_s[:,pl.ds(d,HB)]=x_ref[c,0:64,pl.ds(l,HB)]*bf16(0.125)
        k=x_ref[c,64:128,pl.ds(l,HB)]
        k_s[:,pl.ds(d,HB)]=k*bf16(0.125)
        kt_s[pl.ds(d,HB),:]=k.astype(f32).T.astype(bf16)
        vt_s[pl.ds(d,HB),:]=x_ref[c,128:192,pl.ds(l,HB)].astype(f32).T.astype(bf16)
        do=do_ref[c,:,pl.ds(l,HB)]
        do_s[:,pl.ds(d,HB)]=do
        dl_s[:,pl.ds(d,HB)]=jnp.sum(do.astype(f32)*o_ref[c,:,pl.ds(l,HB)].astype(f32),axis=0,keepdims=True)
        return 0
    lax.fori_loop(0,nblk,perm,0,unroll=32)
    S=nblk*HB; nq=S//bq; r=bq//bk
    dk_s[...]=jnp.zeros_like(dk_s); dv_s[...]=jnp.zeros_like(dv_s)
    def step(q,do,lse,dl,ko,dq,mask):
        s=_nn(kt_s[pl.ds(ko,bk),:],q)
        p=jnp.exp(s-lse)
        if mask is not None: p=jnp.where(mask,p,0.0)
        dp=_nn(vt_s[pl.ds(ko,bk),:],do)
        ds=(p*(dp-dl)).astype(bf16)
        pb=p.astype(bf16)
        dv_s[:,pl.ds(ko,bk)]+=_nt(do,pb)
        dk_s[:,pl.ds(ko,bk)]+=_nt(q,ds)
        return dq+_nn(k_s[:,pl.ds(ko,bk)],ds)
    ki=lax.broadcasted_iota(jnp.int32,(bk,bq),0); qi_=lax.broadcasted_iota(jnp.int32,(bk,bq),1)
    def qloop(i,_):
        qo=pl.multiple_of(i*bq,bq)
        q=q_s[:,pl.ds(qo,bq)]; do=do_s[:,pl.ds(qo,bq)]; lse=lse_ref[:,pl.ds(qo,bq)]; dl=dl_s[:,pl.ds(qo,bq)]
        dq=jnp.zeros((64,bq),f32)
        dq=lax.fori_loop(0,i*r,lambda j,c: step(q,do,lse,dl,pl.multiple_of(j*bk,bk),c,None),dq)
        for t in range(r):
            dq=step(q,do,lse,dl,pl.multiple_of(qo+t*bk,bk),dq,ki+t*bk<=qi_)
        dq_s[:,pl.ds(qo,bq)]=dq
        return 0
    lax.fori_loop(0,nq,qloop,0)
    def unperm(i,_):
        p=bm[i]; c=i//per; l=pl.multiple_of((i%per)*HB,HB); d=pl.multiple_of(p*HB,HB)
        cos=cs_ref[0:8,pl.ds(d,HB)]; sin=cs_ref[8:16,pl.ds(d,HB)]
        for n_,src in ((0,dq_s),(1,dk_s)):
            g=src[:,pl.ds(d,HB)]
            a=g[0:8]; b=g[8:16]
            full=jnp.concatenate([a*cos+b*sin,b*cos-a*sin,g[16:64]],axis=0)
            g_ref[c,64*n_:64*n_+64,pl.ds(l,HB)]=full.astype(bf16)
        g_ref[c,128:192,pl.ds(l,HB)]=dv_s[:,pl.ds(d,HB)].astype(bf16)
        return 0
    lax.fori_loop(0,nblk,unperm,0,unroll=32)

def attn_bwd(bm,x,o,do,lse,cs,*,bq=512,bk=512):
    n=x.shape[0]; S=n*x.shape[2]; nblk=S//HB
    bq=math.gcd(S,bq); bk=math.gcd(bq,bk)
    vm=pl.BlockSpec(memory_space=pltpu.VMEM)
    return pl.pallas_call(
        lambda *a: attn_bwd_kernel(*a,nblk=nblk,per=x.shape[2]//HB,bq=bq,bk=bk),
        out_shape=jax.ShapeDtypeStruct((n,192,x.shape[2]),bf16),
        in_specs=[pl.BlockSpec(memory_space=pltpu.SMEM)]+[vm]*5,
        out_specs=vm,
        scratch_shapes=[pltpu.VMEM((64,S),bf16),pltpu.VMEM((S,64),bf16),pltpu.VMEM((64,S),bf16),pltpu.VMEM((S,64),bf16),pltpu.VMEM((64,S),bf16),
                        pltpu.VMEM((1,S),f32),pltpu.VMEM((64,S),f32),pltpu.VMEM((64,S),f32),pltpu.VMEM((64,S),f32)],
        compiler_params=pltpu.CompilerParams(vmem_limit_bytes=56<<20),name="attn_bwd")(bm,x,o,do,lse,cs)


SWAP = [(0, 1), (1, 0)]


def fast_fits(mesh):
    return mesh.shape["wsh"] == 2 and mesh.shape["ctx"] == H


def _params(mb=56):
    return pltpu.CompilerParams(vmem_limit_bytes=mb << 20)


def _norm(x):
    xf = x.astype(f32)
    cen = xf - jnp.mean(xf, axis=-1, keepdims=True)
    inv = lax.rsqrt(jnp.mean(cen * cen, axis=-1, keepdims=True) + epsilon)
    return cen * inv, inv


def _full(v):
    return pl.BlockSpec(v.shape, lambda *a: (0,) * v.ndim)


def _wq_specs(half, width, cols, quarter, at):
    own = lambda p: pl.BlockSpec(
        (half, cols),
        lambda *a: (0, p * (width // cols) + a[-1][0] * (half // cols) + a[-1][1] * (quarter // cols) + at(*a)),
    )
    got = lambda p: pl.BlockSpec((half, cols), lambda *a: (0, p * (quarter // cols) + at(*a)))
    return [own(p) for p in range(3)] + [got(p) for p in range(3)]


def norm_kernel(ids, a_ref, b_ref, n_ref, *refs):
    x_ref, ain_ref, min_ref = refs[-3:]
    mine = pl.program_id(0) == ids[1]
    x = jnp.where(mine, a_ref[...].astype(f32), b_ref[...].astype(f32))
    x_ref[...] = x.astype(bf16)
    xhat, _ = _norm(x)
    ain_ref[...] = (xhat * n_ref[0:1, :] + n_ref[1:2, :]).astype(bf16)
    min_ref[...] = (xhat * n_ref[2:3, :] + n_ref[3:4, :]).astype(bf16)


def norm_rows(ids, a, b, norms, before=()):
    rows, width = a.shape
    slot = 2 if before else 0
    out = jax.ShapeDtypeStruct((4 * rows, width), bf16)
    return pl.pallas_call(
        norm_kernel,
        grid_spec=pltpu.PrefetchScalarGridSpec(
            num_scalar_prefetch=1,
            grid=(2,),
            in_specs=[_full(a), _full(b), _full(norms)] + [pl.BlockSpec(memory_space=pl.ANY)] * len(before),
            out_specs=(pl.BlockSpec((rows, width), lambda i, ids: (slot + i, 0)),) * 3,
        ),
        out_shape=(out,) * 3,
        input_output_aliases={4 + k: k for k in range(len(before))},
        compiler_params=_params(),
        cost_estimate=pl.CostEstimate(flops=0, transcendentals=0, bytes_accessed=1 << 20),
        name="norm_rows",
    )(ids, a, b, norms, *before)


def turn_kernel(a_ref, b_ref, at_ref, bt_ref):
    at_ref[...] = a_ref[...].astype(f32).T.astype(bf16)
    bt_ref[...] = b_ref[...].astype(f32).T.astype(bf16)


def turn(a, b, steps=4):
    rows, width = a.shape
    src = pl.BlockSpec((rows // steps, width), lambda i: (i, 0))
    dst = pl.BlockSpec((width, rows // steps), lambda i: (0, i))
    return pl.pallas_call(
        turn_kernel,
        grid=(steps,),
        in_specs=[src, src],
        out_specs=(dst, dst),
        out_shape=(jax.ShapeDtypeStruct((width, rows), a.dtype),) * 2,
        compiler_params=_params(),
        cost_estimate=pl.CostEstimate(flops=0, transcendentals=0, bytes_accessed=1 << 20),
        name="turn",
    )(a, b)


def mask_kernel(ids, a_ref, b_ref, c_ref, d_ref, live_ref, w_ref, o_ref, f_ref):
    i = pl.program_id(0)
    mine = (i % 2) == ids[1]
    for slot, (own, sib) in enumerate(((a_ref, b_ref), (c_ref, d_ref))):
        @pl.when((i // 2) == slot)
        def _(own=own, sib=sib):
            v = jnp.where(mine, own[...].astype(f32), sib[...].astype(f32))
            o_ref[...] = (live_ref[...] * v).astype(bf16)

    f = _nt(w_ref[...], o_ref[...]).astype(bf16)
    for k in range(f_ref.shape[0]):
        f_ref[k] = f[k * HD : (k + 1) * HD, :]


def mask_rows(ids, own, own_sib, got, got_sib, live, w_out, quarter):
    rows, width = own.shape
    heads = quarter // HD
    return pl.pallas_call(
        mask_kernel,
        grid_spec=pltpu.PrefetchScalarGridSpec(
            num_scalar_prefetch=1,
            grid=(4,),
            in_specs=[_full(v) for v in (own, own_sib, got, got_sib)]
            + [
                pl.BlockSpec((rows, 1), lambda i, ids: (i, 0)),
                pl.BlockSpec((quarter, width), lambda i, ids: (ids[1], 0)),
            ],
            out_specs=(
                pl.BlockSpec((rows, width), lambda i, ids: (i, 0)),
                pl.BlockSpec((heads, HD, rows), lambda i, ids: (i // 2, 0, i % 2)),
            ),
        ),
        out_shape=(
            jax.ShapeDtypeStruct((4 * rows, width), bf16),
            jax.ShapeDtypeStruct((2 * heads, HD, 2 * rows), bf16),
        ),
        compiler_params=_params(),
        cost_estimate=pl.CostEstimate(flops=0, transcendentals=0, bytes_accessed=1 << 20),
        name="mask_rows",
    )(ids, own, own_sib, got, got_sib, live, w_out)


def qkv_kernel(
    ids, ain_ref, wq_ref, wk_ref, wv_ref, gq_ref, gk_ref, gv_ref, bq_ref, bk_ref, bv_ref, cs_ref, send_ref
):
    width = ain_ref.shape[1]
    half = width // 2
    me = ids[0]
    a_own = ain_ref[:, pl.ds(pl.multiple_of(me * half, half), half)]
    a_got = ain_ref[:, pl.ds(pl.multiple_of((1 - me) * half, half), half)]
    cos = cs_ref[0:8, :]
    sin = cs_ref[8:16, :]
    for n, (w, g, b) in enumerate(((wq_ref, gq_ref, bq_ref), (wk_ref, gk_ref, bk_ref), (wv_ref, gv_ref, bv_ref))):
        t = _nn(a_own, w[...]) + _nn(a_got, g[...]) + b[...]
        t = t.T
        for k in range(send_ref.shape[1]):
            v = t[k * HD : (k + 1) * HD]
            if n < 2:
                lead = v[0:8]
                trail = v[8:16]
                v = jnp.concatenate([lead * cos - trail * sin, trail * cos + lead * sin, v[16:]], axis=0)
            send_ref[0, k, n * HD : (n + 1) * HD, :] = v.astype(bf16)


def qkv_forward(ids, attn_in, w_own, w_got, bias, cs, cols=256):
    rows, width = attn_in.shape[0] // 2, attn_in.shape[1]
    half = width // 2
    quarter = w_got.shape[1] // 3
    bsp = lambda p: pl.BlockSpec((1, cols), lambda s, i, ids: (0, p * (quarter // cols) + i))
    return pl.pallas_call(
        qkv_kernel,
        grid_spec=pltpu.PrefetchScalarGridSpec(
            num_scalar_prefetch=1,
            grid=(2, quarter // cols),
            in_specs=[pl.BlockSpec((rows, width), lambda s, i, ids: (s, 0))]
            + _wq_specs(half, width, cols, quarter, lambda s, i, ids: i)
            + [bsp(p) for p in range(3)]
            + [_full(cs)],
            out_specs=pl.BlockSpec((1, cols // HD, 3 * HD, rows), lambda s, i, ids: (s, i, 0, 0)),
        ),
        out_shape=jax.ShapeDtypeStruct((2, quarter // HD, 3 * HD, rows), bf16),
        compiler_params=_params(),
        cost_estimate=pl.CostEstimate(flops=1 << 20, transcendentals=0, bytes_accessed=1 << 20),
        name="qkv_forward",
    )(ids, attn_in, w_own, w_own, w_own, w_got, w_got, w_got, bias, bias, bias, cs)


MLP_CHUNKS = 2


def mlp_kernel(ids, x_ref, xt_ref, dy_ref, wo_ref, wg_ref, wd_ref, bu_ref, y_ref, dx_ref, uk_ref, us_ref, dk_ref, ds_ref, gb_ref,
    g_s, act_s, du_s, y_s, dx_s
):
    rows, width = x_ref.shape
    half = width // 2
    me = ids[0]
    spans = (
        (pl.multiple_of(me * half, half), wo_ref[...]),
        (pl.multiple_of((1 - me) * half, half), wg_ref[...]),
    )

    @pl.when(pl.program_id(0) == 0)
    def _():
        y_s[...] = jnp.zeros_like(y_s)
        dx_s[...] = jnp.zeros_like(dx_s)

    wd = wd_ref[...]
    bias = bu_ref[...]
    step = rows // MLP_CHUNKS
    for c in range(MLP_CHUNKS):
        at = slice(c * step, (c + 1) * step)
        u = bias + sum(_nn(x_ref[at, pl.ds(o, half)], w) for o, w in spans)
        cdf = 0.5 * (1.0 + lax.erf(u * (1.0 / math.sqrt(2.0))))
        pdf = jnp.exp(-0.5 * u * u) * (1.0 / math.sqrt(2.0 * math.pi))
        act = (u * cdf).astype(bf16)
        du = (_nt(dy_ref[at, :], wd) * (cdf + u * pdf)).astype(bf16)
        y_s[at, :] += _nn(act, wd)
        for o, w in spans:
            dx_s[at, pl.ds(o, half)] += _nt(du, w)
        act_s[at, :] = act
        du_s[at, :] = du
    du = du_s[...]
    gd = lax.dot_general(
        act_s[...], dy_ref[...], (((0,), (0,)), ((), ())), preferred_element_type=f32
    ).astype(bf16)
    k, r, _ = dk_ref.shape
    k = gd.shape[0] // r
    early = pl.program_id(0) < pl.num_programs(0) // 2
    for c in range(k):
        v = gd[c * r : (c + 1) * r, :]

        @pl.when(early)
        def _(v=v, c=c):
            ds_ref[c] = v

        @pl.when(jnp.logical_not(early))
        def _(v=v, c=c):
            dk_ref[c] = v

    g_s[...] = _nn(xt_ref[...], du).astype(bf16)
    n = uk_ref.shape[0]
    r = uk_ref.shape[1] // 2
    for ref, side in ((uk_ref, ids[3]), (us_ref, 1 - ids[3])):
        for h in range(2):
            for c in range(n):
                at = pl.multiple_of(h * half + (side * n + c) * r, r)
                ref[c, h * r : (h + 1) * r, :] = g_s[pl.ds(at, r), :]
    gb_ref[...] = jnp.sum(du.astype(f32), axis=0, keepdims=True)

    @pl.when(pl.program_id(0) == pl.num_programs(0) - 1)
    def _():
        y_ref[...] = y_s[...].astype(bf16)
        dx_ref[...] = dx_s[...].astype(bf16)


def mlp(ids, x, xt, dy, w_own, w_got, wd, bu, n, tile=512):
    rows, width = x.shape
    half = width // 2
    hidden = w_got.shape[1]
    steps = hidden // tile
    mid = steps // 2
    whole = pl.BlockSpec((rows, width), lambda i, ids: (0, 0))
    per = hidden // n
    order = lambda i, ids: i % mid + mid * jnp.where(i < mid, 1 - ids[2], ids[2])
    part = lambda i, ids: ids[1] * steps + order(i, ids)
    up_spec = pl.BlockSpec((n // 2, width // n, tile), lambda i, ids: (0, 0, order(i, ids)))
    down_spec = lambda f: pl.BlockSpec((tile // per, per, width), lambda i, ids: (f(i), 0, 0))
    up_shape = jax.ShapeDtypeStruct((n // 2, width // n, hidden), bf16)
    down_shape = jax.ShapeDtypeStruct((n // 2, per, width), bf16)
    return pl.pallas_call(
        mlp_kernel,
        grid_spec=pltpu.PrefetchScalarGridSpec(
            num_scalar_prefetch=1,
            grid=(steps,),
            in_specs=[
                whole,
                pl.BlockSpec((width, rows), lambda i, ids: (0, 0)),
                whole,
                pl.BlockSpec((half, tile), lambda i, ids: (0, ids[0] * 2 * steps + part(i, ids))),
                pl.BlockSpec((half, tile), lambda i, ids: (0, order(i, ids))),
                pl.BlockSpec((tile, width), lambda i, ids: (part(i, ids), 0)),
                pl.BlockSpec((1, tile), lambda i, ids: (0, part(i, ids))),
            ],
            out_specs=(
                whole,
                whole,
                up_spec,
                up_spec,
                down_spec(lambda i: jnp.maximum(i - mid, 0)),
                down_spec(lambda i: jnp.minimum(i, mid - 1)),
                pl.BlockSpec((1, tile), lambda i, ids: (0, order(i, ids))),
            ),
            scratch_shapes=[pltpu.VMEM((width, tile), bf16), pltpu.VMEM((rows, tile), bf16), pltpu.VMEM((rows, tile), bf16)]
            + [pltpu.VMEM((rows, width), f32)] * 2,
        ),
        out_shape=(
            jax.ShapeDtypeStruct((rows, width), bf16),
            jax.ShapeDtypeStruct((rows, width), bf16),
            up_shape,
            up_shape,
            down_shape,
            down_shape,
            jax.ShapeDtypeStruct((1, hidden), f32),
        ),
        compiler_params=_params(),
        cost_estimate=pl.CostEstimate(
            flops=12 * rows * width * hidden, transcendentals=2 * rows * hidden, bytes_accessed=24 << 20
        ),
        name="mlp",
    )(ids, x, xt, dy, w_own, w_got, wd, bu)


def qkv_back_kernel(
    ids, d_ref, at_ref, x_ref, n_ref, wq_ref, wk_ref, wv_ref, gq_ref, gk_ref, gv_ref, dm_ref, ob_ref, dy_ref, gb_ref,
    a_ref, b_ref, e_ref, g_s, go_s, bias_s, sum_s
):
    rows, width = x_ref.shape
    half = width // 2
    me = ids[0]
    core = ids[1]
    i = pl.program_id(0)
    outs = (a_ref, b_ref)
    n = a_ref.shape[0]
    nh = d_ref.shape[1]
    cols = nh * HD
    r = half // (2 * n)

    @pl.when(i == 0)
    def _():
        g_s[...] = jnp.zeros_like(g_s)
        go_s[...] = jnp.zeros_like(go_s)
        bias_s[...] = jnp.zeros_like(bias_s)
        sum_s[...] = jnp.zeros_like(sum_s)

    ones = jnp.ones((8, rows), bf16)
    at = at_ref[...]
    dts = []
    for p in range(3):
        dp = jnp.concatenate([d_ref[0, k, p * HD : (p + 1) * HD, :] for k in range(nh)], axis=0)
        g_s[p] += _nt(at, dp)
        bias_s[p * 8 : (p + 1) * 8, :] += _nt(ones, dp)
        dts.append(dp.astype(f32).T.astype(bf16))
    go_s[...] += _nn(ob_ref[0], dy_ref[...])
    dt = jnp.concatenate(dts, axis=1)
    w_own = jnp.concatenate([wq_ref[...], wk_ref[...], wv_ref[...]], axis=1)
    w_got = jnp.concatenate([gq_ref[...], gk_ref[...], gv_ref[...]], axis=1)
    d_own = _nt(dt, w_own)
    d_got = _nt(dt, w_got)
    first = me == 0
    xhat, _ = _norm(x_ref[...])
    for h in range(2):
        lanes = slice(h * half, (h + 1) * half)
        da = jnp.where(first, d_own, d_got) if h == 0 else jnp.where(first, d_got, d_own)
        dm = dm_ref[:, lanes].astype(f32)
        xh = xhat[:, lanes]
        e_ref[0, :, lanes] = da * n_ref[0:1, lanes] + dm * n_ref[2:3, lanes]
        for k, v in enumerate((da * xh, da, dm * xh, dm)):
            sum_s[k : k + 1, lanes] += jnp.sum(v, axis=0, keepdims=True)

    @pl.when(i == core)
    def _():
        sum_s[4:5, :] = jnp.sum(dy_ref[...].astype(f32), axis=0, keepdims=True)

    @pl.when(i == pl.num_programs(0) - 1)
    def _():
        for p in range(3):
            g = g_s[p].astype(bf16)
            for h in range(2):
                for c in range(n):
                    for a in range(2):
                        row = h * half + (c * 2 + a) * r
                        u = (h * 3 + p) * r
                        outs[a][c, u : u + r, :] = g[row : row + r, :]
        go = go_s[...].astype(bf16)
        q = cols // (2 * n)
        for c in range(n):
            for a in range(2):
                row = (c * 2 + a) * q
                for k in range(width // cols):
                    u = 6 * r + k * q
                    outs[a][c, u : u + q, :] = go[row : row + q, k * cols : (k + 1) * cols]
        flat = [sum_s[k : k + 1, t * cols : (t + 1) * cols] for k in range(5) for t in range(width // cols)]
        zero = jnp.zeros((1, cols), f32)
        for p in range(3):
            flat += [
                jnp.where((me == k) & (core == j), bias_s[p * 8 : p * 8 + 1, :], zero) for k in range(2) for j in range(2)
            ]
        flat += [
            jnp.where((me == k) & (core == j), gb_ref[:, t * cols : (t + 1) * cols], zero)
            for k in range(2)
            for j in range(2)
            for t in range(gb_ref.shape[1] // cols)
        ]
        top = 6 * r + (width // cols) * q
        per = len(flat) // n
        pad = [zero] * (8 - per)
        for c in range(n):
            b_ref[c, top : top + 8, :] = jnp.concatenate(flat[c * per : (c + 1) * per] + pad, axis=0).astype(bf16)


def qkv_backward(ids, d, at, x2, norms, w_own, w_got, d_mlp, ob, dy, gb_up, n):
    rows, width = x2.shape[0] // 4, x2.shape[1]
    half = width // 2
    cols = w_got.shape[1] // 3
    size = 6 * (half // (2 * n)) + width // (2 * n)
    row = lambda: pl.BlockSpec((rows, width), lambda s, ids: (s, 0))
    out = [
        jax.ShapeDtypeStruct((n, size, cols), bf16),
        jax.ShapeDtypeStruct((n, size + 8, cols), bf16),
    ]
    return pl.pallas_call(
        qkv_back_kernel,
        grid_spec=pltpu.PrefetchScalarGridSpec(
            num_scalar_prefetch=1,
            grid=(4,),
            in_specs=[
                pl.BlockSpec((1, cols // HD, 3 * HD, rows), lambda s, ids: (s // 2, 0, 0, s % 2)),
                pl.BlockSpec((width, rows), lambda s, ids: (0, s)),
                row(),
                _full(norms),
            ]
            + _wq_specs(half, width, cols, cols, lambda s, ids: 0)
            + [row(), pl.BlockSpec((1, cols, rows), lambda s, ids: (s // 2, 0, s % 2)), row(), _full(gb_up)],
            out_specs=(*[_full(v) for v in out], pl.BlockSpec((1, rows, width), lambda s, ids: (s // 2, s % 2, 0))),
            scratch_shapes=[
                pltpu.VMEM((3, width, cols), f32),
                pltpu.VMEM((cols, width), f32),
                pltpu.VMEM((24, cols), f32),
                pltpu.VMEM((8, width), f32),
            ],
        ),
        out_shape=(*out, jax.ShapeDtypeStruct((2, 2 * rows, width), f32)),
        compiler_params=_params(),
        name="qkv_backward",
    )(ids, d, at, x2, norms, w_own, w_own, w_own, w_got, w_got, w_got, d_mlp, ob, dy, gb_up)


def _mine(ids):
    return (pl.program_id(0) // 2) == ids[1]


def _own_block(i, ids):
    return jnp.clip(i - 2 * ids[1], 0, 1)


def _got_block(i, ids):
    return jnp.clip(i - 2 * (1 - ids[1]), 0, 1)


def join_kernel(ids, own_ref, got_ref, o_ref):
    mine = _mine(ids)
    shape = o_ref.shape

    @pl.when(mine)
    def _():
        o_ref[...] = own_ref[...].astype(f32).reshape(shape)

    @pl.when(jnp.logical_not(mine))
    def _():
        o_ref[...] = got_ref[...].astype(f32).reshape(shape)


def join_rows_kernel(ids, own_ref, got_ref, o_ref):
    mine = pl.program_id(0) == ids[1]

    @pl.when(mine)
    def _():
        o_ref[...] = own_ref[...].astype(f32).reshape(o_ref.shape)

    @pl.when(jnp.logical_not(mine))
    def _():
        o_ref[...] = got_ref[...].astype(f32).reshape(o_ref.shape)


def join_rows(ids, own, got):
    n, r, w = own.shape
    return pl.pallas_call(
        join_rows_kernel,
        grid_spec=pltpu.PrefetchScalarGridSpec(
            num_scalar_prefetch=1,
            grid=(2,),
            in_specs=[_full(own), _full(got)],
            out_specs=pl.BlockSpec((n * r, w), lambda i, ids: (i, 0)),
        ),
        out_shape=jax.ShapeDtypeStruct((2 * n * r, w), f32),
        compiler_params=_params(),
        name="join_rows",
    )(ids, own, got)


def join_cols(ids, own, got):
    n, _, r, w = own.shape
    src = lambda f: pl.BlockSpec((n, 1, r, w), lambda i, ids: (0, f(i, ids), 0, 0))
    return pl.pallas_call(
        join_kernel,
        grid_spec=pltpu.PrefetchScalarGridSpec(
            num_scalar_prefetch=1,
            grid=(4,),
            in_specs=[src(_own_block), src(_got_block)],
            out_specs=pl.BlockSpec((n * r, w), lambda i, ids: (0, (i % 2) * 2 + i // 2)),
        ),
        out_shape=jax.ShapeDtypeStruct((n * r, 4 * w), f32),
        compiler_params=_params(),
        name="join_cols",
    )(ids, own, got)


def unpack_kernel(ids, ao_ref, ag_ref, bo_ref, bg_ref, q_ref, o_ref, s_ref):
    first = ids[1] == 0
    k, _, cols = ao_ref.shape
    r = q_ref.shape[0] // (2 * k)
    q = o_ref.shape[1] // (2 * k)
    for a, (own, got) in enumerate(((ao_ref, ag_ref), (bo_ref, bg_ref))):
        for c in range(k):
            x = own[c].astype(f32)
            y = got[c].astype(f32)
            to = slice((c * 2 + a) * r, (c * 2 + a + 1) * r)
            tq = slice((c * 2 + a) * q, (c * 2 + a + 1) * q)
            for j in range(2):
                v = jnp.where(first, x, y) if j == 0 else jnp.where(first, y, x)
                for w in range(2):
                    for p in range(3):
                        u = (w * 3 + p) * r
                        at = ((p * 2 + w) * 2 + j) * cols
                        q_ref[to, at : at + cols] = v[u : u + r, :]
                for t in range(o_ref.shape[2] // cols):
                    u = 6 * r + t * q
                    o_ref[j, tq, t * cols : (t + 1) * cols] = v[u : u + q, :]
            if a == 1:
                s_ref[c] = (x + y)[-8:, :]


def unpack(ids, a_own, a_got, b_own, b_got, width, steps=4):
    n, _, cols = a_own.shape
    half = width // 2
    k = n // steps
    spec = lambda v: pl.BlockSpec((k,) + v.shape[1:], lambda i, ids: (i, 0, 0))
    return pl.pallas_call(
        unpack_kernel,
        grid_spec=pltpu.PrefetchScalarGridSpec(
            num_scalar_prefetch=1,
            grid=(steps,),
            in_specs=[spec(v) for v in (a_own, a_got, b_own, b_got)],
            out_specs=(
                pl.BlockSpec((half // steps, 3 * width), lambda i, ids: (i, 0)),
                pl.BlockSpec((2, cols // steps, width), lambda i, ids: (0, i, 0)),
                pl.BlockSpec((k, 8, cols), lambda i, ids: (i, 0, 0)),
            ),
        ),
        out_shape=(
            jax.ShapeDtypeStruct((half, 3 * width), f32),
            jax.ShapeDtypeStruct((2, cols, width), f32),
            jax.ShapeDtypeStruct((n, 8, cols), f32),
        ),
        compiler_params=_params(),
        name="unpack",
    )(ids, a_own, a_got, b_own, b_got)


def last_kernel(eo_ref, er_ref, x_ref, c_ref, live_ref, o_ref):
    xhat, inv = _norm(x_ref[...])
    e = eo_ref[...] + er_ref[...].astype(f32)
    dx = inv * (
        e - jnp.mean(e, axis=-1, keepdims=True) - xhat * jnp.mean(e * xhat, axis=-1, keepdims=True)
    )
    o_ref[...] = live_ref[...] * c_ref[...].astype(f32) + dx


def last(e_own, e_got, x, cot, live):
    return pl.pallas_call(
        last_kernel,
        out_shape=jax.ShapeDtypeStruct(x.shape, f32),
        compiler_params=_params(),
        name="token_grad",
    )(e_own, e_got, x, cot, live)


def fast_shards(
    tokens,
    ln1_gain,
    ln1_bias,
    ln2_gain,
    ln2_bias,
    w_qkv,
    b_qkv,
    w_out,
    b_out,
    w_up,
    b_up,
    w_down,
    b_down,
    lengths,
    block_map,
    cotangent,
):
    ctx = lax.axis_index("ctx")
    me = lax.axis_index("wsh")
    core = ctx % 2
    n_ctx = lax.axis_size("ctx")
    chips = n_ctx // 2
    own_rows, width = tokens.shape[1:]
    rows = 2 * own_rows
    half = width // 2
    quarter = half // 2
    seq = own_rows * n_ctx
    heads = H // 4
    hid = w_up.shape[1] // 4
    CORE, X, ZN, ZF = 0, 1, 2, 3

    def swap(v):
        return lax.ppermute(v, "wsh", SWAP)

    def flip(v, bit):
        return lax.ppermute(v, "ctx", [(i, i ^ (1 << bit)) for i in range(n_ctx)])

    def bit_of(bit):
        return (ctx >> bit) & 1

    ids = jnp.stack([me, core, bit_of(X), bit_of(ZN)]).astype(jnp.int32)

    def add(*terms):
        return sum(v.astype(f32) for v in terms).astype(bf16) if len(terms) > 1 else terms[0]

    def halve(terms, bit):
        b = bit_of(bit)
        cut = [v.reshape((2, v.shape[0] // 2) + v.shape[1:]) for v in terms]
        part = lambda k: [lax.dynamic_index_in_dim(v, k, 0, keepdims=False) for v in cut]
        return part(b) + [flip(add(*part(1 - b)), bit)]

    def ordered(first, a, b, axis=0):
        return jnp.where(first == 0, jnp.concatenate([a, b], axis), jnp.concatenate([b, a], axis))

    def double(v, bit):
        return ordered(bit_of(bit), v, flip(v, bit))

    def exchange(v):
        groups = [[2 * i + c for i in range(chips)] for c in range(2)]
        return lax.all_to_all(v, "ctx", 0, 0, axis_index_groups=groups, tiled=False)

    def rows_of(v, at, n, axis=0):
        return lax.dynamic_slice_in_dim(v, at, n, axis)

    x_own = tokens[0]
    x_got = swap(x_own)
    x_sib = flip(x_own, CORE)
    mine = me * half + core * quarter
    other = (1 - me) * half + core * quarter
    wq_send = jnp.concatenate([rows_of(w_qkv, p * width + other, quarter, 1) for p in range(3)], axis=1)
    wq_send, ln1_gain = lax.optimization_barrier((wq_send, ln1_gain))
    len_parts = jnp.stack([lengths[0] // 64, lengths[0] % 64]).astype(bf16)
    parts = [ln1_gain, ln1_bias, ln2_gain, ln2_bias, b_out, b_down, b_qkv, jnp.pad(len_parts, (0, half - 2))]
    small = jnp.concatenate([v.reshape(-1, half) for v in parts])
    small = ordered(me, small[None], swap(small)[None])
    wq_got = swap(wq_send)
    vec = lambda i: small[:, i].reshape(width).astype(f32)
    norms = jnp.stack([vec(i) for i in range(4)])
    bias_out = vec(4) + vec(5)
    qkv_bias = small[:, 6:9].astype(f32).reshape(3, width)
    qkv_bias = rows_of(qkv_bias, mine, quarter, 1).reshape(1, 3 * quarter)
    lens = small[:, 9, :2].astype(jnp.int32)
    lens = lens[:, 0] * 64 + lens[:, 1]
    other_len = lens[1 - me]

    normed = norm_rows(ids, x_own, x_sib, norms)
    cot_own = cotangent[0]
    wu_send = rows_of(w_up, ((1 - me) * 2 + core) * hid, hid, 1)
    wq_got, cot_send, normed = lax.optimization_barrier((wq_got, cot_own, normed))
    cot_got = swap(cot_send)
    cot_got, wu_send = lax.optimization_barrier((cot_got, wu_send))
    wu_got = swap(wu_send)
    normed = norm_rows(ids, x_got, flip(x_got, CORE), norms, normed)
    x2, attn_in, mlp_in = normed
    cot_sib = flip(cot_own, CORE)

    blocks = rows_of(block_map, (rows // HB) * (ctx // 2), rows // HB)
    offs = jnp.arange(HB, dtype=jnp.int32)
    positions = (blocks[:, None] * HB + offs[None, :]).reshape(rows)
    live2 = jnp.concatenate([positions < lengths[0], positions < other_len]).astype(f32)[:, None]
    live_own = rows_of(live2, core * own_rows, own_rows)
    freq = 10000.0 ** (-jnp.arange(ROT // 2, dtype=f32) * 2.0 / ROT)
    ang = freq[:, None] * jnp.arange(seq, dtype=jnp.int32).astype(f32)[None, :]
    table = jnp.concatenate([jnp.cos(ang), jnp.sin(ang)])
    own_ang = freq[:, None] * positions.astype(f32)[None, :]
    own_table = jnp.concatenate([jnp.cos(own_ang), jnp.sin(own_ang)])

    attn_in, table = lax.optimization_barrier((attn_in, table))
    send = qkv_forward(ids, attn_in, w_qkv, wq_got, qkv_bias, own_table)
    qkv_head = exchange(send.reshape(2 * heads, 3 * HD, rows))
    dy, dctx = mask_rows(ids, cot_own, cot_sib, cot_got, flip(cot_got, CORE), live2, w_out, quarter)
    w_out_mine = rows_of(w_out, core * quarter, quarter)
    do_head = exchange(dctx)

    attn_t, mlp_t = turn(attn_in, mlp_in)
    do_head = exchange(dctx.reshape(2 * heads, HD, rows))
    y_mlp, d_mlp, up_keep, up_send, down_keep, down_send, gb_up = mlp(
        ids, mlp_in, mlp_t, dy, w_up, wu_got, w_down, b_up.astype(f32)[None, :], chips
    )

    chain_a = (X, ZN, ZF)
    chain_b = (ZN, ZF, X)
    qkv_head, up_send, down_send = lax.optimization_barrier((qkv_head, up_send, down_send))
    down = [down_keep, flip(down_send, chain_a[0])]
    up = [up_keep, flip(up_send, chain_b[0])]

    o_head, lse = attn_fwd(block_map, qkv_head, bq=1024, bk=1024)
    qkv_head, o_head, do_head, down[-1], up[-1] = lax.optimization_barrier((qkv_head, o_head, do_head, down[-1], up[-1]))
    ob = exchange(o_head).reshape(2, quarter, rows)
    down = halve(down, chain_a[1])
    up = halve(up, chain_b[1])
    g_head = attn_bwd(block_map, qkv_head, o_head, do_head, lse, table)
    g_head, ob = lax.optimization_barrier((g_head, ob))
    d_qkv = exchange(g_head).reshape(2, heads, 3 * HD, rows)

    down = add(*halve(down, chain_a[2]))
    up = add(*halve(up, chain_b[2]))
    up = up.reshape(1, 2, up.shape[1] // 2, up.shape[2])
    up_keep = rows_of(up, me, 1, 1)
    up_got = swap(rows_of(up, 1 - me, 1, 1))
    up = ordered(me, up_keep, up_got, axis=1)
    for a, b in zip(chain_a[::-1], chain_b[::-1]):
        down = double(down, a)
        up = double(up, b)
    tot_down = join_rows(ids, down, flip(down, CORE))
    tot_up = join_cols(ids, up, flip(up, CORE))

    def settle(v):
        give = rows_of(v, (1 - core) * own_rows, own_rows, 1).astype(bf16)
        v = rows_of(v, core * own_rows, own_rows, 1) + flip(give, CORE).astype(f32)
        return v[0], swap(v[1].astype(bf16))

    part = jnp.einsum("sct,cd->std", ob, w_out_mine, preferred_element_type=f32) + y_mlp.reshape(2, rows, width).astype(f32)
    part, part_got = settle(part)
    output = (live_own * (x_own.astype(f32) + part + part_got.astype(f32) + bias_out)).astype(bf16)

    v_a, v_b, e = qkv_backward(
        ids, d_qkv, attn_t, x2, norms, w_qkv, wq_got, d_mlp, ob, dy, gb_up, chips
    )
    v_a = [v_a]
    v_b = [v_b]
    for a, b in zip(chain_a, chain_b):
        v_a = halve(v_a, a)
        v_b = halve(v_b, b)
    e_own, e_got = settle(e)
    n3 = 3 * half // (2 * chips)
    size = 2 * n3 + width // (2 * chips)
    tail = []
    for v in (add(*v_a)[0], add(*v_b)[0]):
        extra = v[size:]
        back = swap(jnp.concatenate([rows_of(v, (1 - me) * n3, n3), extra]))
        extra = add(extra, back[n3:])
        tail.append(jnp.concatenate([ordered(me, rows_of(v, me * n3, n3), back[:n3]), v[2 * n3 : size], extra])[None])
    grad_tokens = last(e_own, e_got, x_own, cot_own, live_own)
    cover = [[grad_tokens, output], [tot_down], [tot_up]]
    for k, (a, b) in enumerate(zip(chain_a[::-1], chain_b[::-1])):
        tail = [double(tail[0], a), double(tail[1], b)]
        tail, cover[k] = lax.optimization_barrier((tail, cover[k]))
    mixed = tail
    (grad_tokens, output), (tot_down,), (tot_up,) = cover
    tot_qkv, tot_out, flat = unpack(ids, mixed[0], flip(mixed[0], CORE), mixed[1], flip(mixed[1], CORE), width)
    flat = flat[:, :6].reshape(12 * width)

    def own(start, size):
        return lax.dynamic_slice_in_dim(flat, start + me * size, size)

    gb_out = own(4 * width, half)
    return (
        output[None],
        grad_tokens[None],
        own(0, half),
        own(width, half),
        own(2 * width, half),
        own(3 * width, half),
        tot_qkv,
        own(5 * width, 3 * half),
        tot_out.reshape(half, width),
        gb_out,
        tot_up,
        own(8 * width, 2 * hid),
        tot_down,
        gb_out,
    )


def solution(mesh):
    placed = (
        P("wsh", "ctx", None),
        P("wsh"),
        P("wsh"),
        P("wsh"),
        P("wsh"),
        P("wsh", None),
        P("wsh"),
        P("wsh", None),
        P("wsh"),
        P("wsh", None),
        P("wsh"),
        P("wsh", None),
        P("wsh"),
        P("wsh"),
        P(),
        P("wsh", "ctx", None),
    )
    body = fast_shards if fast_fits(mesh) else shards
    return jax.shard_map(
        body,
        mesh=mesh,
        in_specs=placed,
        out_specs=(
            P("wsh", "ctx", None),
            P("wsh", "ctx", None),
            P("wsh"),
            P("wsh"),
            P("wsh"),
            P("wsh"),
            P("wsh", None),
            P("wsh"),
            P("wsh", None),
            P("wsh"),
            P("wsh", None),
            P("wsh"),
            P("wsh", None),
            P("wsh"),
        ),
        check_vma=False,
    )
```
